32 devices in a mesh: dp: 16 (over z, y, core), tensor: 2 (over x).
Axes of the slice: x: 2, y: 2, z: 4, core: 2. Of those that a mesh axis runs over, the one named last changes fastest.
Arguments:
- tokens: bfloat16 [24576, 896], P('dp'), may hold values from -6 to 6
- cotangent: bfloat16 [24576, 896], P('dp'), may hold values from -6 to 6
- order: int32 [16, 1536], P('dp'), may hold values from 0 to 1535, each once within a row
- lengths: int32 [16, 3], P('dp'), may hold values from 1 to 1024, 1536 in all within a row
- adapter_ids: int32 [16, 3], P('dp'), may hold values from 0 to 7
- norm_gains: bfloat16 [2, 896], replicated, may hold values from 0.099609375 to 1.8984375
- w_query: bfloat16 [896, 896], P(None, 'tensor'), may hold values from -0.25 to 0.25
- w_key: bfloat16 [896, 128], P(None, 'tensor'), may hold values from -0.25 to 0.25
- w_value: bfloat16 [896, 128], P(None, 'tensor'), may hold values from -0.1875 to 0.1875
- b_query: bfloat16 [896], P('tensor'), may hold values from -3 to 3
- b_key: bfloat16 [128], P('tensor'), may hold values from -3 to 3
- b_value: bfloat16 [128], P('tensor'), may hold values from -3 to 3
- w_out: bfloat16 [896, 896], P('tensor'), may hold values from -0.25 to 0.25
- w_gate: bfloat16 [896, 4864], P(None, 'tensor'), may hold values from -0.1875 to 0.1875
- w_up: bfloat16 [896, 4864], P(None, 'tensor'), may hold values from -0.1875 to 0.1875
- w_down: bfloat16 [4864, 896], P('tensor'), may hold values from -0.078125 to 0.078125
- adapters: float32 [22912, 128], P(('dp', 'tensor'))
- first_moment: float32 [22912, 128], P(('dp', 'tensor'))
- second_moment: float32 [22912, 128], P(('dp', 'tensor')), as said below
Outputs:
- layer_output: bfloat16 [24576, 896], P('dp')
- input_grad: bfloat16 [24576, 896], P('dp')
- adapter_grad: float32 [22912, 128], P(('dp', 'tensor'))
- first_moment_new: float32 [22912, 128], P(('dp', 'tensor'))
- second_moment_new: float32 [22912, 128], P(('dp', 'tensor'))
- adapters_new: float32 [22912, 128], P(('dp', 'tensor'))
- adapter_copy: bfloat16 [22912, 128], P(('dp', 'tensor'))
The draws below stay inside these ranges and needn't reach their ends.
Inputs may be any that keep to these rules, and one draw needn't show every extreme that they name: Each row of order is a permutation of 0 to 1535. Each row of lengths sums to 1536 and holds a sequence of exactly 1024 tokens. `second_moment`: positive.
All inputs are finite; a program needn't handle non-finite values.
Results may differ from the reference program's by a relative error of at most 0.017.
Values may be sent and summed in bfloat16 or wider, within the bound.
A program may use at most 256 MiB of HBM per device.

```python
import math
import jax
import jax.numpy as jnp
import numpy as np
from jax import lax

MODEL_DIMENSION = 896
QUERY_HEADS = 14
KEY_VALUE_HEADS = 2
HEAD_DIMENSION = 64
FEED_HIDDEN = 4864
EA = 8
RANK = 16
LMAX = 1024
QUERY_BLOCK_ROWS = 512
STEP = 3
TOK_DEV = 1536
TOKENS = 24576
SEQ_DEV = 3
QW = 896
KVW = 128
CAT = 22912
N_DP = 16


ADAPTER_SCALE = 2.0


SECOND_DECAY = 0.6


BASE_TARGET = 0.64


KEY_TARGET = 0.9


def section_terms():
    query_width = QUERY_HEADS * HEAD_DIMENSION
    pair_width = KEY_VALUE_HEADS * HEAD_DIMENSION
    hidden_ratio = math.sqrt(MODEL_DIMENSION / FEED_HIDDEN)
    shape_list = [(MODEL_DIMENSION, query_width), (MODEL_DIMENSION, pair_width), (MODEL_DIMENSION, pair_width), (query_width, MODEL_DIMENSION), (MODEL_DIMENSION, FEED_HIDDEN), (MODEL_DIMENSION, FEED_HIDDEN), (FEED_HIDDEN, MODEL_DIMENSION)]
    signal_sizes = [1.2, 3.0, 1.9, 0.74, 0.55 * hidden_ratio, 0.6 * hidden_ratio, 0.6]
    targets = [BASE_TARGET, KEY_TARGET, BASE_TARGET, BASE_TARGET, BASE_TARGET, BASE_TARGET, BASE_TARGET]
    return [(shape_list[number][0], shape_list[number][1], signal_sizes[number], targets[number]) for number in range(7)]


def adapter_rows():
    pieces = []
    for fan_in, fan_out, signal_size, target in section_terms():
        amplitude = target / signal_size
        pieces.append(jnp.full((fan_in,), amplitude / math.sqrt(fan_in), jnp.float32))
        pieces.append(jnp.full((fan_out,), amplitude / math.sqrt(fan_out), jnp.float32))
    return jnp.concatenate(pieces)[:, None]


def moment_scale():
    per_adapter = math.sqrt(TOKENS / EA)
    pieces = []
    for fan_in, fan_out, signal_size, target in section_terms():
        pieces.append(jnp.full((fan_in + fan_out,), ADAPTER_SCALE * target * per_adapter, jnp.float32))
    return jnp.concatenate(pieces)[:, None]


def draw_adapters(key, part):
    normal_draw = jax.random.normal(jax.random.fold_in(key, 303), (CAT, EA * RANK), jnp.float32)
    return adapter_rows() * jnp.clip(normal_draw, -6.0, 6.0)


def draw_first_moment(key, part):
    normal_draw = jax.random.normal(jax.random.fold_in(key, 101), (CAT, EA * RANK), jnp.float32)
    return moment_scale() * normal_draw


def draw_second_moment(key, part):
    spread_draw = jax.random.uniform(jax.random.fold_in(key, 202), (CAT, EA * RANK), jnp.float32, 0.0, math.log(4.0))
    decay_ratio = (1.0 - SECOND_DECAY) / SECOND_DECAY
    scale_rows = moment_scale()
    return decay_ratio * scale_rows * scale_rows * jnp.exp(spread_draw)


def with_ends(drawn, own_key, smallest, largest):
    longest = drawn.shape.index(max(drawn.shape))
    spots = []
    for shift in (0, 1):
        where = [jax.random.randint(jax.random.fold_in(own_key, axis), (), 0, length) for axis, length in enumerate(drawn.shape)]
        where[longest] = (where[longest] + shift) % drawn.shape[longest]
        spots.append(tuple(where))
    return drawn.at[spots[0]].set(smallest).at[spots[1]].set(largest)


def shard_levels(key, shape, split, smallest, top_value):
    def one(axis_at, parts):
        draws = jax.random.uniform(jax.random.fold_in(jax.random.fold_in(key, 6), axis_at), (parts,), jnp.float32, smallest / len(split), top_value / len(split))
        return jnp.repeat(jnp.exp(draws), shape[axis_at] // parts).reshape((-1,) + (1,) * (len(shape) - axis_at - 1))

    level = one(*split[0])
    for cut in split[1:]:
        level = level * one(*cut)
    return level


def length_profile(count, total, bound, skew):
    weights = [(1 << 20) // math.isqrt(rank ** skew) + 1 for rank in range(2, count + 1)]
    spare, holding = total - bound - (count - 1), [1] * (count - 1)
    while spare > 0:
        movable = [i for i in range(count - 1) if holding[i] < bound]
        pool, budget = sum([weights[i] for i in movable]), spare
        for i in movable:
            more = min(bound - holding[i], max(1, budget * weights[i] // pool), spare)
            holding[i] = holding[i] + more
            spare = spare - more
    return np.array([bound] + holding)


def ragged_sizes(stream_key, number_of, total, reach, slope):
    if number_of == 2:
        one = jax.random.randint(stream_key, (), max(1, total - reach), min(reach, total - 1) + 1)
        return jnp.stack([one, total - one])
    sizes = jnp.asarray(length_profile(number_of, total, reach, slope), jnp.int32)
    pairs = (number_of - 1) // 2
    source_of, taker = sizes[1:1 + 2 * pairs:2], sizes[2:2 + 2 * pairs:2]
    room = jnp.minimum(source_of - 1, reach - taker)
    shifted = jax.random.randint(jax.random.fold_in(stream_key, 1), (pairs,), 0, 1 << 20) % (room + 1)
    sizes = sizes.at[1:1 + 2 * pairs:2].set(source_of - shifted).at[2:2 + 2 * pairs:2].set(taker + shifted)
    return sizes[jax.random.permutation(jax.random.fold_in(stream_key, 2), number_of)]


def bell_draw(key, extent, width, bound, cuts=(), kind=jnp.bfloat16):
    drawn = width * jax.random.normal(key, extent, jnp.float32)
    if cuts:
        drawn = drawn * shard_levels(key, extent, cuts, -0.22, 0.18)
    return jnp.clip(drawn, -bound, bound).astype(kind)


def setup_inputs(seed: int = 0) -> dict:
    key_list = jax.random.split(jax.random.key(seed), 20)
    return {
        "tokens": bell_draw(key_list[0], (TOKENS, MODEL_DIMENSION), 1.0, 6.0, ((0, 16),)),
        "cotangent": bell_draw(key_list[1], (TOKENS, MODEL_DIMENSION), 1.0, 6.0, ((0, 16),)),
        "order": jax.vmap(lambda own: jax.random.permutation(own, TOK_DEV))(jax.random.split(key_list[2], N_DP)).reshape((N_DP, TOK_DEV)).astype(jnp.int32),
        "lengths": jax.vmap(lambda own: ragged_sizes(own, SEQ_DEV, TOK_DEV, LMAX, 2))(jax.random.split(key_list[3], N_DP)).reshape((N_DP, SEQ_DEV)).astype(jnp.int32),
        "adapter_ids": with_ends(jax.random.randint(key_list[4], (N_DP, SEQ_DEV), 0, EA), jax.random.fold_in(key_list[4], 1), 0, EA - 1).astype(jnp.int32),
        "norm_gains": jnp.clip(1.0 + 0.18 * jax.random.normal(key_list[5], (2, MODEL_DIMENSION), jnp.float32), 0.099609375, 1.8984375).astype(jnp.bfloat16),
        "w_query": bell_draw(key_list[6], (MODEL_DIMENSION, QW), (MODEL_DIMENSION // 2) ** -0.5, 0.25, ((1, 2),)),
        "w_key": bell_draw(key_list[7], (MODEL_DIMENSION, KVW), (MODEL_DIMENSION // 2) ** -0.5, 0.25, ((1, 2),)),
        "w_value": bell_draw(key_list[8], (MODEL_DIMENSION, KVW), MODEL_DIMENSION ** -0.5, 0.1875, ((1, 2),)),
        "b_query": bell_draw(key_list[9], (QW,), 0.5, 3.0, ((0, 2),)),
        "b_key": bell_draw(key_list[10], (KVW,), 0.5, 3.0, ((0, 2),)),
        "b_value": bell_draw(key_list[11], (KVW,), 0.5, 3.0, ((0, 2),)),
        "w_out": bell_draw(key_list[12], (QW, MODEL_DIMENSION), (QW // 2) ** -0.5, 0.25, ((0, 2),)),
        "w_gate": bell_draw(key_list[13], (MODEL_DIMENSION, FEED_HIDDEN), MODEL_DIMENSION ** -0.5, 0.1875, ((1, 2),)),
        "w_up": bell_draw(key_list[14], (MODEL_DIMENSION, FEED_HIDDEN), MODEL_DIMENSION ** -0.5, 0.1875, ((1, 2),)),
        "w_down": bell_draw(key_list[15], (FEED_HIDDEN, MODEL_DIMENSION), FEED_HIDDEN ** -0.5, 0.078125, ((0, 2),)),
        "adapters": draw_adapters(jax.random.fold_in(key_list[19], 71), 0),
        "first_moment": draw_first_moment(jax.random.fold_in(key_list[19], 71), 0),
        "second_moment": draw_second_moment(jax.random.fold_in(key_list[19], 71), 0),
    }


ADAPTER_SCALE = 2.0
NORM_EPS = 1e-06
ROPE_BASE = 1000000.0
BETA_ONE = 0.5
BETA_TWO = 0.6
LEARN_RATE = 0.04
WEIGHT_DECAY = 0.01
ADAM_EPS = 1e-08
MASKED_SCORE = -1e+30
FULL_PRECISION = lax.Precision.HIGHEST

@jax.custom_vjp
def low_rank_result(v):
    return lax.optimization_barrier(v.astype(jnp.bfloat16)).astype(jnp.float32)

@jax.custom_vjp
def low_back(v):
    return v

def low_keep(v):
    return (low_rank_result(v), None)

def low_pass(kept, grad):
    return (grad,)

def back_keep(v):
    return (v, None)

def back_low(kept, grad):
    return (low_rank_result(grad),)
low_rank_result.defvjp(low_keep, low_pass)
low_back.defvjp(back_keep, back_low)

def matmul(left, right):
    return jnp.dot(left, right, precision=FULL_PRECISION)

def section_list(model_width, query_width, pair_width, hidden_width):
    return [(model_width, query_width), (model_width, pair_width), (model_width, pair_width), (query_width, model_width), (model_width, hidden_width), (model_width, hidden_width), (hidden_width, model_width)]

def section_row_list(packed_rows, shape_list):
    pieces = []
    cursor = 0
    for fan_in, fan_out in shape_list:
        pieces.append((packed_rows[cursor:cursor + fan_in], packed_rows[cursor + fan_in:cursor + fan_in + fan_out]))
        cursor = cursor + fan_in + fan_out
    return pieces

def rms_scale(values, gain):
    return values * lax.rsqrt(lax.optimization_barrier(jnp.mean(values * values, axis=-1, keepdims=True)) + NORM_EPS) * gain

def rotate_pairs(values, cosine_lookup, sine_lookup):
    half_size = values.shape[-1] // 2
    turned = jnp.concatenate([-values[..., half_size:], values[..., :half_size]], axis=-1)
    return values * cosine_lookup + turned * sine_lookup

def token_tables(lengths_row, adapter_row, count_of_rows):
    seq_ends = jnp.cumsum(lengths_row).astype(jnp.int32)
    starts = (seq_ends - lengths_row).astype(jnp.int32)
    places = jnp.arange(count_of_rows, dtype=jnp.int32)
    member = ((places[:, None] >= starts[None, :]) & (places[:, None] < seq_ends[None, :])).astype(jnp.int32)
    seq_index = jnp.arange(lengths_row.shape[0], dtype=jnp.int32)
    segment = lax.optimization_barrier(jnp.sum(member * seq_index[None, :], axis=1)).astype(jnp.int32)
    position = (places - lax.optimization_barrier(jnp.sum(member * starts[None, :], axis=1))).astype(jnp.int32)
    chosen = lax.optimization_barrier(jnp.sum(member * adapter_row[None, :], axis=1)).astype(jnp.int32)
    return (segment, position, chosen)

def rope_tables(position, head_size):
    freq_index = jnp.arange(head_size // 2, dtype=jnp.float32)
    inv_freq = jnp.power(jnp.float32(ROPE_BASE), -2.0 * freq_index / head_size)
    angles = position.astype(jnp.float32)[:, None] * inv_freq[None, :]
    angles = jnp.concatenate([angles, angles], axis=1)
    return (jnp.cos(angles)[:, None, :], jnp.sin(angles)[:, None, :])

def adapter_mask(chosen, rank_all):
    columns = jnp.arange(rank_all, dtype=jnp.int32) // RANK
    return (columns[None, :] == chosen[:, None]).astype(jnp.float32)

def block_forward(residual, packed_rows, frozen, tables):
    norm_gains, w_query, w_key, w_value, b_query, b_key, b_value, w_out, w_gate, w_up, w_down = frozen
    segment, cosine_lookup, sine_lookup, rank_mask = tables
    count_of_rows = residual.shape[0]
    adapter_row_list = section_row_list(low_rank_result(packed_rows), section_list(MODEL_DIMENSION, QUERY_HEADS * HEAD_DIMENSION, KEY_VALUE_HEADS * HEAD_DIMENSION, FEED_HIDDEN))

    def adapted(inputs, number):
        enter_rows, leave_rows = adapter_row_list[number]
        rank_part = low_back(low_rank_result(rank_mask * matmul(inputs, enter_rows)))
        return ADAPTER_SCALE * matmul(rank_part, leave_rows.T)
    normed = low_rank_result(rms_scale(residual, norm_gains[0]))
    query_rows = low_back(matmul(normed, w_query) + b_query + adapted(normed, 0))
    key_vectors = low_back(matmul(normed, w_key) + b_key + adapted(normed, 1))
    value_vectors = low_back(low_rank_result(matmul(normed, w_value) + b_value + adapted(normed, 2)))
    query_rows = low_rank_result(rotate_pairs(query_rows.reshape(count_of_rows, QUERY_HEADS, HEAD_DIMENSION), cosine_lookup, sine_lookup))
    key_vectors = low_rank_result(rotate_pairs(key_vectors.reshape(count_of_rows, KEY_VALUE_HEADS, HEAD_DIMENSION), cosine_lookup, sine_lookup))
    value_vectors = value_vectors.reshape(count_of_rows, KEY_VALUE_HEADS, HEAD_DIMENSION)
    group_width = QUERY_HEADS // KEY_VALUE_HEADS
    query_rows = query_rows.reshape(count_of_rows // QUERY_BLOCK_ROWS, QUERY_BLOCK_ROWS, KEY_VALUE_HEADS, group_width, HEAD_DIMENSION)
    score_scale = HEAD_DIMENSION ** (-0.5)
    key_index = jnp.arange(count_of_rows, dtype=jnp.int32)

    def attend(block_in):
        query_block, row_start = block_in
        query_index = row_start + jnp.arange(QUERY_BLOCK_ROWS, dtype=jnp.int32)
        query_segment = lax.dynamic_slice_in_dim(segment, row_start, QUERY_BLOCK_ROWS)
        allowed = (key_index[None, :] <= query_index[:, None]) & (segment[None, :] == query_segment[:, None])
        scores = low_back(jnp.einsum('qkgd,skd->kgqs', query_block, key_vectors, precision=FULL_PRECISION) * score_scale)
        scores = jnp.where(allowed[None, None], scores, MASKED_SCORE)
        weights = low_rank_result(jax.nn.softmax(scores, axis=-1))
        return jnp.einsum('kgqs,skd->qkgd', weights, value_vectors, precision=FULL_PRECISION)
    firsts = (jnp.arange(count_of_rows // QUERY_BLOCK_ROWS, dtype=jnp.int32) * QUERY_BLOCK_ROWS).astype(jnp.int32)
    attended = lax.map(jax.checkpoint(attend), (query_rows, firsts))
    attended = low_back(low_rank_result(attended.reshape(count_of_rows, QUERY_HEADS * HEAD_DIMENSION)))
    branch = low_back(matmul(attended, w_out) + adapted(attended, 3))
    middle = residual + branch
    normed_two = low_rank_result(rms_scale(middle, norm_gains[1]))
    gate_pre = low_back(matmul(normed_two, w_gate) + adapted(normed_two, 4))
    up_pre = low_back(matmul(normed_two, w_up) + adapted(normed_two, 5))
    hidden = low_rank_result(jax.nn.silu(gate_pre) * up_pre)
    return middle + low_back(matmul(hidden, w_down) + adapted(hidden, 6))

def reference(tokens, cotangent, order, lengths, adapter_ids, norm_gains, w_query, w_key, w_value, b_query, b_key, b_value, w_out, w_gate, w_up, w_down, adapters, first_moment, second_moment):
    piece_rows = TOK_DEV // N_DP
    owner_dev = jnp.arange(N_DP, dtype=jnp.int32)[:, None]
    source = (order // piece_rows * TOK_DEV + owner_dev * piece_rows + order % piece_rows).astype(jnp.int32)
    inputs = tokens.astype(jnp.float32)[source]
    back_rows = cotangent.astype(jnp.float32)[source]
    frozen = tuple((weight.astype(jnp.float32) for weight in (norm_gains, w_query, w_key, w_value, b_query, b_key, b_value, w_out, w_gate, w_up, w_down)))

    def per_block(grad_total, block_in):
        rows_in, rows_back, lengths_row, adapter_row = block_in
        segment, position, chosen = token_tables(lengths_row, adapter_row, TOK_DEV)
        cosine_lookup, sine_lookup = rope_tables(position, HEAD_DIMENSION)
        tables = (segment, cosine_lookup, sine_lookup, adapter_mask(chosen, adapters.shape[1]))
        outputs, pullback = jax.vjp(lambda residual, weights_in: block_forward(residual, weights_in, frozen, tables), rows_in, adapters)
        grad_rows, grad_packed = pullback(rows_back)
        return (grad_total + grad_packed, (outputs.astype(jnp.bfloat16), grad_rows.astype(jnp.bfloat16)))
    zero_grad = jnp.zeros(adapters.shape, jnp.float32)
    adapter_grad, (outs_bal, grads_bal) = lax.scan(per_block, zero_grad, (inputs, back_rows, lengths, adapter_ids))
    flat_rows = source.reshape(-1)
    layer_output = jnp.zeros(tokens.shape, jnp.bfloat16).at[flat_rows].set(outs_bal.reshape(-1, MODEL_DIMENSION))
    input_grad = jnp.zeros(tokens.shape, jnp.bfloat16).at[flat_rows].set(grads_bal.reshape(-1, MODEL_DIMENSION))
    moment_one = BETA_ONE * first_moment + (1.0 - BETA_ONE) * adapter_grad
    moment_two = BETA_TWO * second_moment + (1.0 - BETA_TWO) * adapter_grad * adapter_grad
    corrected_one = moment_one / (1.0 - BETA_ONE ** STEP)
    corrected_two = moment_two / (1.0 - BETA_TWO ** STEP)
    updated = adapters - LEARN_RATE * (corrected_one / (jnp.sqrt(corrected_two) + ADAM_EPS) + WEIGHT_DECAY * adapters)
    return (layer_output, input_grad, adapter_grad, moment_one, moment_two, updated, updated.astype(jnp.bfloat16))
```

```python
import functools

import jax
import jax.numpy as jnp
from jax import lax
from jax.experimental import pallas as pl
from jax.experimental.pallas import tpu as pltpu
from jax.sharding import PartitionSpec as P

HEAD = 64
RANK = 16
STEP = 3

ADAPTER_SCALE = 2.0
NORM_EPS = 1e-06
ROPE_BASE = 1000000.0
BETA_ONE = 0.5
BETA_TWO = 0.6
LEARN_RATE = 0.04
WEIGHT_DECAY = 0.01
ADAM_EPS = 1e-08
MASKED_SCORE = -1e30

LANES = 128
ROW_TILE = 256
QUERY_TILE = 128
KEY_TILE = 256
HIDDEN_TILE = 512

F32 = jnp.float32
BF16 = jnp.bfloat16
I32 = jnp.int32


def nn(left, right):
    return lax.dot_general(left, right, (((1,), (0,)), ((), ())), preferred_element_type=F32)


def nt(left, right):
    return lax.dot_general(left, right, (((1,), (1,)), ((), ())), preferred_element_type=F32)


def tn(left, right):
    return lax.dot_general(left, right, (((0,), (0,)), ((), ())), preferred_element_type=F32)


def lane_iota(shape):
    return lax.broadcasted_iota(I32, shape, 1)


def row_iota(shape):
    return lax.broadcasted_iota(I32, shape, 0)


def whole(array):
    return pl.BlockSpec(array.shape, lambda *_: (0,) * array.ndim)


def row_blocks(array, tile):
    return pl.BlockSpec((tile, array.shape[1]), lambda i, *_: (i, 0))


def rank_mask(adapter_col, width):
    return jnp.where(lane_iota((adapter_col.shape[0], width)) // RANK == adapter_col, 1.0, 0.0)


def turn(values):
    lanes = lane_iota(values.shape) % HEAD
    return jnp.where(
        lanes < HEAD // 2,
        -pltpu.roll(values, LANES - HEAD // 2, 1),
        pltpu.roll(values, HEAD // 2, 1),
    )


def rms(values):
    return lax.rsqrt(jnp.mean(values * values, axis=-1, keepdims=True) + NORM_EPS)


def norm_back(values, gain, grad):
    inverse = rms(values)
    weighted = grad * gain
    return inverse * weighted - values * inverse * inverse * inverse * jnp.mean(
        weighted * values, axis=-1, keepdims=True
    )


def pick_rows(place_col, slots):
    hit = place_col == lane_iota((place_col.shape[0], slots))
    return jnp.where(hit, 1.0, 0.0).astype(BF16)


def place_rows(place_row, slots):
    hit = row_iota((slots, place_row.shape[1])) == place_row
    return jnp.where(hit, 1.0, 0.0).astype(BF16)


def params(**more):
    return pltpu.CompilerParams(vmem_limit_bytes=60 * 1024 * 1024, **more)


def cost(flops, moved):
    return pl.CostEstimate(flops=int(flops), bytes_accessed=int(moved), transcendentals=0)


def project_kernel(
    x_ref, meta_ref, cos_ref, sin_ref, gain_ref, w_ref, bias_ref, bq_ref, bk_ref, bv_ref,
    xs_ref, n_ref, q_ref, kv_ref, z_ref,
):
    rows = meta_ref.shape[0]
    qw, kw = bq_ref.shape[0], bk_ref.shape[0]
    rank = bq_ref.shape[1]
    values = nn(pick_rows(meta_ref[:, 0:1], x_ref.shape[0]), x_ref[...])
    xs_ref[...] = values.astype(BF16)
    normed = (values * rms(values) * gain_ref[...]).astype(BF16)
    n_ref[...] = normed
    base = nn(normed, w_ref[...])
    mask = rank_mask(meta_ref[:, 1:2], rank)
    low = qw + 2 * kw
    lows = [(base[:, low + i * rank : low + (i + 1) * rank] * mask).astype(BF16) for i in range(3)]
    for i in range(3):
        z_ref[:, i * rank : (i + 1) * rank] = lows[i]
    cos, sin = cos_ref[...], sin_ref[...]
    queries = base[:, :qw] + bias_ref[:, :qw] + ADAPTER_SCALE * nt(lows[0], bq_ref[...])
    for pair in range(qw // LANES):
        part = queries[:, pair * LANES : (pair + 1) * LANES]
        turned = (part * cos + turn(part) * sin) * HEAD**-0.5
        q_ref[:, pair * LANES : (pair + 1) * LANES] = turned.astype(BF16)
    keys = base[:, qw : qw + kw] + bias_ref[:, qw : qw + kw] + ADAPTER_SCALE * nt(lows[1], bk_ref[...])
    kv_ref[:, :kw] = (keys * cos + turn(keys) * sin).astype(BF16)
    vals = (
        base[:, qw + kw : low]
        + bias_ref[:, qw + kw : low]
        + ADAPTER_SCALE * nt(lows[2], bv_ref[...])
    )
    kv_ref[:, kw:] = vals.astype(BF16)


def project(x, meta, cos, sin, gain, w_cat, bias, b_q, b_k, b_v):
    rows, width = x.shape
    qw, kw, rank = b_q.shape[0], b_k.shape[0], b_q.shape[1]
    tile = ROW_TILE
    args = (x, meta, cos, sin, gain, w_cat, bias, b_q, b_k, b_v)
    specs = [whole(x), row_blocks(meta, tile), row_blocks(cos, tile), row_blocks(sin, tile)]
    specs += [whole(a) for a in args[4:]]
    outs = [
        jax.ShapeDtypeStruct((rows, width), BF16),
        jax.ShapeDtypeStruct((rows, width), BF16),
        jax.ShapeDtypeStruct((rows, qw), BF16),
        jax.ShapeDtypeStruct((rows, 2 * kw), BF16),
        jax.ShapeDtypeStruct((rows, 3 * rank), BF16),
    ]
    return pl.pallas_call(
        project_kernel,
        grid=(rows // tile,),
        in_specs=specs,
        out_specs=[row_blocks(o, tile) for o in outs],
        out_shape=outs,
        compiler_params=params(),
        cost_estimate=cost(2 * rows * width * (w_cat.shape[1] + rows), 9e6),
        name="project",
    )(*args)


def cotangent_kernel(g_ref, meta_ref, bd_ref, out_ref):
    width = g_ref.shape[1]
    rank = bd_ref.shape[1]
    grad = nn(pick_rows(meta_ref[:, 0:1], g_ref.shape[0]), g_ref[...]).astype(BF16)
    back = ADAPTER_SCALE * nn(grad, bd_ref[...]) * rank_mask(meta_ref[:, 1:2], rank)
    out_ref[:, :width] = grad
    out_ref[:, width:] = back.astype(BF16)


def sort_cotangent(grad, meta, b_down):
    rows, width = grad.shape
    tile = ROW_TILE
    out = jax.ShapeDtypeStruct((rows, width + b_down.shape[1]), BF16)
    return pl.pallas_call(
        cotangent_kernel,
        grid=(rows // tile,),
        in_specs=[whole(grad), row_blocks(meta, tile), whole(b_down)],
        out_specs=row_blocks(out, tile),
        out_shape=out,
        compiler_params=params(),
        cost_estimate=cost(2 * rows * width * (rows + 128), 4e6),
        name="cotangent",
    )(grad, meta, b_down)


def head_groups(heads, kv_heads):
    width = heads // kv_heads
    groups = {}
    for head in range(heads):
        groups.setdefault((head // width, head % 2), []).append(head)
    return [(kv, half, members) for (kv, half), members in sorted(groups.items())]


def spread_heads(tile_f32, kv, half):
    lanes = lane_iota(tile_f32.shape)
    moved = tile_f32 if kv % 2 == half else pltpu.roll(tile_f32, HEAD, 1)
    keep = (lanes >= HEAD) if half else (lanes < HEAD)
    return jnp.where(keep, moved, 0.0).astype(BF16)


def fill_heads(groups, source, keys_ref, values_ref):
    total = keys_ref.shape[1]
    for start in range(0, total, KEY_TILE):
        part = source(start).astype(F32)
        for number, (kv, half, _) in enumerate(groups):
            keys_ref[number, start : start + KEY_TILE, :] = spread_heads(part[:, :LANES], kv, half)
            values_ref[number, start : start + KEY_TILE, :] = spread_heads(
                part[:, LANES:], kv, half
            )


def attend_kernel(
    heads, kv_heads, bounds_ref, q_ref, meta_ref, own_ref, other_ref, column_ref,
    o_ref, log_ref, merged_ref, keys, values, acc, top, total,
):
    step = pl.program_id(0)
    groups = head_groups(heads, kv_heads)
    rows = q_ref.shape[0]

    @pl.when(step == 0)
    def _():
        both = jnp.concatenate([own_ref[...], other_ref[...]], axis=0)

        def merged(start):
            picks = pick_rows(column_ref[start : start + KEY_TILE, :], both.shape[0])
            part = nn(picks, both)
            merged_ref[start : start + KEY_TILE, :] = part.astype(BF16)
            return part

        fill_heads(groups, merged, keys, values)

    acc[...] = jnp.zeros_like(acc)
    total[...] = jnp.zeros_like(total)
    top[...] = jnp.full_like(top, MASKED_SCORE)
    first, last = meta_ref[:, 2:3], meta_ref[:, 3:4]
    offsets = []
    cursor = 0
    for _, _, members in groups:
        offsets.append(cursor)
        cursor += len(members) * rows

    def one_tile(number, carry):
        start = pl.multiple_of(number * KEY_TILE, KEY_TILE)
        index = start + lane_iota((rows, KEY_TILE))
        bias = jnp.where((index >= first) & (index <= last), 0.0, MASKED_SCORE)
        for group, (_, _, members) in enumerate(groups):
            count = len(members)
            span = pl.ds(offsets[group], count * rows)
            stack = jnp.concatenate(
                [q_ref[:, (h // 2) * LANES : (h // 2 + 1) * LANES] for h in members], axis=0
            )
            scores = nt(stack, keys[group, pl.ds(start, KEY_TILE), :])
            scores = scores + jnp.concatenate([bias] * count, axis=0)
            old = top[span, :]
            new = jnp.maximum(old, jnp.max(scores, axis=1, keepdims=True))
            weights = jnp.exp(scores - new)
            shrink = jnp.exp(old - new)
            total[span, :] = total[span, :] * shrink + jnp.sum(weights, axis=1, keepdims=True)
            acc[span, :] = acc[span, :] * shrink + nn(
                weights.astype(BF16), values[group, pl.ds(start, KEY_TILE), :]
            )
            top[span, :] = new
        return carry

    lax.fori_loop(bounds_ref[0, step], bounds_ref[1, step], one_tile, 0)
    pairs = [None] * (heads // 2)
    logs = jnp.zeros((rows, LANES), F32)
    lanes = lane_iota((rows, LANES))
    for group, (_, _, members) in enumerate(groups):
        for at, head in enumerate(members):
            span = pl.ds(offsets[group] + at * rows, rows)
            sums = total[span, :]
            part = acc[span, :] / sums
            logs = jnp.where(lanes == head, top[span, :] + jnp.log(sums), logs)
            pair = head // 2
            pairs[pair] = part if pairs[pair] is None else pairs[pair] + part
    for pair, part in enumerate(pairs):
        o_ref[:, pair * LANES : (pair + 1) * LANES] = part.astype(BF16)
    log_ref[...] = jnp.transpose(logs)[: log_ref.shape[0], :]


def attend(bounds, q, meta, own_kv, other_kv, column, heads, kv_heads):
    rows, qw = q.shape
    tile = QUERY_TILE
    keys = 2 * rows
    groups = len(head_groups(heads, kv_heads))
    outs = [
        jax.ShapeDtypeStruct((rows, qw), BF16),
        jax.ShapeDtypeStruct((16, rows), F32),
        jax.ShapeDtypeStruct((keys, own_kv.shape[1]), BF16),
    ]
    return pl.pallas_call(
        functools.partial(attend_kernel, heads, kv_heads),
        grid_spec=pltpu.PrefetchScalarGridSpec(
            num_scalar_prefetch=1,
            grid=(rows // tile,),
            in_specs=[
                row_blocks(q, tile),
                row_blocks(meta, tile),
                whole(own_kv),
                whole(other_kv),
                whole(column),
            ],
            out_specs=[
                row_blocks(outs[0], tile),
                pl.BlockSpec((16, tile), lambda i, *_: (0, i)),
                whole(outs[2]),
            ],
            scratch_shapes=[
                pltpu.VMEM((groups, keys, LANES), BF16),
                pltpu.VMEM((groups, keys, LANES), BF16),
                pltpu.VMEM((heads * tile, LANES), F32),
                pltpu.VMEM((heads * tile, 1), F32),
                pltpu.VMEM((heads * tile, 1), F32),
            ],
        ),
        out_shape=outs,
        compiler_params=params(),
        cost_estimate=cost(heads * rows * keys * 256, 6e6),
        name="attend",
    )(bounds, q, meta, own_kv, other_kv, column)


def attend_back_kernel(
    heads, kv_heads, bounds_ref, q_ref, g_ref, o_ref, log_ref, metar_ref, cos_ref, sin_ref,
    merged_ref, column_ref,
    gq_ref, own_ref, other_ref, keys, values, dkeys, dvalues, dq, dots,
):
    step = pl.program_id(0)
    groups = head_groups(heads, kv_heads)
    rows = q_ref.shape[0]

    @pl.when(step == 0)
    def _():
        fill_heads(groups, lambda at: merged_ref[at : at + KEY_TILE, :], keys, values)
        dkeys[...] = jnp.zeros_like(dkeys)
        dvalues[...] = jnp.zeros_like(dvalues)

    dq[...] = jnp.zeros_like(dq)
    for pair in range(heads // 2):
        lanes = slice(pair * LANES, (pair + 1) * LANES)
        product = jnp.transpose(g_ref[:, lanes].astype(F32) * o_ref[:, lanes].astype(F32))
        dots[2 * pair : 2 * pair + 1, :] = jnp.sum(product[:HEAD], axis=0, keepdims=True)
        dots[2 * pair + 1 : 2 * pair + 2, :] = jnp.sum(product[HEAD:], axis=0, keepdims=True)
    first, last = metar_ref[2:3, :], metar_ref[3:4, :]

    def one_tile(number, carry):
        start = pl.multiple_of(number * KEY_TILE, KEY_TILE)
        index = start + row_iota((KEY_TILE, rows))
        bias = jnp.where((index >= first) & (index <= last), 0.0, MASKED_SCORE)
        for group, (_, half, members) in enumerate(groups):
            count = len(members)
            span = pl.ds(start, KEY_TILE)
            cut = [slice((h // 2) * LANES, (h // 2 + 1) * LANES) for h in members]
            stack = jnp.concatenate([q_ref[:, c] for c in cut], axis=0)
            grads = jnp.concatenate([g_ref[:, c] for c in cut], axis=0)
            logs = jnp.concatenate([log_ref[h : h + 1, :] for h in members], axis=1)
            drop = jnp.concatenate([dots[h : h + 1, :] for h in members], axis=1)
            key_part = keys[group, span, :]
            scores = nt(key_part, stack) + jnp.concatenate([bias] * count, axis=1)
            weights = jnp.exp(scores - logs)
            change = nt(values[group, span, :], grads)
            dscores = (weights * (change - drop)).astype(BF16)
            dvalues[group, span, :] += nn(weights.astype(BF16), grads)
            dkeys[group, span, :] += nn(dscores, stack)
            back = tn(dscores, key_part)
            for at, head in enumerate(members):
                dq[head // 2, :, :] += back[at * rows : (at + 1) * rows, :]
        return carry

    lax.fori_loop(bounds_ref[0, step], bounds_ref[1, step], one_tile, 0)
    cos, sin = cos_ref[...], sin_ref[...]
    for pair in range(heads // 2):
        grad = dq[pair, :, :] * HEAD**-0.5
        grad = grad * cos - turn(grad) * sin
        gq_ref[:, pair * LANES : (pair + 1) * LANES] = grad.astype(BF16)

    @pl.when(step == pl.num_programs(0) - 1)
    def _():
        total = dkeys.shape[1]

        def join(ref):
            out = None
            for group, (kv, half, _) in enumerate(groups):
                part = ref[group, :, :]
                lanes = lane_iota(part.shape)
                part = jnp.where((lanes >= HEAD) if half else (lanes < HEAD), part, 0.0)
                if kv % 2 != half:
                    part = pltpu.roll(part, HEAD, 1)
                out = part if out is None else out + part
            return out.astype(BF16)

        both = jnp.concatenate([join(dkeys), join(dvalues)], axis=1)
        half_rows = own_ref.shape[0]
        for at in range(0, total, KEY_TILE):
            hit = (at + row_iota((KEY_TILE, total))) == column_ref[...]
            part = nn(jnp.where(hit, 1.0, 0.0).astype(BF16), both).astype(BF16)
            if at < half_rows:
                own_ref[at : at + KEY_TILE, :] = part
            else:
                other_ref[at - half_rows : at - half_rows + KEY_TILE, :] = part


def attend_back(bounds, q, grad, o, logs, meta_rows, cos, sin, merged, column_row, heads, kv_heads):
    rows, qw = q.shape
    tile = QUERY_TILE
    keys, kvw = merged.shape
    groups = len(head_groups(heads, kv_heads))
    outs = [
        jax.ShapeDtypeStruct((rows, qw), BF16),
        jax.ShapeDtypeStruct((rows, kvw), BF16),
        jax.ShapeDtypeStruct((rows, kvw), BF16),
    ]
    return pl.pallas_call(
        functools.partial(attend_back_kernel, heads, kv_heads),
        grid_spec=pltpu.PrefetchScalarGridSpec(
            num_scalar_prefetch=1,
            grid=(rows // tile,),
            in_specs=[
                row_blocks(q, tile),
                row_blocks(grad, tile),
                row_blocks(o, tile),
                pl.BlockSpec((16, tile), lambda i, *_: (0, i)),
                pl.BlockSpec((8, tile), lambda i, *_: (0, i)),
                row_blocks(cos, tile),
                row_blocks(sin, tile),
                whole(merged),
                whole(column_row),
            ],
            out_specs=[row_blocks(outs[0], tile), whole(outs[1]), whole(outs[2])],
            scratch_shapes=[
                pltpu.VMEM((groups, keys, LANES), BF16),
                pltpu.VMEM((groups, keys, LANES), BF16),
                pltpu.VMEM((groups, keys, LANES), F32),
                pltpu.VMEM((groups, keys, LANES), F32),
                pltpu.VMEM((heads // 2, tile, LANES), F32),
                pltpu.VMEM((16, tile), F32),
            ],
        ),
        out_shape=outs,
        compiler_params=params(),
        cost_estimate=cost(heads * rows * keys * 640, 9e6),
        name="attend_back",
    )(bounds, q, grad, o, logs, meta_rows, cos, sin, merged, column_row)


def middle_kernel(o_ref, x_ref, meta_ref, w_ref, b_ref, gain_ref, a_ref, y_ref, xg_ref, xu_ref, z_ref):
    width = x_ref.shape[1]
    rank = b_ref.shape[1]
    mask = rank_mask(meta_ref[:, 1:2], rank)
    base = nn(o_ref[...], w_ref[...])
    low = (base[:, width:] * mask).astype(BF16)
    z_ref[...] = low
    values = x_ref[...].astype(F32) + (base[:, :width] + ADAPTER_SCALE * nt(low, b_ref[...]))
    y_ref[...] = values
    normed = (values * rms(values) * gain_ref[...]).astype(BF16)
    lows = nn(normed, a_ref[...])
    xg_ref[:, :width] = normed
    xu_ref[:, :width] = normed
    xg_ref[:, width:] = (lows[:, :rank] * mask).astype(BF16)
    xu_ref[:, width:] = (lows[:, rank:] * mask).astype(BF16)


def middle(o, x, meta, w_out, b_out, gain, a_pair):
    rows, width = x.shape
    rank = b_out.shape[1]
    tile = ROW_TILE
    outs = [
        jax.ShapeDtypeStruct((rows, width), F32),
        jax.ShapeDtypeStruct((rows, width + rank), BF16),
        jax.ShapeDtypeStruct((rows, width + rank), BF16),
        jax.ShapeDtypeStruct((rows, rank), BF16),
    ]
    return pl.pallas_call(
        middle_kernel,
        grid=(rows // tile,),
        in_specs=[row_blocks(a, tile) for a in (o, x, meta)]
        + [whole(a) for a in (w_out, b_out, gain, a_pair)],
        out_specs=[row_blocks(a, tile) for a in outs],
        out_shape=outs,
        compiler_params=params(),
        cost_estimate=cost(2 * rows * width * 1400, 12e6),
        name="middle",
    )(o, x, meta, w_out, b_out, gain, a_pair)


def finish_kernel(ya_ref, yb_ref, y1_ref, dy_ref, meta_ref, metar_ref, b_ref, out_ref, gb_ref, acc, gacc):
    step = pl.program_id(0)
    width = y1_ref.shape[1]
    rank = b_ref.shape[1]

    @pl.when(step == 0)
    def _():
        acc[...] = jnp.zeros_like(acc)
        gacc[...] = jnp.zeros_like(gacc)

    mask = rank_mask(meta_ref[:, 1:2], rank)
    low = ((ya_ref[:, width:] + yb_ref[:, width:]) * mask).astype(BF16)
    values = y1_ref[...] + (
        (ya_ref[:, :width] + yb_ref[:, :width]) + ADAPTER_SCALE * nt(low, b_ref[...])
    )
    acc[...] += nn(place_rows(metar_ref[0:1, :], acc.shape[0]), values.astype(BF16))
    gacc[...] += ADAPTER_SCALE * tn(dy_ref[:, :width], low)

    @pl.when(step == pl.num_programs(0) - 1)
    def _():
        out_ref[...] = acc[...].astype(BF16)
        gb_ref[...] = gacc[...].astype(gb_ref.dtype)


def finish(y_first, y_second, y1, dy, meta, meta_rows, b_down):
    rows, width = y1.shape
    rank = b_down.shape[1]
    tile = ROW_TILE
    outs = [
        jax.ShapeDtypeStruct((rows, width), BF16),
        jax.ShapeDtypeStruct((width, rank), BF16),
    ]
    return pl.pallas_call(
        finish_kernel,
        grid=(rows // tile,),
        in_specs=[row_blocks(a, tile) for a in (y_first, y_second, y1, dy, meta)]
        + [pl.BlockSpec((8, tile), lambda i: (0, i)), whole(b_down)],
        out_specs=[whole(a) for a in outs],
        out_shape=outs,
        scratch_shapes=[pltpu.VMEM((rows, width), F32), pltpu.VMEM((width, rank), F32)],
        compiler_params=params(),
        cost_estimate=cost(2 * rows * width * (rows + 256), 13e6),
        name="finish",
    )(y_first, y_second, y1, dy, meta, meta_rows, b_down)


def middle_back_kernel(
    da_ref, db_ref, y1_ref, dy_ref, xg_ref, o_ref, z_ref, meta_ref, a_ref, b_ref, w_ref, gain_ref,
    dy1_ref, dar_ref, ga_ref, gbo_ref, gao_ref, acc_a, acc_bo, acc_ao,
):
    step = pl.program_id(0)
    width = y1_ref.shape[1]
    rank = b_ref.shape[1]

    @pl.when(step == 0)
    def _():
        acc_a[...] = jnp.zeros_like(acc_a)
        acc_bo[...] = jnp.zeros_like(acc_bo)
        acc_ao[...] = jnp.zeros_like(acc_ao)

    mask = rank_mask(meta_ref[:, 1:2], rank)
    back = (da_ref[:, width:] + db_ref[:, width:]) * jnp.concatenate([mask, mask], axis=1)
    back = back.astype(BF16)
    grad = da_ref[:, :width] + db_ref[:, :width] + nt(back, a_ref[...])
    values = y1_ref[...]
    dy1 = dy_ref[:, :width].astype(F32) + norm_back(values, gain_ref[...], grad)
    dy1_ref[...] = dy1
    low_grad = dy1.astype(BF16)
    back_out = (ADAPTER_SCALE * nn(low_grad, b_ref[...]) * mask).astype(BF16)
    both = jnp.concatenate([low_grad, back_out], axis=1)
    dar_ref[...] = nt(both, w_ref[...]).astype(BF16)
    acc_a[...] += tn(xg_ref[:, :width], back)
    acc_bo[...] += ADAPTER_SCALE * tn(low_grad, z_ref[...])
    acc_ao[...] += tn(o_ref[...], back_out)

    @pl.when(step == pl.num_programs(0) - 1)
    def _():
        ga_ref[...] = acc_a[...].astype(ga_ref.dtype)
        gbo_ref[...] = acc_bo[...].astype(gbo_ref.dtype)
        gao_ref[...] = acc_ao[...].astype(gao_ref.dtype)


def middle_back(d_first, d_second, y1, dy, xg, o, z, meta, a_pair, b_out, w_out, gain):
    rows, width = y1.shape
    rank = b_out.shape[1]
    qw = o.shape[1]
    tile = ROW_TILE
    outs = [
        jax.ShapeDtypeStruct((rows, width), F32),
        jax.ShapeDtypeStruct((rows, qw), BF16),
        jax.ShapeDtypeStruct((width, 2 * rank), BF16),
        jax.ShapeDtypeStruct((width, rank), BF16),
        jax.ShapeDtypeStruct((qw, rank), BF16),
    ]
    return pl.pallas_call(
        middle_back_kernel,
        grid=(rows // tile,),
        in_specs=[row_blocks(a, tile) for a in (d_first, d_second, y1, dy, xg, o, z, meta)]
        + [whole(a) for a in (a_pair, b_out, w_out, gain)],
        out_specs=[row_blocks(a, tile) for a in outs[:2]] + [whole(a) for a in outs[2:]],
        out_shape=outs,
        scratch_shapes=[
            pltpu.VMEM((width, 2 * rank), F32),
            pltpu.VMEM((width, rank), F32),
            pltpu.VMEM((qw, rank), F32),
        ],
        compiler_params=params(),
        cost_estimate=cost(2 * rows * width * 1900, 20e6),
        name="middle_back",
    )(d_first, d_second, y1, dy, xg, o, z, meta, a_pair, b_out, w_out, gain)


def feed_kernel(
    valid, xg_ref, xu_ref, dy_ref, wg_ref, wu_ref, wd_ref, bg_ref, bu_ref, ad_ref,
    y_ref, d_ref, gbg_ref, gbu_ref, gad_ref, wga, wua, wda,
):
    step = pl.program_id(0)
    width = wd_ref.shape[1]
    tile = wd_ref.shape[0]
    rank = ad_ref.shape[1]
    rows = xg_ref.shape[0]
    wga[:width, :] = wg_ref[...]
    wua[:width, :] = wu_ref[...]
    wga[width:, :] = jnp.transpose(bg_ref[...].astype(F32) * ADAPTER_SCALE).astype(BF16)
    wua[width:, :] = jnp.transpose(bu_ref[...].astype(F32) * ADAPTER_SCALE).astype(BF16)
    wda[:, :width] = wd_ref[...]
    wda[:, width:] = ad_ref[...]
    steps = pl.cdiv(valid, tile)
    rest = valid - (steps - 1) * tile
    if rest < tile:

        @pl.when(step == steps - 1)
        def _():
            wga[:, rest:] = jnp.zeros((width + rank, tile - rest), BF16)
            wua[:, rest:] = jnp.zeros((width + rank, tile - rest), BF16)
            wda[rest:, :] = jnp.zeros((tile - rest, width + rank), BF16)

    @pl.when(step == 0)
    def _():
        y_ref[...] = jnp.zeros_like(y_ref)
        d_ref[...] = jnp.zeros_like(d_ref)

    hids, dgs, dus = [], [], []
    for at in range(0, rows, ROW_TILE):
        span = slice(at, at + ROW_TILE)
        gate = nn(xg_ref[span, :], wga[...])
        up = nn(xu_ref[span, :], wua[...])
        dhid = nt(dy_ref[span, :], wda[...])
        sig = 1.0 / (1.0 + jnp.exp(-gate))
        silu = gate * sig
        hid = (silu * up).astype(BF16)
        dg = (dhid * up * (sig * (1.0 + gate * (1.0 - sig)))).astype(BF16)
        du = (dhid * silu).astype(BF16)
        y_ref[span, :] += nn(hid, wda[...])
        dga = nt(dg, wga[...])
        dua = nt(du, wua[...])
        d_ref[span, :width] += dga[:, :width] + dua[:, :width]
        d_ref[span, width : width + rank] += dga[:, width:]
        d_ref[span, width + rank :] += dua[:, width:]
        hids.append(hid)
        dgs.append(dg)
        dus.append(du)
    hid, dg, du = (jnp.concatenate(v, axis=0) for v in (hids, dgs, dus))
    gbg_ref[...] = (ADAPTER_SCALE * tn(dg, xg_ref[:, width:])).astype(gbg_ref.dtype)
    gbu_ref[...] = (ADAPTER_SCALE * tn(du, xu_ref[:, width:])).astype(gbu_ref.dtype)
    gad_ref[...] = tn(hid, dy_ref[:, width:]).astype(gad_ref.dtype)


def feed(xg, xu, dy, w_gate, w_up, w_down, b_gate, b_up, a_down):
    rows = xg.shape[0]
    hidden, width = w_down.shape
    rank = a_down.shape[1]
    tile = HIDDEN_TILE
    across = pl.BlockSpec((width, tile), lambda i: (0, i))
    down = pl.BlockSpec((tile, width), lambda i: (i, 0))
    thin = pl.BlockSpec((tile, rank), lambda i: (i, 0))
    outs = [
        jax.ShapeDtypeStruct((rows, width + rank), F32),
        jax.ShapeDtypeStruct((rows, width + 2 * rank), F32),
        jax.ShapeDtypeStruct((hidden, rank), BF16),
        jax.ShapeDtypeStruct((hidden, rank), BF16),
        jax.ShapeDtypeStruct((hidden, rank), BF16),
    ]
    return pl.pallas_call(
        functools.partial(feed_kernel, hidden),
        grid=(pl.cdiv(hidden, tile),),
        in_specs=[whole(xg), whole(xu), whole(dy), across, across, down, thin, thin, thin],
        out_specs=[whole(outs[0]), whole(outs[1]), thin, thin, thin],
        out_shape=outs,
        scratch_shapes=[
            pltpu.VMEM((width + rank, tile), BF16),
            pltpu.VMEM((width + rank, tile), BF16),
            pltpu.VMEM((tile, width + rank), BF16),
        ],
        compiler_params=params(),
        cost_estimate=cost(2 * rows * hidden * (6 * width + 9 * rank), 30e6),
        name="feed",
    )(xg, xu, dy, w_gate, w_up, w_down, b_gate, b_up, a_down)


def input_kernel(
    gq_ref, own_ref, got_ref, x_ref, n_ref, z_ref, dy1_ref, meta_ref, metar_ref, cos_ref, sin_ref,
    gain_ref, w_ref, bq_ref, bk_ref, bv_ref,
    out_ref, ga_ref, gb_ref, acc, acc_a, acc_b,
):
    step = pl.program_id(0)
    qw, kw, rank = bq_ref.shape[0], bk_ref.shape[0], bq_ref.shape[1]

    @pl.when(step == 0)
    def _():
        acc[...] = jnp.zeros_like(acc)
        acc_a[...] = jnp.zeros_like(acc_a)
        acc_b[...] = jnp.zeros_like(acc_b)

    mask = rank_mask(meta_ref[:, 1:2], rank)
    both = own_ref[...].astype(F32) + got_ref[...].astype(F32)
    dk = both[:, :kw]
    gq = gq_ref[...]
    gk = (dk * cos_ref[...] - turn(dk) * sin_ref[...]).astype(BF16)
    gv = both[:, kw:].astype(BF16)
    backs = [
        (ADAPTER_SCALE * nn(g, b[...]) * mask).astype(BF16)
        for g, b in ((gq, bq_ref), (gk, bk_ref), (gv, bv_ref))
    ]
    grads = jnp.concatenate([gq, gk, gv] + backs, axis=1)
    dn = nt(grads, w_ref[...])
    values = x_ref[...].astype(F32)
    dx = dy1_ref[...] + norm_back(values, gain_ref[...], dn)
    acc[...] += nn(place_rows(metar_ref[0:1, :], acc.shape[0]), dx.astype(BF16))
    acc_a[...] += tn(n_ref[...], jnp.concatenate(backs, axis=1))
    low = z_ref[...]
    acc_b[:qw, :] += tn(gq, low[:, :rank])
    acc_b[qw : qw + kw, :] += tn(gk, low[:, rank : 2 * rank])
    acc_b[qw + kw :, :] += tn(gv, low[:, 2 * rank :])

    @pl.when(step == pl.num_programs(0) - 1)
    def _():
        out_ref[...] = acc[...].astype(BF16)
        ga_ref[...] = acc_a[...].astype(ga_ref.dtype)
        gb_ref[...] = (ADAPTER_SCALE * acc_b[...]).astype(gb_ref.dtype)


def input_back(gq, own, got, x, n1, z, dy1, meta, meta_rows, cos, sin, gain, w_cat, b_q, b_k, b_v):
    rows, width = x.shape
    qw, kw, rank = b_q.shape[0], b_k.shape[0], b_q.shape[1]
    tile = ROW_TILE
    outs = [
        jax.ShapeDtypeStruct((rows, width), BF16),
        jax.ShapeDtypeStruct((width, 3 * rank), BF16),
        jax.ShapeDtypeStruct((qw + 2 * kw, rank), BF16),
    ]
    return pl.pallas_call(
        input_kernel,
        grid=(rows // tile,),
        in_specs=[row_blocks(a, tile) for a in (gq, own, got, x, n1, z, dy1, meta)]
        + [pl.BlockSpec((8, tile), lambda i: (0, i))]
        + [row_blocks(a, tile) for a in (cos, sin)]
        + [whole(a) for a in (gain, w_cat, b_q, b_k, b_v)],
        out_specs=[whole(a) for a in outs],
        out_shape=outs,
        scratch_shapes=[
            pltpu.VMEM((rows, width), F32),
            pltpu.VMEM((width, 3 * rank), F32),
            pltpu.VMEM((qw + 2 * kw, rank), F32),
        ],
        compiler_params=params(),
        cost_estimate=cost(2 * rows * width * 2900, 14e6),
        name="input_back",
    )(gq, own, got, x, n1, z, dy1, meta, meta_rows, cos, sin, gain, w_cat, b_q, b_k, b_v)


def row_tables(order_row, lengths_row, adapter_row, part, parts, each):
    total = order_row.shape[0]
    piece = each // parts
    local = total // parts
    places = jnp.arange(total, dtype=I32)
    own = (order_row % each) // piece == part
    slot = (order_row // each) * piece + order_row % piece
    upto = jnp.sum((own[None, :] & (places[None, :] <= places[:, None])).astype(I32), axis=1)
    column = jnp.where(own, upto - 1, local + places - upto)
    picks = column[None, :] == jnp.arange(local, dtype=I32)[:, None]
    balanced = jnp.sum(jnp.where(picks, places[None, :], 0), axis=1)
    slots = jnp.sum(jnp.where(picks, slot[None, :], 0), axis=1)
    ends = jnp.cumsum(lengths_row)
    starts = ends - lengths_row
    member = (balanced[:, None] >= starts[None, :]) & (balanced[:, None] < ends[None, :])
    first = jnp.sum(jnp.where(member, starts[None, :], 0), axis=1)
    chosen = jnp.sum(jnp.where(member, adapter_row[None, :], 0), axis=1)
    bounds = jnp.stack(
        [
            first[::QUERY_TILE] // KEY_TILE,
            balanced[QUERY_TILE - 1 :: QUERY_TILE] // KEY_TILE + 1,
        ]
    )
    return slots, chosen, first, balanced, column, bounds


def rope_tables(position):
    freq_index = jnp.arange(HEAD // 2, dtype=F32)
    inv_freq = jnp.power(jnp.float32(ROPE_BASE), -2.0 * freq_index / HEAD)
    angles = position.astype(F32)[:, None] * inv_freq[None, :]
    return (
        jnp.concatenate([jnp.cos(angles)] * 4, axis=1),
        jnp.concatenate([jnp.sin(angles)] * 4, axis=1),
    )


def per_device(
    tokens, cotangent, order, lengths, adapter_ids, norm_gains, w_query, w_key, w_value,
    b_query, b_key, b_value, w_out, w_gate, w_up, w_down, adapters, first_moment, second_moment,
):
    parts = lax.axis_size("tensor")
    part = lax.axis_index("tensor")
    devices = lax.axis_size("dp")
    place = lax.axis_index("dp")
    core = place % 2
    total, width = tokens.shape
    each = total // devices
    piece = each // parts
    local = total // parts
    rank = adapters.shape[1]
    swap = [(i, parts - 1 - i) for i in range(parts)]
    cores = [(i, i ^ 1) for i in range(devices)]
    first_part = part == 0

    def across(values):
        return lax.ppermute(values, "tensor", swap)

    def in_order(mine, theirs, axis):
        return jnp.concatenate(
            [jnp.where(first_part, mine, theirs), jnp.where(first_part, theirs, mine)], axis=axis
        )

    def fetch(values):
        rows = values.shape[0] // 2
        got = across(lax.dynamic_slice_in_dim(values, core * rows, rows, 0))
        more = lax.ppermute(got, "dp", cores)
        return jnp.concatenate(
            [jnp.where(core == 0, got, more), jnp.where(core == 0, more, got)], axis=0
        )

    def receive(values):
        sent = values.reshape(devices, parts, piece, width)
        sent = lax.dynamic_index_in_dim(sent, part, 1, keepdims=False)
        got = lax.all_to_all(sent, "dp", split_axis=0, concat_axis=0, tiled=True)
        return got.reshape(local, width)

    def give_back(values):
        got = lax.all_to_all(
            values.reshape(devices, piece, width), "dp", split_axis=0, concat_axis=0, tiled=True
        )
        theirs = across(got)
        return in_order(got[:, None], theirs[:, None], 1).reshape(total, width)

    moved = receive(tokens)
    moved_back = receive(cotangent)
    small = in_order(
        jnp.concatenate([w_query, w_key, w_value], axis=1)[None],
        across(jnp.concatenate([w_query, w_key, w_value], axis=1))[None],
        0,
    )
    qh, kh = w_query.shape[1], w_key.shape[1]
    w_qkv = [
        jnp.concatenate([small[0, :, a:b], small[1, :, a:b]], axis=1)
        for a, b in ((0, qh), (qh, qh + kh), (qh + kh, qh + 2 * kh))
    ]
    bias = jnp.concatenate([b_query, b_key, b_value])[None].astype(F32)
    bias = in_order(bias, across(bias), 0)
    bias = jnp.concatenate(
        [bias[:, a:b].reshape(1, -1) for a, b in ((0, qh), (qh, qh + kh), (qh + kh, qh + 2 * kh))],
        axis=1,
    )
    copies = lax.all_gather(adapters.astype(BF16), ("dp", "tensor"), axis=0, tiled=True)
    w_out_all = in_order(w_out, across(w_out), 0)
    w_gate_far = fetch(w_gate)
    w_up_far = fetch(w_up)
    w_down_far = fetch(w_down)

    qw, kw, hidden = parts * qh, parts * kh, parts * w_gate.shape[1]
    half = w_gate.shape[1]
    sections = []
    cursor = 0
    for size in (width, qw, width, kw, width, kw, qw, width, width, hidden, width, hidden, hidden, width):
        sections.append(copies[cursor : cursor + size])
        cursor += size
    a_q, b_q, a_k, b_k, a_v, b_v, a_o, b_o, a_g, b_g, a_u, b_u, a_d, b_d = sections

    def near(rows):
        return lax.dynamic_slice_in_dim(rows, part * half, half, 0)

    def far(rows):
        return lax.dynamic_slice_in_dim(rows, (parts - 1 - part) * half, half, 0)

    slots, chosen, first, balanced, column, bounds = row_tables(
        order[0], lengths[0], adapter_ids[0], part, parts, each
    )
    cos, sin = rope_tables(balanced - first)
    meta = jnp.stack([slots, chosen, first, balanced], axis=1)
    meta = jnp.concatenate([meta, jnp.zeros((local, 4), I32)], axis=1)
    meta_rows = meta.T
    gain_one = norm_gains[0:1].astype(F32)
    gain_two = norm_gains[1:2].astype(F32)
    heads, kv_heads = qw // HEAD, kw // HEAD

    w_cat = jnp.concatenate(w_qkv + [a_q, a_k, a_v], axis=1)
    w_out_cat = jnp.concatenate([w_out_all, a_o], axis=1)
    a_pair = jnp.concatenate([a_g, a_u], axis=1)

    xs, n1, q, kv, z = project(moved, meta, cos, sin, gain_one, w_cat, bias, b_q, b_k, b_v)
    other_kv = across(kv)
    dy = sort_cotangent(moved_back, meta, b_d)
    o, logs, merged = attend(bounds, q, meta, kv, other_kv, column[:, None], heads, kv_heads)
    y1, xg, xu, z_out = middle(o, xs, meta, w_out_cat, b_o, gain_two, a_pair)
    y_a, d_a, gbg_a, gbu_a, gad_a = feed(
        xg, xu, dy, w_gate, w_up, w_down, near(b_g), near(b_u), near(a_d)
    )
    y_b, d_b, gbg_b, gbu_b, gad_b = feed(
        xg, xu, dy, w_gate_far, w_up_far, w_down_far, far(b_g), far(b_u), far(a_d)
    )
    out_rows, grad_b_d = finish(y_a, y_b, y1, dy, meta, meta_rows, b_d)
    layer_out = give_back(out_rows)
    dy1, dar, grad_pair, grad_b_o, grad_a_o = middle_back(
        d_a, d_b, y1, dy, xg, o, z_out, meta, a_pair, b_o, w_out_cat, gain_two
    )
    early = jnp.concatenate(
        [
            jnp.zeros((3 * width + qw + 2 * kw, rank), BF16),
            grad_a_o,
            grad_b_o,
            grad_pair[:, :rank],
            in_order(gbg_a, gbg_b, 0),
            grad_pair[:, rank:],
            in_order(gbu_a, gbu_b, 0),
            in_order(gad_a, gad_b, 0),
            grad_b_d,
        ],
        axis=0,
    )
    reduced_early = lax.psum_scatter(early, ("dp", "tensor"), scatter_dimension=0, tiled=True)
    gq, dkv_own, dkv_other = attend_back(
        bounds, q, dar, o, logs, meta_rows, cos, sin, merged, column[None, :], heads, kv_heads
    )
    dkv_got = across(dkv_other)
    dx_rows, grad_a_qkv, grad_b_qkv = input_back(
        gq, dkv_own, dkv_got, xs, n1, z, dy1, meta, meta_rows, cos, sin, gain_one, w_cat,
        b_q, b_k, b_v,
    )
    input_grad = give_back(dx_rows)
    late = jnp.concatenate(
        [
            grad_a_qkv[:, :rank],
            grad_b_qkv[:qw],
            grad_a_qkv[:, rank : 2 * rank],
            grad_b_qkv[qw : qw + kw],
            grad_a_qkv[:, 2 * rank :],
            grad_b_qkv[qw + kw :],
        ],
        axis=0,
    )
    late = lax.psum(late, ("dp", "tensor"))
    own_rows = adapters.shape[0]
    flat = place * parts + part
    late = jnp.concatenate(
        [late, jnp.zeros((copies.shape[0] - late.shape[0], rank), BF16)], axis=0
    )
    reduced_late = lax.dynamic_slice_in_dim(late, flat * own_rows, own_rows, 0)
    reduced = reduced_early.astype(F32) + reduced_late.astype(F32)
    moment_one = BETA_ONE * first_moment + (1.0 - BETA_ONE) * reduced
    moment_two = BETA_TWO * second_moment + (1.0 - BETA_TWO) * reduced * reduced
    corrected_one = moment_one / (1.0 - BETA_ONE**STEP)
    corrected_two = moment_two / (1.0 - BETA_TWO**STEP)
    updated = adapters - LEARN_RATE * (
        corrected_one / (jnp.sqrt(corrected_two) + ADAM_EPS) + WEIGHT_DECAY * adapters
    )
    return (
        layer_out,
        input_grad,
        reduced,
        moment_one,
        moment_two,
        updated,
        updated.astype(BF16),
    )


def solution(mesh):
    both = P(("dp", "tensor"), None)
    rows = P("dp", None)
    return jax.shard_map(
        per_device,
        mesh=mesh,
        in_specs=(rows, rows, rows, rows, rows, P())
        + (P(None, "tensor"),) * 3
        + (P("tensor"),) * 3
        + (P("tensor", None), P(None, "tensor"), P(None, "tensor"), P("tensor", None))
        + (both,) * 3,
        out_specs=(rows, rows) + (both,) * 5,
        check_vma=False,
    )
```

```python
import functools

import jax
import jax.numpy as jnp
from jax import lax
from jax.experimental import pallas as pl
from jax.experimental.pallas import tpu as pltpu
from jax.sharding import PartitionSpec as P

HEAD = 64
RANK = 16
STEP = 3

ADAPTER_SCALE = 2.0
NORM_EPS = 1e-06
ROPE_BASE = 1000000.0
BETA_ONE = 0.5
BETA_TWO = 0.6
LEARN_RATE = 0.04
WEIGHT_DECAY = 0.01
ADAM_EPS = 1e-08
MASKED_SCORE = -1e30
PLANES = 4
MESH = pl.DeviceIdType.MESH

LANES = 128
ROW_TILE = 256
QUERY_TILE = 128
KEY_TILE = 256
HIDDEN_TILE = 512

F32 = jnp.float32
BF16 = jnp.bfloat16
I32 = jnp.int32


def nn(left, right):
    return lax.dot_general(left, right, (((1,), (0,)), ((), ())), preferred_element_type=F32)


def nt(left, right):
    return lax.dot_general(left, right, (((1,), (1,)), ((), ())), preferred_element_type=F32)


def tn(left, right):
    return lax.dot_general(left, right, (((0,), (0,)), ((), ())), preferred_element_type=F32)


def lane_iota(shape):
    return lax.broadcasted_iota(I32, shape, 1)


def row_iota(shape):
    return lax.broadcasted_iota(I32, shape, 0)


def whole(array):
    return pl.BlockSpec(array.shape, lambda *_: (0,) * array.ndim)


def row_blocks(array, tile):
    return pl.BlockSpec((tile, array.shape[1]), lambda i, *_: (i, 0))


def rank_mask(adapter_col, width):
    return jnp.where(lane_iota((adapter_col.shape[0], width)) // RANK == adapter_col, 1.0, 0.0)


def turn(values):
    lanes = lane_iota(values.shape) % HEAD
    return jnp.where(
        lanes < HEAD // 2,
        -pltpu.roll(values, LANES - HEAD // 2, 1),
        pltpu.roll(values, HEAD // 2, 1),
    )


def rms(values):
    return lax.rsqrt(jnp.mean(values * values, axis=-1, keepdims=True) + NORM_EPS)


def norm_back(values, gain, grad):
    inverse = rms(values)
    weighted = grad * gain
    return inverse * weighted - values * inverse * inverse * inverse * jnp.mean(
        weighted * values, axis=-1, keepdims=True
    )


def pick_rows(place_col, slots):
    hit = place_col == lane_iota((place_col.shape[0], slots))
    return jnp.where(hit, 1.0, 0.0).astype(BF16)


def place_rows(place_row, slots):
    hit = row_iota((slots, place_row.shape[1])) == place_row
    return jnp.where(hit, 1.0, 0.0).astype(BF16)


def params(**more):
    return pltpu.CompilerParams(vmem_limit_bytes=60 * 1024 * 1024, **more)


def cost(flops, moved):
    return pl.CostEstimate(flops=int(flops), bytes_accessed=int(moved), transcendentals=0)


def xor_bit(value, bit):
    size = 2**bit
    return value + size * (1 - 2 * lax.rem(value // size, 2))


def subsets(axes):
    out = [()]
    for axis in axes:
        out += [chosen + (axis,) for chosen in out]
    return out


def flip(place, part, axes):
    for axis in axes:
        if axis == "tensor":
            part = 1 - part
        else:
            place = xor_bit(place, axis)
    return place, part


def front_kernel(
    devices, rows_ref, chunk_ref, wq_ref, wo_ref, got_ref, copies_ref, wq_out, wo_out,
    local_sem, tsend, trecv, csend, crecv, wsend, wrecv,
):
    place, part = lax.axis_index("dp"), lax.axis_index("tensor")
    plane = devices // PLANES
    depth, inside = place // plane, lax.rem(place, plane)
    core = lax.rem(place, 2)
    own = 2 * place + part
    barrier = pltpu.get_barrier_semaphore()
    for k in range(1, devices):
        pl.semaphore_signal(
            barrier, inc=1, device_id=(lax.rem(place + k, devices), part), device_id_type=MESH
        )
    pl.semaphore_signal(barrier, inc=1, device_id=(place, 1 - part), device_id_type=MESH)
    pl.semaphore_wait(barrier, devices)

    keep = [
        pltpu.make_async_copy(chunk_ref, copies_ref.at[own], local_sem.at[0]),
        pltpu.make_async_copy(rows_ref.at[place, part], got_ref.at[place], local_sem.at[1]),
    ]
    for copy in keep:
        copy.start()
    sent = []

    def chunk_copy(source, index, number, where):
        return pltpu.make_async_remote_copy(
            src_ref=source,
            dst_ref=copies_ref.at[index],
            send_sem=csend.at[number],
            recv_sem=crecv.at[index],
            device_id=where,
            device_id_type=MESH,
        )

    def send_chunk(source, index, where):
        copy = chunk_copy(source, index, len(sent), where)
        copy.start()
        sent.append(copy)

    def take_chunk(index):
        chunk_copy(chunk_ref, index, 0, (place, 1 - part)).wait_recv()

    def layer(turn):
        return lax.rem(depth + turn, PLANES)

    for turn in (2, 3, 1):
        send_chunk(chunk_ref, own, (layer(turn) * plane + inside, part))

    def weight_copy(ref, out, number, slot, where):
        return pltpu.make_async_remote_copy(
            src_ref=ref.at[slot],
            dst_ref=out.at[slot],
            send_sem=wsend.at[number],
            recv_sem=wrecv.at[number],
            device_id=where,
            device_id_type=MESH,
        )

    direct = [
        weight_copy(wq_ref, wq_out, 0, core, (place, 1 - part)),
        weight_copy(wo_ref, wo_out, 1, core, (place, 1 - part)),
    ]
    for copy in direct:
        copy.start()

    rows_sent = []
    for turn in (2, 3, 1, 0):
        for step in range(plane):
            if turn == 0 and step == 0:
                continue
            target = layer(turn) * plane + lax.rem(inside + step, plane)
            copy = pltpu.make_async_remote_copy(
                src_ref=rows_ref.at[target, part],
                dst_ref=got_ref.at[place],
                send_sem=tsend.at[len(rows_sent)],
                recv_sem=trecv.at[place],
                device_id=(target, part),
                device_id_type=MESH,
            )
            copy.start()
            rows_sent.append((copy, target))

    bits = [2**b for b in range(plane.bit_length() - 1)]
    bits = list(range(len(bits)))[::-1]
    orders = [["tensor"] + bits, bits[:-1] + ["tensor"] + bits[-1:]]
    relayed = []
    for stage in range(len(bits) + 1):
        for turn in (0, 1, 2, 3):
            order = orders[turn % 2]
            origin = layer(turn) * plane + inside
            where = flip(place, part, [order[stage]])
            for chosen in subsets(order[:stage]):
                at, side = flip(origin, part, chosen)
                index = 2 * at + side
                if turn == 0 and not chosen:
                    send_chunk(chunk_ref, index, where)
                    continue
                if stage == 0 or order[stage - 1] in chosen:
                    take_chunk(index)
                send_chunk(copies_ref.at[index], index, where)
        if stage == 0:
            partner = (xor_bit(place, 0), part)
            for number, (ref, out) in enumerate(((wq_ref, wq_out), (wo_ref, wo_out))):
                direct[number].wait_recv()
                copy = weight_copy(out, out, 2 + number, core, partner)
                copy.start()
                relayed.append(copy)
    for turn in (0, 1, 2, 3):
        order = orders[turn % 2]
        origin = layer(turn) * plane + inside
        for chosen in subsets(order):
            if order[-1] in chosen:
                at, side = flip(origin, part, chosen)
                take_chunk(2 * at + side)
    for number, (ref, out) in enumerate(((wq_ref, wq_out), (wo_ref, wo_out))):
        weight_copy(out, out, 2 + number, 1 - core, (place, 1 - part)).wait_recv()
    for copy, source in rows_sent:
        pltpu.make_async_remote_copy(
            src_ref=rows_ref.at[source, part],
            dst_ref=got_ref.at[source],
            send_sem=tsend.at[0],
            recv_sem=trecv.at[source],
            device_id=(source, part),
            device_id_type=MESH,
        ).wait_recv()
    for copy, _ in rows_sent:
        copy.wait_send()
    for copy in sent + direct + relayed:
        copy.wait_send()
    for copy in keep:
        copy.wait()


def front(rows, chunk, wq, wo, devices):
    _, _, piece, width = rows.shape
    anywhere = pl.BlockSpec(memory_space=pl.ANY)
    outs = [
        jax.ShapeDtypeStruct((devices, piece, width), BF16),
        jax.ShapeDtypeStruct((2 * devices,) + chunk.shape, BF16),
        jax.ShapeDtypeStruct(wq.shape, BF16),
        jax.ShapeDtypeStruct(wo.shape, BF16),
    ]
    return pl.pallas_call(
        functools.partial(front_kernel, devices),
        in_specs=[anywhere] * 4,
        out_specs=[anywhere] * 4,
        out_shape=outs,
        scratch_shapes=[
            pltpu.SemaphoreType.DMA((2,)),
            pltpu.SemaphoreType.DMA((devices,)),
            pltpu.SemaphoreType.DMA((devices,)),
            pltpu.SemaphoreType.DMA((2 * devices,)),
            pltpu.SemaphoreType.DMA((2 * devices,)),
            pltpu.SemaphoreType.DMA((4,)),
            pltpu.SemaphoreType.DMA((4,)),
        ],
        compiler_params=pltpu.CompilerParams(collective_id=0, has_side_effects=True),
        cost_estimate=cost(0, 100e6),
        name="front",
    )(rows, chunk, wq, wo)


def in_order(part, mine, theirs, place):
    @pl.when(part == 0)
    def _():
        place(mine, theirs)

    @pl.when(part == 1)
    def _():
        place(theirs, mine)


def project_kernel(
    part_ref, x_ref, meta_ref, cos_ref, sin_ref, gain_ref, mine_ref, theirs_ref,
    aq_ref, ak_ref, av_ref, bq_ref, bk_ref, bv_ref,
    n_ref, q_ref, kv_ref, z_ref, w_ref, bias,
):
    width = x_ref.shape[1]
    qw, kw = bq_ref.shape[0], bk_ref.shape[0]
    rank = bq_ref.shape[1]
    low = qw + 2 * kw

    @pl.when(pl.program_id(0) == 0)
    def _():
        def fill(first, second):
            at, to = 0, 0
            for size in (qw // 2, kw // 2, kw // 2):
                cut = slice(at, at + size)
                both = jnp.concatenate(
                    [first[:width, cut].astype(F32), second[:width, cut].astype(F32)], axis=1
                )
                w_ref[:, to : to + 2 * size] = both.astype(BF16)
                extra = jnp.concatenate(
                    [first[width : width + 8, cut].astype(F32), second[width : width + 8, cut].astype(F32)],
                    axis=1,
                )
                bias[:, to : to + 2 * size] = extra
                at += size
                to += 2 * size

        in_order(part_ref[0], mine_ref, theirs_ref, fill)
        for i, a_ref in enumerate((aq_ref, ak_ref, av_ref)):
            w_ref[:, low + i * rank : low + (i + 1) * rank] = a_ref[...]

    values = x_ref[...].astype(F32)
    normed = (values * rms(values) * gain_ref[...]).astype(BF16)
    n_ref[...] = normed
    base = nn(normed, w_ref[...])
    mask = rank_mask(meta_ref[:, 0:1], rank)
    lows = [(base[:, low + i * rank : low + (i + 1) * rank] * mask).astype(BF16) for i in range(3)]
    for i in range(3):
        z_ref[:, i * rank : (i + 1) * rank] = lows[i]
    cos, sin = cos_ref[...], sin_ref[...]
    queries = base[:, :qw] + bias[0:1, :qw] + ADAPTER_SCALE * nt(lows[0], bq_ref[...])
    for pair in range(qw // LANES):
        part = queries[:, pair * LANES : (pair + 1) * LANES]
        turned = (part * cos + turn(part) * sin) * HEAD**-0.5
        q_ref[:, pair * LANES : (pair + 1) * LANES] = turned.astype(BF16)
    keys = base[:, qw : qw + kw] + bias[0:1, qw : qw + kw] + ADAPTER_SCALE * nt(lows[1], bk_ref[...])
    kv_ref[:, :kw] = (keys * cos + turn(keys) * sin).astype(BF16)
    vals = base[:, qw + kw : low] + bias[0:1, qw + kw : low] + ADAPTER_SCALE * nt(lows[2], bv_ref[...])
    kv_ref[:, kw:] = vals.astype(BF16)


def project(part, x, meta, cos, sin, gain, mine, theirs, a_rows, b_rows):
    rows, width = x.shape
    b_q, b_k, _ = b_rows
    qw, kw, rank = b_q.shape[0], b_k.shape[0], b_q.shape[1]
    tile = ROW_TILE
    rest = (gain, mine, theirs, *a_rows, *b_rows)
    outs = [
        jax.ShapeDtypeStruct((rows, width), BF16),
        jax.ShapeDtypeStruct((rows, qw), BF16),
        jax.ShapeDtypeStruct((rows, 2 * kw), BF16),
        jax.ShapeDtypeStruct((rows, 3 * rank), BF16),
        jax.ShapeDtypeStruct((width, qw + 2 * kw + 3 * rank), BF16),
    ]
    return pl.pallas_call(
        project_kernel,
        grid_spec=pltpu.PrefetchScalarGridSpec(
            num_scalar_prefetch=1,
            grid=(rows // tile,),
            in_specs=[row_blocks(a, tile) for a in (x, meta, cos, sin)] + [whole(a) for a in rest],
            out_specs=[row_blocks(o, tile) for o in outs[:4]] + [whole(outs[4])],
            scratch_shapes=[pltpu.VMEM((8, qw + 2 * kw), F32)],
        ),
        out_shape=outs,
        compiler_params=params(),
        cost_estimate=cost(2 * rows * width * 1600, 9e6),
        name="project",
    )(part, x, meta, cos, sin, *rest)


def head_groups(heads, kv_heads):
    width = heads // kv_heads
    groups = {}
    for head in range(heads):
        groups.setdefault((head // width, head % 2), []).append(head)
    return [(kv, half, members) for (kv, half), members in sorted(groups.items())]


def spread_heads(tile_f32, kv, half):
    lanes = lane_iota(tile_f32.shape)
    moved = tile_f32 if kv % 2 == half else pltpu.roll(tile_f32, HEAD, 1)
    keep = (lanes >= HEAD) if half else (lanes < HEAD)
    return jnp.where(keep, moved, 0.0).astype(BF16)


def fill_heads(groups, source, keys_ref, values_ref):
    total = keys_ref.shape[1]
    for start in range(0, total, KEY_TILE):
        part = source(start).astype(F32)
        for number, (kv, half, _) in enumerate(groups):
            keys_ref[number, start : start + KEY_TILE, :] = spread_heads(part[:, :LANES], kv, half)
            values_ref[number, start : start + KEY_TILE, :] = spread_heads(
                part[:, LANES:], kv, half
            )


def attend_kernel(
    heads, kv_heads, bounds_ref, all_ref, meta_ref, metar_ref, own_ref, other_ref, column_ref,
    q_ref, o_ref, log_ref, merged_ref, slot_ref, keys, values, acc, top, total, held,
):
    step = pl.program_id(0)
    groups = head_groups(heads, kv_heads)
    rows = q_ref.shape[0]
    q_ref[...] = nn(pick_rows(meta_ref[:, 0:1], all_ref.shape[0]), all_ref[...]).astype(BF16)

    @pl.when(step == 0)
    def _():
        both = jnp.concatenate([own_ref[...], other_ref[...]], axis=0)

        def merged(start):
            picks = pick_rows(column_ref[start : start + KEY_TILE, :], both.shape[0])
            part = nn(picks, both)
            merged_ref[start : start + KEY_TILE, :] = part.astype(BF16)
            return part

        fill_heads(groups, merged, keys, values)

    acc[...] = jnp.zeros_like(acc)
    total[...] = jnp.zeros_like(total)
    top[...] = jnp.full_like(top, MASKED_SCORE)
    first, last = meta_ref[:, 1:2], meta_ref[:, 2:3]
    offsets = []
    cursor = 0
    for _, _, members in groups:
        offsets.append(cursor)
        cursor += len(members) * rows

    def one_tile(number, carry):
        start = pl.multiple_of(number * KEY_TILE, KEY_TILE)
        index = start + lane_iota((rows, KEY_TILE))
        bias = jnp.where((index >= first) & (index <= last), 0.0, MASKED_SCORE)
        for group, (_, _, members) in enumerate(groups):
            count = len(members)
            span = pl.ds(offsets[group], count * rows)
            stack = jnp.concatenate(
                [q_ref[:, (h // 2) * LANES : (h // 2 + 1) * LANES] for h in members], axis=0
            )
            scores = nt(stack, keys[group, pl.ds(start, KEY_TILE), :])
            scores = scores + jnp.concatenate([bias] * count, axis=0)
            old = top[span, :]
            new = jnp.maximum(old, jnp.max(scores, axis=1, keepdims=True))
            weights = jnp.exp(scores - new)
            shrink = jnp.exp(old - new)
            total[span, :] = total[span, :] * shrink + jnp.sum(weights, axis=1, keepdims=True)
            acc[span, :] = acc[span, :] * shrink + nn(
                weights.astype(BF16), values[group, pl.ds(start, KEY_TILE), :]
            )
            top[span, :] = new
        return carry

    lax.fori_loop(bounds_ref[0, step], bounds_ref[1, step], one_tile, 0)
    pairs = [None] * (heads // 2)
    logs = jnp.zeros((rows, LANES), F32)
    lanes = lane_iota((rows, LANES))
    for group, (_, _, members) in enumerate(groups):
        for at, head in enumerate(members):
            span = pl.ds(offsets[group] + at * rows, rows)
            sums = total[span, :]
            part = acc[span, :] / sums
            logs = jnp.where(lanes == head, top[span, :] + jnp.log(sums), logs)
            pair = head // 2
            pairs[pair] = part if pairs[pair] is None else pairs[pair] + part
    for pair, part in enumerate(pairs):
        o_ref[:, pair * LANES : (pair + 1) * LANES] = part.astype(BF16)
    log_ref[...] = jnp.transpose(logs)[: log_ref.shape[0], :]
    held[pl.ds(pl.multiple_of(step * rows, rows), rows), :] = o_ref[...]

    @pl.when(step == pl.num_programs(0) - 1)
    def _():
        slot_ref[...] = nn(place_rows(metar_ref[0:1, :], held.shape[0]), held[...]).astype(BF16)


def attend(bounds, q, meta, meta_rows, own_kv, other_kv, column, heads, kv_heads):
    rows, qw = q.shape
    tile = QUERY_TILE
    keys = 2 * rows
    groups = len(head_groups(heads, kv_heads))
    outs = [
        jax.ShapeDtypeStruct((rows, qw), BF16),
        jax.ShapeDtypeStruct((rows, qw), BF16),
        jax.ShapeDtypeStruct((16, rows), F32),
        jax.ShapeDtypeStruct((keys, own_kv.shape[1]), BF16),
        jax.ShapeDtypeStruct((rows, qw), BF16),
    ]
    return pl.pallas_call(
        functools.partial(attend_kernel, heads, kv_heads),
        grid_spec=pltpu.PrefetchScalarGridSpec(
            num_scalar_prefetch=1,
            grid=(rows // tile,),
            in_specs=[
                whole(q),
                row_blocks(meta, tile),
                whole(meta_rows),
                whole(own_kv),
                whole(other_kv),
                whole(column),
            ],
            out_specs=[
                row_blocks(outs[0], tile),
                row_blocks(outs[1], tile),
                pl.BlockSpec((16, tile), lambda i, *_: (0, i)),
                whole(outs[3]),
                whole(outs[4]),
            ],
            scratch_shapes=[
                pltpu.VMEM((groups, keys, LANES), BF16),
                pltpu.VMEM((groups, keys, LANES), BF16),
                pltpu.VMEM((heads * tile, LANES), F32),
                pltpu.VMEM((heads * tile, 1), F32),
                pltpu.VMEM((heads * tile, 1), F32),
                pltpu.VMEM((rows, qw), BF16),
            ],
        ),
        out_shape=outs,
        compiler_params=params(),
        cost_estimate=cost(heads * rows * keys * 256, 6e6),
        name="attend",
    )(bounds, q, meta, meta_rows, own_kv, other_kv, column)


def attend_back_kernel(
    heads, kv_heads, bounds_ref, q_ref, all_ref, o_ref, log_ref, meta_ref, metar_ref, cos_ref,
    sin_ref, merged_ref, column_ref, place_ref,
    gq_ref, own_ref, other_ref, keys, values, dkeys, dvalues, dq, dots, g_ref, held,
):
    step = pl.program_id(0)
    groups = head_groups(heads, kv_heads)
    rows = q_ref.shape[0]
    g_ref[...] = nn(pick_rows(meta_ref[:, 0:1], all_ref.shape[0]), all_ref[...]).astype(BF16)

    @pl.when(step == 0)
    def _():
        fill_heads(groups, lambda at: merged_ref[at : at + KEY_TILE, :], keys, values)
        dkeys[...] = jnp.zeros_like(dkeys)
        dvalues[...] = jnp.zeros_like(dvalues)

    dq[...] = jnp.zeros_like(dq)
    for pair in range(heads // 2):
        lanes = slice(pair * LANES, (pair + 1) * LANES)
        product = jnp.transpose(g_ref[:, lanes].astype(F32) * o_ref[:, lanes].astype(F32))
        dots[2 * pair : 2 * pair + 1, :] = jnp.sum(product[:HEAD], axis=0, keepdims=True)
        dots[2 * pair + 1 : 2 * pair + 2, :] = jnp.sum(product[HEAD:], axis=0, keepdims=True)
    first, last = metar_ref[1:2, :], metar_ref[2:3, :]

    def one_tile(number, carry):
        start = pl.multiple_of(number * KEY_TILE, KEY_TILE)
        index = start + row_iota((KEY_TILE, rows))
        bias = jnp.where((index >= first) & (index <= last), 0.0, MASKED_SCORE)
        for group, (_, half, members) in enumerate(groups):
            count = len(members)
            span = pl.ds(start, KEY_TILE)
            cut = [slice((h // 2) * LANES, (h // 2 + 1) * LANES) for h in members]
            stack = jnp.concatenate([q_ref[:, c] for c in cut], axis=0)
            grads = jnp.concatenate([g_ref[:, c] for c in cut], axis=0)
            logs = jnp.concatenate([log_ref[h : h + 1, :] for h in members], axis=1)
            drop = jnp.concatenate([dots[h : h + 1, :] for h in members], axis=1)
            key_part = keys[group, span, :]
            scores = nt(key_part, stack) + jnp.concatenate([bias] * count, axis=1)
            weights = jnp.exp(scores - logs)
            change = nt(values[group, span, :], grads)
            dscores = (weights * (change - drop)).astype(BF16)
            dvalues[group, span, :] += nn(weights.astype(BF16), grads)
            dkeys[group, span, :] += nn(dscores, stack)
            back = tn(dscores, key_part)
            for at, head in enumerate(members):
                dq[head // 2, :, :] += back[at * rows : (at + 1) * rows, :]
        return carry

    lax.fori_loop(bounds_ref[0, step], bounds_ref[1, step], one_tile, 0)
    cos, sin = cos_ref[...], sin_ref[...]
    for pair in range(heads // 2):
        grad = dq[pair, :, :] * HEAD**-0.5
        grad = grad * cos - turn(grad) * sin
        held[
            pl.ds(pl.multiple_of(step * rows, rows), rows), pair * LANES : (pair + 1) * LANES
        ] = grad.astype(BF16)

    @pl.when(step == pl.num_programs(0) - 1)
    def _():
        gq_ref[...] = nn(place_rows(place_ref[0:1, :], held.shape[0]), held[...]).astype(BF16)
        total = dkeys.shape[1]

        def join(ref):
            out = None
            for group, (kv, half, _) in enumerate(groups):
                part = ref[group, :, :]
                lanes = lane_iota(part.shape)
                part = jnp.where((lanes >= HEAD) if half else (lanes < HEAD), part, 0.0)
                if kv % 2 != half:
                    part = pltpu.roll(part, HEAD, 1)
                out = part if out is None else out + part
            return out.astype(BF16)

        both = jnp.concatenate([join(dkeys), join(dvalues)], axis=1)
        half_rows = own_ref.shape[0]
        for at in range(0, total, KEY_TILE):
            hit = (at + row_iota((KEY_TILE, total))) == column_ref[...]
            part = nn(jnp.where(hit, 1.0, 0.0).astype(BF16), both).astype(BF16)
            if at < half_rows:
                own_ref[at : at + KEY_TILE, :] = part
            else:
                other_ref[at - half_rows : at - half_rows + KEY_TILE, :] = part


def attend_back(
    bounds, q, grad, o, logs, meta, meta_rows, cos, sin, merged, column_row, heads, kv_heads
):
    rows, qw = q.shape
    tile = QUERY_TILE
    keys, kvw = merged.shape
    groups = len(head_groups(heads, kv_heads))
    outs = [
        jax.ShapeDtypeStruct((rows, qw), BF16),
        jax.ShapeDtypeStruct((rows, kvw), BF16),
        jax.ShapeDtypeStruct((rows, kvw), BF16),
    ]
    return pl.pallas_call(
        functools.partial(attend_back_kernel, heads, kv_heads),
        grid_spec=pltpu.PrefetchScalarGridSpec(
            num_scalar_prefetch=1,
            grid=(rows // tile,),
            in_specs=[
                row_blocks(q, tile),
                whole(grad),
                row_blocks(o, tile),
                pl.BlockSpec((16, tile), lambda i, *_: (0, i)),
                row_blocks(meta, tile),
                pl.BlockSpec((8, tile), lambda i, *_: (0, i)),
                row_blocks(cos, tile),
                row_blocks(sin, tile),
                whole(merged),
                whole(column_row),
                whole(meta_rows),
            ],
            out_specs=[whole(o) for o in outs],
            scratch_shapes=[
                pltpu.VMEM((groups, keys, LANES), BF16),
                pltpu.VMEM((groups, keys, LANES), BF16),
                pltpu.VMEM((groups, keys, LANES), F32),
                pltpu.VMEM((groups, keys, LANES), F32),
                pltpu.VMEM((heads // 2, tile, LANES), F32),
                pltpu.VMEM((16, tile), F32),
                pltpu.VMEM((tile, qw), BF16),
                pltpu.VMEM((rows, qw), BF16),
            ],
        ),
        out_shape=outs,
        compiler_params=params(),
        cost_estimate=cost(heads * rows * keys * 640, 9e6),
        name="attend_back",
    )(bounds, q, grad, o, logs, meta, meta_rows, cos, sin, merged, column_row, meta_rows)


def middle_kernel(
    part_ref, o_ref, x_ref, meta_ref, mine_ref, theirs_ref, a_ref, b_ref, gain_ref,
    y_ref, n_ref, z_ref, w_ref,
):
    width = x_ref.shape[1]
    rank = b_ref.shape[1]
    half = mine_ref.shape[0]

    @pl.when(pl.program_id(0) == 0)
    def _():
        def fill(first, second):
            w_ref[:half, :width] = first[...]
            w_ref[half:, :width] = second[...]

        in_order(part_ref[0], mine_ref, theirs_ref, fill)
        w_ref[:, width:] = a_ref[...]

    mask = rank_mask(meta_ref[:, 0:1], rank)
    base = nn(o_ref[...], w_ref[...])
    low = (base[:, width:] * mask).astype(BF16)
    z_ref[...] = low
    values = x_ref[...].astype(F32) + (base[:, :width] + ADAPTER_SCALE * nt(low, b_ref[...]))
    y_ref[...] = values
    n_ref[...] = (values * rms(values) * gain_ref[...]).astype(BF16)


def middle(part, o, x, meta, mine, theirs, a_out, b_out, gain):
    rows, width = x.shape
    rank = b_out.shape[1]
    tile = ROW_TILE
    rest = (mine, theirs, a_out, b_out, gain)
    outs = [
        jax.ShapeDtypeStruct((rows, width), F32),
        jax.ShapeDtypeStruct((rows, width), BF16),
        jax.ShapeDtypeStruct((rows, rank), BF16),
        jax.ShapeDtypeStruct((o.shape[1], width + rank), BF16),
    ]
    return pl.pallas_call(
        middle_kernel,
        grid_spec=pltpu.PrefetchScalarGridSpec(
            num_scalar_prefetch=1,
            grid=(rows // tile,),
            in_specs=[row_blocks(a, tile) for a in (o, x, meta)] + [whole(a) for a in rest],
            out_specs=[row_blocks(a, tile) for a in outs[:3]] + [whole(outs[3])],
        ),
        out_shape=outs,
        compiler_params=params(),
        cost_estimate=cost(2 * rows * width * 1100, 12e6),
        name="middle",
    )(part, o, x, meta, *rest)


def finish_kernel(ya_ref, yb_ref, y1_ref, dy_ref, meta_ref, b_ref, out_ref, gb_ref, gacc):
    step = pl.program_id(0)
    width = y1_ref.shape[1]
    rank = b_ref.shape[1]

    @pl.when(step == 0)
    def _():
        gacc[...] = jnp.zeros_like(gacc)

    mask = rank_mask(meta_ref[:, 0:1], rank)
    low = ((ya_ref[:, width:] + yb_ref[:, width:].astype(F32)) * mask).astype(BF16)
    values = y1_ref[...] + (
        (ya_ref[:, :width] + yb_ref[:, :width].astype(F32)) + ADAPTER_SCALE * nt(low, b_ref[...])
    )
    out_ref[...] = values.astype(BF16)
    gacc[...] += ADAPTER_SCALE * tn(dy_ref[...], low)

    @pl.when(step == pl.num_programs(0) - 1)
    def _():
        gb_ref[...] = gacc[...].astype(gb_ref.dtype)


def finish(y_first, y_second, y1, dy, meta, b_down):
    rows, width = y1.shape
    rank = b_down.shape[1]
    tile = ROW_TILE
    outs = [
        jax.ShapeDtypeStruct((rows, width), BF16),
        jax.ShapeDtypeStruct((width, rank), BF16),
    ]
    return pl.pallas_call(
        finish_kernel,
        grid=(rows // tile,),
        in_specs=[row_blocks(a, tile) for a in (y_first, y_second, y1, dy, meta)] + [whole(b_down)],
        out_specs=[row_blocks(outs[0], tile), whole(outs[1])],
        out_shape=outs,
        scratch_shapes=[pltpu.VMEM((width, rank), F32)],
        compiler_params=params(),
        cost_estimate=cost(2 * rows * width * 512, 11e6),
        name="finish",
    )(y_first, y_second, y1, dy, meta, b_down)


def middle_back_kernel(
    da_ref, db_ref, y1_ref, dy_ref, n_ref, o_ref, z_ref, meta_ref, a_ref, b_ref, w_ref, gain_ref,
    dy1_ref, dar_ref, ga_ref, gbo_ref, gao_ref, acc_a, acc_bo, acc_ao,
):
    step = pl.program_id(0)
    width = y1_ref.shape[1]
    rank = b_ref.shape[1]

    @pl.when(step == 0)
    def _():
        acc_a[...] = jnp.zeros_like(acc_a)
        acc_bo[...] = jnp.zeros_like(acc_bo)
        acc_ao[...] = jnp.zeros_like(acc_ao)

    mask = rank_mask(meta_ref[:, 0:1], rank)
    back = da_ref[:, width:] + db_ref[:, width:].astype(F32)
    back = (back * jnp.concatenate([mask, mask], axis=1)).astype(BF16)
    grad = da_ref[:, :width] + db_ref[:, :width].astype(F32) + nt(back, a_ref[...])
    values = y1_ref[...]
    dy1 = dy_ref[...].astype(F32) + norm_back(values, gain_ref[...], grad)
    dy1_ref[...] = dy1
    low_grad = dy1.astype(BF16)
    back_out = (ADAPTER_SCALE * nn(low_grad, b_ref[...]) * mask).astype(BF16)
    both = jnp.concatenate([low_grad, back_out], axis=1)
    dar_ref[...] = nt(both, w_ref[...]).astype(BF16)
    acc_a[...] += tn(n_ref[...], back)
    acc_bo[...] += ADAPTER_SCALE * tn(low_grad, z_ref[...])
    acc_ao[...] += tn(o_ref[...], back_out)

    @pl.when(step == pl.num_programs(0) - 1)
    def _():
        ga_ref[...] = acc_a[...].astype(ga_ref.dtype)
        gbo_ref[...] = acc_bo[...].astype(gbo_ref.dtype)
        gao_ref[...] = acc_ao[...].astype(gao_ref.dtype)


def middle_back(d_first, d_second, y1, dy, n2, o, z, meta, a_pair, b_out, w_out, gain):
    rows, width = y1.shape
    rank = b_out.shape[1]
    qw = o.shape[1]
    tile = ROW_TILE
    outs = [
        jax.ShapeDtypeStruct((rows, width), F32),
        jax.ShapeDtypeStruct((rows, qw), BF16),
        jax.ShapeDtypeStruct((width, 2 * rank), BF16),
        jax.ShapeDtypeStruct((width, rank), BF16),
        jax.ShapeDtypeStruct((qw, rank), BF16),
    ]
    return pl.pallas_call(
        middle_back_kernel,
        grid=(rows // tile,),
        in_specs=[row_blocks(a, tile) for a in (d_first, d_second, y1, dy, n2, o, z, meta)]
        + [whole(a) for a in (a_pair, b_out, w_out, gain)],
        out_specs=[row_blocks(a, tile) for a in outs[:2]] + [whole(a) for a in outs[2:]],
        out_shape=outs,
        scratch_shapes=[
            pltpu.VMEM((width, 2 * rank), F32),
            pltpu.VMEM((width, rank), F32),
            pltpu.VMEM((qw, rank), F32),
        ],
        compiler_params=params(),
        cost_estimate=cost(2 * rows * width * 1900, 20e6),
        name="middle_back",
    )(d_first, d_second, y1, dy, n2, o, z, meta, a_pair, b_out, w_out, gain)


def feed_kernel(
    theirs, n_ref, dy_ref, meta_ref, ap_ref, bd_ref, wg_hbm, wu_hbm, wd_hbm, bg_hbm, bu_hbm, ad_hbm,
    *more,
):
    if theirs:
        grad_hbm, y_ref, d_got, gbg_ref, gbu_ref, gad_ref = more[:6]
        (wga, wua, wda, raw, grads, xg, xu, dya, yacc, dacc, wsem, gsem, held, ssem, rsem) = more[6:]
    else:
        y_ref, d_ref, grad_out = more[:3]
        wga, wua, wda, raw, grads, xg, xu, dya, yacc, dacc, wsem = more[3:]
    step = pl.program_id(0)
    steps = pl.num_programs(0)
    width, half = wg_hbm.shape
    rank = bd_ref.shape[1]
    rows = n_ref.shape[0]
    tile = HIDDEN_TILE
    tiles = pl.cdiv(half, tile)
    lap = tiles * tile - half

    def loads(number):
        at = pl.multiple_of(jnp.minimum(number * tile, half - tile), LANES)
        to = pl.multiple_of(number * tile, tile)
        here, there = pl.ds(at, tile), pl.ds(to, tile)
        top, side = pl.ds(0, width), pl.ds(width, rank)
        pairs = [
            (wg_hbm.at[:, here], wga.at[top, there]),
            (wu_hbm.at[:, here], wua.at[top, there]),
            (wd_hbm.at[here, :], wda.at[there, top]),
            (bg_hbm.at[here, :], raw.at[0, there, :]),
            (bu_hbm.at[here, :], raw.at[1, there, :]),
            (ad_hbm.at[here, :], wda.at[there, side]),
        ]
        return [
            pltpu.make_async_copy(source, target, wsem.at[number, at])
            for at, (source, target) in enumerate(pairs)
        ]

    if theirs:
        place, part = lax.axis_index("dp"), lax.axis_index("tensor")

        def reply(number):
            return pltpu.make_async_remote_copy(
                src_ref=held.at[number],
                dst_ref=d_got.at[number],
                send_sem=ssem.at[number],
                recv_sem=rsem.at[number],
                device_id=(place, 1 - part),
                device_id_type=MESH,
            )

        @pl.when(step == 0)
        def _():
            barrier = pltpu.get_barrier_semaphore()
            pl.semaphore_signal(barrier, inc=1, device_id=(place, 1 - part), device_id_type=MESH)
            pl.semaphore_wait(barrier, 1)

    @pl.when(step == 0)
    def _():
        for number in range(tiles):
            for copy in loads(number):
                copy.start()
        if theirs:
            copy = pltpu.make_async_copy(grad_hbm, grads, gsem)
            copy.start()
            copy.wait()
        else:
            grads[...] = jnp.zeros_like(grads)

    mask = rank_mask(meta_ref[:, 0:1], rank)
    normed = n_ref[...]
    lows = nn(normed, ap_ref[...])
    xg[:, :width] = normed
    xu[:, :width] = normed
    xg[:, width:] = (lows[:, :rank] * mask).astype(BF16)
    xu[:, width:] = (lows[:, rank:] * mask).astype(BF16)
    dya[:, :width] = dy_ref[...]
    dya[:, width:] = (ADAPTER_SCALE * nn(dy_ref[...], bd_ref[...]) * mask).astype(BF16)
    yacc[...] = jnp.zeros_like(yacc)
    dacc[...] = jnp.zeros_like(dacc)

    def hidden(number, carry):
        span = pl.ds(pl.multiple_of(number * tile, tile), tile)

        @pl.when(step == 0)
        def _():
            for copy in loads(number):
                copy.wait()
            for at, target in enumerate((wga, wua)):
                turned = jnp.transpose(raw[at, span, :].astype(F32) * ADAPTER_SCALE)
                target[width:, span] = turned.astype(BF16)
            if lap:

                @pl.when(number == tiles - 1)
                def _():
                    edge = slice((tiles - 1) * tile, (tiles - 1) * tile + lap)
                    wga[:, edge] = jnp.zeros((width + rank, lap), BF16)
                    wua[:, edge] = jnp.zeros((width + rank, lap), BF16)
                    wda[edge, :] = jnp.zeros((lap, width + rank), BF16)

        gate = nn(xg[...], wga[:, span])
        up = nn(xu[...], wua[:, span])
        dhid = nt(dya[...], wda[span, :])
        sig = 1.0 / (1.0 + jnp.exp(-gate))
        silu = gate * sig
        hid = (silu * up).astype(BF16)
        dg = (dhid * up * (sig * (1.0 + gate * (1.0 - sig)))).astype(BF16)
        du = (dhid * silu).astype(BF16)
        yacc[...] += nn(hid, wda[span, :])
        dga = nt(dg, wga[:, span])
        dua = nt(du, wua[:, span])
        dacc[:, :width] += dga[:, :width] + dua[:, :width]
        dacc[:, width : width + rank] += dga[:, width:]
        dacc[:, width + rank :] += dua[:, width:]
        grads[0, span, :] += ADAPTER_SCALE * tn(dg, xg[:, width:])
        grads[1, span, :] += ADAPTER_SCALE * tn(du, xu[:, width:])
        grads[2, span, :] += tn(hid, dya[:, width:])
        return carry

    lax.fori_loop(0, tiles, hidden, 0)
    y_ref[...] = yacc[...].astype(y_ref.dtype)
    if not theirs:
        d_ref[...] = dacc[...]

        @pl.when(step == steps - 1)
        def _():
            grad_out[...] = grads[...]

        return
    held[step] = dacc[...].astype(BF16)
    reply(step).start()

    @pl.when(step == steps - 1)
    def _():
        last = (tiles - 1) * tile
        for at, target in enumerate((gbg_ref, gbu_ref, gad_ref)):
            target[:last, :] = grads[at, :last, :].astype(BF16)
            target[last:, :] = grads[at, last + lap : tiles * tile, :].astype(BF16)
        for number in range(held.shape[0]):
            reply(number).wait_send()
        for number in range(held.shape[0]):
            reply(number).wait_recv()


def feed(n2, dy, meta, a_pair, b_down, w_gate, w_up, w_down, b_gate, b_up, a_down, grads=None):
    rows, width = n2.shape
    half, rank = a_down.shape
    tile = ROW_TILE
    tiles = pl.cdiv(half, HIDDEN_TILE)
    padded = tiles * HIDDEN_TILE
    theirs = grads is not None
    anywhere = pl.BlockSpec(memory_space=pl.ANY)
    wide, deep = width + rank, width + 2 * rank
    args = [n2, dy, meta, a_pair, b_down, w_gate, w_up, w_down, b_gate, b_up, a_down]
    in_specs = [row_blocks(a, tile) for a in args[:3]] + [whole(a) for a in args[3:5]] + [anywhere] * 6
    scratch = [
        pltpu.VMEM((wide, padded), BF16),
        pltpu.VMEM((wide, padded), BF16),
        pltpu.VMEM((padded, wide), BF16),
        pltpu.VMEM((2, padded, rank), BF16),
        pltpu.VMEM((3, padded, rank), F32),
        pltpu.VMEM((tile, wide), BF16),
        pltpu.VMEM((tile, wide), BF16),
        pltpu.VMEM((tile, wide), BF16),
        pltpu.VMEM((tile, wide), F32),
        pltpu.VMEM((tile, deep), F32),
        pltpu.SemaphoreType.DMA((tiles, 6)),
    ]
    if theirs:
        args.append(grads)
        in_specs.append(anywhere)
        thin = jax.ShapeDtypeStruct((half, rank), BF16)
        outs = [
            jax.ShapeDtypeStruct((rows, wide), BF16),
            jax.ShapeDtypeStruct((rows // tile, tile, deep), BF16),
            thin,
            thin,
            thin,
        ]
        out_specs = [row_blocks(outs[0], tile), anywhere] + [whole(thin)] * 3
        scratch += [
            pltpu.SemaphoreType.DMA,
            pltpu.VMEM((rows // tile, tile, deep), BF16),
            pltpu.SemaphoreType.DMA((rows // tile,)),
            pltpu.SemaphoreType.DMA((rows // tile,)),
        ]
        extra = dict(collective_id=1, has_side_effects=True)
    else:
        outs = [
            jax.ShapeDtypeStruct((rows, wide), F32),
            jax.ShapeDtypeStruct((rows, deep), F32),
            jax.ShapeDtypeStruct((3, padded, rank), F32),
        ]
        out_specs = [row_blocks(outs[0], tile), row_blocks(outs[1], tile), whole(outs[2])]
        extra = {}
    return pl.pallas_call(
        functools.partial(feed_kernel, theirs),
        grid=(rows // tile,),
        in_specs=in_specs,
        out_specs=out_specs,
        out_shape=outs,
        scratch_shapes=scratch,
        compiler_params=params(**extra),
        cost_estimate=cost(2 * rows * half * (6 * width + 9 * rank), 30e6),
        name="feed_theirs" if theirs else "feed_own",
    )(*args)


def input_kernel(
    gq_ref, own_ref, got_ref, x_ref, n_ref, z_ref, dy1_ref, meta_ref, cos_ref, sin_ref,
    gain_ref, w_ref, bq_ref, bk_ref, bv_ref,
    out_ref, ga_ref, gb_ref, acc_a, acc_b,
):
    step = pl.program_id(0)
    qw, kw, rank = bq_ref.shape[0], bk_ref.shape[0], bq_ref.shape[1]

    @pl.when(step == 0)
    def _():
        acc_a[...] = jnp.zeros_like(acc_a)
        acc_b[...] = jnp.zeros_like(acc_b)

    mask = rank_mask(meta_ref[:, 0:1], rank)
    both = own_ref[...].astype(F32) + got_ref[...].astype(F32)
    dk = both[:, :kw]
    gq = gq_ref[...]
    gk = (dk * cos_ref[...] - turn(dk) * sin_ref[...]).astype(BF16)
    gv = both[:, kw:].astype(BF16)
    backs = [
        (ADAPTER_SCALE * nn(g, b[...]) * mask).astype(BF16)
        for g, b in ((gq, bq_ref), (gk, bk_ref), (gv, bv_ref))
    ]
    grads = jnp.concatenate([gq, gk, gv] + backs, axis=1)
    dn = nt(grads, w_ref[...])
    values = x_ref[...].astype(F32)
    dx = dy1_ref[...] + norm_back(values, gain_ref[...], dn)
    out_ref[...] = dx.astype(BF16)
    acc_a[...] += tn(n_ref[...], jnp.concatenate(backs, axis=1))
    low = z_ref[...]
    acc_b[:qw, :] += tn(gq, low[:, :rank])
    acc_b[qw : qw + kw, :] += tn(gk, low[:, rank : 2 * rank])
    acc_b[qw + kw :, :] += tn(gv, low[:, 2 * rank :])

    @pl.when(step == pl.num_programs(0) - 1)
    def _():
        ga_ref[...] = acc_a[...].astype(ga_ref.dtype)
        gb_ref[...] = (ADAPTER_SCALE * acc_b[...]).astype(gb_ref.dtype)


def input_back(gq, own, got, x, n1, z, dy1, meta, cos, sin, gain, w_cat, b_q, b_k, b_v):
    rows, width = x.shape
    qw, kw, rank = b_q.shape[0], b_k.shape[0], b_q.shape[1]
    tile = ROW_TILE
    outs = [
        jax.ShapeDtypeStruct((rows, width), BF16),
        jax.ShapeDtypeStruct((width, 3 * rank), BF16),
        jax.ShapeDtypeStruct((qw + 2 * kw, rank), BF16),
    ]
    return pl.pallas_call(
        input_kernel,
        grid=(rows // tile,),
        in_specs=[row_blocks(a, tile) for a in (gq, own, got, x, n1, z, dy1, meta, cos, sin)]
        + [whole(a) for a in (gain, w_cat, b_q, b_k, b_v)],
        out_specs=[row_blocks(outs[0], tile)] + [whole(a) for a in outs[1:]],
        out_shape=outs,
        scratch_shapes=[
            pltpu.VMEM((width, 3 * rank), F32),
            pltpu.VMEM((qw + 2 * kw, rank), F32),
        ],
        compiler_params=params(),
        cost_estimate=cost(2 * rows * width * 2900, 14e6),
        name="input_back",
    )(gq, own, got, x, n1, z, dy1, meta, cos, sin, gain, w_cat, b_q, b_k, b_v)


def row_tables(order_row, lengths_row, adapter_row, part, parts, each):
    total = order_row.shape[0]
    piece = each // parts
    local = total // parts
    places = jnp.arange(total, dtype=I32)
    own = (order_row % each) // piece == part
    slot = (order_row // each) * piece + order_row % piece
    column = jnp.where(own, slot, local + slot)
    upto = jnp.sum((own[None, :] & (places[None, :] <= places[:, None])).astype(I32), axis=1)
    rank = jnp.where(own, upto - 1, total)
    picks = rank[None, :] == jnp.arange(local, dtype=I32)[:, None]
    sorted_place = jnp.sum(jnp.where(picks, places[None, :], 0), axis=1)
    sorted_slot = jnp.sum(jnp.where(picks, slot[None, :], 0), axis=1)
    slot_place = jnp.sum(jnp.where(column[None, :] == places[:, None], places[None, :], 0), axis=1)
    ends = jnp.cumsum(lengths_row)
    starts = ends - lengths_row
    both = jnp.concatenate([slot_place, sorted_place])
    member = (both[:, None] >= starts[None, :]) & (both[:, None] < ends[None, :])
    first = jnp.sum(jnp.where(member, starts[None, :], 0), axis=1)
    chosen = jnp.sum(jnp.where(member, adapter_row[None, :], 0), axis=1)
    position = both - first
    sorted_first = first[total:]
    bounds = jnp.stack(
        [
            sorted_first[::QUERY_TILE] // KEY_TILE,
            sorted_place[QUERY_TILE - 1 :: QUERY_TILE] // KEY_TILE + 1,
        ]
    )
    blank = jnp.zeros_like(sorted_place)
    meta_sorted = jnp.stack([sorted_slot, sorted_first, sorted_place] + [blank] * 5, axis=1)
    meta_rows = jnp.stack([sorted_slot, sorted_first, sorted_place] + [blank] * 5, axis=0)
    meta_own = jnp.broadcast_to(chosen[:local, None], (local, 8))
    meta_other = jnp.broadcast_to(chosen[local:total, None], (local, 8))
    slot_position = position[:local]
    return (
        meta_own, meta_other, meta_sorted, meta_rows, slot_position, position[total:], column, bounds,
    )


def rope_tables(position):
    freq_index = jnp.arange(HEAD // 2, dtype=F32)
    inv_freq = jnp.power(jnp.float32(ROPE_BASE), -2.0 * freq_index / HEAD)
    angles = position.astype(F32)[:, None] * inv_freq[None, :]
    return (
        jnp.concatenate([jnp.cos(angles)] * 4, axis=1),
        jnp.concatenate([jnp.sin(angles)] * 4, axis=1),
    )


def per_device(
    tokens, cotangent, order, lengths, adapter_ids, norm_gains, w_query, w_key, w_value,
    b_query, b_key, b_value, w_out, w_gate, w_up, w_down, adapters, first_moment, second_moment,
):
    parts = lax.axis_size("tensor")
    part = lax.axis_index("tensor")
    devices = lax.axis_size("dp")
    place = lax.axis_index("dp")
    total, width = tokens.shape
    each = total // devices
    piece = each // parts
    local = total // parts
    rank = adapters.shape[1]
    own_rows = adapters.shape[0]
    swap = [(i, parts - 1 - i) for i in range(parts)]
    first_part = part == 0

    def across(values):
        return lax.ppermute(values, "tensor", swap)

    def pair(mine, theirs, axis):
        return jnp.concatenate(
            [jnp.where(first_part, mine, theirs), jnp.where(first_part, theirs, mine)], axis=axis
        )

    def give_back(values):
        got = lax.all_to_all(
            values.reshape(devices, piece, width), "dp", split_axis=0, concat_axis=0, tiled=True
        )
        theirs = across(got)
        return pair(got[:, None], theirs[:, None], 1).reshape(total, width)

    qh, kh, half = w_query.shape[1], w_key.shape[1], w_gate.shape[1]
    qw, kw, hidden = parts * qh, parts * kh, parts * half
    heads, kv_heads = qw // HEAD, kw // HEAD
    mine_qkv = jnp.concatenate(
        [
            jnp.concatenate([w_query, w_key, w_value], axis=1),
            jnp.broadcast_to(
                jnp.concatenate([b_query, b_key, b_value])[None], (32, qh + 2 * kh)
            ),
        ],
        axis=0,
    )
    lines = mine_qkv.shape[0]
    moved, copies, their_qkv, their_out = front(
        tokens.reshape(devices, parts, piece, width),
        adapters.astype(BF16),
        mine_qkv.reshape(2, lines // 2, -1),
        w_out.reshape(2, w_out.shape[0] // 2, width),
        devices,
    )
    moved = moved.reshape(local, width)
    sent = cotangent.reshape(devices, parts, piece, width)
    sent = lax.dynamic_index_in_dim(sent, part, 1, keepdims=False)
    dy = lax.all_to_all(sent, "dp", split_axis=0, concat_axis=0, tiled=True).reshape(local, width)
    dy_theirs = across(dy)

    sizes = (width, qw, width, kw, width, kw, qw, width, width, hidden, width, hidden, hidden, width)
    early = 3 * width + qw + 2 * kw
    lead = pl.cdiv(early, own_rows)
    flat = copies[:lead].reshape(lead * own_rows, rank)
    late_flat = copies.reshape(2 * devices * own_rows, rank)
    sections = []
    cursor = 0
    for number, size in enumerate(sizes):
        source = flat if number < 6 else late_flat
        sections.append(source[cursor : cursor + size])
        cursor += size
    a_q, b_q, a_k, b_k, a_v, b_v, a_o, b_o, a_g, b_g, a_u, b_u, a_d, b_d = sections

    def near(rows):
        return lax.dynamic_slice_in_dim(rows, part * half, half, 0)

    meta_own, meta_other, meta_sorted, meta_rows, slot_position, sorted_position, column, bounds = (
        row_tables(order[0], lengths[0], adapter_ids[0], part, parts, each)
    )
    cos, sin = rope_tables(slot_position)
    cos_sorted, sin_sorted = rope_tables(sorted_position)
    gain_one = norm_gains[0:1].astype(F32)
    gain_two = norm_gains[1:2].astype(F32)
    side = jnp.reshape(part, (1,)).astype(I32)
    a_pair = jnp.concatenate([a_g, a_u], axis=1)

    n1, q, kv, z, w_cat = project(
        side, moved, meta_own, cos, sin, gain_one, mine_qkv, their_qkv.reshape(mine_qkv.shape),
        (a_q, a_k, a_v), (b_q, b_k, b_v),
    )
    other_kv = across(kv)
    q_sorted, o_sorted, logs, merged, o = attend(
        bounds, q, meta_sorted, meta_rows, kv, other_kv, column[:, None], heads, kv_heads
    )
    y1, n2, z_out, w_out_cat = middle(
        side, o, moved, meta_own, w_out, their_out.reshape(w_out.shape), a_o, b_o, gain_two
    )
    n2_theirs = across(n2)
    share = (a_pair, b_d, w_gate, w_up, w_down, near(b_g), near(b_u), near(a_d))
    y_own, d_own, grads = feed(n2, dy, meta_own, *share)
    y_theirs, d_got, grad_b_g, grad_b_u, grad_a_d = feed(
        n2_theirs, dy_theirs, meta_other, *share, grads
    )
    y_got = across(y_theirs)
    d_got = d_got.reshape(local, -1)
    dy1, dar, grad_pair, grad_b_o, grad_a_o = middle_back(
        d_own, d_got, y1, dy, n2, o, z_out, meta_own, a_pair, b_o, w_out_cat, gain_two
    )
    out_rows, grad_b_d = finish(y_own, y_got, y1, dy, meta_own, b_d)
    layer_out = give_back(out_rows)
    gq, dkv_own, dkv_other = attend_back(
        bounds, q_sorted, dar, o_sorted, logs, meta_sorted, meta_rows, cos_sorted, sin_sorted,
        merged, column[None, :], heads, kv_heads,
    )
    dkv_got = across(dkv_other)
    dx_rows, grad_a_qkv, grad_b_qkv = input_back(
        gq, dkv_own, dkv_got, moved, n1, z, dy1, meta_own, cos, sin, gain_one, w_cat, b_q, b_k, b_v
    )
    input_grad = give_back(dx_rows)

    def spread(rows):
        blank = jnp.zeros_like(rows)
        return pair(rows, blank, 0)

    everything = jnp.concatenate(
        [
            grad_a_qkv[:, :rank],
            grad_b_qkv[:qw],
            grad_a_qkv[:, rank : 2 * rank],
            grad_b_qkv[qw : qw + kw],
            grad_a_qkv[:, 2 * rank :],
            grad_b_qkv[qw + kw :],
            grad_a_o,
            grad_b_o,
            grad_pair[:, :rank],
            spread(grad_b_g),
            grad_pair[:, rank:],
            spread(grad_b_u),
            spread(grad_a_d),
            grad_b_d,
        ],
        axis=0,
    )
    reduced = lax.psum_scatter(
        everything, ("dp", "tensor"), scatter_dimension=0, tiled=True
    ).astype(F32)
    moment_one = BETA_ONE * first_moment + (1.0 - BETA_ONE) * reduced
    moment_two = BETA_TWO * second_moment + (1.0 - BETA_TWO) * reduced * reduced
    corrected_one = moment_one / (1.0 - BETA_ONE**STEP)
    corrected_two = moment_two / (1.0 - BETA_TWO**STEP)
    updated = adapters - LEARN_RATE * (
        corrected_one / (jnp.sqrt(corrected_two) + ADAM_EPS) + WEIGHT_DECAY * adapters
    )
    return (
        layer_out,
        input_grad,
        reduced,
        moment_one,
        moment_two,
        updated,
        updated.astype(BF16),
    )


def solution(mesh):
    both = P(("dp", "tensor"), None)
    rows = P("dp", None)
    return jax.shard_map(
        per_device,
        mesh=mesh,
        in_specs=(rows, rows, rows, rows, rows, P())
        + (P(None, "tensor"),) * 3
        + (P("tensor"),) * 3
        + (P("tensor", None), P(None, "tensor"), P(None, "tensor"), P("tensor", None))
        + (both,) * 3,
        out_specs=(rows, rows) + (both,) * 5,
        check_vma=False,
    )
```

```python
import functools

import jax
import jax.numpy as jnp
from jax import lax
from jax.experimental import pallas as pl
from jax.experimental.pallas import tpu as pltpu
from jax.sharding import PartitionSpec as P

HEAD = 64
RANK = 16
STEP = 3

ADAPTER_SCALE = 2.0
NORM_EPS = 1e-06
ROPE_BASE = 1000000.0
BETA_ONE = 0.5
BETA_TWO = 0.6
LEARN_RATE = 0.04
WEIGHT_DECAY = 0.01
ADAM_EPS = 1e-08
MASKED_SCORE = -1e30
PLANES = 4
FLAT_PAD = 64
MESH = pl.DeviceIdType.MESH

LANES = 128
ROW_TILE = 256
QUERY_TILE = 128
KEY_TILE = 256
HIDDEN_TILE = 512

F32 = jnp.float32
BF16 = jnp.bfloat16
I32 = jnp.int32


def nn(left, right):
    return lax.dot_general(left, right, (((1,), (0,)), ((), ())), preferred_element_type=F32)


def nt(left, right):
    return lax.dot_general(left, right, (((1,), (1,)), ((), ())), preferred_element_type=F32)


def tn(left, right):
    return lax.dot_general(left, right, (((0,), (0,)), ((), ())), preferred_element_type=F32)


def lane_iota(shape):
    return lax.broadcasted_iota(I32, shape, 1)


def row_iota(shape):
    return lax.broadcasted_iota(I32, shape, 0)


def whole(array):
    return pl.BlockSpec(array.shape, lambda *_: (0,) * array.ndim)


def row_blocks(array, tile):
    return pl.BlockSpec((tile, array.shape[1]), lambda i, *_: (i, 0))


def rank_mask(adapter_col, width):
    return jnp.where(lane_iota((adapter_col.shape[0], width)) // RANK == adapter_col, 1.0, 0.0)


def turn(values):
    lanes = lane_iota(values.shape) % HEAD
    return jnp.where(
        lanes < HEAD // 2,
        -pltpu.roll(values, LANES - HEAD // 2, 1),
        pltpu.roll(values, HEAD // 2, 1),
    )


def rms(values):
    return lax.rsqrt(jnp.mean(values * values, axis=-1, keepdims=True) + NORM_EPS)


def norm_back(values, gain, grad):
    inverse = rms(values)
    weighted = grad * gain
    return inverse * weighted - values * inverse * inverse * inverse * jnp.mean(
        weighted * values, axis=-1, keepdims=True
    )


def pick_rows(place_col, slots):
    hit = place_col == lane_iota((place_col.shape[0], slots))
    return jnp.where(hit, 1.0, 0.0).astype(BF16)


def place_rows(place_row, slots):
    hit = row_iota((slots, place_row.shape[1])) == place_row
    return jnp.where(hit, 1.0, 0.0).astype(BF16)


def params(**more):
    return pltpu.CompilerParams(vmem_limit_bytes=60 * 1024 * 1024, **more)


def cost(flops, moved):
    return pl.CostEstimate(flops=int(flops), bytes_accessed=int(moved), transcendentals=0)


def xor_bit(value, bit):
    size = 2**bit
    return value + size * (1 - 2 * lax.rem(value // size, 2))


def subsets(axes):
    out = [()]
    for axis in axes:
        out += [chosen + (axis,) for chosen in out]
    return out


def flip(place, part, axes):
    for axis in axes:
        if axis == "tensor":
            part = 1 - part
        else:
            place = xor_bit(place, axis)
    return place, part


def front_kernel(
    devices, rows_ref, chunk_ref, wq_ref, wo_ref, got_ref, copies_ref, wq_out, wo_out,
    local_sem, tsend, trecv, csend, crecv, wsend, wrecv,
):
    place, part = lax.axis_index("dp"), lax.axis_index("tensor")
    plane = devices // PLANES
    depth, inside = place // plane, lax.rem(place, plane)
    core = lax.rem(place, 2)
    own = 2 * place + part
    units = chunk_ref.shape[0]

    def rows_of(index):
        return copies_ref.at[pl.ds(index * units, units)]

    barrier = pltpu.get_barrier_semaphore()
    for k in range(1, devices):
        pl.semaphore_signal(
            barrier, inc=1, device_id=(lax.rem(place + k, devices), part), device_id_type=MESH
        )
    pl.semaphore_signal(barrier, inc=1, device_id=(place, 1 - part), device_id_type=MESH)
    pl.semaphore_wait(barrier, devices)

    keep = [
        pltpu.make_async_copy(chunk_ref, rows_of(own), local_sem.at[0]),
        pltpu.make_async_copy(rows_ref.at[place, part], got_ref.at[place], local_sem.at[1]),
    ]
    for copy in keep:
        copy.start()
    sent = []

    def chunk_copy(source, index, number, where):
        return pltpu.make_async_remote_copy(
            src_ref=source,
            dst_ref=rows_of(index),
            send_sem=csend.at[number],
            recv_sem=crecv.at[index],
            device_id=where,
            device_id_type=MESH,
        )

    def send_chunk(source, index, where):
        copy = chunk_copy(source, index, len(sent), where)
        copy.start()
        sent.append(copy)

    def take_chunk(index):
        chunk_copy(chunk_ref, index, 0, (place, 1 - part)).wait_recv()

    def layer(turn):
        return lax.rem(depth + turn, PLANES)

    for turn in (2, 3, 1):
        send_chunk(chunk_ref, own, (layer(turn) * plane + inside, part))

    def weight_copy(ref, out, number, slot, where):
        return pltpu.make_async_remote_copy(
            src_ref=ref.at[slot],
            dst_ref=out.at[slot],
            send_sem=wsend.at[number],
            recv_sem=wrecv.at[number],
            device_id=where,
            device_id_type=MESH,
        )

    direct = [
        weight_copy(wq_ref, wq_out, 0, core, (place, 1 - part)),
        weight_copy(wo_ref, wo_out, 1, core, (place, 1 - part)),
    ]
    for copy in direct:
        copy.start()

    rows_sent = []
    for turn in (2, 3, 1, 0):
        for step in range(plane):
            if turn == 0 and step == 0:
                continue
            target = layer(turn) * plane + lax.rem(inside + step, plane)
            copy = pltpu.make_async_remote_copy(
                src_ref=rows_ref.at[target, part],
                dst_ref=got_ref.at[place],
                send_sem=tsend.at[len(rows_sent)],
                recv_sem=trecv.at[place],
                device_id=(target, part),
                device_id_type=MESH,
            )
            copy.start()
            rows_sent.append((copy, target))

    bits = [2**b for b in range(plane.bit_length() - 1)]
    bits = list(range(len(bits)))[::-1]
    orders = [["tensor"] + bits, bits[:-1] + ["tensor"] + bits[-1:]]
    relayed = []
    for stage in range(len(bits) + 1):
        for turn in (0, 1, 2, 3):
            order = orders[turn % 2]
            origin = layer(turn) * plane + inside
            where = flip(place, part, [order[stage]])
            for chosen in subsets(order[:stage]):
                at, side = flip(origin, part, chosen)
                index = 2 * at + side
                if turn == 0 and not chosen:
                    send_chunk(chunk_ref, index, where)
                    continue
                if stage == 0 or order[stage - 1] in chosen:
                    take_chunk(index)
                send_chunk(rows_of(index), index, where)
        if stage == 0:
            partner = (xor_bit(place, 0), part)
            for number, (ref, out) in enumerate(((wq_ref, wq_out), (wo_ref, wo_out))):
                direct[number].wait_recv()
                copy = weight_copy(out, out, 2 + number, core, partner)
                copy.start()
                relayed.append(copy)
    for turn in (0, 1, 2, 3):
        order = orders[turn % 2]
        origin = layer(turn) * plane + inside
        for chosen in subsets(order):
            if order[-1] in chosen:
                at, side = flip(origin, part, chosen)
                take_chunk(2 * at + side)
    for number, (ref, out) in enumerate(((wq_ref, wq_out), (wo_ref, wo_out))):
        weight_copy(out, out, 2 + number, 1 - core, (place, 1 - part)).wait_recv()
    for copy, source in rows_sent:
        pltpu.make_async_remote_copy(
            src_ref=rows_ref.at[source, part],
            dst_ref=got_ref.at[source],
            send_sem=tsend.at[0],
            recv_sem=trecv.at[source],
            device_id=(source, part),
            device_id_type=MESH,
        ).wait_recv()
    for copy, _ in rows_sent:
        copy.wait_send()
    for copy in sent + direct + relayed:
        copy.wait_send()
    for copy in keep:
        copy.wait()


def front(rows, chunk, wq, wo, devices):
    _, _, piece, width = rows.shape
    anywhere = pl.BlockSpec(memory_space=pl.ANY)
    outs = [
        jax.ShapeDtypeStruct((devices, piece, width), BF16),
        jax.ShapeDtypeStruct((2 * devices * chunk.shape[0],) + chunk.shape[1:], BF16),
        jax.ShapeDtypeStruct(wq.shape, BF16),
        jax.ShapeDtypeStruct(wo.shape, BF16),
    ]
    return pl.pallas_call(
        functools.partial(front_kernel, devices),
        in_specs=[anywhere] * 4,
        out_specs=[anywhere] * 4,
        out_shape=outs,
        scratch_shapes=[
            pltpu.SemaphoreType.DMA((2,)),
            pltpu.SemaphoreType.DMA((devices,)),
            pltpu.SemaphoreType.DMA((devices,)),
            pltpu.SemaphoreType.DMA((2 * devices,)),
            pltpu.SemaphoreType.DMA((2 * devices,)),
            pltpu.SemaphoreType.DMA((4,)),
            pltpu.SemaphoreType.DMA((4,)),
        ],
        compiler_params=pltpu.CompilerParams(collective_id=0, has_side_effects=True),
        cost_estimate=cost(0, 100e6),
        name="front",
    )(rows, chunk, wq, wo)


def in_order(part, mine, theirs, place):
    @pl.when(part == 0)
    def _():
        place(mine, theirs)

    @pl.when(part == 1)
    def _():
        place(theirs, mine)


def project_kernel(
    part_ref, x_ref, meta_ref, cos_ref, sin_ref, gain_ref, mine_ref, theirs_ref,
    aq_ref, ak_ref, av_ref, bq_ref, bk_ref, bv_ref,
    n_ref, q_ref, kv_ref, z_ref, w_ref, bias,
):
    width = x_ref.shape[1]
    qw, kw = bq_ref.shape[0], bk_ref.shape[0]
    rank = bq_ref.shape[1]
    low = qw + 2 * kw

    @pl.when(pl.program_id(0) == 0)
    def _():
        def fill(first, second):
            at, to = 0, 0
            for size in (qw // 2, kw // 2, kw // 2):
                cut = slice(at, at + size)
                both = jnp.concatenate(
                    [first[:width, cut].astype(F32), second[:width, cut].astype(F32)], axis=1
                )
                w_ref[:, to : to + 2 * size] = both.astype(BF16)
                extra = jnp.concatenate(
                    [first[width : width + 8, cut].astype(F32), second[width : width + 8, cut].astype(F32)],
                    axis=1,
                )
                bias[:, to : to + 2 * size] = extra
                at += size
                to += 2 * size

        in_order(part_ref[0], mine_ref, theirs_ref, fill)
        for i, a_ref in enumerate((aq_ref, ak_ref, av_ref)):
            w_ref[:, low + i * rank : low + (i + 1) * rank] = a_ref[...]

    values = x_ref[...].astype(F32)
    normed = (values * rms(values) * gain_ref[...]).astype(BF16)
    n_ref[...] = normed
    base = nn(normed, w_ref[...])
    mask = rank_mask(meta_ref[:, 0:1], rank)
    lows = [(base[:, low + i * rank : low + (i + 1) * rank] * mask).astype(BF16) for i in range(3)]
    for i in range(3):
        z_ref[:, i * rank : (i + 1) * rank] = lows[i]
    cos, sin = cos_ref[...], sin_ref[...]
    queries = base[:, :qw] + bias[0:1, :qw] + ADAPTER_SCALE * nt(lows[0], bq_ref[...])
    for pair in range(qw // LANES):
        part = queries[:, pair * LANES : (pair + 1) * LANES]
        turned = (part * cos + turn(part) * sin) * HEAD**-0.5
        q_ref[:, pair * LANES : (pair + 1) * LANES] = turned.astype(BF16)
    keys = base[:, qw : qw + kw] + bias[0:1, qw : qw + kw] + ADAPTER_SCALE * nt(lows[1], bk_ref[...])
    kv_ref[:, :kw] = (keys * cos + turn(keys) * sin).astype(BF16)
    vals = base[:, qw + kw : low] + bias[0:1, qw + kw : low] + ADAPTER_SCALE * nt(lows[2], bv_ref[...])
    kv_ref[:, kw:] = vals.astype(BF16)


def project(part, x, meta, cos, sin, gain, mine, theirs, a_rows, b_rows):
    rows, width = x.shape
    b_q, b_k, _ = b_rows
    qw, kw, rank = b_q.shape[0], b_k.shape[0], b_q.shape[1]
    tile = ROW_TILE
    rest = (gain, mine, theirs, *a_rows, *b_rows)
    outs = [
        jax.ShapeDtypeStruct((rows, width), BF16),
        jax.ShapeDtypeStruct((rows, qw), BF16),
        jax.ShapeDtypeStruct((rows, 2 * kw), BF16),
        jax.ShapeDtypeStruct((rows, 3 * rank), BF16),
        jax.ShapeDtypeStruct((width, qw + 2 * kw + 3 * rank), BF16),
    ]
    return pl.pallas_call(
        project_kernel,
        grid_spec=pltpu.PrefetchScalarGridSpec(
            num_scalar_prefetch=1,
            grid=(rows // tile,),
            in_specs=[row_blocks(a, tile) for a in (x, meta, cos, sin)] + [whole(a) for a in rest],
            out_specs=[row_blocks(o, tile) for o in outs[:4]] + [whole(outs[4])],
            scratch_shapes=[pltpu.VMEM((8, qw + 2 * kw), F32)],
        ),
        out_shape=outs,
        compiler_params=params(),
        cost_estimate=cost(2 * rows * width * 1600, 9e6),
        name="project",
    )(part, x, meta, cos, sin, *rest)


def head_groups(heads, kv_heads):
    width = heads // kv_heads
    groups = {}
    for head in range(heads):
        groups.setdefault((head // width, head % 2), []).append(head)
    return [(kv, half, members) for (kv, half), members in sorted(groups.items())]


def spread_heads(tile_f32, kv, half):
    lanes = lane_iota(tile_f32.shape)
    moved = tile_f32 if kv % 2 == half else pltpu.roll(tile_f32, HEAD, 1)
    keep = (lanes >= HEAD) if half else (lanes < HEAD)
    return jnp.where(keep, moved, 0.0).astype(BF16)


def fill_heads(groups, source, keys_ref, values_ref):
    total = keys_ref.shape[1]
    for start in range(0, total, KEY_TILE):
        part = source(start).astype(F32)
        for number, (kv, half, _) in enumerate(groups):
            keys_ref[number, start : start + KEY_TILE, :] = spread_heads(part[:, :LANES], kv, half)
            values_ref[number, start : start + KEY_TILE, :] = spread_heads(
                part[:, LANES:], kv, half
            )


def attend_kernel(
    heads, kv_heads, bounds_ref, all_ref, meta_ref, metar_ref, own_ref, other_ref, column_ref,
    q_ref, o_ref, log_ref, merged_ref, slot_ref, keys, values, acc, top, total, held,
):
    step = pl.program_id(0)
    groups = head_groups(heads, kv_heads)
    rows = q_ref.shape[0]
    q_ref[...] = nn(pick_rows(meta_ref[:, 0:1], all_ref.shape[0]), all_ref[...]).astype(BF16)

    @pl.when(step == 0)
    def _():
        both = jnp.concatenate([own_ref[...], other_ref[...]], axis=0)

        def merged(start):
            picks = pick_rows(column_ref[start : start + KEY_TILE, :], both.shape[0])
            part = nn(picks, both)
            merged_ref[start : start + KEY_TILE, :] = part.astype(BF16)
            return part

        fill_heads(groups, merged, keys, values)

    acc[...] = jnp.zeros_like(acc)
    total[...] = jnp.zeros_like(total)
    top[...] = jnp.full_like(top, MASKED_SCORE)
    first, last = meta_ref[:, 1:2], meta_ref[:, 2:3]
    offsets = []
    cursor = 0
    for _, _, members in groups:
        offsets.append(cursor)
        cursor += len(members) * rows

    def one_tile(number, carry):
        start = pl.multiple_of(number * KEY_TILE, KEY_TILE)
        index = start + lane_iota((rows, KEY_TILE))
        bias = jnp.where((index >= first) & (index <= last), 0.0, MASKED_SCORE)
        for group, (_, _, members) in enumerate(groups):
            count = len(members)
            span = pl.ds(offsets[group], count * rows)
            stack = jnp.concatenate(
                [q_ref[:, (h // 2) * LANES : (h // 2 + 1) * LANES] for h in members], axis=0
            )
            scores = nt(stack, keys[group, pl.ds(start, KEY_TILE), :])
            scores = scores + jnp.concatenate([bias] * count, axis=0)
            old = top[span, :]
            new = jnp.maximum(old, jnp.max(scores, axis=1, keepdims=True))
            weights = jnp.exp(scores - new)
            shrink = jnp.exp(old - new)
            total[span, :] = total[span, :] * shrink + jnp.sum(weights, axis=1, keepdims=True)
            acc[span, :] = acc[span, :] * shrink + nn(
                weights.astype(BF16), values[group, pl.ds(start, KEY_TILE), :]
            )
            top[span, :] = new
        return carry

    lax.fori_loop(bounds_ref[0, step], bounds_ref[1, step], one_tile, 0)
    pairs = [None] * (heads // 2)
    logs = jnp.zeros((rows, LANES), F32)
    lanes = lane_iota((rows, LANES))
    for group, (_, _, members) in enumerate(groups):
        for at, head in enumerate(members):
            span = pl.ds(offsets[group] + at * rows, rows)
            sums = total[span, :]
            part = acc[span, :] / sums
            logs = jnp.where(lanes == head, top[span, :] + jnp.log(sums), logs)
            pair = head // 2
            pairs[pair] = part if pairs[pair] is None else pairs[pair] + part
    for pair, part in enumerate(pairs):
        o_ref[:, pair * LANES : (pair + 1) * LANES] = part.astype(BF16)
    log_ref[...] = jnp.transpose(logs)[: log_ref.shape[0], :]
    held[pl.ds(pl.multiple_of(step * rows, rows), rows), :] = o_ref[...]

    @pl.when(step == pl.num_programs(0) - 1)
    def _():
        slot_ref[...] = nn(place_rows(metar_ref[0:1, :], held.shape[0]), held[...]).astype(BF16)


def attend(bounds, q, meta, meta_rows, own_kv, other_kv, column, heads, kv_heads):
    rows, qw = q.shape
    tile = QUERY_TILE
    keys = 2 * rows
    groups = len(head_groups(heads, kv_heads))
    outs = [
        jax.ShapeDtypeStruct((rows, qw), BF16),
        jax.ShapeDtypeStruct((rows, qw), BF16),
        jax.ShapeDtypeStruct((16, rows), F32),
        jax.ShapeDtypeStruct((keys, own_kv.shape[1]), BF16),
        jax.ShapeDtypeStruct((rows, qw), BF16),
    ]
    return pl.pallas_call(
        functools.partial(attend_kernel, heads, kv_heads),
        grid_spec=pltpu.PrefetchScalarGridSpec(
            num_scalar_prefetch=1,
            grid=(rows // tile,),
            in_specs=[
                whole(q),
                row_blocks(meta, tile),
                whole(meta_rows),
                whole(own_kv),
                whole(other_kv),
                whole(column),
            ],
            out_specs=[
                row_blocks(outs[0], tile),
                row_blocks(outs[1], tile),
                pl.BlockSpec((16, tile), lambda i, *_: (0, i)),
                whole(outs[3]),
                whole(outs[4]),
            ],
            scratch_shapes=[
                pltpu.VMEM((groups, keys, LANES), BF16),
                pltpu.VMEM((groups, keys, LANES), BF16),
                pltpu.VMEM((heads * tile, LANES), F32),
                pltpu.VMEM((heads * tile, 1), F32),
                pltpu.VMEM((heads * tile, 1), F32),
                pltpu.VMEM((rows, qw), BF16),
            ],
        ),
        out_shape=outs,
        compiler_params=params(),
        cost_estimate=cost(heads * rows * keys * 256, 6e6),
        name="attend",
    )(bounds, q, meta, meta_rows, own_kv, other_kv, column)


def attend_back_kernel(
    heads, kv_heads, bounds_ref, q_ref, all_ref, o_ref, log_ref, meta_ref, metar_ref, cos_ref,
    sin_ref, merged_ref, column_ref, place_ref,
    gq_ref, own_ref, other_ref, keys, values, dkeys, dvalues, dq, dots, g_ref, held,
):
    step = pl.program_id(0)
    groups = head_groups(heads, kv_heads)
    rows = q_ref.shape[0]
    g_ref[...] = nn(pick_rows(meta_ref[:, 0:1], all_ref.shape[0]), all_ref[...]).astype(BF16)

    @pl.when(step == 0)
    def _():
        fill_heads(groups, lambda at: merged_ref[at : at + KEY_TILE, :], keys, values)
        dkeys[...] = jnp.zeros_like(dkeys)
        dvalues[...] = jnp.zeros_like(dvalues)

    dq[...] = jnp.zeros_like(dq)
    for pair in range(heads // 2):
        lanes = slice(pair * LANES, (pair + 1) * LANES)
        product = jnp.transpose(g_ref[:, lanes].astype(F32) * o_ref[:, lanes].astype(F32))
        dots[2 * pair : 2 * pair + 1, :] = jnp.sum(product[:HEAD], axis=0, keepdims=True)
        dots[2 * pair + 1 : 2 * pair + 2, :] = jnp.sum(product[HEAD:], axis=0, keepdims=True)
    first, last = metar_ref[1:2, :], metar_ref[2:3, :]

    def one_tile(number, carry):
        start = pl.multiple_of(number * KEY_TILE, KEY_TILE)
        index = start + row_iota((KEY_TILE, rows))
        bias = jnp.where((index >= first) & (index <= last), 0.0, MASKED_SCORE)
        for group, (_, half, members) in enumerate(groups):
            count = len(members)
            span = pl.ds(start, KEY_TILE)
            cut = [slice((h // 2) * LANES, (h // 2 + 1) * LANES) for h in members]
            stack = jnp.concatenate([q_ref[:, c] for c in cut], axis=0)
            grads = jnp.concatenate([g_ref[:, c] for c in cut], axis=0)
            logs = jnp.concatenate([log_ref[h : h + 1, :] for h in members], axis=1)
            drop = jnp.concatenate([dots[h : h + 1, :] for h in members], axis=1)
            key_part = keys[group, span, :]
            scores = nt(key_part, stack) + jnp.concatenate([bias] * count, axis=1)
            weights = jnp.exp(scores - logs)
            change = nt(values[group, span, :], grads)
            dscores = (weights * (change - drop)).astype(BF16)
            dvalues[group, span, :] += nn(weights.astype(BF16), grads)
            dkeys[group, span, :] += nn(dscores, stack)
            back = tn(dscores, key_part)
            for at, head in enumerate(members):
                dq[head // 2, :, :] += back[at * rows : (at + 1) * rows, :]
        return carry

    lax.fori_loop(bounds_ref[0, step], bounds_ref[1, step], one_tile, 0)
    cos, sin = cos_ref[...], sin_ref[...]
    for pair in range(heads // 2):
        grad = dq[pair, :, :] * HEAD**-0.5
        grad = grad * cos - turn(grad) * sin
        held[
            pl.ds(pl.multiple_of(step * rows, rows), rows), pair * LANES : (pair + 1) * LANES
        ] = grad.astype(BF16)

    @pl.when(step == pl.num_programs(0) - 1)
    def _():
        gq_ref[...] = nn(place_rows(place_ref[0:1, :], held.shape[0]), held[...]).astype(BF16)
        total = dkeys.shape[1]

        def join(ref):
            out = None
            for group, (kv, half, _) in enumerate(groups):
                part = ref[group, :, :]
                lanes = lane_iota(part.shape)
                part = jnp.where((lanes >= HEAD) if half else (lanes < HEAD), part, 0.0)
                if kv % 2 != half:
                    part = pltpu.roll(part, HEAD, 1)
                out = part if out is None else out + part
            return out.astype(BF16)

        both = jnp.concatenate([join(dkeys), join(dvalues)], axis=1)
        half_rows = own_ref.shape[0]
        for at in range(0, total, KEY_TILE):
            hit = (at + row_iota((KEY_TILE, total))) == column_ref[...]
            part = nn(jnp.where(hit, 1.0, 0.0).astype(BF16), both).astype(BF16)
            if at < half_rows:
                own_ref[at : at + KEY_TILE, :] = part
            else:
                other_ref[at - half_rows : at - half_rows + KEY_TILE, :] = part


def attend_back(
    bounds, q, grad, o, logs, meta, meta_rows, cos, sin, merged, column_row, heads, kv_heads
):
    rows, qw = q.shape
    tile = QUERY_TILE
    keys, kvw = merged.shape
    groups = len(head_groups(heads, kv_heads))
    outs = [
        jax.ShapeDtypeStruct((rows, qw), BF16),
        jax.ShapeDtypeStruct((rows, kvw), BF16),
        jax.ShapeDtypeStruct((rows, kvw), BF16),
    ]
    return pl.pallas_call(
        functools.partial(attend_back_kernel, heads, kv_heads),
        grid_spec=pltpu.PrefetchScalarGridSpec(
            num_scalar_prefetch=1,
            grid=(rows // tile,),
            in_specs=[
                row_blocks(q, tile),
                whole(grad),
                row_blocks(o, tile),
                pl.BlockSpec((16, tile), lambda i, *_: (0, i)),
                row_blocks(meta, tile),
                pl.BlockSpec((8, tile), lambda i, *_: (0, i)),
                row_blocks(cos, tile),
                row_blocks(sin, tile),
                whole(merged),
                whole(column_row),
                whole(meta_rows),
            ],
            out_specs=[whole(o) for o in outs],
            scratch_shapes=[
                pltpu.VMEM((groups, keys, LANES), BF16),
                pltpu.VMEM((groups, keys, LANES), BF16),
                pltpu.VMEM((groups, keys, LANES), F32),
                pltpu.VMEM((groups, keys, LANES), F32),
                pltpu.VMEM((heads // 2, tile, LANES), F32),
                pltpu.VMEM((16, tile), F32),
                pltpu.VMEM((tile, qw), BF16),
                pltpu.VMEM((rows, qw), BF16),
            ],
        ),
        out_shape=outs,
        compiler_params=params(),
        cost_estimate=cost(heads * rows * keys * 640, 9e6),
        name="attend_back",
    )(bounds, q, grad, o, logs, meta, meta_rows, cos, sin, merged, column_row, meta_rows)


def middle_kernel(
    part_ref, o_ref, x_ref, meta_ref, mine_ref, theirs_ref, a_ref, b_ref, gain_ref,
    y_ref, n_ref, z_ref, w_ref,
):
    width = x_ref.shape[1]
    rank = b_ref.shape[1]
    half = mine_ref.shape[0]

    @pl.when(pl.program_id(0) == 0)
    def _():
        def fill(first, second):
            w_ref[:half, :width] = first[...]
            w_ref[half:, :width] = second[...]

        in_order(part_ref[0], mine_ref, theirs_ref, fill)
        w_ref[:, width:] = a_ref[...]

    mask = rank_mask(meta_ref[:, 0:1], rank)
    base = nn(o_ref[...], w_ref[...])
    low = (base[:, width:] * mask).astype(BF16)
    z_ref[...] = low
    values = x_ref[...].astype(F32) + (base[:, :width] + ADAPTER_SCALE * nt(low, b_ref[...]))
    y_ref[...] = values
    n_ref[...] = (values * rms(values) * gain_ref[...]).astype(BF16)


def middle(part, o, x, meta, mine, theirs, a_out, b_out, gain):
    rows, width = x.shape
    rank = b_out.shape[1]
    tile = ROW_TILE
    rest = (mine, theirs, a_out, b_out, gain)
    outs = [
        jax.ShapeDtypeStruct((rows, width), F32),
        jax.ShapeDtypeStruct((rows, width), BF16),
        jax.ShapeDtypeStruct((rows, rank), BF16),
        jax.ShapeDtypeStruct((o.shape[1], width + rank), BF16),
    ]
    return pl.pallas_call(
        middle_kernel,
        grid_spec=pltpu.PrefetchScalarGridSpec(
            num_scalar_prefetch=1,
            grid=(rows // tile,),
            in_specs=[row_blocks(a, tile) for a in (o, x, meta)] + [whole(a) for a in rest],
            out_specs=[row_blocks(a, tile) for a in outs[:3]] + [whole(outs[3])],
        ),
        out_shape=outs,
        compiler_params=params(),
        cost_estimate=cost(2 * rows * width * 1100, 12e6),
        name="middle",
    )(part, o, x, meta, *rest)


class Windows:
    def __init__(self, devices, own_rows):
        self.devices = devices
        self.own_rows = own_rows
        self.plane = devices // PLANES
        self.axes = list(range(self.plane.bit_length() - 1)) + ["tensor"]
        self.rows = 16 * ((own_rows + 30) // 16)
        self.last = 16 * (((2 * devices - 1) * own_rows) // 16) + self.rows

    def start(self, zz, at, side):
        row = (2 * (zz * self.plane + at) + side) * self.own_rows
        return pl.multiple_of((row // 16) * 16, 16)

    def span(self, zz, at, side):
        return pl.ds(self.start(zz, at, side), self.rows)

    def boxes(self, stage):
        return 2 ** (len(self.axes) - 1 - stage)

    def box(self, stage, at, side):
        index = 0
        for order, axis in enumerate(self.axes[stage + 1 :]):
            bit = side if axis == "tensor" else lax.rem(at // 2**axis, 2)
            index = index + bit * 2**order
        return index

    def leaving(self, stage, inside, part):
        for chosen in subsets(self.axes[stage + 1 :]):
            yield flip(inside, part, [self.axes[stage]] + list(chosen))

    def staying(self, stage, inside, part):
        for chosen in subsets(self.axes[stage + 1 :]):
            yield flip(inside, part, list(chosen))


def middle_back_kernel(
    plan, da_ref, db_ref, y1_ref, dy_ref, o_ref, z_ref, meta_ref, b_ref, w_ref, gain_ref, flat_ref,
    dy1_ref, dar_ref, grad_ref, on_ref, kept_ref, acc_bo, acc_ao, mine, inbox, msem, ssem, rsem,
):
    step = pl.program_id(0)
    rank = b_ref.shape[1]
    qw = o_ref.shape[1]
    place, part = lax.axis_index("dp"), lax.axis_index("tensor")
    inside = lax.rem(place, plan.plane)
    partner = flip(place, part, [plan.axes[0]])
    boxes = plan.boxes(0)

    def moves():
        local, remote = [], []
        for zz in range(1, PLANES):
            for at, side in plan.leaving(0, inside, part):
                index = (zz - 1) * boxes + plan.box(0, at, side)
                remote.append(
                    pltpu.make_async_remote_copy(
                        src_ref=flat_ref.at[plan.span(zz, at, side), :],
                        dst_ref=inbox.at[index],
                        send_sem=ssem.at[len(remote)],
                        recv_sem=rsem.at[index],
                        device_id=partner,
                        device_id_type=MESH,
                    )
                )
            for at, side in plan.staying(0, inside, part):
                index = (zz - 1) * boxes + plan.box(0, at, side)
                local.append(
                    pltpu.make_async_copy(
                        flat_ref.at[plan.span(zz, at, side), :], mine.at[index], msem.at[len(local)]
                    )
                )
        return local, remote

    @pl.when(step == 0)
    def _():
        acc_bo[...] = jnp.zeros_like(acc_bo)
        acc_ao[...] = jnp.zeros_like(acc_ao)
        barrier = pltpu.get_barrier_semaphore()
        pl.semaphore_signal(barrier, inc=1, device_id=partner, device_id_type=MESH)
        pl.semaphore_wait(barrier, 1)
        local, remote = moves()
        for copy in remote + local:
            copy.start()

    mask = rank_mask(meta_ref[:, 0:1], rank)
    grad = da_ref[...] + db_ref[...].astype(F32)
    dy1 = dy_ref[...].astype(F32) + norm_back(y1_ref[...], gain_ref[...], grad)
    dy1_ref[...] = dy1
    low_grad = dy1.astype(BF16)
    back_out = (ADAPTER_SCALE * nn(low_grad, b_ref[...]) * mask).astype(BF16)
    both = jnp.concatenate([low_grad, back_out], axis=1)
    dar_ref[...] = nt(both, w_ref[...]).astype(BF16)
    acc_bo[...] += ADAPTER_SCALE * tn(low_grad, z_ref[...])
    acc_ao[...] += tn(o_ref[...], back_out)

    @pl.when(step == pl.num_programs(0) - 1)
    def _():
        grad_ref[:qw, :] = acc_ao[...].astype(BF16)
        grad_ref[qw:, :] = acc_bo[...].astype(BF16)
        local, remote = moves()
        for copy in local:
            copy.wait()
        for copy in remote:
            copy.wait_recv()
        later = plan.boxes(1)

        def total(zz, at, side):
            index = (zz - 1) * boxes + plan.box(0, at, side)
            return mine[index].astype(F32) + inbox[index].astype(F32)

        for zz in range(1, PLANES):
            for at, side in plan.leaving(1, inside, part):
                on_ref[(zz - 1) * later + plan.box(1, at, side)] = total(zz, at, side).astype(BF16)
            for at, side in plan.staying(1, inside, part):
                kept_ref[(zz - 1) * later + plan.box(1, at, side)] = total(zz, at, side)
        for copy in remote:
            copy.wait_send()


def middle_back(
    devices, own_rows, d_first, d_second, y1, dy, o, z, meta, b_out, w_out, gain, flat
):
    rows, width = y1.shape
    rank = b_out.shape[1]
    qw = o.shape[1]
    tile = ROW_TILE
    plan = Windows(devices, own_rows)
    first, second = (PLANES - 1) * plan.boxes(0), (PLANES - 1) * plan.boxes(1)
    outs = [
        jax.ShapeDtypeStruct((rows, width), F32),
        jax.ShapeDtypeStruct((rows, qw), BF16),
        jax.ShapeDtypeStruct((qw + width, rank), BF16),
        jax.ShapeDtypeStruct((second, plan.rows, rank), BF16),
        jax.ShapeDtypeStruct((second, plan.rows, rank), F32),
    ]
    return pl.pallas_call(
        functools.partial(middle_back_kernel, plan),
        grid=(rows // tile,),
        in_specs=[row_blocks(a, tile) for a in (d_first, d_second, y1, dy, o, z, meta)]
        + [whole(a) for a in (b_out, w_out, gain)]
        + [pl.BlockSpec(memory_space=pl.ANY)],
        out_specs=[row_blocks(a, tile) for a in outs[:2]] + [whole(a) for a in outs[2:]],
        out_shape=outs,
        scratch_shapes=[
            pltpu.VMEM((width, rank), F32),
            pltpu.VMEM((qw, rank), F32),
            pltpu.VMEM((first, plan.rows, rank), BF16),
            pltpu.VMEM((first, plan.rows, rank), BF16),
            pltpu.SemaphoreType.DMA((first,)),
            pltpu.SemaphoreType.DMA((first,)),
            pltpu.SemaphoreType.DMA((first,)),
        ],
        compiler_params=params(collective_id=3, has_side_effects=True),
        cost_estimate=cost(2 * rows * width * 1500, 20e6),
        name="middle_back",
    )(d_first, d_second, y1, dy, o, z, meta, b_out, w_out, gain, flat)


def own_tile(step, tiles):
    return jnp.maximum(step - tiles, 0)


def their_tile(step, tiles):
    return jnp.clip(step - 1, 0, tiles - 1)


def feed_kernel(
    n_ref, n_hbm, dy_ref, dyt_ref, meta_ref, metat_ref, ap_ref, bd_ref, wg_hbm, wu_hbm, wd_hbm,
    bg_hbm, bu_hbm, ad_hbm,
    y_ref, d_ref, y_got, d_got, last_ref, flat_ref,
    wga, wua, wda, raw, grads, extras, xg, xu, dya, yacc, dacc, mask_s, n_got, held_d, held_y,
    packed, blank, wsem, gsem, nsend, nrecv, dsend, drecv, ysend, yrecv,
):
    step = pl.program_id(0)
    steps = pl.num_programs(0)
    tiles_each = n_got.shape[0]
    width, half = wg_hbm.shape
    rank = bd_ref.shape[1]
    rows = n_ref.shape[0]
    place, part = lax.axis_index("dp"), lax.axis_index("tensor")
    theirs = (step >= 1) & (step <= tiles_each)
    number_t = their_tile(step, tiles_each)
    tile = HIDDEN_TILE
    tiles = pl.cdiv(half, tile)
    lap = tiles * tile - half

    def loads(number):
        at = pl.multiple_of(jnp.minimum(number * tile, half - tile), LANES)
        to = pl.multiple_of(number * tile, tile)
        here, there = pl.ds(at, tile), pl.ds(to, tile)
        top, side = pl.ds(0, width), pl.ds(width, rank)
        pairs = [
            (wg_hbm.at[:, here], wga.at[top, there]),
            (wu_hbm.at[:, here], wua.at[top, there]),
            (wd_hbm.at[here, :], wda.at[there, top]),
            (bg_hbm.at[here, :], raw.at[0, there, :]),
            (bu_hbm.at[here, :], raw.at[1, there, :]),
            (ad_hbm.at[here, :], wda.at[there, side]),
        ]
        return [
            pltpu.make_async_copy(source, target, wsem.at[number, at])
            for at, (source, target) in enumerate(pairs)
        ]

    def swap(source, target, sends, recvs, number):
        return pltpu.make_async_remote_copy(
            src_ref=source,
            dst_ref=target.at[number],
            send_sem=sends.at[number],
            recv_sem=recvs.at[number],
            device_id=(place, 1 - part),
            device_id_type=MESH,
        )

    def send_n(number):
        return swap(n_hbm.at[pl.ds(number * rows, rows), :], n_got, nsend, nrecv, number)

    def send_d(number):
        return swap(held_d.at[number], d_got, dsend, drecv, number)

    def send_y(number):
        return swap(held_y.at[number], y_got, ysend, yrecv, number)

    @pl.when(step == 0)
    def _():
        for number in range(tiles):
            for copy in loads(number):
                copy.start()
        barrier = pltpu.get_barrier_semaphore()
        pl.semaphore_signal(barrier, inc=1, device_id=(place, 1 - part), device_id_type=MESH)
        pl.semaphore_wait(barrier, 1)
        for number in range(tiles_each):
            send_n(number).start()
        grads[...] = jnp.zeros_like(grads)
        extras[...] = jnp.zeros_like(extras)

    def prepare(normed, dy, adapter):
        mask = rank_mask(adapter, rank)
        mask_s[...] = mask
        lows = nn(normed, ap_ref[...])
        xg[:, :width] = normed
        xu[:, :width] = normed
        xg[:, width:] = (lows[:, :rank] * mask).astype(BF16)
        xu[:, width:] = (lows[:, rank:] * mask).astype(BF16)
        dya[:, :width] = dy
        dya[:, width:] = (ADAPTER_SCALE * nn(dy, bd_ref[...]) * mask).astype(BF16)

    @pl.when(jnp.logical_not(theirs))
    def _():
        prepare(n_ref[...], dy_ref[...], meta_ref[:, 0:1])

    @pl.when(theirs)
    def _():
        send_n(number_t).wait_recv()
        prepare(n_got[number_t], dyt_ref[...], metat_ref[:, 0:1])

    yacc[...] = jnp.zeros_like(yacc)
    dacc[...] = jnp.zeros_like(dacc)

    def hidden(number, carry):
        span = pl.ds(pl.multiple_of(number * tile, tile), tile)

        @pl.when(step == 0)
        def _():
            for copy in loads(number):
                copy.wait()
            for at, target in enumerate((wga, wua)):
                turned = jnp.transpose(raw[at, span, :].astype(F32) * ADAPTER_SCALE)
                target[width:, span] = turned.astype(BF16)
            if lap:

                @pl.when(number == tiles - 1)
                def _():
                    edge = slice((tiles - 1) * tile, (tiles - 1) * tile + lap)
                    wga[:, edge] = jnp.zeros((width + rank, lap), BF16)
                    wua[:, edge] = jnp.zeros((width + rank, lap), BF16)
                    wda[edge, :] = jnp.zeros((lap, width + rank), BF16)

        gate = nn(xg[...], wga[:, span])
        up = nn(xu[...], wua[:, span])
        dhid = nt(dya[...], wda[span, :])
        sig = 1.0 / (1.0 + jnp.exp(-gate))
        silu = gate * sig
        hid = (silu * up).astype(BF16)
        dg = (dhid * up * (sig * (1.0 + gate * (1.0 - sig)))).astype(BF16)
        du = (dhid * silu).astype(BF16)
        yacc[...] += nn(hid, wda[span, :])
        dga = nt(dg, wga[:, span])
        dua = nt(du, wua[:, span])
        dacc[:, :width] += dga[:, :width] + dua[:, :width]
        dacc[:, width : width + rank] += dga[:, width:]
        dacc[:, width + rank :] += dua[:, width:]
        grads[0, span, :] += ADAPTER_SCALE * tn(dg, xg[:, width:])
        grads[1, span, :] += ADAPTER_SCALE * tn(du, xu[:, width:])
        grads[2, span, :] += tn(hid, dya[:, width:])
        return carry

    lax.fori_loop(0, tiles, hidden, 0)
    mask = mask_s[...]
    low = (yacc[:, width:] * mask).astype(BF16)
    result = yacc[:, :width] + ADAPTER_SCALE * nt(low, bd_ref[...])
    back = (dacc[:, width:] * jnp.concatenate([mask, mask], axis=1)).astype(BF16)
    change = dacc[:, :width] + nt(back, ap_ref[...])
    pair = tn(xg[:, :width], back)
    extras[0] += pair[:, :rank]
    extras[1] += pair[:, rank:]
    extras[2] += ADAPTER_SCALE * tn(dya[:, :width], low)

    @pl.when(jnp.logical_not(theirs))
    def _():
        y_ref[...] = result
        d_ref[...] = change

    @pl.when(theirs)
    def _():
        held_d[number_t] = change.astype(BF16)
        send_d(number_t).start()

        @pl.when(number_t < tiles_each - 1)
        def _():
            held_y[number_t] = result.astype(BF16)

        @pl.when(number_t == tiles_each - 1)
        def _():
            last_ref[...] = result.astype(BF16)
            for number in range(tiles_each - 1):
                send_y(number).start()

    @pl.when(step == steps - 1)
    def _():
        last = (tiles - 1) * tile
        for at in range(3):
            packed[at, :last, :] = grads[at, :last, :].astype(BF16)
            packed[at, last:half, :] = grads[at, last + lap : tiles * tile, :].astype(BF16)
            packed[at, half:, :] = extras[at].astype(BF16)
        blank[...] = jnp.zeros_like(blank)
        a_gate = flat_ref.shape[0] - FLAT_PAD - 3 * width - 6 * half
        a_up = a_gate + width + 2 * half
        a_down = a_up + width + 2 * half
        b_down = a_down + 2 * half
        moves = []
        for at, base in enumerate((a_gate + width, a_up + width, a_down)):
            mine = pl.multiple_of(base + part * half, 16)
            other = pl.multiple_of(base + (1 - part) * half, 16)
            moves.append((packed.at[at, pl.ds(0, half), :], flat_ref.at[pl.ds(mine, half), :]))
            moves.append((blank, flat_ref.at[pl.ds(other, half), :]))
        for at, base in enumerate((a_gate, a_up, b_down)):
            moves.append((packed.at[at, pl.ds(half, width), :], flat_ref.at[pl.ds(base, width), :]))
        moves = [
            pltpu.make_async_copy(source, target, gsem.at[at])
            for at, (source, target) in enumerate(moves)
        ]
        for copy in moves:
            copy.start()
        for copy in moves:
            copy.wait()
        for number in range(tiles_each):
            send_n(number).wait_send()
            send_d(number).wait_send()
            send_d(number).wait_recv()
        for number in range(tiles_each - 1):
            send_y(number).wait_send()
            send_y(number).wait_recv()


def feed(
    total, n2, dy, dy_theirs, meta, meta_theirs, a_pair, b_down, w_gate, w_up, w_down, b_gate, b_up,
    a_down,
):
    rows, width = n2.shape
    half, rank = a_down.shape
    tile = ROW_TILE
    count = rows // tile
    tiles = pl.cdiv(half, HIDDEN_TILE)
    padded = tiles * HIDDEN_TILE
    anywhere = pl.BlockSpec(memory_space=pl.ANY)
    wide, deep = width + rank, width + 2 * rank

    def own_rows(array):
        return pl.BlockSpec((tile, array.shape[1]), lambda i: (own_tile(i, count), 0))

    def their_rows(array):
        return pl.BlockSpec((tile, array.shape[1]), lambda i: (their_tile(i, count), 0))

    dma = pltpu.SemaphoreType.DMA
    outs = [
        jax.ShapeDtypeStruct((rows, width), F32),
        jax.ShapeDtypeStruct((rows, width), F32),
        jax.ShapeDtypeStruct((count - 1, tile, width), BF16),
        jax.ShapeDtypeStruct((count, tile, width), BF16),
        jax.ShapeDtypeStruct((tile, width), BF16),
        jax.ShapeDtypeStruct((total + FLAT_PAD, rank), BF16),
    ]
    return pl.pallas_call(
        feed_kernel,
        grid=(2 * count,),
        in_specs=[
            own_rows(n2), anywhere, own_rows(dy), their_rows(dy_theirs), own_rows(meta),
            their_rows(meta_theirs), whole(a_pair), whole(b_down),
        ]
        + [anywhere] * 6,
        out_specs=[own_rows(outs[0]), own_rows(outs[1]), anywhere, anywhere, whole(outs[4]), anywhere],
        out_shape=outs,
        scratch_shapes=[
            pltpu.VMEM((wide, padded), BF16),
            pltpu.VMEM((wide, padded), BF16),
            pltpu.VMEM((padded, wide), BF16),
            pltpu.VMEM((2, padded, rank), BF16),
            pltpu.VMEM((3, padded, rank), F32),
            pltpu.VMEM((3, width, rank), F32),
            pltpu.VMEM((tile, wide), BF16),
            pltpu.VMEM((tile, wide), BF16),
            pltpu.VMEM((tile, wide), BF16),
            pltpu.VMEM((tile, wide), F32),
            pltpu.VMEM((tile, deep), F32),
            pltpu.VMEM((tile, rank), F32),
            pltpu.VMEM((count, tile, width), BF16),
            pltpu.VMEM((count, tile, width), BF16),
            pltpu.VMEM((count - 1, tile, width), BF16),
            pltpu.VMEM((3, half + width, rank), BF16),
            pltpu.VMEM((half, rank), BF16),
            dma((tiles, 6)),
            dma((9,)),
            dma((count,)),
            dma((count,)),
            dma((count,)),
            dma((count,)),
            dma((count - 1,)),
            dma((count - 1,)),
        ],
        compiler_params=params(collective_id=1, has_side_effects=True),
        cost_estimate=cost(4 * rows * half * (6 * width + 9 * rank), 40e6),
        name="feed",
    )(n2, n2, dy, dy_theirs, meta, meta_theirs, a_pair, b_down, w_gate, w_up, w_down, b_gate, b_up, a_down)


def tail_kernel(plan, early, key_width, direct, *refs):
    sources = refs[:9]
    other_ref, layer_ref, w_hbm, b_ref, gain_ref, flat_ref, out_grad_ref, kept_hbm, gots_hbm = refs[9:18]
    layer_out, out_ref, sum_ref = refs[18:21]
    held = refs[21:30]
    w, grads, dxs, acc_a, acc_b, outbox, last_in, got_s, kept, gots, *rest = refs[30:]
    inboxes = rest[:-15]
    (
        load_sem, grad_sem, dsend, drecv, fsend, frecv, rsend, rrecv, zrecv, keep_sem, ksend, krecv,
        lsend, lrecv, hsem,
    ) = rest[-15:]
    gq_s, own_s, x_s, n_s, z_s, dy1_s, meta_s, cos_s, sin_s = held
    place, part = lax.axis_index("dp"), lax.axis_index("tensor")
    devices, plane, axes = plan.devices, plan.plane, plan.axes
    depth, inside = place // plane, lax.rem(place, plane)
    count = len(axes)
    tile = x_s.shape[1]
    rank = b_ref.shape[1]
    width = x_s.shape[2]
    qw, kw = gq_s.shape[2], key_width
    over = (place, 1 - part)

    def layer(hop):
        return lax.rem(depth + hop, PLANES)

    def turn_of(number):
        return lax.rem(number + 2, PLANES)

    def rows_at(number):
        return pl.ds(pl.multiple_of(layer(turn_of(number)) * tile, 16), tile)

    def tile_loads(number):
        return [
            pltpu.make_async_copy(
                source.at[rows_at(number), :], target.at[number], load_sem.at[number, which]
            )
            for which, (source, target) in enumerate(zip(sources, held))
        ]

    sums_loads = [
        pltpu.make_async_copy(kept_hbm, kept, grad_sem.at[3]),
        pltpu.make_async_copy(gots_hbm, gots, grad_sem.at[4]),
    ]
    w_load = pltpu.make_async_copy(w_hbm, w, grad_sem.at[0])
    middle = out_grad_ref.shape[0]
    late_rows = grads.shape[0] - early - middle
    grad_loads = [
        pltpu.make_async_copy(out_grad_ref, grads.at[pl.ds(early, middle), :], grad_sem.at[1]),
        pltpu.make_async_copy(
            flat_ref.at[pl.ds(early + middle, late_rows), :],
            grads.at[pl.ds(early + middle, late_rows), :],
            grad_sem.at[2],
        ),
    ]
    for copy in sums_loads + [w_load]:
        copy.start()
    for number in range(PLANES):
        for copy in tile_loads(number):
            copy.start()
    for copy in grad_loads:
        copy.start()

    barrier = pltpu.get_barrier_semaphore()
    for k in range(1, devices):
        pl.semaphore_signal(
            barrier, inc=1, device_id=(lax.rem(place + k, devices), part), device_id_type=MESH
        )
    pl.semaphore_signal(barrier, inc=1, device_id=over, device_id_type=MESH)
    pl.semaphore_wait(barrier, devices)

    def key_copy(number):
        return pltpu.make_async_remote_copy(
            src_ref=other_ref.at[rows_at(number), :],
            dst_ref=got_s.at[number],
            send_sem=ksend.at[number],
            recv_sem=krecv.at[number],
            device_id=over,
            device_id_type=MESH,
        )

    for number in range(PLANES):
        key_copy(number).start()

    bases = []
    cursor = 0
    for stage in range(count):
        bases.append(cursor)
        cursor += plan.boxes(stage) * (1 if stage < 2 else PLANES)

    def box_of(stage, zz, at, side):
        return plan.box(stage, at, side) + (0 if stage < 2 else zz * plan.boxes(stage))

    def window_sum(stages, zz, at, side):
        if zz == 0:
            total = grads[plan.span(0, at, side), :].astype(F32)
            for stage in range(min(2, stages)):
                total = total + inboxes[stage][box_of(stage, 0, at, side)].astype(F32)
        else:
            index = (zz - 1) * plan.boxes(1) + plan.box(1, at, side)
            total = kept[index] + gots[index].astype(F32)
        for stage in range(2, stages):
            total = total + inboxes[stage][box_of(stage, zz, at, side)].astype(F32)
        return total

    def take(stages, zz, at, side):
        for stage in range(0 if zz == 0 else 2, stages):
            index = box_of(stage, zz, at, side)
            pltpu.make_async_remote_copy(
                src_ref=inboxes[stage].at[index],
                dst_ref=inboxes[stage].at[index],
                send_sem=rsend.at[0],
                recv_sem=rrecv.at[bases[stage] + index],
                device_id=over,
                device_id_type=MESH,
            ).wait_recv()

    sent = []
    posted = [0]

    def pass_on(stage, zz, source_of):
        partner = flip(place, part, [axes[stage]])
        for at, side in plan.leaving(stage, inside, part):
            index = box_of(stage, zz, at, side)
            copy = pltpu.make_async_remote_copy(
                src_ref=source_of(at, side),
                dst_ref=inboxes[stage].at[index],
                send_sem=rsend.at[len(sent)],
                recv_sem=rrecv.at[bases[stage] + index],
                device_id=partner,
                device_id_type=MESH,
            )
            copy.start()
            sent.append(copy)

    def post(total):
        slot = posted[0]
        posted[0] += 1
        outbox[slot] = total.astype(BF16)
        return outbox.at[slot]

    def stage_sends(stage, zz):
        def source_of(at, side):
            take(stage, zz, at, side)
            return post(window_sum(stage, zz, at, side))

        pass_on(stage, zz, source_of)

    for copy in sums_loads:
        copy.wait()
    for zz in range(1, PLANES):
        stage_sends(2, zz)

    def step_at(step):
        return lax.rem(inside + step, plane)

    def layer_copy(hop, step):
        target = layer(hop) * plane + step_at(step)
        return pltpu.make_async_remote_copy(
            src_ref=layer_ref.at[target],
            dst_ref=layer_out.at[place, part],
            send_sem=lsend.at[hop, step],
            recv_sem=lrecv.at[place],
            device_id=(target, part),
            device_id_type=MESH,
        )

    layer_keep = pltpu.make_async_copy(
        layer_ref.at[place], layer_out.at[place, part], keep_sem.at[1]
    )
    layer_sends = [(hop, step) for hop in (2, 3, 1, 0) for step in range(plane) if hop or step]
    if direct:
        for hop, step in layer_sends:
            layer_copy(hop, step).start()
        layer_keep.start()

    acc_a[...] = jnp.zeros_like(acc_a)
    acc_b[...] = jnp.zeros_like(acc_b)
    w_load.wait()

    def piece_copy(number, step, where, target):
        return pltpu.make_async_remote_copy(
            src_ref=dxs.at[number, step_at(step)],
            dst_ref=target,
            send_sem=dsend.at[number, step],
            recv_sem=drecv.at[place],
            device_id=where,
            device_id_type=MESH,
        )

    def one_tile(number, carry):
        for copy in tile_loads(number):
            copy.wait()
        key_copy(number).wait_recv()
        mask = rank_mask(meta_s[number][:, 0:1], rank)
        both = own_s[number].astype(F32) + got_s[number].astype(F32)
        cos, sin = cos_s[number], sin_s[number]
        dk = both[:, :kw]
        gq = gq_s[number]
        gk = (dk * cos - turn(dk) * sin).astype(BF16)
        gv = both[:, kw:].astype(BF16)
        at_k, at_v = 2 * width + qw, 3 * width + qw + kw
        b_parts = (
            b_ref[width : width + qw, :],
            b_ref[at_k : at_k + kw, :],
            b_ref[at_v : at_v + kw, :],
        )
        backs = [
            (ADAPTER_SCALE * nn(g, b) * mask).astype(BF16) for g, b in zip((gq, gk, gv), b_parts)
        ]
        dn = nt(jnp.concatenate([gq, gk, gv] + backs, axis=1), w[...])
        values = x_s[number].astype(F32)
        dx = (dy1_s[number] + norm_back(values, gain_ref[...], dn)).astype(BF16)
        acc_a[...] += tn(n_s[number], jnp.concatenate(backs, axis=1))
        low = z_s[number]
        acc_b[:qw, :] += tn(gq, low[:, :rank])
        acc_b[qw : qw + kw, :] += tn(gk, low[:, rank : 2 * rank])
        acc_b[qw + kw :, :] += tn(gv, low[:, 2 * rank :])
        turn_now = turn_of(number)
        if not direct:
            dxs[number] = dx
            copy = pltpu.make_async_copy(
                dxs.at[number], out_ref.at[rows_at(number), :], keep_sem.at[0]
            )
            copy.start()
            copy.wait()
            return carry
        dxs[number] = dx.reshape(dxs.shape[1:])
        for step in range(plane):
            target = layer(turn_now) * plane + step_at(step)
            if step > 0:
                piece_copy(number, step, (target, part), out_ref.at[place, part]).start()
                continue

            @pl.when(turn_now == 0)
            def _():
                pltpu.make_async_copy(
                    dxs.at[number, inside], out_ref.at[place, part], keep_sem.at[0]
                ).start()

            @pl.when(turn_now > 0)
            def _():
                piece_copy(number, 0, (target, part), out_ref.at[place, part]).start()

        return carry

    lax.fori_loop(0, PLANES, one_tile, 0)
    for copy in grad_loads:
        copy.wait()

    at = 0
    for order, size in enumerate((qw, kw, kw)):
        grads[at : at + width, :] = acc_a[:, order * rank : (order + 1) * rank].astype(BF16)
        base = (0, qw, qw + kw)[order]
        grads[at + width : at + width + size, :] = (
            ADAPTER_SCALE * acc_b[base : base + size, :]
        ).astype(BF16)
        at += width + size
    pass_on(0, 0, lambda at, side: grads.at[plan.span(0, at, side), :])

    forwards = []

    def forward(which, back):
        target, recvs, keep = ((layer_out, lrecv, 1), (out_ref, drecv, 0))[which]
        source = layer(back)
        for step in range(plane):
            at = source * plane + step_at(step)
            if step > 0 or back > 0:
                pltpu.make_async_remote_copy(
                    src_ref=target.at[at, part],
                    dst_ref=target.at[at, part],
                    send_sem=hsem.at[0],
                    recv_sem=recvs.at[at],
                    device_id=over,
                    device_id_type=MESH,
                ).wait_recv()
            else:
                pltpu.make_async_copy(
                    target.at[place, part], target.at[place, part], keep_sem.at[keep]
                ).wait()
        copy = forward_copy(which, source, part, len(forwards))
        copy.start()
        forwards.append(copy)

    def forward_copy(which, source, side, number):
        target = (layer_out, out_ref)[which]
        span = pl.ds(source * plane, plane)
        return pltpu.make_async_remote_copy(
            src_ref=target.at[span, side],
            dst_ref=target.at[span, side],
            send_sem=fsend.at[number],
            recv_sem=frecv.at[which, source],
            device_id=over,
            device_id_type=MESH,
        )

    zsends = []

    def across_planes(zz):
        take(count, zz, inside, part)
        total = window_sum(count, zz, inside, part)
        slot = posted[0]
        posted[0] += 1
        number = len(sent) + len(zsends)
        copy = pltpu.make_async_remote_copy(
            src_ref=outbox.at[slot],
            dst_ref=last_in.at[depth],
            send_sem=rsend.at[number],
            recv_sem=zrecv.at[depth],
            device_id=(zz * plane + inside, part),
            device_id_type=MESH,
        )
        zsends.append((zz, copy))

        @pl.when(depth != zz)
        def _():
            outbox[slot] = total.astype(BF16)
            copy.start()

        @pl.when(depth == zz)
        def _():
            sum_ref[...] = total

    if direct:
        forward(0, 0)
        forward(0, 3)
        forward(0, 1)
    stage_sends(1, 0)
    for stage in range(3, count):
        for zz in (1, 2, 3):
            stage_sends(stage, zz)
    if direct:
        forward(0, 2)
        forward(1, 0)
    for stage in range(2, count):
        stage_sends(stage, 0)
    for zz in (1, 2, 3):
        across_planes(zz)
    if direct:
        forward(1, 3)
        forward(1, 1)
    across_planes(0)
    if direct:
        forward(1, 2)
    for hop in (1, 2, 3):
        source = layer(hop)
        pltpu.make_async_remote_copy(
            src_ref=last_in.at[source],
            dst_ref=last_in.at[source],
            send_sem=hsem.at[0],
            recv_sem=zrecv.at[source],
            device_id=over,
            device_id_type=MESH,
        ).wait_recv()
        sum_ref[...] += last_in[source].astype(F32)

    if direct:
        for which in range(2):
            for back in range(PLANES):
                forward_copy(which, layer(back), 1 - part, 0).wait_recv()
        for copy in forwards:
            copy.wait_send()
        for number in range(PLANES):
            for step in range(plane):
                if step == 0 and (number + 2) % PLANES == 0:
                    continue
                piece_copy(number, step, over, out_ref.at[place, part]).wait_send()
        for hop, step in layer_sends:
            layer_copy(hop, step).wait_send()
    else:
        layer_out[...] = jnp.zeros_like(layer_out)
    for copy in sent:
        copy.wait_send()
    for zz, copy in zsends:

        @pl.when(depth != zz)
        def _():
            copy.wait_send()

    for number in range(PLANES):
        key_copy(number).wait_send()


def tail(
    devices, own_rows, early, rows_in, other, layer_rows, w_cat, b_rows, gain, flat, grad_out, kept,
    gots, key_width, piece,
):
    gq, _, x = rows_in[:3]
    rows, width = x.shape
    plan = Windows(devices, own_rows)
    plane, count, window = plan.plane, len(plan.axes), plan.rows
    rank = flat.shape[1]
    tile = rows // PLANES
    direct = piece % 16 == 0
    anywhere = pl.BlockSpec(memory_space=pl.ANY)
    boxes = [plan.boxes(stage) * (1 if stage < 2 else PLANES) for stage in range(count)]
    sends = sum(boxes) + PLANES
    qw = gq.shape[1]
    first_plane = 16 * (((2 * plane - 1) * own_rows) // 16) + window
    dma = pltpu.SemaphoreType.DMA
    if direct:
        shape = (devices, 2, piece, width)
        outs = [jax.ShapeDtypeStruct(shape, BF16), jax.ShapeDtypeStruct(shape, BF16)]
        out_specs = [anywhere, anywhere]
        held = (plane, piece, width)
    else:
        outs = [jax.ShapeDtypeStruct((8, LANES), BF16), jax.ShapeDtypeStruct((rows, width), BF16)]
        out_specs = [whole(outs[0]), anywhere]
        held = (tile, width)
    outs.append(jax.ShapeDtypeStruct((window, rank), F32))
    scratch = [pltpu.VMEM((PLANES, tile, a.shape[1]), a.dtype) for a in rows_in]
    scratch += [
        pltpu.VMEM(w_cat.shape, BF16),
        pltpu.VMEM((first_plane, rank), BF16),
        pltpu.VMEM((PLANES,) + held, BF16),
        pltpu.VMEM((width, 3 * rank), F32),
        pltpu.VMEM((qw + 2 * key_width, rank), F32),
        pltpu.VMEM((sends, window, rank), BF16),
        pltpu.VMEM((PLANES, window, rank), BF16),
        pltpu.VMEM((PLANES, tile, other.shape[1]), BF16),
        pltpu.VMEM(kept.shape, F32),
        pltpu.VMEM(gots.shape, BF16),
    ]
    scratch += [pltpu.VMEM((size, window, rank), BF16) for size in boxes]
    scratch += [
        dma((PLANES, len(rows_in))),
        dma((5,)),
        dma((PLANES, plane)),
        dma((devices,)),
        dma((2 * PLANES,)),
        dma((2, PLANES)),
        dma((sends,)),
        dma((sum(boxes),)),
        dma((PLANES,)),
        dma((2,)),
        dma((PLANES,)),
        dma((PLANES,)),
        dma((PLANES, plane)),
        dma((devices,)),
        dma((1,)),
    ]
    layer_out, dx, total = pl.pallas_call(
        functools.partial(tail_kernel, plan, early, key_width, direct),
        grid=(1,),
        in_specs=[anywhere] * 12
        + [pl.BlockSpec((early, rank), lambda i: (0, 0)), whole(gain)]
        + [anywhere] * 4,
        out_specs=out_specs + [whole(outs[2])],
        out_shape=outs,
        scratch_shapes=scratch,
        compiler_params=params(collective_id=2, has_side_effects=True),
        cost_estimate=cost(2 * rows * width * 2900, 200e6),
        name="tail",
    )(
        *rows_in, other, layer_rows.reshape(devices, piece, width), w_cat, b_rows, gain, flat, grad_out,
        kept, gots,
    )
    return (layer_out if direct else layer_rows), dx, total


def row_tables(order_row, lengths_row, adapter_row, part, parts, each):
    total = order_row.shape[0]
    piece = each // parts
    local = total // parts
    places = jnp.arange(total, dtype=I32)
    own = (order_row % each) // piece == part
    slot = (order_row // each) * piece + order_row % piece
    column = jnp.where(own, slot, local + slot)
    upto = jnp.sum((own[None, :] & (places[None, :] <= places[:, None])).astype(I32), axis=1)
    rank = jnp.where(own, upto - 1, total)
    picks = rank[None, :] == jnp.arange(local, dtype=I32)[:, None]
    sorted_place = jnp.sum(jnp.where(picks, places[None, :], 0), axis=1)
    sorted_slot = jnp.sum(jnp.where(picks, slot[None, :], 0), axis=1)
    slot_place = jnp.sum(jnp.where(column[None, :] == places[:, None], places[None, :], 0), axis=1)
    ends = jnp.cumsum(lengths_row)
    starts = ends - lengths_row
    both = jnp.concatenate([slot_place, sorted_place])
    member = (both[:, None] >= starts[None, :]) & (both[:, None] < ends[None, :])
    first = jnp.sum(jnp.where(member, starts[None, :], 0), axis=1)
    chosen = jnp.sum(jnp.where(member, adapter_row[None, :], 0), axis=1)
    position = both - first
    sorted_first = first[total:]
    bounds = jnp.stack(
        [
            sorted_first[::QUERY_TILE] // KEY_TILE,
            sorted_place[QUERY_TILE - 1 :: QUERY_TILE] // KEY_TILE + 1,
        ]
    )
    blank = jnp.zeros_like(sorted_place)
    meta_sorted = jnp.stack([sorted_slot, sorted_first, sorted_place] + [blank] * 5, axis=1)
    meta_rows = jnp.stack([sorted_slot, sorted_first, sorted_place] + [blank] * 5, axis=0)
    meta_own = jnp.broadcast_to(chosen[:local, None], (local, 8))
    meta_other = jnp.broadcast_to(chosen[local:total, None], (local, 8))
    slot_position = position[:local]
    return (
        meta_own, meta_other, meta_sorted, meta_rows, slot_position, position[total:], column, bounds,
    )


def rope_tables(position):
    freq_index = jnp.arange(HEAD // 2, dtype=F32)
    inv_freq = jnp.power(jnp.float32(ROPE_BASE), -2.0 * freq_index / HEAD)
    angles = position.astype(F32)[:, None] * inv_freq[None, :]
    return (
        jnp.concatenate([jnp.cos(angles)] * 4, axis=1),
        jnp.concatenate([jnp.sin(angles)] * 4, axis=1),
    )


def per_device(
    tokens, cotangent, order, lengths, adapter_ids, norm_gains, w_query, w_key, w_value,
    b_query, b_key, b_value, w_out, w_gate, w_up, w_down, adapters, first_moment, second_moment,
):
    parts = lax.axis_size("tensor")
    part = lax.axis_index("tensor")
    devices = lax.axis_size("dp")
    place = lax.axis_index("dp")
    total, width = tokens.shape
    each = total // devices
    piece = each // parts
    local = total // parts
    rank = adapters.shape[1]
    own_rows = adapters.shape[0]
    swap = [(i, parts - 1 - i) for i in range(parts)]
    first_part = part == 0

    def across(values):
        return lax.ppermute(values, "tensor", swap)

    def pair(mine, theirs, axis):
        return jnp.concatenate(
            [jnp.where(first_part, mine, theirs), jnp.where(first_part, theirs, mine)], axis=axis
        )

    def give_back(values):
        got = lax.all_to_all(
            values.reshape(devices, piece, width), "dp", split_axis=0, concat_axis=0, tiled=True
        )
        theirs = across(got)
        return pair(got[:, None], theirs[:, None], 1).reshape(total, width)

    qh, kh, half = w_query.shape[1], w_key.shape[1], w_gate.shape[1]
    qw, kw, hidden = parts * qh, parts * kh, parts * half
    heads, kv_heads = qw // HEAD, kw // HEAD
    mine_qkv = jnp.concatenate(
        [
            jnp.concatenate([w_query, w_key, w_value], axis=1),
            jnp.broadcast_to(
                jnp.concatenate([b_query, b_key, b_value])[None], (32, qh + 2 * kh)
            ),
        ],
        axis=0,
    )
    lines = mine_qkv.shape[0]
    unit = 4 if own_rows % 4 == 0 else 1
    moved, copies, their_qkv, their_out = front(
        tokens.reshape(devices, parts, piece, width),
        adapters.astype(BF16).reshape(own_rows // unit, unit, rank),
        mine_qkv.reshape(2, lines // 2, -1),
        w_out.reshape(2, w_out.shape[0] // 2, width),
        devices,
    )
    cotangent, moved = lax.optimization_barrier((cotangent, moved))
    moved = moved.reshape(local, width)
    dy_all = lax.all_to_all(
        cotangent.reshape(devices, each, width), "dp", split_axis=0, concat_axis=0, tiled=True
    ).reshape(devices, parts, piece, width)

    def half_of(which):
        return lax.dynamic_index_in_dim(dy_all, which, 1, keepdims=False).reshape(local, width)

    dy = half_of(part)
    dy_theirs = half_of(parts - 1 - part)

    sizes = (width, qw, width, kw, width, kw, qw, width, width, hidden, width, hidden, hidden, width)
    early = 3 * width + qw + 2 * kw
    flat = copies.reshape(2 * devices * own_rows, rank)
    sections = []
    cursor = 0
    for size in sizes:
        sections.append(flat[cursor : cursor + size])
        cursor += size
    a_q, b_q, a_k, b_k, a_v, b_v, a_o, b_o, a_g, b_g, a_u, b_u, a_d, b_d = sections

    def near(rows):
        return lax.dynamic_slice_in_dim(rows, part * half, half, 0)

    meta_own, meta_other, meta_sorted, meta_rows, slot_position, sorted_position, column, bounds = (
        row_tables(order[0], lengths[0], adapter_ids[0], part, parts, each)
    )
    cos, sin = rope_tables(slot_position)
    cos_sorted, sin_sorted = rope_tables(sorted_position)
    gain_one = norm_gains[0:1].astype(F32)
    gain_two = norm_gains[1:2].astype(F32)
    side = jnp.reshape(part, (1,)).astype(I32)
    a_pair = jnp.concatenate([a_g, a_u], axis=1)

    n1, q, kv, z, w_cat = project(
        side, moved, meta_own, cos, sin, gain_one, mine_qkv, their_qkv.reshape(mine_qkv.shape),
        (a_q, a_k, a_v), (b_q, b_k, b_v),
    )
    other_kv = across(kv)
    q_sorted, o_sorted, logs, merged, o = attend(
        bounds, q, meta_sorted, meta_rows, kv, other_kv, column[:, None], heads, kv_heads
    )
    y1, n2, z_out, w_out_cat = middle(
        side, o, moved, meta_own, w_out, their_out.reshape(w_out.shape), a_o, b_o, gain_two
    )
    y_own, d_own, y_got, d_got, y_last, flat_grads = feed(
        2 * devices * own_rows, n2, dy, dy_theirs, meta_own, meta_other, a_pair, b_d,
        w_gate, w_up, w_down, near(b_g), near(b_u), near(a_d),
    )
    y_got = jnp.concatenate([y_got, across(y_last)[None]], axis=0).reshape(local, width)
    dy1, dar, grad_out, on_sums, kept_sums = middle_back(
        devices, own_rows, d_own, d_got.reshape(local, width), y1, dy, o, z_out, meta_own, b_o,
        w_out_cat, gain_two, flat_grads,
    )
    got_sums = lax.ppermute(on_sums, "dp", [(i, i ^ 2) for i in range(devices)])
    layer_rows = (y1 + (y_own + y_got.astype(F32))).astype(BF16)
    gq, dkv_own, dkv_other = attend_back(
        bounds, q_sorted, dar, o_sorted, logs, meta_sorted, meta_rows, cos_sorted, sin_sorted,
        merged, column[None, :], heads, kv_heads,
    )
    layer_out, dx, window = tail(
        devices, own_rows, early,
        (gq, dkv_own, moved, n1, z, dy1, meta_own, cos, sin),
        dkv_other, layer_rows, w_cat, flat[:early], gain_one, flat_grads, grad_out, kept_sums,
        got_sums, kw, piece,
    )
    if dx.ndim == 4:
        input_grad = dx.reshape(total, width)
        layer_out = layer_out.reshape(total, width)
    else:
        input_grad = give_back(dx)
        layer_out = give_back(layer_out)
    offset = lax.rem((2 * place + part) * own_rows, 16)
    reduced = lax.dynamic_slice_in_dim(window, offset, own_rows, 0)
    moment_one = BETA_ONE * first_moment + (1.0 - BETA_ONE) * reduced
    moment_two = BETA_TWO * second_moment + (1.0 - BETA_TWO) * reduced * reduced
    corrected_one = moment_one / (1.0 - BETA_ONE**STEP)
    corrected_two = moment_two / (1.0 - BETA_TWO**STEP)
    updated = adapters - LEARN_RATE * (
        corrected_one / (jnp.sqrt(corrected_two) + ADAM_EPS) + WEIGHT_DECAY * adapters
    )
    return (
        layer_out,
        input_grad,
        reduced,
        moment_one,
        moment_two,
        updated,
        updated.astype(BF16),
    )


def solution(mesh):
    both = P(("dp", "tensor"), None)
    rows = P("dp", None)
    return jax.shard_map(
        per_device,
        mesh=mesh,
        in_specs=(rows, rows, rows, rows, rows, P())
        + (P(None, "tensor"),) * 3
        + (P("tensor"),) * 3
        + (P("tensor", None), P(None, "tensor"), P(None, "tensor"), P("tensor", None))
        + (both,) * 3,
        out_specs=(rows, rows) + (both,) * 5,
        check_vma=False,
    )
```

```python
import functools

import jax
import jax.numpy as jnp
from jax import lax
from jax.experimental import pallas as pl
from jax.experimental.pallas import tpu as pltpu
from jax.sharding import PartitionSpec as P

HEAD = 64
RANK = 16
STEP = 3

ADAPTER_SCALE = 2.0
NORM_EPS = 1e-06
ROPE_BASE = 1000000.0
BETA_ONE = 0.5
BETA_TWO = 0.6
LEARN_RATE = 0.04
WEIGHT_DECAY = 0.01
ADAM_EPS = 1e-08
MASKED_SCORE = -1e30
PLANES = 4
FLAT_PAD = 64
MESH = pl.DeviceIdType.MESH

LANES = 128
ROW_TILE = 256
QUERY_TILE = 128
KEY_TILE = 256
HIDDEN_TILE = 512

F32 = jnp.float32
BF16 = jnp.bfloat16
I32 = jnp.int32


def nn(left, right):
    return lax.dot_general(left, right, (((1,), (0,)), ((), ())), preferred_element_type=F32)


def nt(left, right):
    return lax.dot_general(left, right, (((1,), (1,)), ((), ())), preferred_element_type=F32)


def tn(left, right):
    return lax.dot_general(left, right, (((0,), (0,)), ((), ())), preferred_element_type=F32)


def lane_iota(shape):
    return lax.broadcasted_iota(I32, shape, 1)


def row_iota(shape):
    return lax.broadcasted_iota(I32, shape, 0)


def whole(array):
    return pl.BlockSpec(array.shape, lambda *_: (0,) * array.ndim)


def row_blocks(array, tile):
    return pl.BlockSpec((tile, array.shape[1]), lambda i, *_: (i, 0))


def rows_from(array, start, count):
    return pl.BlockSpec(
        (pl.Element(count), pl.Element(array.shape[1])), lambda *_: (start, 0)
    )


def lane_table(table):
    return jnp.transpose(jnp.concatenate([table] * (LANES // table.shape[0]), axis=0))


def rank_mask(adapter_col, width):
    return jnp.where(lane_iota((adapter_col.shape[0], width)) // RANK == adapter_col, 1.0, 0.0)


def turn(values):
    lanes = lane_iota(values.shape) % HEAD
    return jnp.where(
        lanes < HEAD // 2,
        -pltpu.roll(values, LANES - HEAD // 2, 1),
        pltpu.roll(values, HEAD // 2, 1),
    )


def rms(values):
    return lax.rsqrt(jnp.mean(values * values, axis=-1, keepdims=True) + NORM_EPS)


def norm_back(values, gain, grad):
    inverse = rms(values)
    weighted = grad * gain
    return inverse * weighted - values * inverse * inverse * inverse * jnp.mean(
        weighted * values, axis=-1, keepdims=True
    )


def pick_rows(place_col, slots):
    hit = place_col == lane_iota((place_col.shape[0], slots))
    return jnp.where(hit, 1.0, 0.0).astype(BF16)


def place_rows(place_row, slots):
    hit = row_iota((slots, place_row.shape[1])) == place_row
    return jnp.where(hit, 1.0, 0.0).astype(BF16)


def params(**more):
    return pltpu.CompilerParams(vmem_limit_bytes=60 * 1024 * 1024, **more)


def cost(flops, moved):
    return pl.CostEstimate(flops=int(flops), bytes_accessed=int(moved), transcendentals=0)


def xor_bit(value, bit):
    size = 2**bit
    return value + size * (1 - 2 * lax.rem(value // size, 2))


def subsets(axes):
    out = [()]
    for axis in axes:
        out += [chosen + (axis,) for chosen in out]
    return out


def flip(place, part, axes):
    for axis in axes:
        if axis == "tensor":
            part = 1 - part
        else:
            place = xor_bit(place, axis)
    return place, part


def front_kernel(
    devices, rows_ref, chunk_ref, wq_ref, wo_ref, got_ref, copies_ref, wq_out, wo_out,
    local_sem, tsend, trecv, csend, crecv, wsend, wrecv,
):
    place, part = lax.axis_index("dp"), lax.axis_index("tensor")
    plane = devices // PLANES
    depth, inside = place // plane, lax.rem(place, plane)
    core = lax.rem(place, 2)
    own = 2 * place + part
    units = chunk_ref.shape[0]

    def rows_of(index):
        return copies_ref.at[pl.ds(index * units, units)]

    barrier = pltpu.get_barrier_semaphore()
    for k in range(1, devices):
        pl.semaphore_signal(
            barrier, inc=1, device_id=(lax.rem(place + k, devices), part), device_id_type=MESH
        )
    pl.semaphore_signal(barrier, inc=1, device_id=(place, 1 - part), device_id_type=MESH)
    pl.semaphore_wait(barrier, devices)

    keep = [
        pltpu.make_async_copy(chunk_ref, rows_of(own), local_sem.at[0]),
        pltpu.make_async_copy(rows_ref.at[place, part], got_ref.at[place], local_sem.at[1]),
    ]
    for copy in keep:
        copy.start()
    sent = []

    def chunk_copy(source, index, number, where):
        return pltpu.make_async_remote_copy(
            src_ref=source,
            dst_ref=rows_of(index),
            send_sem=csend.at[number],
            recv_sem=crecv.at[index],
            device_id=where,
            device_id_type=MESH,
        )

    def send_chunk(source, index, where):
        copy = chunk_copy(source, index, len(sent), where)
        copy.start()
        sent.append(copy)

    def take_chunk(index):
        chunk_copy(chunk_ref, index, 0, (place, 1 - part)).wait_recv()

    def layer(turn):
        return lax.rem(depth + turn, PLANES)

    for turn in (2, 3, 1):
        send_chunk(chunk_ref, own, (layer(turn) * plane + inside, part))

    def weight_copy(ref, out, number, slot, where):
        return pltpu.make_async_remote_copy(
            src_ref=ref.at[slot],
            dst_ref=out.at[slot],
            send_sem=wsend.at[number],
            recv_sem=wrecv.at[number],
            device_id=where,
            device_id_type=MESH,
        )

    direct = [
        weight_copy(wq_ref, wq_out, 0, core, (place, 1 - part)),
        weight_copy(wo_ref, wo_out, 1, core, (place, 1 - part)),
    ]
    for copy in direct:
        copy.start()

    rows_sent = []
    for turn in (2, 3, 1, 0):
        for step in range(plane):
            if turn == 0 and step == 0:
                continue
            target = layer(turn) * plane + lax.rem(inside + step, plane)
            copy = pltpu.make_async_remote_copy(
                src_ref=rows_ref.at[target, part],
                dst_ref=got_ref.at[place],
                send_sem=tsend.at[len(rows_sent)],
                recv_sem=trecv.at[place],
                device_id=(target, part),
                device_id_type=MESH,
            )
            copy.start()
            rows_sent.append((copy, target))

    bits = [2**b for b in range(plane.bit_length() - 1)]
    bits = list(range(len(bits)))[::-1]
    orders = [["tensor"] + bits, bits[:-1] + ["tensor"] + bits[-1:]]
    relayed = []
    for stage in range(len(bits) + 1):
        for turn in (0, 1, 2, 3):
            order = orders[turn % 2]
            origin = layer(turn) * plane + inside
            where = flip(place, part, [order[stage]])
            for chosen in subsets(order[:stage]):
                at, side = flip(origin, part, chosen)
                index = 2 * at + side
                if turn == 0 and not chosen:
                    send_chunk(chunk_ref, index, where)
                    continue
                if stage == 0 or order[stage - 1] in chosen:
                    take_chunk(index)
                send_chunk(rows_of(index), index, where)
        if stage == 0:
            partner = (xor_bit(place, 0), part)
            for number, (ref, out) in enumerate(((wq_ref, wq_out), (wo_ref, wo_out))):
                direct[number].wait_recv()
                copy = weight_copy(out, out, 2 + number, core, partner)
                copy.start()
                relayed.append(copy)
    for turn in (0, 1, 2, 3):
        order = orders[turn % 2]
        origin = layer(turn) * plane + inside
        for chosen in subsets(order):
            if order[-1] in chosen:
                at, side = flip(origin, part, chosen)
                take_chunk(2 * at + side)
    for number, (ref, out) in enumerate(((wq_ref, wq_out), (wo_ref, wo_out))):
        weight_copy(out, out, 2 + number, 1 - core, (place, 1 - part)).wait_recv()
    for copy, source in rows_sent:
        pltpu.make_async_remote_copy(
            src_ref=rows_ref.at[source, part],
            dst_ref=got_ref.at[source],
            send_sem=tsend.at[0],
            recv_sem=trecv.at[source],
            device_id=(source, part),
            device_id_type=MESH,
        ).wait_recv()
    for copy, _ in rows_sent:
        copy.wait_send()
    for copy in sent + direct + relayed:
        copy.wait_send()
    for copy in keep:
        copy.wait()


def front(rows, chunk, wq, wo, devices):
    _, _, piece, width = rows.shape
    anywhere = pl.BlockSpec(memory_space=pl.ANY)
    outs = [
        jax.ShapeDtypeStruct((devices, piece, width), BF16),
        jax.ShapeDtypeStruct((2 * devices * chunk.shape[0],) + chunk.shape[1:], BF16),
        jax.ShapeDtypeStruct(wq.shape, BF16),
        jax.ShapeDtypeStruct(wo.shape, BF16),
    ]
    return pl.pallas_call(
        functools.partial(front_kernel, devices),
        in_specs=[anywhere] * 4,
        out_specs=[anywhere] * 4,
        out_shape=outs,
        scratch_shapes=[
            pltpu.SemaphoreType.DMA((2,)),
            pltpu.SemaphoreType.DMA((devices,)),
            pltpu.SemaphoreType.DMA((devices,)),
            pltpu.SemaphoreType.DMA((2 * devices,)),
            pltpu.SemaphoreType.DMA((2 * devices,)),
            pltpu.SemaphoreType.DMA((4,)),
            pltpu.SemaphoreType.DMA((4,)),
        ],
        compiler_params=pltpu.CompilerParams(collective_id=0, has_side_effects=True),
        cost_estimate=cost(0, 100e6),
        name="front",
    )(rows, chunk, wq, wo)


def in_order(part, mine, theirs, place):
    @pl.when(part == 0)
    def _():
        place(mine, theirs)

    @pl.when(part == 1)
    def _():
        place(theirs, mine)


def project_kernel(
    part_ref, x_ref, meta_ref, turns_ref, sines_ref, gain_ref, mine_ref, theirs_ref, flat_ref,
    n_ref, q_ref, kv_ref, z_ref, cos_ref, sin_ref, w_ref, bias,
):
    width = x_ref.shape[1]
    qw, kw = q_ref.shape[1], kv_ref.shape[1] // 2
    rank = flat_ref.shape[1]
    low = qw + 2 * kw
    a_rows, b_rows = [], []
    cursor = 0
    for size in (qw, kw, kw):
        a_rows.append(slice(cursor, cursor + width))
        b_rows.append(slice(cursor + width, cursor + width + size))
        cursor += width + size

    @pl.when(pl.program_id(0) == 0)
    def _():
        def fill(first, second):
            at, to = 0, 0
            for size in (qw // 2, kw // 2, kw // 2):
                cut = slice(at, at + size)
                both = jnp.concatenate(
                    [first[:width, cut].astype(F32), second[:width, cut].astype(F32)], axis=1
                )
                w_ref[:, to : to + 2 * size] = both.astype(BF16)
                extra = jnp.concatenate(
                    [first[width : width + 8, cut].astype(F32), second[width : width + 8, cut].astype(F32)],
                    axis=1,
                )
                bias[:, to : to + 2 * size] = extra
                at += size
                to += 2 * size

        in_order(part_ref[0], mine_ref, theirs_ref, fill)
        for i, rows in enumerate(a_rows):
            w_ref[:, low + i * rank : low + (i + 1) * rank] = flat_ref[rows, :]

    values = x_ref[...].astype(F32)
    normed = (values * rms(values) * gain_ref[...]).astype(BF16)
    n_ref[...] = normed
    base = nn(normed, w_ref[...])
    mask = rank_mask(meta_ref[:, 0:1], rank)
    lows = [(base[:, low + i * rank : low + (i + 1) * rank] * mask).astype(BF16) for i in range(3)]
    for i in range(3):
        z_ref[:, i * rank : (i + 1) * rank] = lows[i]
    cos, sin = lane_table(turns_ref[...]), lane_table(sines_ref[...])
    cos_ref[...] = cos
    sin_ref[...] = sin
    queries = base[:, :qw] + bias[0:1, :qw] + ADAPTER_SCALE * nt(lows[0], flat_ref[b_rows[0], :])
    for pair in range(qw // LANES):
        part = queries[:, pair * LANES : (pair + 1) * LANES]
        turned = (part * cos + turn(part) * sin) * HEAD**-0.5
        q_ref[:, pair * LANES : (pair + 1) * LANES] = turned.astype(BF16)
    keys = base[:, qw : qw + kw] + bias[0:1, qw : qw + kw] + ADAPTER_SCALE * nt(lows[1], flat_ref[b_rows[1], :])
    kv_ref[:, :kw] = (keys * cos + turn(keys) * sin).astype(BF16)
    vals = base[:, qw + kw : low] + bias[0:1, qw + kw : low] + ADAPTER_SCALE * nt(lows[2], flat_ref[b_rows[2], :])
    kv_ref[:, kw:] = vals.astype(BF16)


def project(part, x, meta, turns, sines, gain, mine, theirs, flat, qw, kw):
    rows, width = x.shape
    rank = flat.shape[1]
    tile = ROW_TILE
    early = 3 * width + qw + 2 * kw
    columns = pl.BlockSpec((turns.shape[0], tile), lambda i, *_: (0, i))
    outs = [
        jax.ShapeDtypeStruct((rows, width), BF16),
        jax.ShapeDtypeStruct((rows, qw), BF16),
        jax.ShapeDtypeStruct((rows, 2 * kw), BF16),
        jax.ShapeDtypeStruct((rows, 3 * rank), BF16),
        jax.ShapeDtypeStruct((rows, LANES), F32),
        jax.ShapeDtypeStruct((rows, LANES), F32),
        jax.ShapeDtypeStruct((width, qw + 2 * kw + 3 * rank), BF16),
    ]
    return pl.pallas_call(
        project_kernel,
        grid_spec=pltpu.PrefetchScalarGridSpec(
            num_scalar_prefetch=1,
            grid=(rows // tile,),
            in_specs=[row_blocks(a, tile) for a in (x, meta)]
            + [columns, columns]
            + [whole(a) for a in (gain, mine, theirs)]
            + [rows_from(flat, 0, early)],
            out_specs=[row_blocks(o, tile) for o in outs[:6]] + [whole(outs[6])],
            scratch_shapes=[pltpu.VMEM((8, qw + 2 * kw), F32)],
        ),
        out_shape=outs,
        compiler_params=params(),
        cost_estimate=cost(2 * rows * width * 1600, 9e6),
        name="project",
    )(part, x, meta, turns, sines, gain, mine, theirs, flat)


def head_groups(heads, kv_heads):
    width = heads // kv_heads
    groups = {}
    for head in range(heads):
        groups.setdefault((head // width, head % 2), []).append(head)
    return [(kv, half, members) for (kv, half), members in sorted(groups.items())]


def spread_heads(tile_f32, kv, half, ones=False):
    lanes = lane_iota(tile_f32.shape)
    moved = tile_f32 if kv % 2 == half else pltpu.roll(tile_f32, HEAD, 1)
    keep = (lanes >= HEAD) if half else (lanes < HEAD)
    rest = jnp.where(lanes == (0 if half else HEAD), 1.0, 0.0) if ones else 0.0
    return jnp.where(keep, moved, rest)


def stack_heads(groups, source, target):
    rows = source.shape[0]
    at = 0
    for _, _, members in groups:
        for head in members:
            pair = slice((head // 2) * LANES, (head // 2 + 1) * LANES)
            target[at : at + rows, :] = source[:, pair]
            at += rows


def attend_kernel(
    heads, kv_heads, bounds_ref, all_ref, meta_ref, metar_ref, place_ref, own_ref, other_ref,
    column_ref,
    q_ref, o_ref, log_ref, merged_ref, slot_ref, keys, values, acc, top, held, stack, scores,
):
    step = pl.program_id(0)
    groups = head_groups(heads, kv_heads)
    rows = q_ref.shape[0]
    q_ref[...] = nn(pick_rows(meta_ref[:, 0:1], all_ref.shape[0]), all_ref[...]).astype(BF16)
    stack_heads(groups, q_ref, stack)

    @pl.when(step == 0)
    def _():
        both = jnp.concatenate([own_ref[...], other_ref[...]], axis=0)
        for start in range(0, keys.shape[1], KEY_TILE):
            span = slice(start, start + KEY_TILE)
            part = nn(pick_rows(column_ref[span, :], both.shape[0]), both)
            merged_ref[span, :] = part.astype(BF16)
            for number, (kv, half, _) in enumerate(groups):
                keys[number, span, :] = spread_heads(part[:, :LANES], kv, half).astype(BF16)
                turned = jnp.transpose(spread_heads(part[:, LANES:], kv, half, True))
                values[number, :, span] = turned.astype(BF16)

    acc[...] = jnp.zeros_like(acc)
    top[...] = jnp.full_like(top, MASKED_SCORE)
    first, last = metar_ref[1:2, :], metar_ref[2:3, :]
    cuts = []
    at = 0
    for _, _, members in groups:
        cuts.append(slice(at * rows, (at + len(members)) * rows))
        at += len(members)

    def find_top(number, carry):
        start = pl.multiple_of(number * KEY_TILE, KEY_TILE)
        span = pl.ds(start, KEY_TILE)
        index = start + row_iota((KEY_TILE, rows))
        bias = jnp.where((index >= first) & (index <= last), 0.0, MASKED_SCORE)
        for group, cut in enumerate(cuts):
            count = (cut.stop - cut.start) // rows
            part = nt(keys[group, span, :], stack[cut, :])
            part = part + jnp.concatenate([bias] * count, axis=1)
            scores[span, cut] = part
            most = jnp.max(part.reshape(KEY_TILE // 8, 8, -1), axis=0)
            top[:, cut] = jnp.maximum(top[:, cut], most)
        return carry

    def weigh(number, carry):
        start = pl.multiple_of(number * KEY_TILE, KEY_TILE)
        span = pl.ds(start, KEY_TILE)
        for group, cut in enumerate(cuts):
            weights = jnp.exp(scores[span, cut] - top[0:1, cut]).astype(BF16)
            acc[:, cut] += nn(values[group, :, span], weights)
        return carry

    lax.fori_loop(bounds_ref[0, step], bounds_ref[1, step], find_top, 0)
    top[0:1, :] = jnp.max(top[...], axis=0, keepdims=True)
    lax.fori_loop(bounds_ref[0, step], bounds_ref[1, step], weigh, 0)
    parts = {}
    at = 0
    for _, half, members in groups:
        for head in members:
            cut = slice(at * rows, (at + 1) * rows)
            at += 1
            block = acc[:, cut]
            sums = block[0:1, :] if half else block[HEAD : HEAD + 1, :]
            log_ref[head : head + 1, :] = top[0:1, cut] + jnp.log(sums)
            parts[head] = block / sums
    low = row_iota((LANES, rows)) < HEAD
    for pair in range(heads // 2):
        both = jnp.where(low, parts[2 * pair], parts[2 * pair + 1])
        o_ref[:, pair * LANES : (pair + 1) * LANES] = jnp.transpose(both).astype(BF16)
    for head in range(heads, log_ref.shape[0]):
        log_ref[head : head + 1, :] = jnp.zeros((1, rows), F32)
    held[pl.ds(pl.multiple_of(step * rows, rows), rows), :] = o_ref[...]

    @pl.when(step == pl.num_programs(0) - 1)
    def _():
        slot_ref[...] = nn(place_rows(place_ref[0:1, :], held.shape[0]), held[...]).astype(BF16)


def attend(bounds, q, meta, meta_rows, own_kv, other_kv, column, heads, kv_heads):
    rows, qw = q.shape
    tile = QUERY_TILE
    keys = 2 * rows
    groups = len(head_groups(heads, kv_heads))
    outs = [
        jax.ShapeDtypeStruct((rows, qw), BF16),
        jax.ShapeDtypeStruct((rows, qw), BF16),
        jax.ShapeDtypeStruct((16, rows), F32),
        jax.ShapeDtypeStruct((keys, own_kv.shape[1]), BF16),
        jax.ShapeDtypeStruct((rows, qw), BF16),
    ]
    return pl.pallas_call(
        functools.partial(attend_kernel, heads, kv_heads),
        grid_spec=pltpu.PrefetchScalarGridSpec(
            num_scalar_prefetch=1,
            grid=(rows // tile,),
            in_specs=[
                whole(q),
                row_blocks(meta, tile),
                pl.BlockSpec((8, tile), lambda i, *_: (0, i)),
                whole(meta_rows),
                whole(own_kv),
                whole(other_kv),
                whole(column),
            ],
            out_specs=[
                row_blocks(outs[0], tile),
                row_blocks(outs[1], tile),
                pl.BlockSpec((16, tile), lambda i, *_: (0, i)),
                whole(outs[3]),
                whole(outs[4]),
            ],
            scratch_shapes=[
                pltpu.VMEM((groups, keys, LANES), BF16),
                pltpu.VMEM((groups, LANES, keys), BF16),
                pltpu.VMEM((LANES, heads * tile), F32),
                pltpu.VMEM((8, heads * tile), F32),
                pltpu.VMEM((rows, qw), BF16),
                pltpu.VMEM((heads * tile, LANES), BF16),
                pltpu.VMEM((keys, heads * tile), F32),
            ],
        ),
        out_shape=outs,
        compiler_params=params(),
        cost_estimate=cost(heads * rows * keys * 2000, 6e6),
        name="attend",
    )(bounds, q, meta, meta_rows, meta_rows, own_kv, other_kv, column)


def attend_back_kernel(
    heads, kv_heads, bounds_ref, q_ref, all_ref, o_ref, log_ref, meta_ref, metar_ref, cos_ref,
    sin_ref, merged_ref, column_ref, place_ref,
    gq_ref, own_ref, other_ref, keys, values, dkeys, dvalues, dq, dots, g_ref, held, stack, grads,
):
    step = pl.program_id(0)
    groups = head_groups(heads, kv_heads)
    rows = q_ref.shape[0]
    g_ref[...] = nn(pick_rows(meta_ref[:, 0:1], all_ref.shape[0]), all_ref[...]).astype(BF16)

    @pl.when(step == 0)
    def _():
        for start in range(0, keys.shape[1], KEY_TILE):
            span = slice(start, start + KEY_TILE)
            part = merged_ref[span, :].astype(F32)
            for number, (kv, half, _) in enumerate(groups):
                keys[number, span, :] = spread_heads(part[:, :LANES], kv, half).astype(BF16)
                values[number, span, :] = spread_heads(part[:, LANES:], kv, half).astype(BF16)
        dkeys[...] = jnp.zeros_like(dkeys)
        dvalues[...] = jnp.zeros_like(dvalues)

    stack_heads(groups, q_ref, stack)
    stack_heads(groups, g_ref, grads)
    dq[...] = jnp.zeros_like(dq)
    for pair in range(heads // 2):
        lanes = slice(pair * LANES, (pair + 1) * LANES)
        product = jnp.transpose(g_ref[:, lanes].astype(F32) * o_ref[:, lanes].astype(F32))
        dots[2 * pair : 2 * pair + 1, :] = jnp.sum(product[:HEAD], axis=0, keepdims=True)
        dots[2 * pair + 1 : 2 * pair + 2, :] = jnp.sum(product[HEAD:], axis=0, keepdims=True)
    first, last = metar_ref[1:2, :], metar_ref[2:3, :]

    def one_tile(number, carry):
        start = pl.multiple_of(number * KEY_TILE, KEY_TILE)
        index = start + row_iota((KEY_TILE, rows))
        bias = jnp.where((index >= first) & (index <= last), 0.0, MASKED_SCORE)
        span = pl.ds(start, KEY_TILE)
        begin = 0
        for group, (_, half, members) in enumerate(groups):
            count = len(members)
            cut = slice(begin * rows, (begin + count) * rows)
            begin += count
            logs = jnp.concatenate([log_ref[h : h + 1, :] for h in members], axis=1)
            drop = jnp.concatenate([dots[h : h + 1, :] for h in members], axis=1)
            key_part = keys[group, span, :]
            scores = nt(key_part, stack[cut, :]) + jnp.concatenate([bias] * count, axis=1)
            weights = jnp.exp(scores - logs)
            change = nt(values[group, span, :], grads[cut, :])
            dscores = (weights * (change - drop)).astype(BF16)
            dvalues[group, span, :] += nn(weights.astype(BF16), grads[cut, :])
            dkeys[group, span, :] += nn(dscores, stack[cut, :])
            back = tn(dscores, key_part)
            for at, head in enumerate(members):
                dq[head // 2, :, :] += back[at * rows : (at + 1) * rows, :]
        return carry

    lax.fori_loop(bounds_ref[0, step], bounds_ref[1, step], one_tile, 0)
    cos, sin = lane_table(cos_ref[...]), lane_table(sin_ref[...])
    for pair in range(heads // 2):
        grad = dq[pair, :, :] * HEAD**-0.5
        grad = grad * cos - turn(grad) * sin
        held[
            pl.ds(pl.multiple_of(step * rows, rows), rows), pair * LANES : (pair + 1) * LANES
        ] = grad.astype(BF16)

    @pl.when(step == pl.num_programs(0) - 1)
    def _():
        gq_ref[...] = nn(place_rows(place_ref[0:1, :], held.shape[0]), held[...]).astype(BF16)
        total = dkeys.shape[1]

        def join(ref):
            out = None
            for group, (kv, half, _) in enumerate(groups):
                part = ref[group, :, :]
                lanes = lane_iota(part.shape)
                part = jnp.where((lanes >= HEAD) if half else (lanes < HEAD), part, 0.0)
                if kv % 2 != half:
                    part = pltpu.roll(part, HEAD, 1)
                out = part if out is None else out + part
            return out.astype(BF16)

        both = jnp.concatenate([join(dkeys), join(dvalues)], axis=1)
        half_rows = own_ref.shape[0]
        for at in range(0, total, KEY_TILE):
            hit = (at + row_iota((KEY_TILE, total))) == column_ref[...]
            part = nn(jnp.where(hit, 1.0, 0.0).astype(BF16), both).astype(BF16)
            if at < half_rows:
                own_ref[at : at + KEY_TILE, :] = part
            else:
                other_ref[at - half_rows : at - half_rows + KEY_TILE, :] = part


def attend_back(
    bounds, q, grad, o, logs, meta, meta_rows, cos, sin, merged, column_row, heads, kv_heads
):
    rows, qw = q.shape
    tile = QUERY_TILE
    keys, kvw = merged.shape
    groups = len(head_groups(heads, kv_heads))
    outs = [
        jax.ShapeDtypeStruct((rows, qw), BF16),
        jax.ShapeDtypeStruct((rows, kvw), BF16),
        jax.ShapeDtypeStruct((rows, kvw), BF16),
    ]
    return pl.pallas_call(
        functools.partial(attend_back_kernel, heads, kv_heads),
        grid_spec=pltpu.PrefetchScalarGridSpec(
            num_scalar_prefetch=1,
            grid=(rows // tile,),
            in_specs=[
                row_blocks(q, tile),
                whole(grad),
                row_blocks(o, tile),
                pl.BlockSpec((16, tile), lambda i, *_: (0, i)),
                row_blocks(meta, tile),
                pl.BlockSpec((8, tile), lambda i, *_: (0, i)),
                pl.BlockSpec((cos.shape[0], tile), lambda i, *_: (0, rows // tile + i)),
                pl.BlockSpec((cos.shape[0], tile), lambda i, *_: (0, rows // tile + i)),
                whole(merged),
                whole(column_row),
                whole(meta_rows),
            ],
            out_specs=[whole(o) for o in outs],
            scratch_shapes=[
                pltpu.VMEM((groups, keys, LANES), BF16),
                pltpu.VMEM((groups, keys, LANES), BF16),
                pltpu.VMEM((groups, keys, LANES), F32),
                pltpu.VMEM((groups, keys, LANES), F32),
                pltpu.VMEM((heads // 2, tile, LANES), F32),
                pltpu.VMEM((16, tile), F32),
                pltpu.VMEM((tile, qw), BF16),
                pltpu.VMEM((rows, qw), BF16),
                pltpu.VMEM((heads * tile, LANES), BF16),
                pltpu.VMEM((heads * tile, LANES), BF16),
            ],
        ),
        out_shape=outs,
        compiler_params=params(),
        cost_estimate=cost(heads * rows * keys * 3000, 9e6),
        name="attend_back",
    )(bounds, q, grad, o, logs, meta, meta_rows, cos, sin, merged, column_row, meta_rows)


def middle_kernel(
    part_ref, o_ref, x_ref, meta_ref, mine_ref, theirs_ref, gain_ref, flat_ref,
    y_ref, n_ref, z_ref, w_ref,
):
    width = x_ref.shape[1]
    rank = flat_ref.shape[1]
    half = mine_ref.shape[0]

    @pl.when(pl.program_id(0) == 0)
    def _():
        def fill(first, second):
            w_ref[:half, :width] = first[...]
            w_ref[half:, :width] = second[...]

        in_order(part_ref[0], mine_ref, theirs_ref, fill)
        w_ref[:, width:] = flat_ref[: 2 * half, :]

    mask = rank_mask(meta_ref[:, 0:1], rank)
    base = nn(o_ref[...], w_ref[...])
    low = (base[:, width:] * mask).astype(BF16)
    z_ref[...] = low
    values = x_ref[...].astype(F32) + (base[:, :width] + ADAPTER_SCALE * nt(low, flat_ref[2 * half :, :]))
    y_ref[...] = values
    n_ref[...] = (values * rms(values) * gain_ref[...]).astype(BF16)


def middle(part, o, x, meta, mine, theirs, gain, flat, start):
    rows, width = x.shape
    rank = flat.shape[1]
    tile = ROW_TILE
    rest = (mine, theirs, gain)
    outs = [
        jax.ShapeDtypeStruct((rows, width), F32),
        jax.ShapeDtypeStruct((rows, width), BF16),
        jax.ShapeDtypeStruct((rows, rank), BF16),
        jax.ShapeDtypeStruct((o.shape[1], width + rank), BF16),
    ]
    return pl.pallas_call(
        middle_kernel,
        grid_spec=pltpu.PrefetchScalarGridSpec(
            num_scalar_prefetch=1,
            grid=(rows // tile,),
            in_specs=[row_blocks(a, tile) for a in (o, x, meta)]
            + [whole(a) for a in rest]
            + [rows_from(flat, start, o.shape[1] + width)],
            out_specs=[row_blocks(a, tile) for a in outs[:3]] + [whole(outs[3])],
        ),
        out_shape=outs,
        compiler_params=params(),
        cost_estimate=cost(2 * rows * width * 1100, 12e6),
        name="middle",
    )(part, o, x, meta, *rest, flat)


class Windows:
    def __init__(self, devices, own_rows):
        self.devices = devices
        self.own_rows = own_rows
        self.plane = devices // PLANES
        self.axes = list(range(self.plane.bit_length() - 1)) + ["tensor"]
        self.rows = 16 * ((own_rows + 30) // 16)
        self.last = 16 * (((2 * devices - 1) * own_rows) // 16) + self.rows

    def start(self, zz, at, side):
        row = (2 * (zz * self.plane + at) + side) * self.own_rows
        return pl.multiple_of((row // 16) * 16, 16)

    def span(self, zz, at, side):
        return pl.ds(self.start(zz, at, side), self.rows)

    def boxes(self, stage):
        return 2 ** (len(self.axes) - 1 - stage)

    def box(self, stage, at, side):
        index = 0
        for order, axis in enumerate(self.axes[stage + 1 :]):
            bit = side if axis == "tensor" else lax.rem(at // 2**axis, 2)
            index = index + bit * 2**order
        return index

    def leaving(self, stage, inside, part):
        for chosen in subsets(self.axes[stage + 1 :]):
            yield flip(inside, part, [self.axes[stage]] + list(chosen))

    def staying(self, stage, inside, part):
        for chosen in subsets(self.axes[stage + 1 :]):
            yield flip(inside, part, list(chosen))


def middle_back_kernel(
    plan, first_b, da_ref, db_ref, y1_ref, dy_ref, o_ref, z_ref, meta_ref, copies_ref, w_ref,
    gain_ref, flat_ref,
    dy1_ref, dar_ref, grad_ref, on_ref, kept_ref, acc_bo, acc_ao, mine, inbox, b_ref, msem, ssem,
    rsem, bsem,
):
    step = pl.program_id(0)
    b_load = pltpu.make_async_copy(
        copies_ref.at[pl.ds(first_b, b_ref.shape[0]), :], b_ref, bsem.at[0]
    )
    rank = b_ref.shape[1]
    qw = o_ref.shape[1]
    place, part = lax.axis_index("dp"), lax.axis_index("tensor")
    inside = lax.rem(place, plan.plane)
    partner = flip(place, part, [plan.axes[0]])
    boxes = plan.boxes(0)

    def moves():
        local, remote = [], []
        for zz in range(1, PLANES):
            for at, side in plan.leaving(0, inside, part):
                index = (zz - 1) * boxes + plan.box(0, at, side)
                remote.append(
                    pltpu.make_async_remote_copy(
                        src_ref=flat_ref.at[plan.span(zz, at, side), :],
                        dst_ref=inbox.at[index],
                        send_sem=ssem.at[len(remote)],
                        recv_sem=rsem.at[index],
                        device_id=partner,
                        device_id_type=MESH,
                    )
                )
            for at, side in plan.staying(0, inside, part):
                index = (zz - 1) * boxes + plan.box(0, at, side)
                local.append(
                    pltpu.make_async_copy(
                        flat_ref.at[plan.span(zz, at, side), :], mine.at[index], msem.at[len(local)]
                    )
                )
        return local, remote

    @pl.when(step == 0)
    def _():
        acc_bo[...] = jnp.zeros_like(acc_bo)
        acc_ao[...] = jnp.zeros_like(acc_ao)
        b_load.start()
        barrier = pltpu.get_barrier_semaphore()
        pl.semaphore_signal(barrier, inc=1, device_id=partner, device_id_type=MESH)
        pl.semaphore_wait(barrier, 1)
        local, remote = moves()
        for copy in remote + local:
            copy.start()
        b_load.wait()

    mask = rank_mask(meta_ref[:, 0:1], rank)
    grad = da_ref[...] + db_ref[...].astype(F32)
    dy1 = dy_ref[...].astype(F32) + norm_back(y1_ref[...], gain_ref[...], grad)
    dy1_ref[...] = dy1
    low_grad = dy1.astype(BF16)
    back_out = (ADAPTER_SCALE * nn(low_grad, b_ref[...]) * mask).astype(BF16)
    both = jnp.concatenate([low_grad, back_out], axis=1)
    dar_ref[...] = nt(both, w_ref[...]).astype(BF16)
    acc_bo[...] += ADAPTER_SCALE * tn(low_grad, z_ref[...])
    acc_ao[...] += tn(o_ref[...], back_out)

    @pl.when(step == pl.num_programs(0) - 1)
    def _():
        grad_ref[:qw, :] = acc_ao[...].astype(BF16)
        grad_ref[qw:, :] = acc_bo[...].astype(BF16)
        local, remote = moves()
        for copy in local:
            copy.wait()
        for copy in remote:
            copy.wait_recv()
        later = plan.boxes(1)

        def total(zz, at, side):
            index = (zz - 1) * boxes + plan.box(0, at, side)
            return mine[index].astype(F32) + inbox[index].astype(F32)

        for zz in range(1, PLANES):
            for at, side in plan.leaving(1, inside, part):
                on_ref[(zz - 1) * later + plan.box(1, at, side)] = total(zz, at, side).astype(BF16)
            for at, side in plan.staying(1, inside, part):
                kept_ref[(zz - 1) * later + plan.box(1, at, side)] = total(zz, at, side)
        for copy in remote:
            copy.wait_send()


def middle_back(
    devices, own_rows, d_first, d_second, y1, dy, o, z, meta, copies, start, w_out, gain, flat
):
    rows, width = y1.shape
    rank = copies.shape[1]
    qw = o.shape[1]
    tile = ROW_TILE
    plan = Windows(devices, own_rows)
    first, second = (PLANES - 1) * plan.boxes(0), (PLANES - 1) * plan.boxes(1)
    outs = [
        jax.ShapeDtypeStruct((rows, width), F32),
        jax.ShapeDtypeStruct((rows, qw), BF16),
        jax.ShapeDtypeStruct((qw + width, rank), BF16),
        jax.ShapeDtypeStruct((second, plan.rows, rank), BF16),
        jax.ShapeDtypeStruct((second, plan.rows, rank), F32),
    ]
    return pl.pallas_call(
        functools.partial(middle_back_kernel, plan, start),
        grid=(rows // tile,),
        in_specs=[row_blocks(a, tile) for a in (d_first, d_second, y1, dy, o, z, meta)]
        + [pl.BlockSpec(memory_space=pl.ANY)]
        + [whole(a) for a in (w_out, gain)]
        + [pl.BlockSpec(memory_space=pl.ANY)],
        out_specs=[row_blocks(a, tile) for a in outs[:2]] + [whole(a) for a in outs[2:]],
        out_shape=outs,
        scratch_shapes=[
            pltpu.VMEM((width, rank), F32),
            pltpu.VMEM((qw, rank), F32),
            pltpu.VMEM((first, plan.rows, rank), BF16),
            pltpu.VMEM((first, plan.rows, rank), BF16),
            pltpu.VMEM((width, rank), BF16),
            pltpu.SemaphoreType.DMA((first,)),
            pltpu.SemaphoreType.DMA((first,)),
            pltpu.SemaphoreType.DMA((first,)),
            pltpu.SemaphoreType.DMA((1,)),
        ],
        compiler_params=params(collective_id=3, has_side_effects=True),
        cost_estimate=cost(2 * rows * width * 1500, 20e6),
        name="middle_back",
    )(d_first, d_second, y1, dy, o, z, meta, copies, w_out, gain, flat)


def own_tile(step, tiles):
    return jnp.maximum(step - tiles, 0)


def their_tile(step, tiles):
    return jnp.clip(step - 1, 0, tiles - 1)


def feed_kernel(
    n_ref, n_hbm, dy_ref, dyt_ref, meta_ref, metat_ref, wg_hbm, wu_hbm,
    wd_hbm, copies,
    y_ref, d_ref, y_got, d_got, last_ref, flat_ref,
    wga, wua, wda, raw, grads, extras, xg, xu, dya, yacc, dacc, mask_s, n_got, held_d, held_y,
    packed, blank, ap_ref, bd_ref, wsem, gsem, nsend, nrecv, dsend, drecv, ysend, yrecv,
):
    step = pl.program_id(0)
    steps = pl.num_programs(0)
    tiles_each = n_got.shape[0]
    width, half = wg_hbm.shape
    rank = bd_ref.shape[1]
    rows = n_ref.shape[0]
    place, part = lax.axis_index("dp"), lax.axis_index("tensor")
    theirs = (step >= 1) & (step <= tiles_each)
    number_t = their_tile(step, tiles_each)
    tile = HIDDEN_TILE
    tiles = pl.cdiv(half, tile)
    lap = tiles * tile - half
    a_gate = copies.shape[0] - 3 * width - 6 * half
    a_up = a_gate + width + 2 * half
    a_down = a_up + width + 2 * half
    b_down = a_down + 2 * half

    def loads(number):
        at = pl.multiple_of(jnp.minimum(number * tile, half - tile), LANES)
        to = pl.multiple_of(number * tile, tile)
        here, there = pl.ds(at, tile), pl.ds(to, tile)

        def own_half(base):
            return copies.at[pl.ds(pl.multiple_of(base + part * half + at, 16), tile), :]

        top, side = pl.ds(0, width), pl.ds(width, rank)
        pairs = [
            (wg_hbm.at[:, here], wga.at[top, there]),
            (wu_hbm.at[:, here], wua.at[top, there]),
            (wd_hbm.at[here, :], wda.at[there, top]),
            (own_half(a_gate + width), raw.at[0, there, :]),
            (own_half(a_up + width), raw.at[1, there, :]),
            (own_half(a_down), wda.at[there, side]),
        ]
        return [
            pltpu.make_async_copy(source, target, wsem.at[number, at])
            for at, (source, target) in enumerate(pairs)
        ]

    def swap(source, target, sends, recvs, number):
        return pltpu.make_async_remote_copy(
            src_ref=source,
            dst_ref=target.at[number],
            send_sem=sends.at[number],
            recv_sem=recvs.at[number],
            device_id=(place, 1 - part),
            device_id_type=MESH,
        )

    def send_n(number):
        return swap(n_hbm.at[pl.ds(number * rows, rows), :], n_got, nsend, nrecv, number)

    def send_d(number):
        return swap(held_d.at[number], d_got, dsend, drecv, number)

    def send_y(number):
        return swap(held_y.at[number], y_got, ysend, yrecv, number)

    thin_loads = [
        pltpu.make_async_copy(copies.at[pl.ds(base, width), :], target, gsem.at[at])
        for at, (base, target) in enumerate(
            (
                (a_gate, ap_ref.at[:, pl.ds(0, rank)]),
                (a_up, ap_ref.at[:, pl.ds(rank, rank)]),
                (b_down, bd_ref),
            )
        )
    ]

    @pl.when(step == 0)
    def _():
        for copy in thin_loads:
            copy.start()
        for number in range(tiles):
            for copy in loads(number):
                copy.start()
        barrier = pltpu.get_barrier_semaphore()
        pl.semaphore_signal(barrier, inc=1, device_id=(place, 1 - part), device_id_type=MESH)
        pl.semaphore_wait(barrier, 1)
        for number in range(tiles_each):
            send_n(number).start()
        grads[...] = jnp.zeros_like(grads)
        extras[...] = jnp.zeros_like(extras)
        for copy in thin_loads:
            copy.wait()

    def prepare(normed, dy, adapter):
        mask = rank_mask(adapter, rank)
        mask_s[...] = mask
        lows = nn(normed, ap_ref[...])
        xg[:, :width] = normed
        xu[:, :width] = normed
        xg[:, width:] = (lows[:, :rank] * mask).astype(BF16)
        xu[:, width:] = (lows[:, rank:] * mask).astype(BF16)
        dya[:, :width] = dy
        dya[:, width:] = (ADAPTER_SCALE * nn(dy, bd_ref[...]) * mask).astype(BF16)

    @pl.when(jnp.logical_not(theirs))
    def _():
        prepare(n_ref[...], dy_ref[...], meta_ref[:, 0:1])

    @pl.when(theirs)
    def _():
        send_n(number_t).wait_recv()
        prepare(n_got[number_t], dyt_ref[...], metat_ref[:, 0:1])

    yacc[...] = jnp.zeros_like(yacc)
    dacc[...] = jnp.zeros_like(dacc)

    def hidden(number, carry):
        span = pl.ds(pl.multiple_of(number * tile, tile), tile)

        @pl.when(step == 0)
        def _():
            for copy in loads(number):
                copy.wait()
            for at, target in enumerate((wga, wua)):
                turned = jnp.transpose(raw[at, span, :].astype(F32) * ADAPTER_SCALE)
                target[width:, span] = turned.astype(BF16)
            if lap:

                @pl.when(number == tiles - 1)
                def _():
                    edge = slice((tiles - 1) * tile, (tiles - 1) * tile + lap)
                    wga[:, edge] = jnp.zeros((width + rank, lap), BF16)
                    wua[:, edge] = jnp.zeros((width + rank, lap), BF16)
                    wda[edge, :] = jnp.zeros((lap, width + rank), BF16)

        gate = nn(xg[...], wga[:, span])
        up = nn(xu[...], wua[:, span])
        dhid = nt(dya[...], wda[span, :])
        sig = 1.0 / (1.0 + jnp.exp(-gate))
        silu = gate * sig
        hid = (silu * up).astype(BF16)
        dg = (dhid * up * (sig * (1.0 + gate * (1.0 - sig)))).astype(BF16)
        du = (dhid * silu).astype(BF16)
        yacc[...] += nn(hid, wda[span, :])
        dga = nt(dg, wga[:, span])
        dua = nt(du, wua[:, span])
        dacc[:, :width] += dga[:, :width] + dua[:, :width]
        dacc[:, width : width + rank] += dga[:, width:]
        dacc[:, width + rank :] += dua[:, width:]
        grads[0, span, :] += ADAPTER_SCALE * tn(dg, xg[:, width:])
        grads[1, span, :] += ADAPTER_SCALE * tn(du, xu[:, width:])
        grads[2, span, :] += tn(hid, dya[:, width:])
        return carry

    lax.fori_loop(0, tiles, hidden, 0)
    mask = mask_s[...]
    low = (yacc[:, width:] * mask).astype(BF16)
    result = yacc[:, :width] + ADAPTER_SCALE * nt(low, bd_ref[...])
    back = (dacc[:, width:] * jnp.concatenate([mask, mask], axis=1)).astype(BF16)
    change = dacc[:, :width] + nt(back, ap_ref[...])
    pair = tn(xg[:, :width], back)
    extras[0] += pair[:, :rank]
    extras[1] += pair[:, rank:]
    extras[2] += ADAPTER_SCALE * tn(dya[:, :width], low)

    @pl.when(jnp.logical_not(theirs))
    def _():
        y_ref[...] = result
        d_ref[...] = change

    @pl.when(theirs)
    def _():
        held_d[number_t] = change.astype(BF16)
        send_d(number_t).start()

        @pl.when(number_t < tiles_each - 1)
        def _():
            held_y[number_t] = result.astype(BF16)

        @pl.when(number_t == tiles_each - 1)
        def _():
            last_ref[...] = result.astype(BF16)
            for number in range(tiles_each - 1):
                send_y(number).start()

    @pl.when(step == steps - 1)
    def _():
        last = (tiles - 1) * tile
        for at in range(3):
            packed[at, :last, :] = grads[at, :last, :].astype(BF16)
            packed[at, last:half, :] = grads[at, last + lap : tiles * tile, :].astype(BF16)
            packed[at, half:, :] = extras[at].astype(BF16)
        blank[...] = jnp.zeros_like(blank)
        moves = []
        for at, base in enumerate((a_gate + width, a_up + width, a_down)):
            mine = pl.multiple_of(base + part * half, 16)
            other = pl.multiple_of(base + (1 - part) * half, 16)
            moves.append((packed.at[at, pl.ds(0, half), :], flat_ref.at[pl.ds(mine, half), :]))
            moves.append((blank, flat_ref.at[pl.ds(other, half), :]))
        for at, base in enumerate((a_gate, a_up, b_down)):
            moves.append((packed.at[at, pl.ds(half, width), :], flat_ref.at[pl.ds(base, width), :]))
        moves = [
            pltpu.make_async_copy(source, target, gsem.at[at])
            for at, (source, target) in enumerate(moves)
        ]
        for copy in moves:
            copy.start()
        for copy in moves:
            copy.wait()
        for number in range(tiles_each):
            send_n(number).wait_send()
            send_d(number).wait_send()
            send_d(number).wait_recv()
        for number in range(tiles_each - 1):
            send_y(number).wait_send()
            send_y(number).wait_recv()


def feed(n2, dy, dy_theirs, meta, meta_theirs, w_gate, w_up, w_down, copies):
    rows, width = n2.shape
    half = w_down.shape[0]
    total, rank = copies.shape
    tile = ROW_TILE
    count = rows // tile
    tiles = pl.cdiv(half, HIDDEN_TILE)
    padded = tiles * HIDDEN_TILE
    anywhere = pl.BlockSpec(memory_space=pl.ANY)
    wide, deep = width + rank, width + 2 * rank

    def own_rows(array):
        return pl.BlockSpec((tile, array.shape[1]), lambda i: (own_tile(i, count), 0))

    def their_rows(array):
        return pl.BlockSpec((tile, array.shape[1]), lambda i: (their_tile(i, count), 0))

    dma = pltpu.SemaphoreType.DMA
    outs = [
        jax.ShapeDtypeStruct((rows, width), F32),
        jax.ShapeDtypeStruct((rows, width), F32),
        jax.ShapeDtypeStruct((count - 1, tile, width), BF16),
        jax.ShapeDtypeStruct((count, tile, width), BF16),
        jax.ShapeDtypeStruct((tile, width), BF16),
        jax.ShapeDtypeStruct((total + FLAT_PAD, rank), BF16),
    ]
    return pl.pallas_call(
        feed_kernel,
        grid=(2 * count,),
        in_specs=[
            own_rows(n2), anywhere, own_rows(dy), their_rows(dy_theirs), own_rows(meta),
            their_rows(meta_theirs),
        ]
        + [anywhere] * 4,
        out_specs=[own_rows(outs[0]), own_rows(outs[1]), anywhere, anywhere, whole(outs[4]), anywhere],
        out_shape=outs,
        scratch_shapes=[
            pltpu.VMEM((wide, padded), BF16),
            pltpu.VMEM((wide, padded), BF16),
            pltpu.VMEM((padded, wide), BF16),
            pltpu.VMEM((2, padded, rank), BF16),
            pltpu.VMEM((3, padded, rank), F32),
            pltpu.VMEM((3, width, rank), F32),
            pltpu.VMEM((tile, wide), BF16),
            pltpu.VMEM((tile, wide), BF16),
            pltpu.VMEM((tile, wide), BF16),
            pltpu.VMEM((tile, wide), F32),
            pltpu.VMEM((tile, deep), F32),
            pltpu.VMEM((tile, rank), F32),
            pltpu.VMEM((count, tile, width), BF16),
            pltpu.VMEM((count, tile, width), BF16),
            pltpu.VMEM((count - 1, tile, width), BF16),
            pltpu.VMEM((3, half + width, rank), BF16),
            pltpu.VMEM((half, rank), BF16),
            pltpu.VMEM((width, 2 * rank), BF16),
            pltpu.VMEM((width, rank), BF16),
            dma((tiles, 6)),
            dma((9,)),
            dma((count,)),
            dma((count,)),
            dma((count,)),
            dma((count,)),
            dma((count - 1,)),
            dma((count - 1,)),
        ],
        compiler_params=params(collective_id=1, has_side_effects=True),
        cost_estimate=cost(4 * rows * half * (6 * width + 9 * rank), 40e6),
        name="feed",
    )(
        n2, n2, dy, dy_theirs, meta, meta_theirs, w_gate, w_up, w_down, copies
    )


def tail_kernel(plan, early, key_width, direct, *refs):
    sources = refs[:9]
    other_ref, w_hbm, b_ref, gain_ref, flat_ref, out_grad_ref, kept_hbm, gots_hbm = refs[9:17]
    out_ref, sum_ref = refs[17:19]
    held = refs[19:28]
    w, grads, dxs, acc_a, acc_b, outbox, last_in, got_s, kept, gots, *rest = refs[28:]
    inboxes = rest[:-13]
    (
        load_sem, grad_sem, dsend, drecv, fsend, frecv, rsend, rrecv, zrecv, keep_sem, ksend, krecv,
        hsem,
    ) = rest[-13:]
    gq_s, own_s, x_s, n_s, z_s, dy1_s, meta_s, cos_s, sin_s = held
    place, part = lax.axis_index("dp"), lax.axis_index("tensor")
    devices, plane, axes = plan.devices, plan.plane, plan.axes
    depth, inside = place // plane, lax.rem(place, plane)
    count = len(axes)
    tile = x_s.shape[1]
    rank = b_ref.shape[1]
    width = x_s.shape[2]
    qw, kw = gq_s.shape[2], key_width
    over = (place, 1 - part)

    def layer(hop):
        return lax.rem(depth + hop, PLANES)

    def turn_of(number):
        return lax.rem(number + 2, PLANES)

    def rows_at(number):
        return pl.ds(pl.multiple_of(layer(turn_of(number)) * tile, 16), tile)

    def tile_loads(number):
        return [
            pltpu.make_async_copy(
                source.at[rows_at(number), :], target.at[number], load_sem.at[number, which]
            )
            for which, (source, target) in enumerate(zip(sources, held))
        ]

    sums_loads = [
        pltpu.make_async_copy(kept_hbm, kept, grad_sem.at[3]),
        pltpu.make_async_copy(gots_hbm, gots, grad_sem.at[4]),
    ]
    w_load = pltpu.make_async_copy(w_hbm, w, grad_sem.at[0])
    middle = out_grad_ref.shape[0]
    late_rows = grads.shape[0] - early - middle
    grad_loads = [
        pltpu.make_async_copy(out_grad_ref, grads.at[pl.ds(early, middle), :], grad_sem.at[1]),
        pltpu.make_async_copy(
            flat_ref.at[pl.ds(early + middle, late_rows), :],
            grads.at[pl.ds(early + middle, late_rows), :],
            grad_sem.at[2],
        ),
    ]
    for copy in sums_loads + [w_load]:
        copy.start()
    for number in range(PLANES):
        for copy in tile_loads(number):
            copy.start()
    for copy in grad_loads:
        copy.start()

    barrier = pltpu.get_barrier_semaphore()
    for k in range(1, devices):
        pl.semaphore_signal(
            barrier, inc=1, device_id=(lax.rem(place + k, devices), part), device_id_type=MESH
        )
    pl.semaphore_signal(barrier, inc=1, device_id=over, device_id_type=MESH)
    pl.semaphore_wait(barrier, devices)

    def key_copy(number):
        return pltpu.make_async_remote_copy(
            src_ref=other_ref.at[rows_at(number), :],
            dst_ref=got_s.at[number],
            send_sem=ksend.at[number],
            recv_sem=krecv.at[number],
            device_id=over,
            device_id_type=MESH,
        )

    for number in range(PLANES):
        key_copy(number).start()

    bases = []
    cursor = 0
    for stage in range(count):
        bases.append(cursor)
        cursor += plan.boxes(stage) * (1 if stage < 2 else PLANES)

    def box_of(stage, zz, at, side):
        return plan.box(stage, at, side) + (0 if stage < 2 else zz * plan.boxes(stage))

    def window_sum(stages, zz, at, side):
        if zz == 0:
            total = grads[plan.span(0, at, side), :].astype(F32)
            for stage in range(min(2, stages)):
                total = total + inboxes[stage][box_of(stage, 0, at, side)].astype(F32)
        else:
            index = (zz - 1) * plan.boxes(1) + plan.box(1, at, side)
            total = kept[index] + gots[index].astype(F32)
        for stage in range(2, stages):
            total = total + inboxes[stage][box_of(stage, zz, at, side)].astype(F32)
        return total

    def take(stages, zz, at, side):
        for stage in range(0 if zz == 0 else 2, stages):
            index = box_of(stage, zz, at, side)
            pltpu.make_async_remote_copy(
                src_ref=inboxes[stage].at[index],
                dst_ref=inboxes[stage].at[index],
                send_sem=rsend.at[0],
                recv_sem=rrecv.at[bases[stage] + index],
                device_id=over,
                device_id_type=MESH,
            ).wait_recv()

    sent = []
    posted = [0]

    def pass_on(stage, zz, source_of):
        partner = flip(place, part, [axes[stage]])
        for at, side in plan.leaving(stage, inside, part):
            index = box_of(stage, zz, at, side)
            copy = pltpu.make_async_remote_copy(
                src_ref=source_of(at, side),
                dst_ref=inboxes[stage].at[index],
                send_sem=rsend.at[len(sent)],
                recv_sem=rrecv.at[bases[stage] + index],
                device_id=partner,
                device_id_type=MESH,
            )
            copy.start()
            sent.append(copy)

    def post(total):
        slot = posted[0]
        posted[0] += 1
        outbox[slot] = total.astype(BF16)
        return outbox.at[slot]

    def stage_sends(stage, zz):
        def source_of(at, side):
            take(stage, zz, at, side)
            return post(window_sum(stage, zz, at, side))

        pass_on(stage, zz, source_of)

    for copy in sums_loads:
        copy.wait()
    for zz in range(1, PLANES):
        stage_sends(2, zz)

    def step_at(step):
        return lax.rem(inside + step, plane)

    acc_a[...] = jnp.zeros_like(acc_a)
    acc_b[...] = jnp.zeros_like(acc_b)
    w_load.wait()

    def piece_copy(number, step, where, target):
        return pltpu.make_async_remote_copy(
            src_ref=dxs.at[number, step_at(step)],
            dst_ref=target,
            send_sem=dsend.at[number, step],
            recv_sem=drecv.at[place],
            device_id=where,
            device_id_type=MESH,
        )

    def one_tile(number, carry):
        for copy in tile_loads(number):
            copy.wait()
        key_copy(number).wait_recv()
        mask = rank_mask(meta_s[number][:, 0:1], rank)
        both = own_s[number].astype(F32) + got_s[number].astype(F32)
        cos, sin = cos_s[number], sin_s[number]
        dk = both[:, :kw]
        gq = gq_s[number]
        gk = (dk * cos - turn(dk) * sin).astype(BF16)
        gv = both[:, kw:].astype(BF16)
        at_k, at_v = 2 * width + qw, 3 * width + qw + kw
        b_parts = (
            b_ref[width : width + qw, :],
            b_ref[at_k : at_k + kw, :],
            b_ref[at_v : at_v + kw, :],
        )
        backs = [
            (ADAPTER_SCALE * nn(g, b) * mask).astype(BF16) for g, b in zip((gq, gk, gv), b_parts)
        ]
        dn = nt(jnp.concatenate([gq, gk, gv] + backs, axis=1), w[...])
        values = x_s[number].astype(F32)
        dx = (dy1_s[number] + norm_back(values, gain_ref[...], dn)).astype(BF16)
        acc_a[...] += tn(n_s[number], jnp.concatenate(backs, axis=1))
        low = z_s[number]
        acc_b[:qw, :] += tn(gq, low[:, :rank])
        acc_b[qw : qw + kw, :] += tn(gk, low[:, rank : 2 * rank])
        acc_b[qw + kw :, :] += tn(gv, low[:, 2 * rank :])
        turn_now = turn_of(number)
        if not direct:
            dxs[number] = dx
            copy = pltpu.make_async_copy(
                dxs.at[number], out_ref.at[rows_at(number), :], keep_sem.at[0]
            )
            copy.start()
            copy.wait()
            return carry
        dxs[number] = dx.reshape(dxs.shape[1:])
        for step in range(plane):
            target = layer(turn_now) * plane + step_at(step)
            if step > 0:
                piece_copy(number, step, (target, part), out_ref.at[place, part]).start()
                continue

            @pl.when(turn_now == 0)
            def _():
                pltpu.make_async_copy(
                    dxs.at[number, inside], out_ref.at[place, part], keep_sem.at[0]
                ).start()

            @pl.when(turn_now > 0)
            def _():
                piece_copy(number, 0, (target, part), out_ref.at[place, part]).start()

        return carry

    lax.fori_loop(0, PLANES, one_tile, 0)
    for copy in grad_loads:
        copy.wait()

    at = 0
    for order, size in enumerate((qw, kw, kw)):
        grads[at : at + width, :] = acc_a[:, order * rank : (order + 1) * rank].astype(BF16)
        base = (0, qw, qw + kw)[order]
        grads[at + width : at + width + size, :] = (
            ADAPTER_SCALE * acc_b[base : base + size, :]
        ).astype(BF16)
        at += width + size
    pass_on(0, 0, lambda at, side: grads.at[plan.span(0, at, side), :])

    forwards = []

    def forward(back):
        source = layer(back)
        for step in range(plane):
            at = source * plane + step_at(step)
            if step > 0 or back > 0:
                pltpu.make_async_remote_copy(
                    src_ref=out_ref.at[at, part],
                    dst_ref=out_ref.at[at, part],
                    send_sem=hsem.at[0],
                    recv_sem=drecv.at[at],
                    device_id=over,
                    device_id_type=MESH,
                ).wait_recv()
            else:
                pltpu.make_async_copy(
                    out_ref.at[place, part], out_ref.at[place, part], keep_sem.at[0]
                ).wait()
        copy = forward_copy(source, part, len(forwards))
        copy.start()
        forwards.append(copy)

    def forward_copy(source, side, number):
        span = pl.ds(source * plane, plane)
        return pltpu.make_async_remote_copy(
            src_ref=out_ref.at[span, side],
            dst_ref=out_ref.at[span, side],
            send_sem=fsend.at[number],
            recv_sem=frecv.at[source],
            device_id=over,
            device_id_type=MESH,
        )

    zsends = []

    def across_planes(zz):
        take(count, zz, inside, part)
        total = window_sum(count, zz, inside, part)
        slot = posted[0]
        posted[0] += 1
        number = len(sent) + len(zsends)
        copy = pltpu.make_async_remote_copy(
            src_ref=outbox.at[slot],
            dst_ref=last_in.at[depth],
            send_sem=rsend.at[number],
            recv_sem=zrecv.at[depth],
            device_id=(zz * plane + inside, part),
            device_id_type=MESH,
        )
        zsends.append((zz, copy))

        @pl.when(depth != zz)
        def _():
            outbox[slot] = total.astype(BF16)
            copy.start()

        @pl.when(depth == zz)
        def _():
            sum_ref[...] = total

    if direct:
        forward(0)
    for stage in range(3, count):
        for zz in (1, 2, 3):
            stage_sends(stage, zz)
    for zz in (1, 2, 3):
        across_planes(zz)
    stage_sends(1, 0)
    if direct:
        forward(3)
        forward(1)
    for stage in range(2, count):
        stage_sends(stage, 0)
    across_planes(0)
    if direct:
        forward(2)
    for hop in (1, 2, 3):
        source = layer(hop)
        pltpu.make_async_remote_copy(
            src_ref=last_in.at[source],
            dst_ref=last_in.at[source],
            send_sem=hsem.at[0],
            recv_sem=zrecv.at[source],
            device_id=over,
            device_id_type=MESH,
        ).wait_recv()
        sum_ref[...] += last_in[source].astype(F32)

    if direct:
        for back in range(PLANES):
            forward_copy(layer(back), 1 - part, 0).wait_recv()
        for copy in forwards:
            copy.wait_send()
        for number in range(PLANES):
            for step in range(plane):
                if step == 0 and (number + 2) % PLANES == 0:
                    continue
                piece_copy(number, step, over, out_ref.at[place, part]).wait_send()
    for copy in sent:
        copy.wait_send()
    for zz, copy in zsends:

        @pl.when(depth != zz)
        def _():
            copy.wait_send()

    for number in range(PLANES):
        key_copy(number).wait_send()


def tail(
    devices, own_rows, early, rows_in, other, w_cat, b_rows, gain, flat, grad_out, kept, gots,
    key_width, piece,
):
    gq, _, x = rows_in[:3]
    rows, width = x.shape
    plan = Windows(devices, own_rows)
    plane, count, window = plan.plane, len(plan.axes), plan.rows
    rank = flat.shape[1]
    tile = rows // PLANES
    direct = piece % 16 == 0
    anywhere = pl.BlockSpec(memory_space=pl.ANY)
    boxes = [plan.boxes(stage) * (1 if stage < 2 else PLANES) for stage in range(count)]
    sends = sum(boxes) + PLANES
    qw = gq.shape[1]
    first_plane = 16 * (((2 * plane - 1) * own_rows) // 16) + window
    dma = pltpu.SemaphoreType.DMA
    if direct:
        shape = (devices, 2, piece, width)
        held = (plane, piece, width)
    else:
        shape = (rows, width)
        held = (tile, width)
    outs = [jax.ShapeDtypeStruct(shape, BF16)]
    outs.append(jax.ShapeDtypeStruct((window, rank), F32))
    scratch = [pltpu.VMEM((PLANES, tile, a.shape[1]), a.dtype) for a in rows_in]
    scratch += [
        pltpu.VMEM(w_cat.shape, BF16),
        pltpu.VMEM((first_plane, rank), BF16),
        pltpu.VMEM((PLANES,) + held, BF16),
        pltpu.VMEM((width, 3 * rank), F32),
        pltpu.VMEM((qw + 2 * key_width, rank), F32),
        pltpu.VMEM((sends, window, rank), BF16),
        pltpu.VMEM((PLANES, window, rank), BF16),
        pltpu.VMEM((PLANES, tile, other.shape[1]), BF16),
        pltpu.VMEM(kept.shape, F32),
        pltpu.VMEM(gots.shape, BF16),
    ]
    scratch += [pltpu.VMEM((size, window, rank), BF16) for size in boxes]
    scratch += [
        dma((PLANES, len(rows_in))),
        dma((5,)),
        dma((PLANES, plane)),
        dma((devices,)),
        dma((PLANES,)),
        dma((PLANES,)),
        dma((sends,)),
        dma((sum(boxes),)),
        dma((PLANES,)),
        dma((1,)),
        dma((PLANES,)),
        dma((PLANES,)),
        dma((1,)),
    ]
    return pl.pallas_call(
        functools.partial(tail_kernel, plan, early, key_width, direct),
        grid=(1,),
        in_specs=[anywhere] * 11
        + [pl.BlockSpec((early, rank), lambda i: (0, 0)), whole(gain)]
        + [anywhere] * 4,
        out_specs=[anywhere, whole(outs[1])],
        out_shape=outs,
        scratch_shapes=scratch,
        compiler_params=params(collective_id=2, has_side_effects=True),
        cost_estimate=cost(2 * rows * width * 2900, 200e6),
        name="tail",
    )(*rows_in, other, w_cat, b_rows, gain, flat, grad_out, kept, gots)


def row_tables(order_row, lengths_row, adapter_row, part, parts, each):
    total = order_row.shape[0]
    piece = each // parts
    local = total // parts
    places = jnp.arange(total, dtype=I32)
    own = (order_row % each) // piece == part
    slot = (order_row // each) * piece + order_row % piece
    column = jnp.where(own, slot, local + slot)
    upto = jnp.sum((own[None, :] & (places[None, :] <= places[:, None])).astype(I32), axis=1)
    rank = jnp.where(own, upto - 1, total)
    picks = rank[None, :] == jnp.arange(local, dtype=I32)[:, None]
    sorted_place = jnp.sum(jnp.where(picks, places[None, :], 0), axis=1)
    sorted_slot = jnp.sum(jnp.where(picks, slot[None, :], 0), axis=1)
    slot_place = jnp.sum(jnp.where(column[None, :] == places[:, None], places[None, :], 0), axis=1)
    ends = jnp.cumsum(lengths_row)
    starts = ends - lengths_row
    both = jnp.concatenate([slot_place, sorted_place])
    member = (both[:, None] >= starts[None, :]) & (both[:, None] < ends[None, :])
    first = jnp.sum(jnp.where(member, starts[None, :], 0), axis=1)
    chosen = jnp.sum(jnp.where(member, adapter_row[None, :], 0), axis=1)
    position = both - first
    sorted_first = first[total:]
    bounds = jnp.stack(
        [
            sorted_first[::QUERY_TILE] // KEY_TILE,
            sorted_place[QUERY_TILE - 1 :: QUERY_TILE] // KEY_TILE + 1,
        ]
    )
    blank = jnp.zeros_like(sorted_place)
    meta_sorted = jnp.stack([sorted_slot, sorted_first, sorted_place] + [blank] * 5, axis=1)
    meta_rows = jnp.stack([sorted_slot, sorted_first, sorted_place] + [blank] * 5, axis=0)
    meta_own = jnp.broadcast_to(chosen[:local, None], (local, 8))
    meta_other = jnp.broadcast_to(chosen[local:total, None], (local, 8))
    slot_position = position[:local]
    return (
        meta_own, meta_other, meta_sorted, meta_rows, slot_position, position[total:], column, bounds,
    )


def rope_tables(position):
    freq_index = jnp.arange(HEAD // 2, dtype=F32)
    inv_freq = jnp.power(jnp.float32(ROPE_BASE), -2.0 * freq_index / HEAD)
    angles = position.astype(F32)[None, :] * inv_freq[:, None]
    return jnp.cos(angles), jnp.sin(angles)


def per_device(
    tokens, cotangent, order, lengths, adapter_ids, norm_gains, w_query, w_key, w_value,
    b_query, b_key, b_value, w_out, w_gate, w_up, w_down, adapters, first_moment, second_moment,
):
    parts = lax.axis_size("tensor")
    part = lax.axis_index("tensor")
    devices = lax.axis_size("dp")
    place = lax.axis_index("dp")
    total, width = tokens.shape
    each = total // devices
    piece = each // parts
    local = total // parts
    rank = adapters.shape[1]
    own_rows = adapters.shape[0]
    swap = [(i, parts - 1 - i) for i in range(parts)]
    first_part = part == 0

    def across(values):
        return lax.ppermute(values, "tensor", swap)

    def pair(mine, theirs, axis):
        return jnp.concatenate(
            [jnp.where(first_part, mine, theirs), jnp.where(first_part, theirs, mine)], axis=axis
        )

    def give_back(values):
        got = lax.all_to_all(
            values.reshape(devices, piece, width), "dp", split_axis=0, concat_axis=0, tiled=True
        )
        theirs = across(got)
        return pair(got[:, None], theirs[:, None], 1).reshape(total, width)

    qh, kh, half = w_query.shape[1], w_key.shape[1], w_gate.shape[1]
    qw, kw, hidden = parts * qh, parts * kh, parts * half
    heads, kv_heads = qw // HEAD, kw // HEAD
    mine_qkv = jnp.concatenate(
        [
            jnp.concatenate([w_query, w_key, w_value], axis=1),
            jnp.broadcast_to(
                jnp.concatenate([b_query, b_key, b_value])[None], (32, qh + 2 * kh)
            ),
        ],
        axis=0,
    )
    lines = mine_qkv.shape[0]
    unit = 4 if own_rows % 4 == 0 else 1
    moved, copies, their_qkv, their_out = front(
        tokens.reshape(devices, parts, piece, width),
        adapters.astype(BF16).reshape(own_rows // unit, unit, rank),
        mine_qkv.reshape(2, lines // 2, -1),
        w_out.reshape(2, w_out.shape[0] // 2, width),
        devices,
    )
    cotangent, moved = lax.optimization_barrier((cotangent, moved))
    moved = moved.reshape(local, width)
    dy_all = lax.all_to_all(
        cotangent.reshape(devices, each, width), "dp", split_axis=0, concat_axis=0, tiled=True
    ).reshape(devices, parts, piece, width)

    def half_of(which):
        return lax.dynamic_index_in_dim(dy_all, which, 1, keepdims=False).reshape(local, width)

    dy = half_of(part)
    dy_theirs = half_of(parts - 1 - part)

    early = 3 * width + qw + 2 * kw
    flat = copies.reshape(2 * devices * own_rows, rank)
    meta_own, meta_other, meta_sorted, meta_rows, slot_position, sorted_position, column, bounds = (
        row_tables(order[0], lengths[0], adapter_ids[0], part, parts, each)
    )
    turns, sines = rope_tables(jnp.concatenate([slot_position, sorted_position]))
    gain_one = norm_gains[0:1].astype(F32)
    gain_two = norm_gains[1:2].astype(F32)
    side = jnp.reshape(part, (1,)).astype(I32)

    n1, q, kv, z, cos, sin, w_cat = project(
        side, moved, meta_own, turns, sines, gain_one, mine_qkv, their_qkv.reshape(mine_qkv.shape),
        flat, qw, kw,
    )
    other_kv = across(kv)
    q_sorted, o_sorted, logs, merged, o = attend(
        bounds, q, meta_sorted, meta_rows, kv, other_kv, column[:, None], heads, kv_heads
    )
    y1, n2, z_out, w_out_cat = middle(
        side, o, moved, meta_own, w_out, their_out.reshape(w_out.shape), gain_two, flat, early
    )
    y_own, d_own, y_got, d_got, y_last, flat_grads = feed(
        n2, dy, dy_theirs, meta_own, meta_other, w_gate, w_up, w_down, flat
    )
    y_got = jnp.concatenate([y_got, across(y_last)[None]], axis=0).reshape(local, width)
    dy1, dar, grad_out, on_sums, kept_sums = middle_back(
        devices, own_rows, d_own, d_got.reshape(local, width), y1, dy, o, z_out, meta_own, flat,
        early + qw, w_out_cat, gain_two, flat_grads,
    )
    got_sums = lax.ppermute(on_sums, "dp", [(i, i ^ 2) for i in range(devices)])
    layer_rows = (y1 + (y_own + y_got.astype(F32))).astype(BF16).reshape(devices, 1, piece, width)
    layer_rows = jnp.broadcast_to(layer_rows, (devices, parts, piece, width))
    layer_rows, dar = lax.optimization_barrier((layer_rows, dar))
    layer_out = lax.all_to_all(
        layer_rows.reshape(devices * parts, piece, width),
        ("dp", "tensor"), split_axis=0, concat_axis=0, tiled=True,
    ).reshape(total, width)
    gq, dkv_own, dkv_other = attend_back(
        bounds, q_sorted, dar, o_sorted, logs, meta_sorted, meta_rows, turns, sines,
        merged, column[None, :], heads, kv_heads,
    )
    dx, window = tail(
        devices, own_rows, early,
        (gq, dkv_own, moved, n1, z, dy1, meta_own, cos, sin),
        dkv_other, w_cat, flat, gain_one, flat_grads, grad_out, kept_sums,
        got_sums, kw, piece,
    )
    if dx.ndim == 4:
        input_grad = dx.reshape(total, width)
    else:
        input_grad = give_back(dx)
    offset = lax.rem((2 * place + part) * own_rows, 16)
    reduced = lax.dynamic_slice_in_dim(window, offset, own_rows, 0)
    moment_one = BETA_ONE * first_moment + (1.0 - BETA_ONE) * reduced
    moment_two = BETA_TWO * second_moment + (1.0 - BETA_TWO) * reduced * reduced
    corrected_one = moment_one / (1.0 - BETA_ONE**STEP)
    corrected_two = moment_two / (1.0 - BETA_TWO**STEP)
    updated = adapters - LEARN_RATE * (
        corrected_one / (jnp.sqrt(corrected_two) + ADAM_EPS) + WEIGHT_DECAY * adapters
    )
    return (
        layer_out,
        input_grad,
        reduced,
        moment_one,
        moment_two,
        updated,
        updated.astype(BF16),
    )


def solution(mesh):
    both = P(("dp", "tensor"), None)
    rows = P("dp", None)
    return jax.shard_map(
        per_device,
        mesh=mesh,
        in_specs=(rows, rows, rows, rows, rows, P())
        + (P(None, "tensor"),) * 3
        + (P("tensor"),) * 3
        + (P("tensor", None), P(None, "tensor"), P(None, "tensor"), P("tensor", None))
        + (both,) * 3,
        out_specs=(rows, rows) + (both,) * 5,
        check_vma=False,
    )
```

```python
import functools

import jax
import jax.numpy as jnp
from jax import lax
from jax.experimental import pallas as pl
from jax.experimental.pallas import tpu as pltpu
from jax.sharding import PartitionSpec as P

HEAD = 64
RANK = 16
STEP = 3

ADAPTER_SCALE = 2.0
NORM_EPS = 1e-06
ROPE_BASE = 1000000.0
BETA_ONE = 0.5
BETA_TWO = 0.6
LEARN_RATE = 0.04
WEIGHT_DECAY = 0.01
ADAM_EPS = 1e-08
MASKED_SCORE = -1e30
PLANES = 4
FLAT_PAD = 64
MESH = pl.DeviceIdType.MESH

LANES = 128
ROW_TILE = 256
QUERY_TILE = 128
KEY_TILE = 256
HIDDEN_TILE = 512

F32 = jnp.float32
BF16 = jnp.bfloat16
I32 = jnp.int32


def nn(left, right):
    return lax.dot_general(left, right, (((1,), (0,)), ((), ())), preferred_element_type=F32)


def nt(left, right):
    return lax.dot_general(left, right, (((1,), (1,)), ((), ())), preferred_element_type=F32)


def tn(left, right):
    return lax.dot_general(left, right, (((0,), (0,)), ((), ())), preferred_element_type=F32)


def lane_iota(shape):
    return lax.broadcasted_iota(I32, shape, 1)


def row_iota(shape):
    return lax.broadcasted_iota(I32, shape, 0)


def whole(array):
    return pl.BlockSpec(array.shape, lambda *_: (0,) * array.ndim)


def row_blocks(array, tile):
    return pl.BlockSpec((tile, array.shape[1]), lambda i, *_: (i, 0))


def rows_from(array, start, count):
    return pl.BlockSpec(
        (pl.Element(count), pl.Element(array.shape[1])), lambda *_: (start, 0)
    )


def lane_table(table):
    return jnp.transpose(jnp.concatenate([table] * (LANES // table.shape[0]), axis=0))


def rank_mask(adapter_col, width):
    return jnp.where(lane_iota((adapter_col.shape[0], width)) // RANK == adapter_col, 1.0, 0.0)


def turn(values):
    lanes = lane_iota(values.shape) % HEAD
    return jnp.where(
        lanes < HEAD // 2,
        -pltpu.roll(values, LANES - HEAD // 2, 1),
        pltpu.roll(values, HEAD // 2, 1),
    )


def rms(values):
    return lax.rsqrt(jnp.mean(values * values, axis=-1, keepdims=True) + NORM_EPS)


def norm_back(values, gain, grad):
    inverse = rms(values)
    weighted = grad * gain
    return inverse * weighted - values * inverse * inverse * inverse * jnp.mean(
        weighted * values, axis=-1, keepdims=True
    )


def pick_rows(place_col, slots):
    hit = place_col == lane_iota((place_col.shape[0], slots))
    return jnp.where(hit, 1.0, 0.0).astype(BF16)


def place_rows(place_row, slots):
    hit = row_iota((slots, place_row.shape[1])) == place_row
    return jnp.where(hit, 1.0, 0.0).astype(BF16)


def params(**more):
    return pltpu.CompilerParams(vmem_limit_bytes=60 * 1024 * 1024, **more)


def cost(flops, moved):
    return pl.CostEstimate(flops=int(flops), bytes_accessed=int(moved), transcendentals=0)


def xor_bit(value, bit):
    size = 2**bit
    return value + size * (1 - 2 * lax.rem(value // size, 2))


def subsets(axes):
    out = [()]
    for axis in axes:
        out += [chosen + (axis,) for chosen in out]
    return out


def flip_fixed(place, part, axes):
    for axis in axes:
        if axis == "tensor":
            part = 1 - part
        else:
            place = place ^ 2**axis
    return place, part


def flip(place, part, axes):
    for axis in axes:
        if axis == "tensor":
            part = 1 - part
        else:
            place = xor_bit(place, axis)
    return place, part


def front_kernel(
    devices, rows_ref, chunk_ref, wq_ref, wk_ref, wv_ref, bias_ref,
    got_ref, copies_ref, wq_out, wk_out, wv_out, bias_out,
    local_sem, tsend, trecv, csend, crecv, wsend, wrecv,
):
    place, part = lax.axis_index("dp"), lax.axis_index("tensor")
    plane = devices // PLANES
    depth, inside = place // plane, lax.rem(place, plane)
    core = lax.rem(place, 2)
    own = 2 * place + part
    over = (place, 1 - part)
    units = chunk_ref.shape[0]

    def rows_of(index):
        return copies_ref.at[pl.ds(index * units, units)]

    def layer(hop):
        return lax.rem(depth + hop, PLANES)

    barrier = pltpu.get_barrier_semaphore()
    for k in range(1, devices):
        pl.semaphore_signal(
            barrier, inc=1, device_id=(lax.rem(place + k, devices), part), device_id_type=MESH
        )
    pl.semaphore_signal(barrier, inc=1, device_id=over, device_id_type=MESH)
    pl.semaphore_wait(barrier, devices)

    def chunk_copy(source, index, number, where):
        return pltpu.make_async_remote_copy(
            src_ref=source,
            dst_ref=rows_of(index),
            send_sem=csend.at[number],
            recv_sem=crecv.at[index],
            device_id=where,
            device_id_type=MESH,
        )

    def chain(hop, way):
        origin = depth - way * hop
        index = 2 * (origin * plane + inside) + part
        target = ((depth + way) * plane + inside, part)
        source = chunk_ref if hop == 0 else rows_of(index)
        number = 2 * hop + (0 if way > 0 else 1)
        inner = (origin >= 0) & (origin < PLANES)
        ahead = (depth + way >= 0) & (depth + way < PLANES)
        return chunk_copy(source, index, number, target), inner, ahead

    keep = [
        pltpu.make_async_copy(chunk_ref, rows_of(own), local_sem.at[0]),
        pltpu.make_async_copy(rows_ref.at[place, part], got_ref.at[place], local_sem.at[1]),
    ]
    for way in (1, -1):
        copy, _, ahead = chain(0, way)

        @pl.when(ahead)
        def _():
            copy.start()

    weights = ((wq_ref, wq_out), (wk_ref, wk_out), (wv_ref, wv_out))

    def weight_copy(ref, out, number, slot, where):
        return pltpu.make_async_remote_copy(
            src_ref=ref.at[slot],
            dst_ref=out.at[slot],
            send_sem=wsend.at[number],
            recv_sem=wrecv.at[number],
            device_id=where,
            device_id_type=MESH,
        )

    direct = [
        weight_copy(ref, out, number, core, over) for number, (ref, out) in enumerate(weights)
    ]
    for slot in range(2):
        direct.append(weight_copy(bias_ref, bias_out, 6 + slot, slot, over))
    for copy in direct:
        copy.start()

    rows_sent = []

    def send_rows(hop):
        for step in range(plane):
            if hop == 0 and step == 0:
                continue
            target = layer(hop) * plane + lax.rem(inside + step, plane)
            copy = pltpu.make_async_remote_copy(
                src_ref=rows_ref.at[target, part],
                dst_ref=got_ref.at[place],
                send_sem=tsend.at[len(rows_sent)],
                recv_sem=trecv.at[place],
                device_id=(target, part),
                device_id_type=MESH,
            )
            copy.start()
            rows_sent.append((copy, target))

    send_rows(0)
    for copy in keep:
        copy.start()
    for hop in range(1, PLANES):
        for way in (1, -1):
            copy, inner, ahead = chain(hop, way)

            @pl.when(inner)
            def _():
                copy.wait_recv()

            if hop < PLANES - 1:

                @pl.when(inner & ahead)
                def _():
                    copy.start()

    for hop in (2, 3, 1):
        send_rows(hop)

    sent = []

    def send_chunk(source, index, where):
        copy = chunk_copy(source, index, 2 * PLANES + len(sent), where)
        copy.start()
        sent.append(copy)

    def take_chunk(index):
        chunk_copy(chunk_ref, index, 0, over).wait_recv()

    bits = list(range(plane.bit_length() - 1))[::-1]
    orders = [["tensor"] + bits, bits[:-1] + ["tensor"] + bits[-1:]]
    relayed = []
    for stage in range(len(bits) + 1):
        for hop in range(PLANES):
            order = orders[hop % 2]
            origin = layer(hop) * plane + inside
            where = flip(place, part, [order[stage]])
            for chosen in subsets(order[:stage]):
                at, side = flip(origin, part, chosen)
                index = 2 * at + side
                if hop == 0 and not chosen:
                    send_chunk(chunk_ref, index, where)
                    continue
                if stage > 0 and order[stage - 1] in chosen:
                    take_chunk(index)
                send_chunk(rows_of(index), index, where)
        if stage == 0:
            partner = (xor_bit(place, 0), part)
            for number, (ref, out) in enumerate(weights):
                direct[number].wait_recv()
                copy = weight_copy(out, out, 3 + number, core, partner)
                copy.start()
                relayed.append(copy)
    for hop in range(PLANES):
        order = orders[hop % 2]
        origin = layer(hop) * plane + inside
        for chosen in subsets(order):
            if order[-1] in chosen:
                at, side = flip(origin, part, chosen)
                take_chunk(2 * at + side)
    for number, (ref, out) in enumerate(weights):
        weight_copy(out, out, 3 + number, 1 - core, over).wait_recv()
    for copy in direct[len(weights) :]:
        copy.wait_recv()
    for _, source in rows_sent:
        pltpu.make_async_remote_copy(
            src_ref=rows_ref.at[source, part],
            dst_ref=got_ref.at[source],
            send_sem=tsend.at[0],
            recv_sem=trecv.at[source],
            device_id=(source, part),
            device_id_type=MESH,
        ).wait_recv()
    for copy, _ in rows_sent:
        copy.wait_send()
    for hop in range(PLANES - 1):
        for way in (1, -1):
            copy, inner, ahead = chain(hop, way)

            @pl.when(inner & ahead)
            def _():
                copy.wait_send()

    for copy in sent + direct + relayed:
        copy.wait_send()
    for copy in keep:
        copy.wait()


def front(rows, chunk, wq, wk, wv, bias, devices):
    _, _, piece, width = rows.shape
    anywhere = pl.BlockSpec(memory_space=pl.ANY)
    outs = [
        jax.ShapeDtypeStruct((devices, piece, width), BF16),
        jax.ShapeDtypeStruct((2 * devices * chunk.shape[0],) + chunk.shape[1:], BF16),
    ] + [jax.ShapeDtypeStruct(a.shape, BF16) for a in (wq, wk, wv, bias)]
    dma = pltpu.SemaphoreType.DMA
    return pl.pallas_call(
        functools.partial(front_kernel, devices),
        in_specs=[anywhere] * 6,
        out_specs=[anywhere] * 6,
        out_shape=outs,
        scratch_shapes=[
            dma((2,)),
            dma((devices,)),
            dma((devices,)),
            dma((2 * PLANES + 2 * devices,)),
            dma((2 * devices,)),
            dma((8,)),
            dma((8,)),
        ],
        compiler_params=pltpu.CompilerParams(collective_id=0, has_side_effects=True),
        cost_estimate=cost(0, 100e6),
        name="front",
    )(rows, chunk, wq, wk, wv, bias)


def in_order(part, mine, theirs, place):
    @pl.when(part == 0)
    def _():
        place(mine, theirs)

    @pl.when(part == 1)
    def _():
        place(theirs, mine)


def project_kernel(
    x_ref, meta_ref, turns_ref, sines_ref, gain_ref, mq_ref, mk_ref, mv_ref, mb_ref,
    tq_ref, tk_ref, tv_ref, tb_ref, flat_ref,
    n_ref, q_ref, kv_ref, z_ref, cos_ref, sin_ref, w_ref, other_ref, bias, held, ksend, krecv,
):
    place, part = lax.axis_index("dp"), lax.axis_index("tensor")
    here = pl.program_id(0)
    tiles = held.shape[0]
    width = x_ref.shape[1]
    qw, kw = q_ref.shape[1], kv_ref.shape[1] // 2

    def swap(number):
        return pltpu.make_async_remote_copy(
            src_ref=held.at[number],
            dst_ref=other_ref.at[number],
            send_sem=ksend.at[number],
            recv_sem=krecv.at[number],
            device_id=(place, 1 - part),
            device_id_type=MESH,
        )

    rank = flat_ref.shape[1]
    low = qw + 2 * kw
    a_rows, b_rows = [], []
    cursor = 0
    for size in (qw, kw, kw):
        a_rows.append(slice(cursor, cursor + width))
        b_rows.append(slice(cursor + width, cursor + width + size))
        cursor += width + size

    @pl.when(pl.program_id(0) == 0)
    def _():
        def fill(first, second):
            at, to = 0, 0
            for order, size in enumerate((qw // 2, kw // 2, kw // 2)):
                w_ref[to : to + size, :] = first[order][...]
                w_ref[to + size : to + 2 * size, :] = second[order][...]
                bias[:, to : to + 2 * size] = jnp.concatenate(
                    [
                        first[3][:8, at : at + size].astype(F32),
                        second[3][:8, at : at + size].astype(F32),
                    ],
                    axis=1,
                )
                at += size
                to += 2 * size

        barrier = pltpu.get_barrier_semaphore()
        pl.semaphore_signal(barrier, inc=1, device_id=(place, 1 - part), device_id_type=MESH)
        in_order(
            part, (mq_ref, mk_ref, mv_ref, mb_ref), (tq_ref, tk_ref, tv_ref, tb_ref), fill
        )
        for i, rows in enumerate(a_rows):
            turned = jnp.transpose(flat_ref[rows, :].astype(F32)).astype(BF16)
            w_ref[low + i * rank : low + (i + 1) * rank, :] = turned
        pl.semaphore_wait(barrier, 1)

    values = x_ref[...].astype(F32)
    normed = (values * rms(values) * gain_ref[...]).astype(BF16)
    n_ref[...] = normed
    base = nt(normed, w_ref[qw:, :])
    mask = rank_mask(meta_ref[:, 0:1], rank)
    lows = [
        (base[:, low - qw + i * rank : low - qw + (i + 1) * rank] * mask).astype(BF16)
        for i in range(3)
    ]
    for i in range(3):
        z_ref[:, i * rank : (i + 1) * rank] = lows[i]
    cos, sin = lane_table(turns_ref[...]), lane_table(sines_ref[...])
    cos_ref[...] = cos
    sin_ref[...] = sin
    keys = (
        base[:, :kw]
        + bias[0:1, qw : qw + kw]
        + ADAPTER_SCALE * nt(lows[1], flat_ref[b_rows[1], :])
    )
    vals = (
        base[:, kw : 2 * kw]
        + bias[0:1, qw + kw : low]
        + ADAPTER_SCALE * nt(lows[2], flat_ref[b_rows[2], :])
    )
    both = jnp.concatenate([keys * cos + turn(keys) * sin, vals], axis=1).astype(BF16)
    held[here] = both
    kv_ref[...] = both
    swap(here).start()
    queries = (
        nt(normed, w_ref[:qw, :])
        + bias[0:1, :qw]
        + ADAPTER_SCALE * nt(lows[0], flat_ref[b_rows[0], :])
    )
    for pair in range(qw // LANES):
        some = queries[:, pair * LANES : (pair + 1) * LANES]
        turned = (some * cos + turn(some) * sin) * HEAD**-0.5
        q_ref[:, pair * LANES : (pair + 1) * LANES] = turned.astype(BF16)

    @pl.when(here == tiles - 1)
    def _():
        for number in range(tiles):
            swap(number).wait_send()
        for number in range(tiles):
            swap(number).wait_recv()


def project(x, meta, turns, sines, gain, mine, theirs, flat, qw, kw):
    rows, width = x.shape
    rank = flat.shape[1]
    tile = ROW_TILE
    early = 3 * width + qw + 2 * kw
    columns = pl.BlockSpec((turns.shape[0], tile), lambda i, *_: (0, i))
    outs = [
        jax.ShapeDtypeStruct((rows, width), BF16),
        jax.ShapeDtypeStruct((rows, qw), BF16),
        jax.ShapeDtypeStruct((rows, 2 * kw), BF16),
        jax.ShapeDtypeStruct((rows, 3 * rank), BF16),
        jax.ShapeDtypeStruct((rows, LANES), F32),
        jax.ShapeDtypeStruct((rows, LANES), F32),
        jax.ShapeDtypeStruct((qw + 2 * kw + 3 * rank, width), BF16),
        jax.ShapeDtypeStruct((rows // tile, tile, 2 * kw), BF16),
    ]
    dma = pltpu.SemaphoreType.DMA
    return pl.pallas_call(
        project_kernel,
        grid=(rows // tile,),
        in_specs=[row_blocks(a, tile) for a in (x, meta)]
        + [columns, columns]
        + [whole(a) for a in (gain, *mine, *theirs)]
        + [pl.BlockSpec((early, rank), lambda i: (0, 0))],
        out_specs=[row_blocks(o, tile) for o in outs[:6]]
        + [whole(outs[6]), pl.BlockSpec(memory_space=pl.ANY)],
        out_shape=outs,
        scratch_shapes=[
            pltpu.VMEM((8, qw + 2 * kw), F32),
            pltpu.VMEM((rows // tile, tile, 2 * kw), BF16),
            dma((rows // tile,)),
            dma((rows // tile,)),
        ],
        compiler_params=params(collective_id=4, has_side_effects=True),
        cost_estimate=cost(2 * rows * width * 1600, 9e6),
        name="project",
    )(x, meta, turns, sines, gain, *mine, *theirs, flat)


def head_groups(heads, kv_heads):
    width = heads // kv_heads
    groups = {}
    for head in range(heads):
        groups.setdefault((head // width, head % 2), []).append(head)
    return [(kv, half, members) for (kv, half), members in sorted(groups.items())]


def spread_heads(tile_f32, kv, half, ones=False):
    lanes = lane_iota(tile_f32.shape)
    moved = tile_f32 if kv % 2 == half else pltpu.roll(tile_f32, HEAD, 1)
    keep = (lanes >= HEAD) if half else (lanes < HEAD)
    rest = jnp.where(lanes == (0 if half else HEAD), 1.0, 0.0) if ones else 0.0
    return jnp.where(keep, moved, rest)


def stack_heads(groups, source, target):
    rows = source.shape[0]
    at = 0
    for _, _, members in groups:
        for head in members:
            pair = slice((head // 2) * LANES, (head // 2 + 1) * LANES)
            target[at : at + rows, :] = source[:, pair]
            at += rows


def attend_kernel(
    heads, kv_heads, bounds_ref, all_ref, meta_ref, metar_ref, place_ref, own_ref, other_ref,
    column_ref,
    q_ref, o_ref, log_ref, merged_ref, slot_ref, keys, values, acc, top, held, stack, scores,
):
    step = pl.program_id(0)
    groups = head_groups(heads, kv_heads)
    rows = q_ref.shape[0]
    q_ref[...] = nn(pick_rows(meta_ref[:, 0:1], all_ref.shape[0]), all_ref[...]).astype(BF16)
    stack_heads(groups, q_ref, stack)

    @pl.when(step == 0)
    def _():
        both = jnp.concatenate([own_ref[...], other_ref[...]], axis=0)
        for start in range(0, keys.shape[1], KEY_TILE):
            span = slice(start, start + KEY_TILE)
            part = nn(pick_rows(column_ref[span, 0:1], both.shape[0]), both)
            merged_ref[span, :] = part.astype(BF16)
            for number, (kv, half, _) in enumerate(groups):
                keys[number, span, :] = spread_heads(part[:, :LANES], kv, half).astype(BF16)
                turned = jnp.transpose(spread_heads(part[:, LANES:], kv, half, True))
                values[number, :, span] = turned.astype(BF16)

    acc[...] = jnp.zeros_like(acc)
    top[...] = jnp.full_like(top, MASKED_SCORE)
    first, last = metar_ref[1:2, :], metar_ref[2:3, :]
    cuts = []
    at = 0
    for _, _, members in groups:
        cuts.append(slice(at * rows, (at + len(members)) * rows))
        at += len(members)

    def find_top(number, carry):
        start = pl.multiple_of(number * KEY_TILE, KEY_TILE)
        span = pl.ds(start, KEY_TILE)
        index = start + row_iota((KEY_TILE, rows))
        bias = jnp.where((index >= first) & (index <= last), 0.0, MASKED_SCORE)
        for group, cut in enumerate(cuts):
            count = (cut.stop - cut.start) // rows
            part = nt(keys[group, span, :], stack[cut, :])
            part = part + jnp.concatenate([bias] * count, axis=1)
            scores[span, cut] = part
            most = jnp.max(part.reshape(KEY_TILE // 8, 8, -1), axis=0)
            top[:, cut] = jnp.maximum(top[:, cut], most)
        return carry

    def weigh(number, carry):
        start = pl.multiple_of(number * KEY_TILE, KEY_TILE)
        span = pl.ds(start, KEY_TILE)
        for group, cut in enumerate(cuts):
            weights = jnp.exp(scores[span, cut] - top[0:1, cut]).astype(BF16)
            acc[:, cut] += nn(values[group, :, span], weights)
        return carry

    lax.fori_loop(bounds_ref[0, step], bounds_ref[1, step], find_top, 0)
    top[0:1, :] = jnp.max(top[...], axis=0, keepdims=True)
    lax.fori_loop(bounds_ref[0, step], bounds_ref[1, step], weigh, 0)
    parts = {}
    at = 0
    for _, half, members in groups:
        for head in members:
            cut = slice(at * rows, (at + 1) * rows)
            at += 1
            block = acc[:, cut]
            sums = block[0:1, :] if half else block[HEAD : HEAD + 1, :]
            log_ref[head : head + 1, :] = top[0:1, cut] + jnp.log(sums)
            parts[head] = block / sums
    low = row_iota((LANES, rows)) < HEAD
    for pair in range(heads // 2):
        both = jnp.where(low, parts[2 * pair], parts[2 * pair + 1])
        o_ref[:, pair * LANES : (pair + 1) * LANES] = jnp.transpose(both).astype(BF16)
    for head in range(heads, log_ref.shape[0]):
        log_ref[head : head + 1, :] = jnp.zeros((1, rows), F32)
    held[pl.ds(pl.multiple_of(step * rows, rows), rows), :] = o_ref[...]

    @pl.when(step == pl.num_programs(0) - 1)
    def _():
        slot_ref[...] = nn(place_rows(place_ref[0:1, :], held.shape[0]), held[...]).astype(BF16)


def attend(bounds, q, meta, meta_rows, own_kv, other_kv, column, heads, kv_heads):
    rows, qw = q.shape
    tile = QUERY_TILE
    keys = 2 * rows
    groups = len(head_groups(heads, kv_heads))
    outs = [
        jax.ShapeDtypeStruct((rows, qw), BF16),
        jax.ShapeDtypeStruct((rows, qw), BF16),
        jax.ShapeDtypeStruct((16, rows), F32),
        jax.ShapeDtypeStruct((keys, own_kv.shape[1]), BF16),
        jax.ShapeDtypeStruct((rows, qw), BF16),
    ]
    return pl.pallas_call(
        functools.partial(attend_kernel, heads, kv_heads),
        grid_spec=pltpu.PrefetchScalarGridSpec(
            num_scalar_prefetch=1,
            grid=(rows // tile,),
            in_specs=[
                whole(q),
                row_blocks(meta, tile),
                pl.BlockSpec((8, tile), lambda i, *_: (0, i)),
                whole(meta_rows),
                whole(own_kv),
                whole(other_kv),
                whole(column),
            ],
            out_specs=[
                row_blocks(outs[0], tile),
                row_blocks(outs[1], tile),
                pl.BlockSpec((16, tile), lambda i, *_: (0, i)),
                whole(outs[3]),
                whole(outs[4]),
            ],
            scratch_shapes=[
                pltpu.VMEM((groups, keys, LANES), BF16),
                pltpu.VMEM((groups, LANES, keys), BF16),
                pltpu.VMEM((LANES, heads * tile), F32),
                pltpu.VMEM((8, heads * tile), F32),
                pltpu.VMEM((rows, qw), BF16),
                pltpu.VMEM((heads * tile, LANES), BF16),
                pltpu.VMEM((keys, heads * tile), F32),
            ],
        ),
        out_shape=outs,
        compiler_params=params(),
        cost_estimate=cost(heads * rows * keys * 2000, 6e6),
        name="attend",
    )(bounds, q, meta, meta_rows, meta_rows, own_kv, other_kv, column)


def attend_back_kernel(
    heads, kv_heads, bounds_ref, q_ref, all_ref, o_ref, log_ref, meta_ref, metar_ref, cos_ref,
    sin_ref, merged_ref, column_ref, place_ref,
    gq_ref, own_ref, other_ref, keys, values, dkeys, dvalues, dq, dots, g_ref, held, stack, grads,
):
    step = pl.program_id(0)
    groups = head_groups(heads, kv_heads)
    rows = q_ref.shape[0]
    g_ref[...] = nn(pick_rows(meta_ref[:, 0:1], all_ref.shape[0]), all_ref[...]).astype(BF16)

    @pl.when(step == 0)
    def _():
        for start in range(0, keys.shape[1], KEY_TILE):
            span = slice(start, start + KEY_TILE)
            part = merged_ref[span, :].astype(F32)
            for number, (kv, half, _) in enumerate(groups):
                keys[number, span, :] = spread_heads(part[:, :LANES], kv, half).astype(BF16)
                values[number, span, :] = spread_heads(part[:, LANES:], kv, half).astype(BF16)
        dkeys[...] = jnp.zeros_like(dkeys)
        dvalues[...] = jnp.zeros_like(dvalues)

    stack_heads(groups, q_ref, stack)
    stack_heads(groups, g_ref, grads)
    dq[...] = jnp.zeros_like(dq)
    for pair in range(heads // 2):
        lanes = slice(pair * LANES, (pair + 1) * LANES)
        product = jnp.transpose(g_ref[:, lanes].astype(F32) * o_ref[:, lanes].astype(F32))
        dots[2 * pair : 2 * pair + 1, :] = jnp.sum(product[:HEAD], axis=0, keepdims=True)
        dots[2 * pair + 1 : 2 * pair + 2, :] = jnp.sum(product[HEAD:], axis=0, keepdims=True)
    first, last = metar_ref[1:2, :], metar_ref[2:3, :]

    def one_tile(number, carry):
        start = pl.multiple_of(number * KEY_TILE, KEY_TILE)
        index = start + row_iota((KEY_TILE, rows))
        bias = jnp.where((index >= first) & (index <= last), 0.0, MASKED_SCORE)
        span = pl.ds(start, KEY_TILE)
        begin = 0
        for group, (_, half, members) in enumerate(groups):
            count = len(members)
            cut = slice(begin * rows, (begin + count) * rows)
            begin += count
            logs = jnp.concatenate([log_ref[h : h + 1, :] for h in members], axis=1)
            drop = jnp.concatenate([dots[h : h + 1, :] for h in members], axis=1)
            key_part = keys[group, span, :]
            scores = nt(key_part, stack[cut, :]) + jnp.concatenate([bias] * count, axis=1)
            weights = jnp.exp(scores - logs)
            change = nt(values[group, span, :], grads[cut, :])
            dscores = (weights * (change - drop)).astype(BF16)
            dvalues[group, span, :] += nn(weights.astype(BF16), grads[cut, :])
            dkeys[group, span, :] += nn(dscores, stack[cut, :])
            back = tn(dscores, key_part)
            for at, head in enumerate(members):
                dq[head // 2, :, :] += back[at * rows : (at + 1) * rows, :]
        return carry

    lax.fori_loop(bounds_ref[0, step], bounds_ref[1, step], one_tile, 0)
    cos, sin = lane_table(cos_ref[...]), lane_table(sin_ref[...])
    for pair in range(heads // 2):
        grad = dq[pair, :, :] * HEAD**-0.5
        grad = grad * cos - turn(grad) * sin
        held[
            pl.ds(pl.multiple_of(step * rows, rows), rows), pair * LANES : (pair + 1) * LANES
        ] = grad.astype(BF16)

    @pl.when(step == pl.num_programs(0) - 1)
    def _():
        gq_ref[...] = nn(place_rows(place_ref[0:1, :], held.shape[0]), held[...]).astype(BF16)
        total = dkeys.shape[1]

        def join(ref):
            out = None
            for group, (kv, half, _) in enumerate(groups):
                part = ref[group, :, :]
                lanes = lane_iota(part.shape)
                part = jnp.where((lanes >= HEAD) if half else (lanes < HEAD), part, 0.0)
                if kv % 2 != half:
                    part = pltpu.roll(part, HEAD, 1)
                out = part if out is None else out + part
            return out.astype(BF16)

        both = jnp.concatenate([join(dkeys), join(dvalues)], axis=1)
        half_rows = own_ref.shape[0]
        for at in range(0, total, KEY_TILE):
            hit = (at + row_iota((KEY_TILE, total))) == column_ref[0:1, :]
            part = nn(jnp.where(hit, 1.0, 0.0).astype(BF16), both).astype(BF16)
            if at < half_rows:
                own_ref[at : at + KEY_TILE, :] = part
            else:
                other_ref[at - half_rows : at - half_rows + KEY_TILE, :] = part


def attend_back(
    bounds, q, grad, o, logs, meta, meta_rows, cos, sin, merged, column_row, heads, kv_heads
):
    rows, qw = q.shape
    tile = QUERY_TILE
    keys, kvw = merged.shape
    groups = len(head_groups(heads, kv_heads))
    outs = [
        jax.ShapeDtypeStruct((rows, qw), BF16),
        jax.ShapeDtypeStruct((rows, kvw), BF16),
        jax.ShapeDtypeStruct((rows, kvw), BF16),
    ]
    return pl.pallas_call(
        functools.partial(attend_back_kernel, heads, kv_heads),
        grid_spec=pltpu.PrefetchScalarGridSpec(
            num_scalar_prefetch=1,
            grid=(rows // tile,),
            in_specs=[
                row_blocks(q, tile),
                whole(grad),
                row_blocks(o, tile),
                pl.BlockSpec((16, tile), lambda i, *_: (0, i)),
                row_blocks(meta, tile),
                pl.BlockSpec((8, tile), lambda i, *_: (0, i)),
                pl.BlockSpec((cos.shape[0], tile), lambda i, *_: (0, rows // tile + i)),
                pl.BlockSpec((cos.shape[0], tile), lambda i, *_: (0, rows // tile + i)),
                whole(merged),
                whole(column_row),
                whole(meta_rows),
            ],
            out_specs=[whole(o) for o in outs],
            scratch_shapes=[
                pltpu.VMEM((groups, keys, LANES), BF16),
                pltpu.VMEM((groups, keys, LANES), BF16),
                pltpu.VMEM((groups, keys, LANES), F32),
                pltpu.VMEM((groups, keys, LANES), F32),
                pltpu.VMEM((heads // 2, tile, LANES), F32),
                pltpu.VMEM((16, tile), F32),
                pltpu.VMEM((tile, qw), BF16),
                pltpu.VMEM((rows, qw), BF16),
                pltpu.VMEM((heads * tile, LANES), BF16),
                pltpu.VMEM((heads * tile, LANES), BF16),
            ],
        ),
        out_shape=outs,
        compiler_params=params(),
        cost_estimate=cost(heads * rows * keys * 3000, 9e6),
        name="attend_back",
    )(bounds, q, grad, o, logs, meta, meta_rows, cos, sin, merged, column_row, meta_rows)


def middle_kernel(
    part_ref, o_ref, x_ref, meta_ref, mine_ref, theirs_ref, gain_ref, flat_ref,
    y_ref, n_ref, z_ref, w_ref,
):
    width = x_ref.shape[1]
    rank = flat_ref.shape[1]
    half = mine_ref.shape[0]

    @pl.when(pl.program_id(0) == 0)
    def _():
        def fill(first, second):
            w_ref[:half, :width] = first[...]
            w_ref[half:, :width] = second[...]

        in_order(part_ref[0], mine_ref, theirs_ref, fill)
        w_ref[:, width:] = flat_ref[: 2 * half, :]

    mask = rank_mask(meta_ref[:, 0:1], rank)
    base = nn(o_ref[...], w_ref[...])
    low = (base[:, width:] * mask).astype(BF16)
    z_ref[...] = low
    values = x_ref[...].astype(F32) + (base[:, :width] + ADAPTER_SCALE * nt(low, flat_ref[2 * half :, :]))
    y_ref[...] = values
    n_ref[...] = (values * rms(values) * gain_ref[...]).astype(BF16)


def middle(part, o, x, meta, mine, theirs, gain, flat, start):
    rows, width = x.shape
    rank = flat.shape[1]
    tile = ROW_TILE
    rest = (mine, theirs, gain)
    outs = [
        jax.ShapeDtypeStruct((rows, width), F32),
        jax.ShapeDtypeStruct((rows, width), BF16),
        jax.ShapeDtypeStruct((rows, rank), BF16),
        jax.ShapeDtypeStruct((o.shape[1], width + rank), BF16),
    ]
    return pl.pallas_call(
        middle_kernel,
        grid_spec=pltpu.PrefetchScalarGridSpec(
            num_scalar_prefetch=1,
            grid=(rows // tile,),
            in_specs=[row_blocks(a, tile) for a in (o, x, meta)]
            + [whole(a) for a in rest]
            + [rows_from(flat, start, o.shape[1] + width)],
            out_specs=[row_blocks(a, tile) for a in outs[:3]] + [whole(outs[3])],
        ),
        out_shape=outs,
        compiler_params=params(),
        cost_estimate=cost(2 * rows * width * 1100, 12e6),
        name="middle",
    )(part, o, x, meta, *rest, flat)


class Windows:
    def __init__(self, devices, own_rows):
        self.devices = devices
        self.own_rows = own_rows
        self.plane = devices // PLANES
        self.axes = list(range(self.plane.bit_length() - 1)) + ["tensor"]
        self.rows = 16 * ((own_rows + 30) // 16)
        self.last = 16 * (((2 * devices - 1) * own_rows) // 16) + self.rows

    def start(self, zz, at, side):
        row = (2 * (zz * self.plane + at) + side) * self.own_rows
        return pl.multiple_of((row // 16) * 16, 16)

    def span(self, zz, at, side):
        return pl.ds(self.start(zz, at, side), self.rows)

    def boxes(self, stage):
        return 2 ** (len(self.axes) - 1 - stage)

    def box(self, stage, at, side):
        index = 0
        for order, axis in enumerate(self.axes[stage + 1 :]):
            bit = side if axis == "tensor" else lax.rem(at // 2**axis, 2)
            index = index + bit * 2**order
        return index

    def leaving(self, stage, inside, part):
        for chosen in subsets(self.axes[stage + 1 :]):
            yield flip(inside, part, [self.axes[stage]] + list(chosen))

    def staying(self, stage, inside, part):
        for chosen in subsets(self.axes[stage + 1 :]):
            yield flip(inside, part, list(chosen))


def middle_back_kernel(
    plan, first_b, da_ref, db_ref, y1_ref, dy_ref, o_ref, z_ref, meta_ref, copies_ref, w_ref,
    gain_ref, flat_ref,
    dy1_ref, dar_ref, grad_ref, on_ref, kept_ref, acc_bo, acc_ao, mine, inbox, b_ref, msem, ssem,
    rsem, bsem,
):
    step = pl.program_id(0)
    b_load = pltpu.make_async_copy(
        copies_ref.at[pl.ds(first_b, b_ref.shape[0]), :], b_ref, bsem.at[0]
    )
    rank = b_ref.shape[1]
    qw = o_ref.shape[1]
    place, part = lax.axis_index("dp"), lax.axis_index("tensor")
    inside = lax.rem(place, plan.plane)
    partner = flip(place, part, [plan.axes[0]])
    boxes = plan.boxes(0)

    def moves():
        local, remote = [], []
        for zz in range(1, PLANES):
            for at, side in plan.leaving(0, inside, part):
                index = (zz - 1) * boxes + plan.box(0, at, side)
                remote.append(
                    pltpu.make_async_remote_copy(
                        src_ref=flat_ref.at[plan.span(zz, at, side), :],
                        dst_ref=inbox.at[index],
                        send_sem=ssem.at[len(remote)],
                        recv_sem=rsem.at[index],
                        device_id=partner,
                        device_id_type=MESH,
                    )
                )
            for at, side in plan.staying(0, inside, part):
                index = (zz - 1) * boxes + plan.box(0, at, side)
                local.append(
                    pltpu.make_async_copy(
                        flat_ref.at[plan.span(zz, at, side), :], mine.at[index], msem.at[len(local)]
                    )
                )
        return local, remote

    @pl.when(step == 0)
    def _():
        acc_bo[...] = jnp.zeros_like(acc_bo)
        acc_ao[...] = jnp.zeros_like(acc_ao)
        b_load.start()
        barrier = pltpu.get_barrier_semaphore()
        pl.semaphore_signal(barrier, inc=1, device_id=partner, device_id_type=MESH)
        pl.semaphore_wait(barrier, 1)
        local, remote = moves()
        for copy in remote + local:
            copy.start()
        b_load.wait()

    mask = rank_mask(meta_ref[:, 0:1], rank)
    grad = da_ref[...] + db_ref[...].astype(F32)
    dy1 = dy_ref[...].astype(F32) + norm_back(y1_ref[...], gain_ref[...], grad)
    dy1_ref[...] = dy1
    low_grad = dy1.astype(BF16)
    back_out = (ADAPTER_SCALE * nn(low_grad, b_ref[...]) * mask).astype(BF16)
    both = jnp.concatenate([low_grad, back_out], axis=1)
    dar_ref[...] = nt(both, w_ref[...]).astype(BF16)
    acc_bo[...] += ADAPTER_SCALE * tn(low_grad, z_ref[...])
    acc_ao[...] += tn(o_ref[...], back_out)

    @pl.when(step == pl.num_programs(0) - 1)
    def _():
        grad_ref[:qw, :] = acc_ao[...].astype(BF16)
        grad_ref[qw:, :] = acc_bo[...].astype(BF16)
        local, remote = moves()
        for copy in local:
            copy.wait()
        for copy in remote:
            copy.wait_recv()
        def total(zz, at, side):
            index = (zz - 1) * boxes + plan.box(0, at, side)
            return mine[index].astype(F32) + inbox[index].astype(F32)

        for zz in range(1, PLANES):
            for peer, chosen in enumerate(subsets(plan.axes[1:])):
                at, side = flip(inside, part, chosen)
                if peer == 0:
                    kept_ref[zz - 1] = total(zz, at, side)
                else:
                    on_ref[peer - 1, zz - 1] = total(zz, at, side).astype(BF16)
        for copy in remote:
            copy.wait_send()


def middle_back(
    devices, own_rows, d_first, d_second, y1, dy, o, z, meta, copies, start, w_out, gain, flat
):
    rows, width = y1.shape
    rank = copies.shape[1]
    qw = o.shape[1]
    tile = ROW_TILE
    plan = Windows(devices, own_rows)
    first = (PLANES - 1) * plan.boxes(0)
    outs = [
        jax.ShapeDtypeStruct((rows, width), F32),
        jax.ShapeDtypeStruct((rows, qw), BF16),
        jax.ShapeDtypeStruct((qw + width, rank), BF16),
        jax.ShapeDtypeStruct((plan.boxes(0) - 1, PLANES - 1, plan.rows, rank), BF16),
        jax.ShapeDtypeStruct((PLANES - 1, plan.rows, rank), F32),
    ]
    return pl.pallas_call(
        functools.partial(middle_back_kernel, plan, start),
        grid=(rows // tile,),
        in_specs=[row_blocks(a, tile) for a in (d_first, d_second, y1, dy, o, z, meta)]
        + [pl.BlockSpec(memory_space=pl.ANY)]
        + [whole(a) for a in (w_out, gain)]
        + [pl.BlockSpec(memory_space=pl.ANY)],
        out_specs=[row_blocks(a, tile) for a in outs[:2]] + [whole(a) for a in outs[2:]],
        out_shape=outs,
        scratch_shapes=[
            pltpu.VMEM((width, rank), F32),
            pltpu.VMEM((qw, rank), F32),
            pltpu.VMEM((first, plan.rows, rank), BF16),
            pltpu.VMEM((first, plan.rows, rank), BF16),
            pltpu.VMEM((width, rank), BF16),
            pltpu.SemaphoreType.DMA((first,)),
            pltpu.SemaphoreType.DMA((first,)),
            pltpu.SemaphoreType.DMA((first,)),
            pltpu.SemaphoreType.DMA((1,)),
        ],
        compiler_params=params(collective_id=3, has_side_effects=True),
        cost_estimate=cost(2 * rows * width * 1500, 20e6),
        name="middle_back",
    )(d_first, d_second, y1, dy, o, z, meta, copies, w_out, gain, flat)


def own_tile(step, tiles):
    return jnp.maximum(step - tiles, 0)


def their_tile(step, tiles):
    return jnp.clip(step - 1, 0, tiles - 1)


def feed_kernel(
    n_ref, n_hbm, dy_ref, dyt_ref, meta_ref, metat_ref, wg_hbm, wu_hbm,
    wd_hbm, copies,
    y_ref, d_ref, y_got, d_got, last_ref, flat_ref,
    wga, wua, wda, raw, grads, extras, xg, xu, dya, yacc, dacc, mask_s, n_got, held_d, held_y,
    packed, blank, ap_ref, bd_ref, wsem, gsem, nsend, nrecv, dsend, drecv, ysend, yrecv,
):
    step = pl.program_id(0)
    steps = pl.num_programs(0)
    tiles_each = n_got.shape[0]
    width, half = wg_hbm.shape
    rank = bd_ref.shape[1]
    rows = n_ref.shape[0]
    place, part = lax.axis_index("dp"), lax.axis_index("tensor")
    theirs = (step >= 1) & (step <= tiles_each)
    number_t = their_tile(step, tiles_each)
    tile = HIDDEN_TILE
    tiles = pl.cdiv(half, tile)
    lap = tiles * tile - half
    a_gate = copies.shape[0] - 3 * width - 6 * half
    a_up = a_gate + width + 2 * half
    a_down = a_up + width + 2 * half
    b_down = a_down + 2 * half

    def loads(number):
        at = pl.multiple_of(jnp.minimum(number * tile, half - tile), LANES)
        to = pl.multiple_of(number * tile, tile)
        here, there = pl.ds(at, tile), pl.ds(to, tile)

        def own_half(base):
            return copies.at[pl.ds(pl.multiple_of(base + part * half + at, 16), tile), :]

        top, side = pl.ds(0, width), pl.ds(width, rank)
        pairs = [
            (wg_hbm.at[:, here], wga.at[top, there]),
            (wu_hbm.at[:, here], wua.at[top, there]),
            (wd_hbm.at[here, :], wda.at[there, top]),
            (own_half(a_gate + width), raw.at[0, there, :]),
            (own_half(a_up + width), raw.at[1, there, :]),
            (own_half(a_down), wda.at[there, side]),
        ]
        return [
            pltpu.make_async_copy(source, target, wsem.at[number, at])
            for at, (source, target) in enumerate(pairs)
        ]

    def swap(source, target, sends, recvs, number):
        return pltpu.make_async_remote_copy(
            src_ref=source,
            dst_ref=target.at[number],
            send_sem=sends.at[number],
            recv_sem=recvs.at[number],
            device_id=(place, 1 - part),
            device_id_type=MESH,
        )

    def send_n(number):
        return swap(n_hbm.at[pl.ds(number * rows, rows), :], n_got, nsend, nrecv, number)

    def send_d(number):
        return swap(held_d.at[number], d_got, dsend, drecv, number)

    def send_y(number):
        return swap(held_y.at[number], y_got, ysend, yrecv, number)

    thin_loads = [
        pltpu.make_async_copy(copies.at[pl.ds(base, width), :], target, gsem.at[at])
        for at, (base, target) in enumerate(
            (
                (a_gate, ap_ref.at[:, pl.ds(0, rank)]),
                (a_up, ap_ref.at[:, pl.ds(rank, rank)]),
                (b_down, bd_ref),
            )
        )
    ]

    @pl.when(step == 0)
    def _():
        for copy in thin_loads:
            copy.start()
        for number in range(tiles):
            for copy in loads(number):
                copy.start()
        barrier = pltpu.get_barrier_semaphore()
        pl.semaphore_signal(barrier, inc=1, device_id=(place, 1 - part), device_id_type=MESH)
        pl.semaphore_wait(barrier, 1)
        for number in range(tiles_each):
            send_n(number).start()
        grads[...] = jnp.zeros_like(grads)
        extras[...] = jnp.zeros_like(extras)
        for copy in thin_loads:
            copy.wait()

    def prepare(normed, dy, adapter):
        mask = rank_mask(adapter, rank)
        mask_s[...] = mask
        lows = nn(normed, ap_ref[...])
        xg[:, :width] = normed
        xu[:, :width] = normed
        xg[:, width:] = (lows[:, :rank] * mask).astype(BF16)
        xu[:, width:] = (lows[:, rank:] * mask).astype(BF16)
        dya[:, :width] = dy
        dya[:, width:] = (ADAPTER_SCALE * nn(dy, bd_ref[...]) * mask).astype(BF16)

    @pl.when(jnp.logical_not(theirs))
    def _():
        prepare(n_ref[...], dy_ref[...], meta_ref[:, 0:1])

    @pl.when(theirs)
    def _():
        send_n(number_t).wait_recv()
        prepare(n_got[number_t], dyt_ref[...], metat_ref[:, 0:1])

    yacc[...] = jnp.zeros_like(yacc)
    dacc[...] = jnp.zeros_like(dacc)

    def hidden(number, carry):
        span = pl.ds(pl.multiple_of(number * tile, tile), tile)

        @pl.when(step == 0)
        def _():
            for copy in loads(number):
                copy.wait()
            for at, target in enumerate((wga, wua)):
                turned = jnp.transpose(raw[at, span, :].astype(F32) * ADAPTER_SCALE)
                target[width:, span] = turned.astype(BF16)
            if lap:

                @pl.when(number == tiles - 1)
                def _():
                    edge = slice((tiles - 1) * tile, (tiles - 1) * tile + lap)
                    wga[:, edge] = jnp.zeros((width + rank, lap), BF16)
                    wua[:, edge] = jnp.zeros((width + rank, lap), BF16)
                    wda[edge, :] = jnp.zeros((lap, width + rank), BF16)

        gate = nn(xg[...], wga[:, span])
        up = nn(xu[...], wua[:, span])
        dhid = nt(dya[...], wda[span, :])
        sig = 1.0 / (1.0 + jnp.exp(-gate))
        silu = gate * sig
        hid = (silu * up).astype(BF16)
        dg = (dhid * up * (sig * (1.0 + gate * (1.0 - sig)))).astype(BF16)
        du = (dhid * silu).astype(BF16)
        yacc[...] += nn(hid, wda[span, :])
        dga = nt(dg, wga[:, span])
        dua = nt(du, wua[:, span])
        dacc[:, :width] += dga[:, :width] + dua[:, :width]
        dacc[:, width : width + rank] += dga[:, width:]
        dacc[:, width + rank :] += dua[:, width:]
        grads[0, span, :] += ADAPTER_SCALE * tn(dg, xg[:, width:])
        grads[1, span, :] += ADAPTER_SCALE * tn(du, xu[:, width:])
        grads[2, span, :] += tn(hid, dya[:, width:])
        return carry

    lax.fori_loop(0, tiles, hidden, 0)
    mask = mask_s[...]
    low = (yacc[:, width:] * mask).astype(BF16)
    result = yacc[:, :width] + ADAPTER_SCALE * nt(low, bd_ref[...])
    back = (dacc[:, width:] * jnp.concatenate([mask, mask], axis=1)).astype(BF16)
    change = dacc[:, :width] + nt(back, ap_ref[...])
    pair = tn(xg[:, :width], back)
    extras[0] += pair[:, :rank]
    extras[1] += pair[:, rank:]
    extras[2] += ADAPTER_SCALE * tn(dya[:, :width], low)

    @pl.when(jnp.logical_not(theirs))
    def _():
        y_ref[...] = result
        d_ref[...] = change

    @pl.when(theirs)
    def _():
        held_d[number_t] = change.astype(BF16)
        send_d(number_t).start()

        @pl.when(number_t < tiles_each - 1)
        def _():
            held_y[number_t] = result.astype(BF16)

        @pl.when(number_t == tiles_each - 1)
        def _():
            last_ref[...] = result.astype(BF16)
            for number in range(tiles_each - 1):
                send_y(number).start()

    @pl.when(step == steps - 1)
    def _():
        last = (tiles - 1) * tile
        for at in range(3):
            packed[at, :last, :] = grads[at, :last, :].astype(BF16)
            packed[at, last:half, :] = grads[at, last + lap : tiles * tile, :].astype(BF16)
            packed[at, half:, :] = extras[at].astype(BF16)
        blank[...] = jnp.zeros_like(blank)
        moves = []
        for at, base in enumerate((a_gate + width, a_up + width, a_down)):
            mine = pl.multiple_of(base + part * half, 16)
            other = pl.multiple_of(base + (1 - part) * half, 16)
            moves.append((packed.at[at, pl.ds(0, half), :], flat_ref.at[pl.ds(mine, half), :]))
            moves.append((blank, flat_ref.at[pl.ds(other, half), :]))
        for at, base in enumerate((a_gate, a_up, b_down)):
            moves.append((packed.at[at, pl.ds(half, width), :], flat_ref.at[pl.ds(base, width), :]))
        moves = [
            pltpu.make_async_copy(source, target, gsem.at[at])
            for at, (source, target) in enumerate(moves)
        ]
        for copy in moves:
            copy.start()
        for copy in moves:
            copy.wait()
        for number in range(tiles_each):
            send_n(number).wait_send()
            send_d(number).wait_send()
            send_d(number).wait_recv()
        for number in range(tiles_each - 1):
            send_y(number).wait_send()
            send_y(number).wait_recv()


def feed(n2, dy, dy_theirs, meta, meta_theirs, w_gate, w_up, w_down, copies):
    rows, width = n2.shape
    half = w_down.shape[0]
    total, rank = copies.shape
    tile = ROW_TILE
    count = rows // tile
    tiles = pl.cdiv(half, HIDDEN_TILE)
    padded = tiles * HIDDEN_TILE
    anywhere = pl.BlockSpec(memory_space=pl.ANY)
    wide, deep = width + rank, width + 2 * rank

    def own_rows(array):
        return pl.BlockSpec((tile, array.shape[1]), lambda i: (own_tile(i, count), 0))

    def their_rows(array):
        return pl.BlockSpec((tile, array.shape[1]), lambda i: (their_tile(i, count), 0))

    dma = pltpu.SemaphoreType.DMA
    outs = [
        jax.ShapeDtypeStruct((rows, width), F32),
        jax.ShapeDtypeStruct((rows, width), F32),
        jax.ShapeDtypeStruct((count - 1, tile, width), BF16),
        jax.ShapeDtypeStruct((count, tile, width), BF16),
        jax.ShapeDtypeStruct((tile, width), BF16),
        jax.ShapeDtypeStruct((total + FLAT_PAD, rank), BF16),
    ]
    return pl.pallas_call(
        feed_kernel,
        grid=(2 * count,),
        in_specs=[
            own_rows(n2), anywhere, own_rows(dy), their_rows(dy_theirs), own_rows(meta),
            their_rows(meta_theirs),
        ]
        + [anywhere] * 4,
        out_specs=[own_rows(outs[0]), own_rows(outs[1]), anywhere, anywhere, whole(outs[4]), anywhere],
        out_shape=outs,
        scratch_shapes=[
            pltpu.VMEM((wide, padded), BF16),
            pltpu.VMEM((wide, padded), BF16),
            pltpu.VMEM((padded, wide), BF16),
            pltpu.VMEM((2, padded, rank), BF16),
            pltpu.VMEM((3, padded, rank), F32),
            pltpu.VMEM((3, width, rank), F32),
            pltpu.VMEM((tile, wide), BF16),
            pltpu.VMEM((tile, wide), BF16),
            pltpu.VMEM((tile, wide), BF16),
            pltpu.VMEM((tile, wide), F32),
            pltpu.VMEM((tile, deep), F32),
            pltpu.VMEM((tile, rank), F32),
            pltpu.VMEM((count, tile, width), BF16),
            pltpu.VMEM((count, tile, width), BF16),
            pltpu.VMEM((count - 1, tile, width), BF16),
            pltpu.VMEM((3, half + width, rank), BF16),
            pltpu.VMEM((half, rank), BF16),
            pltpu.VMEM((width, 2 * rank), BF16),
            pltpu.VMEM((width, rank), BF16),
            dma((tiles, 6)),
            dma((9,)),
            dma((count,)),
            dma((count,)),
            dma((count,)),
            dma((count,)),
            dma((count - 1,)),
            dma((count - 1,)),
        ],
        compiler_params=params(collective_id=1, has_side_effects=True),
        cost_estimate=cost(4 * rows * half * (6 * width + 9 * rank), 40e6),
        name="feed",
    )(
        n2, n2, dy, dy_theirs, meta, meta_theirs, w_gate, w_up, w_down, copies
    )


def tail_kernel(plan, early, key_width, direct, *refs):
    sources = refs[:9]
    other_ref, w_hbm, b_ref, gain_ref, flat_ref, out_grad_ref, kept_hbm = refs[9:16]
    peers = plan.boxes(0) - 1
    gots_hbm = refs[16 : 16 + peers]
    refs = refs[16 + peers :]
    out_ref, sum_ref = refs[:2]
    held = refs[2:11]
    w, grads, dxs, acc_a, acc_b, outbox, last_in, got_s, kept, gots, *rest = refs[11:]
    inboxes = rest[:-13]
    (
        load_sem, grad_sem, dsend, drecv, fsend, frecv, rsend, rrecv, zrecv, keep_sem, ksend, krecv,
        hsem,
    ) = rest[-13:]
    gq_s, own_s, x_s, n_s, z_s, dy1_s, meta_s, cos_s, sin_s = held
    place, part = lax.axis_index("dp"), lax.axis_index("tensor")
    devices, plane, axes = plan.devices, plan.plane, plan.axes
    depth, inside = place // plane, lax.rem(place, plane)
    count = len(axes)
    tile = x_s.shape[1]
    rank = b_ref.shape[1]
    width = x_s.shape[2]
    qw, kw = gq_s.shape[2], key_width
    over = (place, 1 - part)

    def layer(hop):
        return lax.rem(depth + hop, PLANES)

    def turn_of(number):
        return lax.rem(number + 2, PLANES)

    def rows_at(number):
        return pl.ds(pl.multiple_of(layer(turn_of(number)) * tile, 16), tile)

    def tile_loads(number):
        return [
            pltpu.make_async_copy(
                source.at[rows_at(number), :], target.at[number], load_sem.at[number, which]
            )
            for which, (source, target) in enumerate(zip(sources, held))
        ]

    sums_loads = [
        pltpu.make_async_copy(kept_hbm, kept, grad_sem.at[3]),
    ] + [
        pltpu.make_async_copy(got, gots.at[peer], grad_sem.at[4 + peer])
        for peer, got in enumerate(gots_hbm)
    ]
    w_load = pltpu.make_async_copy(w_hbm, w, grad_sem.at[0])
    middle = out_grad_ref.shape[0]
    late_rows = grads.shape[0] - early - middle
    grad_loads = [
        pltpu.make_async_copy(out_grad_ref, grads.at[pl.ds(early, middle), :], grad_sem.at[1]),
        pltpu.make_async_copy(
            flat_ref.at[pl.ds(early + middle, late_rows), :],
            grads.at[pl.ds(early + middle, late_rows), :],
            grad_sem.at[2],
        ),
    ]
    for copy in sums_loads + [w_load]:
        copy.start()
    for number in range(PLANES):
        for copy in tile_loads(number):
            copy.start()
    for copy in grad_loads:
        copy.start()

    barrier = pltpu.get_barrier_semaphore()
    for k in range(1, devices):
        pl.semaphore_signal(
            barrier, inc=1, device_id=(lax.rem(place + k, devices), part), device_id_type=MESH
        )
    pl.semaphore_signal(barrier, inc=1, device_id=over, device_id_type=MESH)
    pl.semaphore_wait(barrier, devices)

    def key_copy(number):
        return pltpu.make_async_remote_copy(
            src_ref=other_ref.at[rows_at(number), :],
            dst_ref=got_s.at[number],
            send_sem=ksend.at[number],
            recv_sem=krecv.at[number],
            device_id=over,
            device_id_type=MESH,
        )

    for number in range(PLANES):
        key_copy(number).start()

    bases = []
    cursor = 0
    for stage in range(count):
        bases.append(cursor)
        cursor += plan.boxes(stage)

    def window_sum(stages, zz, at, side):
        if zz:
            total = kept[zz - 1]
            for peer in range(peers):
                total = total + gots[peer, zz - 1].astype(F32)
            return total
        total = grads[plan.span(0, at, side), :].astype(F32)
        for stage in range(stages):
            total = total + inboxes[stage][plan.box(stage, at, side)].astype(F32)
        return total

    def take(stages, zz, at, side):
        for stage in range(0 if zz else stages):
            index = plan.box(stage, at, side)
            pltpu.make_async_remote_copy(
                src_ref=inboxes[stage].at[index],
                dst_ref=inboxes[stage].at[index],
                send_sem=rsend.at[0],
                recv_sem=rrecv.at[bases[stage] + index],
                device_id=over,
                device_id_type=MESH,
            ).wait_recv()

    sent = []
    posted = [0]

    def pass_on(stage, source_of):
        partner = flip(place, part, [axes[stage]])
        for at, side in plan.leaving(stage, inside, part):
            index = plan.box(stage, at, side)
            copy = pltpu.make_async_remote_copy(
                src_ref=source_of(at, side),
                dst_ref=inboxes[stage].at[index],
                send_sem=rsend.at[len(sent)],
                recv_sem=rrecv.at[bases[stage] + index],
                device_id=partner,
                device_id_type=MESH,
            )
            copy.start()
            sent.append(copy)

    def post(total):
        slot = posted[0]
        posted[0] += 1
        outbox[slot] = total.astype(BF16)
        return outbox.at[slot]

    def stage_sends(stage):
        def source_of(at, side):
            take(stage, 0, at, side)
            return post(window_sum(stage, 0, at, side))

        pass_on(stage, source_of)

    zfirst = sum(plan.boxes(stage) for stage in range(count))
    zsends = []

    def plane_copy(slot, box, recv, number, zz):
        return pltpu.make_async_remote_copy(
            src_ref=outbox.at[slot],
            dst_ref=last_in.at[box],
            send_sem=rsend.at[zfirst + number],
            recv_sem=zrecv.at[recv],
            device_id=(zz * plane + inside, part),
            device_id_type=MESH,
        )

    def near(zz):
        slot = posted[0]
        posted[0] += 1
        copy = plane_copy(slot, zz, zz, zz, xor_bit(depth, 0))
        moving = lax.rem(depth, 2) != zz % 2
        zsends.append((moving, copy))
        take(count, zz, inside, part)

        @pl.when(moving)
        def _():
            outbox[slot] = window_sum(count, zz, inside, part).astype(BF16)
            copy.start()

        return copy

    def far(zz, came):
        slot = posted[0]
        posted[0] += 1
        copy = plane_copy(slot, PLANES, PLANES, PLANES + zz, zz)
        staying = lax.rem(depth, 2) == zz % 2
        moving = staying & (depth != zz)
        zsends.append((moving, copy))

        @pl.when(staying)
        def _():
            came.wait_recv()
            total = window_sum(count, zz, inside, part) + last_in[zz].astype(F32)

            @pl.when(depth == zz)
            def _():
                sum_ref[...] = total

            @pl.when(depth != zz)
            def _():
                outbox[slot] = total.astype(BF16)
                copy.start()

    for copy in sums_loads:
        copy.wait()
    came = [near(zz) for zz in range(1, PLANES)]

    def step_at(step):
        return lax.rem(inside + step, plane)

    acc_a[...] = jnp.zeros_like(acc_a)
    acc_b[...] = jnp.zeros_like(acc_b)
    w_load.wait()

    def piece_copy(number, step, where, target):
        return pltpu.make_async_remote_copy(
            src_ref=dxs.at[number, step_at(step)],
            dst_ref=target,
            send_sem=dsend.at[number, step],
            recv_sem=drecv.at[place],
            device_id=where,
            device_id_type=MESH,
        )

    def one_tile(number, carry):
        for copy in tile_loads(number):
            copy.wait()
        key_copy(number).wait_recv()
        mask = rank_mask(meta_s[number][:, 0:1], rank)
        both = own_s[number].astype(F32) + got_s[number].astype(F32)
        cos, sin = cos_s[number], sin_s[number]
        dk = both[:, :kw]
        gq = gq_s[number]
        gk = (dk * cos - turn(dk) * sin).astype(BF16)
        gv = both[:, kw:].astype(BF16)
        at_k, at_v = 2 * width + qw, 3 * width + qw + kw
        b_parts = (
            b_ref[width : width + qw, :],
            b_ref[at_k : at_k + kw, :],
            b_ref[at_v : at_v + kw, :],
        )
        backs = [
            (ADAPTER_SCALE * nn(g, b) * mask).astype(BF16) for g, b in zip((gq, gk, gv), b_parts)
        ]
        dn = nn(jnp.concatenate([gq, gk, gv] + backs, axis=1), w[...])
        values = x_s[number].astype(F32)
        dx = (dy1_s[number] + norm_back(values, gain_ref[...], dn)).astype(BF16)
        acc_a[...] += tn(n_s[number], jnp.concatenate(backs, axis=1))
        low = z_s[number]
        acc_b[:qw, :] += tn(gq, low[:, :rank])
        acc_b[qw : qw + kw, :] += tn(gk, low[:, rank : 2 * rank])
        acc_b[qw + kw :, :] += tn(gv, low[:, 2 * rank :])
        turn_now = turn_of(number)
        if not direct:
            dxs[number] = dx
            copy = pltpu.make_async_copy(
                dxs.at[number], out_ref.at[rows_at(number), :], keep_sem.at[0]
            )
            copy.start()
            copy.wait()
            return carry
        dxs[number] = dx.reshape(dxs.shape[1:])
        for step in range(plane):
            target = layer(turn_now) * plane + step_at(step)
            if step > 0:
                piece_copy(number, step, (target, part), out_ref.at[place, part]).start()
                continue

            @pl.when(turn_now == 0)
            def _():
                pltpu.make_async_copy(
                    dxs.at[number, inside], out_ref.at[place, part], keep_sem.at[0]
                ).start()

            @pl.when(turn_now > 0)
            def _():
                piece_copy(number, 0, (target, part), out_ref.at[place, part]).start()

        return carry

    lax.fori_loop(0, PLANES, one_tile, 0)
    for copy in grad_loads:
        copy.wait()

    at = 0
    for order, size in enumerate((qw, kw, kw)):
        grads[at : at + width, :] = acc_a[:, order * rank : (order + 1) * rank].astype(BF16)
        base = (0, qw, qw + kw)[order]
        grads[at + width : at + width + size, :] = (
            ADAPTER_SCALE * acc_b[base : base + size, :]
        ).astype(BF16)
        at += width + size
    pass_on(0, lambda at, side: grads.at[plan.span(0, at, side), :])

    forwards = []

    def forward(back):
        source = layer(back)
        for step in range(plane):
            at = source * plane + step_at(step)
            if step > 0 or back > 0:
                pltpu.make_async_remote_copy(
                    src_ref=out_ref.at[at, part],
                    dst_ref=out_ref.at[at, part],
                    send_sem=hsem.at[0],
                    recv_sem=drecv.at[at],
                    device_id=over,
                    device_id_type=MESH,
                ).wait_recv()
            else:
                pltpu.make_async_copy(
                    out_ref.at[place, part], out_ref.at[place, part], keep_sem.at[0]
                ).wait()
        copy = forward_copy(source, part, len(forwards))
        copy.start()
        forwards.append(copy)

    def forward_copy(source, side, number):
        span = pl.ds(source * plane, plane)
        return pltpu.make_async_remote_copy(
            src_ref=out_ref.at[span, side],
            dst_ref=out_ref.at[span, side],
            send_sem=fsend.at[number],
            recv_sem=frecv.at[source],
            device_id=over,
            device_id_type=MESH,
        )

    for zz in range(1, PLANES):
        far(zz, came[zz - 1])
    for stage in range(1, count):
        stage_sends(stage)
        if direct and stage <= 2:
            forward((0, 0, 3)[stage])
    late = near(0)
    if direct:
        forward(1)
    far(0, late)
    if direct:
        forward(2)
    plane_copy(0, PLANES, PLANES, 0, depth).wait_recv()
    sum_ref[...] += last_in[PLANES].astype(F32)

    if direct:
        for back in range(PLANES):
            forward_copy(layer(back), 1 - part, 0).wait_recv()
        for copy in forwards:
            copy.wait_send()
        for number in range(PLANES):
            for step in range(plane):
                if step == 0 and (number + 2) % PLANES == 0:
                    continue
                piece_copy(number, step, over, out_ref.at[place, part]).wait_send()
    for copy in sent:
        copy.wait_send()
    for moving, copy in zsends:

        @pl.when(moving)
        def _():
            copy.wait_send()

    for number in range(PLANES):
        key_copy(number).wait_send()


def tail(
    devices, own_rows, early, rows_in, other, w_cat, b_rows, gain, flat, grad_out, kept, gots,
    key_width, piece,
):
    gq, _, x = rows_in[:3]
    rows, width = x.shape
    plan = Windows(devices, own_rows)
    plane, count, window = plan.plane, len(plan.axes), plan.rows
    rank = flat.shape[1]
    tile = rows // PLANES
    direct = piece % 16 == 0
    anywhere = pl.BlockSpec(memory_space=pl.ANY)
    boxes = [plan.boxes(stage) for stage in range(count)]
    peers = boxes[0] - 1
    sends = sum(boxes) + 2 * PLANES
    qw = gq.shape[1]
    first_plane = 16 * (((2 * plane - 1) * own_rows) // 16) + window
    dma = pltpu.SemaphoreType.DMA
    if direct:
        shape = (devices, 2, piece, width)
        held = (plane, piece, width)
    else:
        shape = (rows, width)
        held = (tile, width)
    outs = [jax.ShapeDtypeStruct(shape, BF16)]
    outs.append(jax.ShapeDtypeStruct((window, rank), F32))
    scratch = [pltpu.VMEM((PLANES, tile, a.shape[1]), a.dtype) for a in rows_in]
    scratch += [
        pltpu.VMEM(w_cat.shape, BF16),
        pltpu.VMEM((first_plane, rank), BF16),
        pltpu.VMEM((PLANES,) + held, BF16),
        pltpu.VMEM((width, 3 * rank), F32),
        pltpu.VMEM((qw + 2 * key_width, rank), F32),
        pltpu.VMEM((sends, window, rank), BF16),
        pltpu.VMEM((PLANES + 1, window, rank), BF16),
        pltpu.VMEM((PLANES, tile, other.shape[1]), BF16),
        pltpu.VMEM(kept.shape, F32),
        pltpu.VMEM((peers,) + gots[0].shape, BF16),
    ]
    scratch += [pltpu.VMEM((size, window, rank), BF16) for size in boxes]
    scratch += [
        dma((PLANES, len(rows_in))),
        dma((4 + peers,)),
        dma((PLANES, plane)),
        dma((devices,)),
        dma((PLANES,)),
        dma((PLANES,)),
        dma((sends,)),
        dma((sum(boxes),)),
        dma((PLANES + 1,)),
        dma((1,)),
        dma((PLANES,)),
        dma((PLANES,)),
        dma((1,)),
    ]
    return pl.pallas_call(
        functools.partial(tail_kernel, plan, early, key_width, direct),
        grid=(1,),
        in_specs=[anywhere] * 11
        + [pl.BlockSpec((early, rank), lambda i: (0, 0)), whole(gain)]
        + [anywhere] * (3 + peers),
        out_specs=[anywhere, whole(outs[1])],
        out_shape=outs,
        scratch_shapes=scratch,
        compiler_params=params(collective_id=2, has_side_effects=True),
        cost_estimate=cost(2 * rows * width * 2900, 200e6),
        name="tail",
    )(*rows_in, other, w_cat, b_rows, gain, flat, grad_out, kept, *gots)


def whole_part(values, size):
    return jnp.floor((values + 0.5) * (1.0 / size))


def tables_kernel(
    parts, each, part_ref, lengths_ref, ids_ref, order_ref, freq_ref,
    turns_ref, sines_ref, own_ref, other_ref, sorted_ref, rows_ref, column_ref, column_row_ref,
    bounds_ref,
):
    total = order_ref.shape[1]
    local = total // parts
    piece = each // parts
    block = 256
    order = jnp.broadcast_to(order_ref[0:1, :].astype(F32), (8, total))
    group = whole_part(order, each)
    rest = order - group * each
    part_at = whole_part(rest, piece)
    own = part_at == part_ref[0].astype(F32)
    slot = group * piece + (rest - part_at * piece)
    column = jnp.where(own, slot, slot + local)
    lanes = lane_iota((8, total))
    upto = jnp.where(own, 1.0, 0.0)
    shift = 1
    while shift < total:
        upto = upto + jnp.where(lanes >= shift, pltpu.roll(upto, shift, 1), 0.0)
        shift *= 2
    rank = jnp.where(own, upto - 1.0, 2.0 * total)
    place = lanes.astype(F32)
    number = row_iota((8, total))
    column_row_ref[...] = column.astype(I32)
    turned = jnp.transpose(jnp.where(number == 0, column, rank))
    column_ref[...] = turned.astype(I32)

    def halves(values):
        high = whole_part(values, 256)
        return high, values - high * 256

    place_high, place_low = halves(place)
    slot_high, slot_low = halves(slot)
    left = jnp.where(
        number == 0, place_high, jnp.where(number == 1, place_low, jnp.where(number == 2, slot_high, slot_low))
    ).astype(BF16)

    def chosen_by(keys, start):
        hit = keys == (start + lane_iota((total, block))).astype(F32)
        found = nn(left, jnp.where(hit, 1.0, 0.0).astype(BF16))
        return found[0:1] * 256 + found[1:2], found[2:3] * 256 + found[3:4]

    def sequence(places):
        first = jnp.zeros_like(places)
        adapter = jnp.zeros_like(places) + ids_ref[0].astype(F32)
        start = lengths_ref[0].astype(F32)
        for at in range(1, lengths_ref.shape[0]):
            inside = places >= start
            first = jnp.where(inside, start, first)
            adapter = jnp.where(inside, ids_ref[at].astype(F32), adapter)
            start = start + lengths_ref[at].astype(F32)
        return first, adapter

    def rope(position, at):
        angles = jnp.broadcast_to(position, freq_ref.shape[:1] + position.shape[1:]) * freq_ref[:, 0:1]
        turns_ref[:, at : at + block] = jnp.cos(angles)
        sines_ref[:, at : at + block] = jnp.sin(angles)

    def as_columns(*rows):
        index = row_iota((8, block))
        out = jnp.zeros((8, block), F32)
        for at, row in enumerate(rows):
            out = jnp.where(index == at, jnp.broadcast_to(row, (8, block)), out)
        return out

    for start in range(0, total, block):
        places, _ = chosen_by(turned[:, 0:1], start)
        first, adapter = sequence(places)
        columns = jnp.transpose(as_columns(adapter)).astype(I32)
        if start < local:
            rope(places - first, start)
            own_ref[start : start + block, :] = columns
        else:
            other_ref[start - local : start - local + block, :] = columns
    for start in range(0, local, block):
        places, slots = chosen_by(turned[:, 1:2], start)
        first, _ = sequence(places)
        rope(places - first, local + start)
        rows = as_columns(slots, first, places)
        rows_ref[:, start : start + block] = rows.astype(I32)
        sorted_ref[start : start + block, :] = jnp.transpose(rows).astype(I32)
        at_lane = lane_iota((1, block))
        for tile in range(0, block, QUERY_TILE):
            low = jnp.max(jnp.where(at_lane == tile, first, 0.0))
            high = jnp.max(jnp.where(at_lane == tile + QUERY_TILE - 1, places, 0.0))
            number_at = (start + tile) // QUERY_TILE
            bounds_ref[0, number_at] = low.astype(I32) // KEY_TILE
            bounds_ref[1, number_at] = high.astype(I32) // KEY_TILE + 1


def row_tables(order, lengths, adapter_ids, part, parts, each):
    total = order.shape[1]
    local = total // parts
    freq_index = jnp.arange(HEAD // 2, dtype=F32)
    freq = jnp.power(jnp.float32(ROPE_BASE), -2.0 * freq_index / HEAD)
    freq = jnp.broadcast_to(freq[:, None], (HEAD // 2, LANES))
    shapes = [
        ((HEAD // 2, total), F32),
        ((HEAD // 2, total), F32),
        ((local, 8), I32),
        ((local, 8), I32),
        ((local, 8), I32),
        ((8, local), I32),
        ((total, 8), I32),
        ((8, total), I32),
        ((2, local // QUERY_TILE), I32),
    ]
    outs = [jax.ShapeDtypeStruct(shape, kind) for shape, kind in shapes]
    return pl.pallas_call(
        functools.partial(tables_kernel, parts, each),
        grid_spec=pltpu.PrefetchScalarGridSpec(
            num_scalar_prefetch=3,
            grid=(1,),
            in_specs=[whole(order), whole(freq)],
            out_specs=[whole(o) for o in outs[:-1]] + [pl.BlockSpec(memory_space=pltpu.SMEM)],
        ),
        out_shape=outs,
        compiler_params=params(),
        cost_estimate=cost(1e8, 4e6),
        name="tables",
    )(jnp.reshape(part, (1,)).astype(I32), lengths[0], adapter_ids[0], order, freq)


def per_device(
    tokens, cotangent, order, lengths, adapter_ids, norm_gains, w_query, w_key, w_value,
    b_query, b_key, b_value, w_out, w_gate, w_up, w_down, adapters, first_moment, second_moment,
):
    parts = lax.axis_size("tensor")
    part = lax.axis_index("tensor")
    devices = lax.axis_size("dp")
    place = lax.axis_index("dp")
    total, width = tokens.shape
    each = total // devices
    piece = each // parts
    local = total // parts
    rank = adapters.shape[1]
    own_rows = adapters.shape[0]
    swap = [(i, parts - 1 - i) for i in range(parts)]
    first_part = part == 0

    def across(values):
        return lax.ppermute(values, "tensor", swap)

    def pair(mine, theirs, axis):
        return jnp.concatenate(
            [jnp.where(first_part, mine, theirs), jnp.where(first_part, theirs, mine)], axis=axis
        )

    def give_back(values):
        got = lax.all_to_all(
            values.reshape(devices, piece, width), "dp", split_axis=0, concat_axis=0, tiled=True
        )
        theirs = across(got)
        return pair(got[:, None], theirs[:, None], 1).reshape(total, width)

    qh, kh, half = w_query.shape[1], w_key.shape[1], w_gate.shape[1]
    qw, kw, hidden = parts * qh, parts * kh, parts * half
    heads, kv_heads = qw // HEAD, kw // HEAD
    unit = 4 if own_rows % 4 == 0 else 1
    bias = jnp.concatenate([b_query, b_key, b_value, jnp.zeros((width - qh - 2 * kh,), BF16)])
    mine = (w_query.T, w_key.T, w_value.T, jnp.broadcast_to(bias[None], (16, width)))
    moved, copies, *theirs = front(
        tokens.reshape(devices, parts, piece, width),
        adapters.astype(BF16).reshape(own_rows // unit, unit, rank),
        *[a.reshape(2, a.shape[0] // 2, width) for a in mine],
        devices,
    )
    theirs = [a.reshape(b.shape) for a, b in zip(theirs, mine)]
    cotangent, moved = lax.optimization_barrier((cotangent, moved))
    moved = moved.reshape(local, width)
    dy_all = lax.all_to_all(
        cotangent.reshape(devices, each, width), "dp", split_axis=0, concat_axis=0, tiled=True
    ).reshape(devices, parts, piece, width)

    def half_of(which):
        return lax.dynamic_index_in_dim(dy_all, which, 1, keepdims=False).reshape(local, width)

    dy = half_of(part)
    dy_theirs = half_of(parts - 1 - part)

    early = 3 * width + qw + 2 * kw
    flat = copies.reshape(2 * devices * own_rows, rank)
    (
        turns, sines, meta_own, meta_other, meta_sorted, meta_rows, column, column_row, bounds,
    ) = row_tables(order, lengths, adapter_ids, part, parts, each)
    gain_one = norm_gains[0:1].astype(F32)
    gain_two = norm_gains[1:2].astype(F32)
    side = jnp.reshape(part, (1,)).astype(I32)

    n1, q, kv, z, cos, sin, w_cat, other_kv = project(
        moved, meta_own, turns, sines, gain_one, mine, theirs, flat, qw, kw
    )
    other_kv = other_kv.reshape(kv.shape)
    w_out, kv = lax.optimization_barrier((w_out, kv))
    their_out = across(w_out)
    q_sorted, o_sorted, logs, merged, o = attend(
        bounds, q, meta_sorted, meta_rows, kv, other_kv, column, heads, kv_heads
    )
    y1, n2, z_out, w_out_cat = middle(
        side, o, moved, meta_own, w_out, their_out, gain_two, flat, early
    )
    y_own, d_own, y_got, d_got, y_last, flat_grads = feed(
        n2, dy, dy_theirs, meta_own, meta_other, w_gate, w_up, w_down, flat
    )
    y_got = jnp.concatenate([y_got, across(y_last)[None]], axis=0).reshape(local, width)
    dy1, dar, grad_out, on_sums, kept_sums = middle_back(
        devices, own_rows, d_own, d_got.reshape(local, width), y1, dy, o, z_out, meta_own, flat,
        early + qw, w_out_cat, gain_two, flat_grads,
    )
    got_sums = []
    for number, chosen in enumerate(subsets(Windows(devices, own_rows).axes[1:])):
        if number:
            moves = [
                (2 * at + side, 2 * to + over)
                for at in range(devices)
                for side in range(parts)
                for to, over in [flip_fixed(at, side, chosen)]
            ]
            got_sums.append(lax.ppermute(on_sums[number - 1], ("dp", "tensor"), moves))
    layer_rows = (y1 + (y_own + y_got.astype(F32))).astype(BF16).reshape(devices, 1, piece, width)
    layer_rows = jnp.broadcast_to(layer_rows, (devices, parts, piece, width))
    layer_rows, dar = lax.optimization_barrier((layer_rows, dar))
    layer_out = lax.all_to_all(
        layer_rows.reshape(devices * parts, piece, width),
        ("dp", "tensor"), split_axis=0, concat_axis=0, tiled=True,
    ).reshape(total, width)
    gq, dkv_own, dkv_other = attend_back(
        bounds, q_sorted, dar, o_sorted, logs, meta_sorted, meta_rows, turns, sines,
        merged, column_row, heads, kv_heads,
    )
    dx, window = tail(
        devices, own_rows, early,
        (gq, dkv_own, moved, n1, z, dy1, meta_own, cos, sin),
        dkv_other, w_cat, flat, gain_one, flat_grads, grad_out, kept_sums,
        got_sums, kw, piece,
    )
    if dx.ndim == 4:
        input_grad = dx.reshape(total, width)
    else:
        input_grad = give_back(dx)
    offset = lax.rem((2 * place + part) * own_rows, 16)
    reduced = lax.dynamic_slice_in_dim(window, offset, own_rows, 0)
    moment_one = BETA_ONE * first_moment + (1.0 - BETA_ONE) * reduced
    moment_two = BETA_TWO * second_moment + (1.0 - BETA_TWO) * reduced * reduced
    corrected_one = moment_one / (1.0 - BETA_ONE**STEP)
    corrected_two = moment_two / (1.0 - BETA_TWO**STEP)
    updated = adapters - LEARN_RATE * (
        corrected_one / (jnp.sqrt(corrected_two) + ADAM_EPS) + WEIGHT_DECAY * adapters
    )
    return (
        layer_out,
        input_grad,
        reduced,
        moment_one,
        moment_two,
        updated,
        updated.astype(BF16),
    )


def solution(mesh):
    both = P(("dp", "tensor"), None)
    rows = P("dp", None)
    return jax.shard_map(
        per_device,
        mesh=mesh,
        in_specs=(rows, rows, rows, rows, rows, P())
        + (P(None, "tensor"),) * 3
        + (P("tensor"),) * 3
        + (P("tensor", None), P(None, "tensor"), P(None, "tensor"), P("tensor", None))
        + (both,) * 3,
        out_specs=(rows, rows) + (both,) * 5,
        check_vma=False,
    )
```

```python
import functools

import jax
import jax.numpy as jnp
from jax import lax
from jax.experimental import pallas as pl
from jax.experimental.pallas import tpu as pltpu
from jax.sharding import PartitionSpec as P

HEAD = 64
RANK = 16
STEP = 3

ADAPTER_SCALE = 2.0
NORM_EPS = 1e-06
ROPE_BASE = 1000000.0
BETA_ONE = 0.5
BETA_TWO = 0.6
LEARN_RATE = 0.04
WEIGHT_DECAY = 0.01
ADAM_EPS = 1e-08
MASKED_SCORE = -1e30
PLANES = 4
FLAT_PAD = 64
SWAPPED = 1
MESH = pl.DeviceIdType.MESH

LANES = 128
ROW_TILE = 256
QUERY_TILE = 128
KEY_TILE = 256
HIDDEN_TILE = 512

F32 = jnp.float32
BF16 = jnp.bfloat16
I32 = jnp.int32


def nn(left, right):
    return lax.dot_general(left, right, (((1,), (0,)), ((), ())), preferred_element_type=F32)


def nt(left, right):
    return lax.dot_general(left, right, (((1,), (1,)), ((), ())), preferred_element_type=F32)


def tn(left, right):
    return lax.dot_general(left, right, (((0,), (0,)), ((), ())), preferred_element_type=F32)


def lane_iota(shape):
    return lax.broadcasted_iota(I32, shape, 1)


def row_iota(shape):
    return lax.broadcasted_iota(I32, shape, 0)


def whole(array):
    return pl.BlockSpec(array.shape, lambda *_: (0,) * array.ndim)


def row_blocks(array, tile):
    return pl.BlockSpec((tile, array.shape[1]), lambda i, *_: (i, 0))


def rows_from(array, start, count):
    return pl.BlockSpec(
        (pl.Element(count), pl.Element(array.shape[1])), lambda *_: (start, 0)
    )


def lane_table(table):
    return jnp.transpose(jnp.concatenate([table] * (LANES // table.shape[0]), axis=0))


def rank_mask(adapter_col, width):
    return jnp.where(lane_iota((adapter_col.shape[0], width)) // RANK == adapter_col, 1.0, 0.0)


def turn(values):
    lanes = lane_iota(values.shape) % HEAD
    return jnp.where(
        lanes < HEAD // 2,
        -pltpu.roll(values, LANES - HEAD // 2, 1),
        pltpu.roll(values, HEAD // 2, 1),
    )


def rms(values):
    return lax.rsqrt(jnp.mean(values * values, axis=-1, keepdims=True) + NORM_EPS)


def norm_back(values, gain, grad):
    inverse = rms(values)
    weighted = grad * gain
    return inverse * weighted - values * inverse * inverse * inverse * jnp.mean(
        weighted * values, axis=-1, keepdims=True
    )


def pick_rows(place_col, slots):
    hit = place_col == lane_iota((place_col.shape[0], slots))
    return jnp.where(hit, 1.0, 0.0).astype(BF16)


def place_rows(place_row, slots):
    hit = row_iota((slots, place_row.shape[1])) == place_row
    return jnp.where(hit, 1.0, 0.0).astype(BF16)


def params(**more):
    return pltpu.CompilerParams(vmem_limit_bytes=60 * 1024 * 1024, **more)


def cost(flops, moved):
    return pl.CostEstimate(flops=int(flops), bytes_accessed=int(moved), transcendentals=0)


def xor_bit(value, bit):
    size = 2**bit
    return value + size * (1 - 2 * lax.rem(value // size, 2))


def subsets(axes):
    out = [()]
    for axis in axes:
        out += [chosen + (axis,) for chosen in out]
    return out


def flip_fixed(place, part, axes):
    for axis in axes:
        if axis == "tensor":
            part = 1 - part
        else:
            place = place ^ 2**axis
    return place, part


def flip(place, part, axes):
    for axis in axes:
        if axis == "tensor":
            part = 1 - part
        else:
            place = xor_bit(place, axis)
    return place, part


def front_kernel(
    devices, rows_ref, chunk_ref, wq_ref, wk_ref, wv_ref, bias_ref,
    got_ref, copies_ref, wq_out, wk_out, wv_out, bias_out,
    local_sem, tsend, trecv, csend, crecv, wsend, wrecv,
):
    place, part = lax.axis_index("dp"), lax.axis_index("tensor")
    plane = devices // PLANES
    depth, inside = place // plane, lax.rem(place, plane)
    core = lax.rem(place, 2)
    own = 2 * place + part
    over = (place, 1 - part)
    units = chunk_ref.shape[0]

    def rows_of(index):
        return copies_ref.at[pl.ds(index * units, units)]

    def layer(hop):
        return lax.rem(depth + hop, PLANES)

    barrier = pltpu.get_barrier_semaphore()
    for k in range(1, devices):
        pl.semaphore_signal(
            barrier, inc=1, device_id=(lax.rem(place + k, devices), part), device_id_type=MESH
        )
    pl.semaphore_signal(barrier, inc=1, device_id=over, device_id_type=MESH)
    pl.semaphore_wait(barrier, devices)

    def chunk_copy(source, index, number, where):
        return pltpu.make_async_remote_copy(
            src_ref=source,
            dst_ref=rows_of(index),
            send_sem=csend.at[number],
            recv_sem=crecv.at[index],
            device_id=where,
            device_id_type=MESH,
        )

    def chain(hop, way):
        origin = depth - way * hop
        index = 2 * (origin * plane + inside) + part
        target = ((depth + way) * plane + inside, part)
        source = chunk_ref if hop == 0 else rows_of(index)
        number = 2 * hop + (0 if way > 0 else 1)
        inner = (origin >= 0) & (origin < PLANES)
        ahead = (depth + way >= 0) & (depth + way < PLANES)
        return chunk_copy(source, index, number, target), inner, ahead

    keep = [
        pltpu.make_async_copy(chunk_ref, rows_of(own), local_sem.at[0]),
        pltpu.make_async_copy(rows_ref.at[place, part], got_ref.at[place], local_sem.at[1]),
    ]
    for way in (1, -1):
        copy, _, ahead = chain(0, way)

        @pl.when(ahead)
        def _():
            copy.start()

    weights = ((wq_ref, wq_out), (wk_ref, wk_out), (wv_ref, wv_out))

    def weight_copy(ref, out, number, slot, where):
        return pltpu.make_async_remote_copy(
            src_ref=ref.at[slot],
            dst_ref=out.at[slot],
            send_sem=wsend.at[number],
            recv_sem=wrecv.at[number],
            device_id=where,
            device_id_type=MESH,
        )

    direct = [
        weight_copy(ref, out, number, core, over) for number, (ref, out) in enumerate(weights)
    ]
    for slot in range(2):
        direct.append(weight_copy(bias_ref, bias_out, 6 + slot, slot, over))
    for copy in direct:
        copy.start()

    rows_sent = []

    def send_rows(hop):
        for step in range(plane):
            if hop == 0 and step == 0:
                continue
            target = layer(hop) * plane + lax.rem(inside + step, plane)
            copy = pltpu.make_async_remote_copy(
                src_ref=rows_ref.at[target, part],
                dst_ref=got_ref.at[place],
                send_sem=tsend.at[len(rows_sent)],
                recv_sem=trecv.at[place],
                device_id=(target, part),
                device_id_type=MESH,
            )
            copy.start()
            rows_sent.append((copy, target))

    send_rows(0)
    for copy in keep:
        copy.start()
    for hop in range(1, PLANES):
        for way in (1, -1):
            copy, inner, ahead = chain(hop, way)

            @pl.when(inner)
            def _():
                copy.wait_recv()

            if hop < PLANES - 1:

                @pl.when(inner & ahead)
                def _():
                    copy.start()

    for hop in (2, 3, 1):
        send_rows(hop)

    sent = []

    def send_chunk(source, index, where):
        copy = chunk_copy(source, index, 2 * PLANES + len(sent), where)
        copy.start()
        sent.append(copy)

    def take_chunk(index):
        chunk_copy(chunk_ref, index, 0, over).wait_recv()

    bits = list(range(plane.bit_length() - 1))[::-1]
    orders = [["tensor"] + bits, bits[:-1] + ["tensor"] + bits[-1:]]
    relayed = []
    for stage in range(len(bits) + 1):
        for hop in range(PLANES):
            order = orders[hop % 2]
            origin = layer(hop) * plane + inside
            where = flip(place, part, [order[stage]])
            for chosen in subsets(order[:stage]):
                at, side = flip(origin, part, chosen)
                index = 2 * at + side
                if hop == 0 and not chosen:
                    send_chunk(chunk_ref, index, where)
                    continue
                if stage > 0 and order[stage - 1] in chosen:
                    take_chunk(index)
                send_chunk(rows_of(index), index, where)
        if stage == 0:
            partner = (xor_bit(place, 0), part)
            for number, (ref, out) in enumerate(weights):
                direct[number].wait_recv()
                copy = weight_copy(out, out, 3 + number, core, partner)
                copy.start()
                relayed.append(copy)
    for hop in range(PLANES):
        order = orders[hop % 2]
        origin = layer(hop) * plane + inside
        for chosen in subsets(order):
            if order[-1] in chosen:
                at, side = flip(origin, part, chosen)
                take_chunk(2 * at + side)
    for number, (ref, out) in enumerate(weights):
        weight_copy(out, out, 3 + number, 1 - core, over).wait_recv()
    for copy in direct[len(weights) :]:
        copy.wait_recv()
    for _, source in rows_sent:
        pltpu.make_async_remote_copy(
            src_ref=rows_ref.at[source, part],
            dst_ref=got_ref.at[source],
            send_sem=tsend.at[0],
            recv_sem=trecv.at[source],
            device_id=(source, part),
            device_id_type=MESH,
        ).wait_recv()
    for copy, _ in rows_sent:
        copy.wait_send()
    for hop in range(PLANES - 1):
        for way in (1, -1):
            copy, inner, ahead = chain(hop, way)

            @pl.when(inner & ahead)
            def _():
                copy.wait_send()

    for copy in sent + direct + relayed:
        copy.wait_send()
    for copy in keep:
        copy.wait()


def front(rows, chunk, wq, wk, wv, bias, devices):
    _, _, piece, width = rows.shape
    anywhere = pl.BlockSpec(memory_space=pl.ANY)
    outs = [
        jax.ShapeDtypeStruct((devices, piece, width), BF16),
        jax.ShapeDtypeStruct((2 * devices * chunk.shape[0],) + chunk.shape[1:], BF16),
    ] + [jax.ShapeDtypeStruct(a.shape, BF16) for a in (wq, wk, wv, bias)]
    dma = pltpu.SemaphoreType.DMA
    return pl.pallas_call(
        functools.partial(front_kernel, devices),
        in_specs=[anywhere] * 6,
        out_specs=[anywhere] * 6,
        out_shape=outs,
        scratch_shapes=[
            dma((2,)),
            dma((devices,)),
            dma((devices,)),
            dma((2 * PLANES + 2 * devices,)),
            dma((2 * devices,)),
            dma((8,)),
            dma((8,)),
        ],
        compiler_params=pltpu.CompilerParams(collective_id=0, has_side_effects=True),
        cost_estimate=cost(0, 100e6),
        name="front",
    )(rows, chunk, wq, wk, wv, bias)


def in_order(part, mine, theirs, place):
    @pl.when(part == 0)
    def _():
        place(mine, theirs)

    @pl.when(part == 1)
    def _():
        place(theirs, mine)


def project_kernel(
    x_ref, meta_ref, turns_ref, sines_ref, gain_ref, mq_ref, mk_ref, mv_ref, mb_ref,
    tq_ref, tk_ref, tv_ref, tb_ref, flat_ref,
    n_ref, q_ref, kv_ref, z_ref, cos_ref, sin_ref, w_ref, other_ref, bias, held, ksend, krecv,
):
    place, part = lax.axis_index("dp"), lax.axis_index("tensor")
    here = pl.program_id(0)
    tiles = held.shape[0]
    width = x_ref.shape[1]
    qw, kw = q_ref.shape[1], kv_ref.shape[1] // 2

    def swap(number):
        return pltpu.make_async_remote_copy(
            src_ref=held.at[number],
            dst_ref=other_ref.at[number],
            send_sem=ksend.at[number],
            recv_sem=krecv.at[number],
            device_id=(place, 1 - part),
            device_id_type=MESH,
        )

    rank = flat_ref.shape[1]
    low = qw + 2 * kw
    a_rows, b_rows = [], []
    cursor = 0
    for size in (qw, kw, kw):
        a_rows.append(slice(cursor, cursor + width))
        b_rows.append(slice(cursor + width, cursor + width + size))
        cursor += width + size

    @pl.when(pl.program_id(0) == 0)
    def _():
        def fill(first, second):
            at, to = 0, 0
            for order, size in enumerate((qw // 2, kw // 2, kw // 2)):
                w_ref[to : to + size, :] = first[order][...]
                w_ref[to + size : to + 2 * size, :] = second[order][...]
                bias[:, to : to + 2 * size] = jnp.concatenate(
                    [
                        first[3][:8, at : at + size].astype(F32),
                        second[3][:8, at : at + size].astype(F32),
                    ],
                    axis=1,
                )
                at += size
                to += 2 * size

        barrier = pltpu.get_barrier_semaphore()
        pl.semaphore_signal(barrier, inc=1, device_id=(place, 1 - part), device_id_type=MESH)
        in_order(
            part, (mq_ref, mk_ref, mv_ref, mb_ref), (tq_ref, tk_ref, tv_ref, tb_ref), fill
        )
        for i, rows in enumerate(a_rows):
            turned = jnp.transpose(flat_ref[rows, :].astype(F32)).astype(BF16)
            w_ref[low + i * rank : low + (i + 1) * rank, :] = turned
        pl.semaphore_wait(barrier, 1)

    values = x_ref[...].astype(F32)
    normed = (values * rms(values) * gain_ref[...]).astype(BF16)
    n_ref[...] = normed
    base = nt(normed, w_ref[qw:, :])
    mask = rank_mask(meta_ref[:, 0:1], rank)
    lows = [
        (base[:, low - qw + i * rank : low - qw + (i + 1) * rank] * mask).astype(BF16)
        for i in range(3)
    ]
    for i in range(3):
        z_ref[:, i * rank : (i + 1) * rank] = lows[i]
    cos, sin = lane_table(turns_ref[...]), lane_table(sines_ref[...])
    cos_ref[...] = cos
    sin_ref[...] = sin
    keys = (
        base[:, :kw]
        + bias[0:1, qw : qw + kw]
        + ADAPTER_SCALE * nt(lows[1], flat_ref[b_rows[1], :])
    )
    vals = (
        base[:, kw : 2 * kw]
        + bias[0:1, qw + kw : low]
        + ADAPTER_SCALE * nt(lows[2], flat_ref[b_rows[2], :])
    )
    both = jnp.concatenate([keys * cos + turn(keys) * sin, vals], axis=1).astype(BF16)
    held[here] = both
    kv_ref[...] = both
    swap(here).start()
    queries = (
        nt(normed, w_ref[:qw, :])
        + bias[0:1, :qw]
        + ADAPTER_SCALE * nt(lows[0], flat_ref[b_rows[0], :])
    )
    for pair in range(qw // LANES):
        some = queries[:, pair * LANES : (pair + 1) * LANES]
        turned = (some * cos + turn(some) * sin) * HEAD**-0.5
        q_ref[:, pair * LANES : (pair + 1) * LANES] = turned.astype(BF16)

    @pl.when(here == tiles - 1)
    def _():
        for number in range(tiles):
            swap(number).wait_send()
        for number in range(tiles):
            swap(number).wait_recv()


def project(x, meta, turns, sines, gain, mine, theirs, flat, qw, kw):
    rows, width = x.shape
    rank = flat.shape[1]
    tile = ROW_TILE
    early = 3 * width + qw + 2 * kw
    columns = pl.BlockSpec((turns.shape[0], tile), lambda i, *_: (0, i))
    outs = [
        jax.ShapeDtypeStruct((rows, width), BF16),
        jax.ShapeDtypeStruct((rows, qw), BF16),
        jax.ShapeDtypeStruct((rows, 2 * kw), BF16),
        jax.ShapeDtypeStruct((rows, 3 * rank), BF16),
        jax.ShapeDtypeStruct((rows, LANES), F32),
        jax.ShapeDtypeStruct((rows, LANES), F32),
        jax.ShapeDtypeStruct((qw + 2 * kw + 3 * rank, width), BF16),
        jax.ShapeDtypeStruct((rows // tile, tile, 2 * kw), BF16),
    ]
    dma = pltpu.SemaphoreType.DMA
    return pl.pallas_call(
        project_kernel,
        grid=(rows // tile,),
        in_specs=[row_blocks(a, tile) for a in (x, meta)]
        + [columns, columns]
        + [whole(a) for a in (gain, *mine, *theirs)]
        + [pl.BlockSpec((early, rank), lambda i: (0, 0))],
        out_specs=[row_blocks(o, tile) for o in outs[:6]]
        + [whole(outs[6]), pl.BlockSpec(memory_space=pl.ANY)],
        out_shape=outs,
        scratch_shapes=[
            pltpu.VMEM((8, qw + 2 * kw), F32),
            pltpu.VMEM((rows // tile, tile, 2 * kw), BF16),
            dma((rows // tile,)),
            dma((rows // tile,)),
        ],
        compiler_params=params(collective_id=4, has_side_effects=True),
        cost_estimate=cost(2 * rows * width * 1600, 9e6),
        name="project",
    )(x, meta, turns, sines, gain, *mine, *theirs, flat)


def head_groups(heads, kv_heads):
    width = heads // kv_heads
    groups = {}
    for head in range(heads):
        groups.setdefault((head // width, head % 2), []).append(head)
    return [(kv, half, members) for (kv, half), members in sorted(groups.items())]


def spread_heads(tile_f32, kv, half, ones=False):
    lanes = lane_iota(tile_f32.shape)
    moved = tile_f32 if kv % 2 == half else pltpu.roll(tile_f32, HEAD, 1)
    keep = (lanes >= HEAD) if half else (lanes < HEAD)
    rest = jnp.where(lanes == (0 if half else HEAD), 1.0, 0.0) if ones else 0.0
    return jnp.where(keep, moved, rest)


def stack_heads(groups, source, target):
    rows = source.shape[0]
    at = 0
    for _, _, members in groups:
        for head in members:
            pair = slice((head // 2) * LANES, (head // 2 + 1) * LANES)
            target[at : at + rows, :] = source[:, pair]
            at += rows


def attend_kernel(
    heads, kv_heads, bounds_ref, all_ref, meta_ref, metar_ref, place_ref, own_ref, other_ref,
    column_ref,
    q_ref, o_ref, log_ref, merged_ref, slot_ref, keys, values, acc, top, held, stack, scores,
):
    step = pl.program_id(0)
    groups = head_groups(heads, kv_heads)
    rows = q_ref.shape[0]
    q_ref[...] = nn(pick_rows(meta_ref[:, 0:1], all_ref.shape[0]), all_ref[...]).astype(BF16)
    stack_heads(groups, q_ref, stack)

    @pl.when(step == 0)
    def _():
        both = jnp.concatenate([own_ref[...], other_ref[...]], axis=0)
        for start in range(0, keys.shape[1], KEY_TILE):
            span = slice(start, start + KEY_TILE)
            part = nn(pick_rows(column_ref[span, 0:1], both.shape[0]), both)
            merged_ref[span, :] = part.astype(BF16)
            for number, (kv, half, _) in enumerate(groups):
                keys[number, span, :] = spread_heads(part[:, :LANES], kv, half).astype(BF16)
                turned = jnp.transpose(spread_heads(part[:, LANES:], kv, half, True))
                values[number, :, span] = turned.astype(BF16)

    acc[...] = jnp.zeros_like(acc)
    top[...] = jnp.full_like(top, MASKED_SCORE)
    first, last = metar_ref[1:2, :], metar_ref[2:3, :]
    cuts = []
    at = 0
    for _, _, members in groups:
        cuts.append(slice(at * rows, (at + len(members)) * rows))
        at += len(members)

    def find_top(number, carry):
        start = pl.multiple_of(number * KEY_TILE, KEY_TILE)
        span = pl.ds(start, KEY_TILE)
        index = start + row_iota((KEY_TILE, rows))
        bias = jnp.where((index >= first) & (index <= last), 0.0, MASKED_SCORE)
        for group, cut in enumerate(cuts):
            count = (cut.stop - cut.start) // rows
            part = nt(keys[group, span, :], stack[cut, :])
            part = part + jnp.concatenate([bias] * count, axis=1)
            scores[span, cut] = part
            most = jnp.max(part.reshape(KEY_TILE // 8, 8, -1), axis=0)
            top[:, cut] = jnp.maximum(top[:, cut], most)
        return carry

    def weigh(number, carry):
        start = pl.multiple_of(number * KEY_TILE, KEY_TILE)
        span = pl.ds(start, KEY_TILE)
        for group, cut in enumerate(cuts):
            weights = jnp.exp(scores[span, cut] - top[0:1, cut]).astype(BF16)
            acc[:, cut] += nn(values[group, :, span], weights)
        return carry

    lax.fori_loop(bounds_ref[0, step], bounds_ref[1, step], find_top, 0)
    top[0:1, :] = jnp.max(top[...], axis=0, keepdims=True)
    lax.fori_loop(bounds_ref[0, step], bounds_ref[1, step], weigh, 0)
    parts = {}
    at = 0
    for _, half, members in groups:
        for head in members:
            cut = slice(at * rows, (at + 1) * rows)
            at += 1
            block = acc[:, cut]
            sums = block[0:1, :] if half else block[HEAD : HEAD + 1, :]
            log_ref[head : head + 1, :] = top[0:1, cut] + jnp.log(sums)
            parts[head] = block / sums
    low = row_iota((LANES, rows)) < HEAD
    for pair in range(heads // 2):
        both = jnp.where(low, parts[2 * pair], parts[2 * pair + 1])
        o_ref[:, pair * LANES : (pair + 1) * LANES] = jnp.transpose(both).astype(BF16)
    for head in range(heads, log_ref.shape[0]):
        log_ref[head : head + 1, :] = jnp.zeros((1, rows), F32)
    held[pl.ds(pl.multiple_of(step * rows, rows), rows), :] = o_ref[...]

    @pl.when(step == pl.num_programs(0) - 1)
    def _():
        slot_ref[...] = nn(place_rows(place_ref[0:1, :], held.shape[0]), held[...]).astype(BF16)


def attend(bounds, q, meta, meta_rows, own_kv, other_kv, column, heads, kv_heads):
    rows, qw = q.shape
    tile = QUERY_TILE
    keys = 2 * rows
    groups = len(head_groups(heads, kv_heads))
    outs = [
        jax.ShapeDtypeStruct((rows, qw), BF16),
        jax.ShapeDtypeStruct((rows, qw), BF16),
        jax.ShapeDtypeStruct((16, rows), F32),
        jax.ShapeDtypeStruct((keys, own_kv.shape[1]), BF16),
        jax.ShapeDtypeStruct((rows, qw), BF16),
    ]
    return pl.pallas_call(
        functools.partial(attend_kernel, heads, kv_heads),
        grid_spec=pltpu.PrefetchScalarGridSpec(
            num_scalar_prefetch=1,
            grid=(rows // tile,),
            in_specs=[
                whole(q),
                row_blocks(meta, tile),
                pl.BlockSpec((8, tile), lambda i, *_: (0, i)),
                whole(meta_rows),
                whole(own_kv),
                whole(other_kv),
                whole(column),
            ],
            out_specs=[
                row_blocks(outs[0], tile),
                row_blocks(outs[1], tile),
                pl.BlockSpec((16, tile), lambda i, *_: (0, i)),
                whole(outs[3]),
                whole(outs[4]),
            ],
            scratch_shapes=[
                pltpu.VMEM((groups, keys, LANES), BF16),
                pltpu.VMEM((groups, LANES, keys), BF16),
                pltpu.VMEM((LANES, heads * tile), F32),
                pltpu.VMEM((8, heads * tile), F32),
                pltpu.VMEM((rows, qw), BF16),
                pltpu.VMEM((heads * tile, LANES), BF16),
                pltpu.VMEM((keys, heads * tile), F32),
            ],
        ),
        out_shape=outs,
        compiler_params=params(),
        cost_estimate=cost(heads * rows * keys * 2000, 6e6),
        name="attend",
    )(bounds, q, meta, meta_rows, meta_rows, own_kv, other_kv, column)


def attend_back_kernel(
    heads, kv_heads, bounds_ref, q_ref, all_ref, o_ref, log_ref, meta_ref, metar_ref, cos_ref,
    sin_ref, merged_ref, column_ref, place_ref,
    gq_ref, own_ref, other_ref, keys, values, dkeys, dvalues, dq, dots, g_ref, held, stack, grads,
):
    step = pl.program_id(0)
    groups = head_groups(heads, kv_heads)
    rows = q_ref.shape[0]
    g_ref[...] = nn(pick_rows(meta_ref[:, 0:1], all_ref.shape[0]), all_ref[...]).astype(BF16)

    @pl.when(step == 0)
    def _():
        for start in range(0, keys.shape[1], KEY_TILE):
            span = slice(start, start + KEY_TILE)
            part = merged_ref[span, :].astype(F32)
            for number, (kv, half, _) in enumerate(groups):
                keys[number, span, :] = spread_heads(part[:, :LANES], kv, half).astype(BF16)
                values[number, span, :] = spread_heads(part[:, LANES:], kv, half).astype(BF16)
        dkeys[...] = jnp.zeros_like(dkeys)
        dvalues[...] = jnp.zeros_like(dvalues)

    stack_heads(groups, q_ref, stack)
    stack_heads(groups, g_ref, grads)
    dq[...] = jnp.zeros_like(dq)
    for pair in range(heads // 2):
        lanes = slice(pair * LANES, (pair + 1) * LANES)
        product = jnp.transpose(g_ref[:, lanes].astype(F32) * o_ref[:, lanes].astype(F32))
        dots[2 * pair : 2 * pair + 1, :] = jnp.sum(product[:HEAD], axis=0, keepdims=True)
        dots[2 * pair + 1 : 2 * pair + 2, :] = jnp.sum(product[HEAD:], axis=0, keepdims=True)
    first, last = metar_ref[1:2, :], metar_ref[2:3, :]

    def one_tile(number, carry):
        start = pl.multiple_of(number * KEY_TILE, KEY_TILE)
        index = start + row_iota((KEY_TILE, rows))
        bias = jnp.where((index >= first) & (index <= last), 0.0, MASKED_SCORE)
        span = pl.ds(start, KEY_TILE)
        begin = 0
        for group, (_, half, members) in enumerate(groups):
            count = len(members)
            cut = slice(begin * rows, (begin + count) * rows)
            begin += count
            logs = jnp.concatenate([log_ref[h : h + 1, :] for h in members], axis=1)
            drop = jnp.concatenate([dots[h : h + 1, :] for h in members], axis=1)
            key_part = keys[group, span, :]
            scores = nt(key_part, stack[cut, :]) + jnp.concatenate([bias] * count, axis=1)
            weights = jnp.exp(scores - logs)
            change = nt(values[group, span, :], grads[cut, :])
            dscores = (weights * (change - drop)).astype(BF16)
            dvalues[group, span, :] += nn(weights.astype(BF16), grads[cut, :])
            dkeys[group, span, :] += nn(dscores, stack[cut, :])
            back = tn(dscores, key_part)
            for at, head in enumerate(members):
                dq[head // 2, :, :] += back[at * rows : (at + 1) * rows, :]
        return carry

    lax.fori_loop(bounds_ref[0, step], bounds_ref[1, step], one_tile, 0)
    cos, sin = lane_table(cos_ref[...]), lane_table(sin_ref[...])
    for pair in range(heads // 2):
        grad = dq[pair, :, :] * HEAD**-0.5
        grad = grad * cos - turn(grad) * sin
        held[
            pl.ds(pl.multiple_of(step * rows, rows), rows), pair * LANES : (pair + 1) * LANES
        ] = grad.astype(BF16)

    @pl.when(step == pl.num_programs(0) - 1)
    def _():
        gq_ref[...] = nn(place_rows(place_ref[0:1, :], held.shape[0]), held[...]).astype(BF16)
        total = dkeys.shape[1]

        def join(ref):
            out = None
            for group, (kv, half, _) in enumerate(groups):
                part = ref[group, :, :]
                lanes = lane_iota(part.shape)
                part = jnp.where((lanes >= HEAD) if half else (lanes < HEAD), part, 0.0)
                if kv % 2 != half:
                    part = pltpu.roll(part, HEAD, 1)
                out = part if out is None else out + part
            return out.astype(BF16)

        both = jnp.concatenate([join(dkeys), join(dvalues)], axis=1)
        half_rows = own_ref.shape[0]
        for at in range(0, total, KEY_TILE):
            hit = (at + row_iota((KEY_TILE, total))) == column_ref[0:1, :]
            part = nn(jnp.where(hit, 1.0, 0.0).astype(BF16), both).astype(BF16)
            if at < half_rows:
                own_ref[at : at + KEY_TILE, :] = part
            else:
                other_ref[at - half_rows : at - half_rows + KEY_TILE, :] = part


def attend_back(
    bounds, q, grad, o, logs, meta, meta_rows, cos, sin, merged, column_row, heads, kv_heads
):
    rows, qw = q.shape
    tile = QUERY_TILE
    keys, kvw = merged.shape
    groups = len(head_groups(heads, kv_heads))
    outs = [
        jax.ShapeDtypeStruct((rows, qw), BF16),
        jax.ShapeDtypeStruct((rows, kvw), BF16),
        jax.ShapeDtypeStruct((rows, kvw), BF16),
    ]
    return pl.pallas_call(
        functools.partial(attend_back_kernel, heads, kv_heads),
        grid_spec=pltpu.PrefetchScalarGridSpec(
            num_scalar_prefetch=1,
            grid=(rows // tile,),
            in_specs=[
                row_blocks(q, tile),
                whole(grad),
                row_blocks(o, tile),
                pl.BlockSpec((16, tile), lambda i, *_: (0, i)),
                row_blocks(meta, tile),
                pl.BlockSpec((8, tile), lambda i, *_: (0, i)),
                pl.BlockSpec((cos.shape[0], tile), lambda i, *_: (0, rows // tile + i)),
                pl.BlockSpec((cos.shape[0], tile), lambda i, *_: (0, rows // tile + i)),
                whole(merged),
                whole(column_row),
                whole(meta_rows),
            ],
            out_specs=[whole(o) for o in outs],
            scratch_shapes=[
                pltpu.VMEM((groups, keys, LANES), BF16),
                pltpu.VMEM((groups, keys, LANES), BF16),
                pltpu.VMEM((groups, keys, LANES), F32),
                pltpu.VMEM((groups, keys, LANES), F32),
                pltpu.VMEM((heads // 2, tile, LANES), F32),
                pltpu.VMEM((16, tile), F32),
                pltpu.VMEM((tile, qw), BF16),
                pltpu.VMEM((rows, qw), BF16),
                pltpu.VMEM((heads * tile, LANES), BF16),
                pltpu.VMEM((heads * tile, LANES), BF16),
            ],
        ),
        out_shape=outs,
        compiler_params=params(),
        cost_estimate=cost(heads * rows * keys * 3000, 9e6),
        name="attend_back",
    )(bounds, q, grad, o, logs, meta, meta_rows, cos, sin, merged, column_row, meta_rows)


def middle_kernel(
    part_ref, o_ref, x_ref, meta_ref, mine_ref, theirs_ref, gain_ref, flat_ref,
    y_ref, n_ref, z_ref, w_ref,
):
    width = x_ref.shape[1]
    rank = flat_ref.shape[1]
    half = mine_ref.shape[0]

    @pl.when(pl.program_id(0) == 0)
    def _():
        def fill(first, second):
            w_ref[:half, :width] = first[...]
            w_ref[half:, :width] = second[...]

        in_order(part_ref[0], mine_ref, theirs_ref, fill)
        w_ref[:, width:] = flat_ref[: 2 * half, :]

    mask = rank_mask(meta_ref[:, 0:1], rank)
    base = nn(o_ref[...], w_ref[...])
    low = (base[:, width:] * mask).astype(BF16)
    z_ref[...] = low
    values = x_ref[...].astype(F32) + (base[:, :width] + ADAPTER_SCALE * nt(low, flat_ref[2 * half :, :]))
    y_ref[...] = values
    n_ref[...] = (values * rms(values) * gain_ref[...]).astype(BF16)


def middle(part, o, x, meta, mine, theirs, gain, flat, start):
    rows, width = x.shape
    rank = flat.shape[1]
    tile = ROW_TILE
    rest = (mine, theirs, gain)
    outs = [
        jax.ShapeDtypeStruct((rows, width), F32),
        jax.ShapeDtypeStruct((rows, width), BF16),
        jax.ShapeDtypeStruct((rows, rank), BF16),
        jax.ShapeDtypeStruct((o.shape[1], width + rank), BF16),
    ]
    return pl.pallas_call(
        middle_kernel,
        grid_spec=pltpu.PrefetchScalarGridSpec(
            num_scalar_prefetch=1,
            grid=(rows // tile,),
            in_specs=[row_blocks(a, tile) for a in (o, x, meta)]
            + [whole(a) for a in rest]
            + [rows_from(flat, start, o.shape[1] + width)],
            out_specs=[row_blocks(a, tile) for a in outs[:3]] + [whole(outs[3])],
        ),
        out_shape=outs,
        compiler_params=params(),
        cost_estimate=cost(2 * rows * width * 1100, 12e6),
        name="middle",
    )(part, o, x, meta, *rest, flat)


class Windows:
    def __init__(self, devices, own_rows):
        self.devices = devices
        self.own_rows = own_rows
        self.plane = devices // PLANES
        self.axes = list(range(self.plane.bit_length() - 1)) + ["tensor"]
        self.rows = 16 * ((own_rows + 30) // 16)
        self.last = 16 * (((2 * devices - 1) * own_rows) // 16) + self.rows

    def start(self, zz, at, side):
        row = (2 * (zz * self.plane + at) + side) * self.own_rows
        return pl.multiple_of((row // 16) * 16, 16)

    def span(self, zz, at, side):
        return pl.ds(self.start(zz, at, side), self.rows)

    def boxes(self, stage):
        return 2 ** (len(self.axes) - 1 - stage)

    def box(self, stage, at, side):
        index = 0
        for order, axis in enumerate(self.axes[stage + 1 :]):
            bit = side if axis == "tensor" else lax.rem(at // 2**axis, 2)
            index = index + bit * 2**order
        return index

    def leaving(self, stage, inside, part):
        for chosen in subsets(self.axes[stage + 1 :]):
            yield flip(inside, part, [self.axes[stage]] + list(chosen))

    def staying(self, stage, inside, part):
        for chosen in subsets(self.axes[stage + 1 :]):
            yield flip(inside, part, list(chosen))


def middle_back_kernel(
    plan, first_b, da_ref, db_ref, y1_ref, dy_ref, o_ref, z_ref, meta_ref, copies_ref, w_ref,
    gain_ref, flat_ref,
    dy1_ref, dar_ref, grad_ref, kept_ref, *rest,
):
    step = pl.program_id(0)
    on_refs = rest[: plan.boxes(0) - 1]
    acc_bo, acc_ao, mine, inbox, b_ref, msem, ssem, rsem, bsem = rest[plan.boxes(0) - 1 :]
    b_load = pltpu.make_async_copy(
        copies_ref.at[pl.ds(first_b, b_ref.shape[0]), :], b_ref, bsem.at[0]
    )
    rank = b_ref.shape[1]
    qw = o_ref.shape[1]
    place, part = lax.axis_index("dp"), lax.axis_index("tensor")
    inside = lax.rem(place, plan.plane)
    partner = flip(place, part, [plan.axes[0]])
    boxes = plan.boxes(0)

    def moves():
        local, remote = [], []
        for zz in range(1, PLANES):
            for at, side in plan.leaving(0, inside, part):
                index = (zz - 1) * boxes + plan.box(0, at, side)
                remote.append(
                    pltpu.make_async_remote_copy(
                        src_ref=flat_ref.at[plan.span(zz, at, side), :],
                        dst_ref=inbox.at[index],
                        send_sem=ssem.at[len(remote)],
                        recv_sem=rsem.at[index],
                        device_id=partner,
                        device_id_type=MESH,
                    )
                )
            for at, side in plan.staying(0, inside, part):
                index = (zz - 1) * boxes + plan.box(0, at, side)
                local.append(
                    pltpu.make_async_copy(
                        flat_ref.at[plan.span(zz, at, side), :], mine.at[index], msem.at[len(local)]
                    )
                )
        return local, remote

    @pl.when(step == 0)
    def _():
        acc_bo[...] = jnp.zeros_like(acc_bo)
        acc_ao[...] = jnp.zeros_like(acc_ao)
        b_load.start()
        barrier = pltpu.get_barrier_semaphore()
        pl.semaphore_signal(barrier, inc=1, device_id=partner, device_id_type=MESH)
        pl.semaphore_wait(barrier, 1)
        local, remote = moves()
        for copy in remote + local:
            copy.start()
        b_load.wait()

    mask = rank_mask(meta_ref[:, 0:1], rank)
    grad = da_ref[...] + db_ref[...].astype(F32)
    dy1 = dy_ref[...].astype(F32) + norm_back(y1_ref[...], gain_ref[...], grad)
    dy1_ref[...] = dy1
    low_grad = dy1.astype(BF16)
    back_out = (ADAPTER_SCALE * nn(low_grad, b_ref[...]) * mask).astype(BF16)
    both = jnp.concatenate([low_grad, back_out], axis=1)
    dar_ref[...] = nt(both, w_ref[...]).astype(BF16)
    acc_bo[...] += ADAPTER_SCALE * tn(low_grad, z_ref[...])
    acc_ao[...] += tn(o_ref[...], back_out)

    @pl.when(step == pl.num_programs(0) - 1)
    def _():
        grad_ref[:qw, :] = acc_ao[...].astype(BF16)
        grad_ref[qw:, :] = acc_bo[...].astype(BF16)
        local, remote = moves()
        for copy in local:
            copy.wait()
        for copy in remote:
            copy.wait_recv()
        def total(zz, at, side):
            index = (zz - 1) * boxes + plan.box(0, at, side)
            return mine[index].astype(F32) + inbox[index].astype(F32)

        for zz in range(1, PLANES):
            for peer, chosen in enumerate(subsets(plan.axes[1:])):
                at, side = flip(inside, part, chosen)
                if peer == 0:
                    kept_ref[zz - 1] = total(zz, at, side)
                else:
                    on_refs[peer - 1][zz - 1] = total(zz, at, side).astype(BF16)
        for copy in remote:
            copy.wait_send()


def middle_back(
    devices, own_rows, d_first, d_second, y1, dy, o, z, meta, copies, start, w_out, gain, flat
):
    rows, width = y1.shape
    rank = copies.shape[1]
    qw = o.shape[1]
    tile = ROW_TILE
    plan = Windows(devices, own_rows)
    first = (PLANES - 1) * plan.boxes(0)
    outs = [
        jax.ShapeDtypeStruct((rows, width), F32),
        jax.ShapeDtypeStruct((rows, qw), BF16),
        jax.ShapeDtypeStruct((qw + width, rank), BF16),
        jax.ShapeDtypeStruct((PLANES - 1, plan.rows, rank), F32),
    ] + [jax.ShapeDtypeStruct((PLANES - 1, plan.rows, rank), BF16)] * (plan.boxes(0) - 1)
    return pl.pallas_call(
        functools.partial(middle_back_kernel, plan, start),
        grid=(rows // tile,),
        in_specs=[row_blocks(a, tile) for a in (d_first, d_second, y1, dy, o, z, meta)]
        + [pl.BlockSpec(memory_space=pl.ANY)]
        + [whole(a) for a in (w_out, gain)]
        + [pl.BlockSpec(memory_space=pl.ANY)],
        out_specs=[row_blocks(a, tile) for a in outs[:2]] + [whole(a) for a in outs[2:]],
        out_shape=outs,
        scratch_shapes=[
            pltpu.VMEM((width, rank), F32),
            pltpu.VMEM((qw, rank), F32),
            pltpu.VMEM((first, plan.rows, rank), BF16),
            pltpu.VMEM((first, plan.rows, rank), BF16),
            pltpu.VMEM((width, rank), BF16),
            pltpu.SemaphoreType.DMA((first,)),
            pltpu.SemaphoreType.DMA((first,)),
            pltpu.SemaphoreType.DMA((first,)),
            pltpu.SemaphoreType.DMA((1,)),
        ],
        compiler_params=params(collective_id=3, has_side_effects=True),
        cost_estimate=cost(2 * rows * width * 1500, 20e6),
        name="middle_back",
    )(d_first, d_second, y1, dy, o, z, meta, copies, w_out, gain, flat)


def own_tile(step, tiles):
    return jnp.maximum(step - tiles, 0)


def their_tile(step, tiles):
    return jnp.clip(step - 1, 0, tiles - 1)


def feed_kernel(
    n_ref, n_hbm, dy_ref, dyt_ref, meta_ref, metat_ref, wg_hbm, wu_hbm,
    wd_hbm, copies,
    y_ref, d_ref, y_got, d_got, last_ref, flat_ref,
    wga, wua, wda, raw, grads, extras, xg, xu, dya, yacc, dacc, mask_s, n_got, held_d, held_y,
    packed, blank, ap_ref, bd_ref, wsem, gsem, nsend, nrecv, dsend, drecv, ysend, yrecv,
):
    step = pl.program_id(0)
    steps = pl.num_programs(0)
    tiles_each, swapped = n_got.shape[0], held_y.shape[0]
    width, half = wg_hbm.shape
    rank = bd_ref.shape[1]
    rows = n_ref.shape[0]
    place, part = lax.axis_index("dp"), lax.axis_index("tensor")
    theirs = (step >= 1) & (step <= tiles_each)
    number_t = their_tile(step, tiles_each)
    tile = HIDDEN_TILE
    tiles = pl.cdiv(half, tile)
    lap = tiles * tile - half
    a_gate = copies.shape[0] - 3 * width - 6 * half
    a_up = a_gate + width + 2 * half
    a_down = a_up + width + 2 * half
    b_down = a_down + 2 * half

    def loads(number):
        at = pl.multiple_of(jnp.minimum(number * tile, half - tile), LANES)
        to = pl.multiple_of(number * tile, tile)
        here, there = pl.ds(at, tile), pl.ds(to, tile)

        def own_half(base):
            return copies.at[pl.ds(pl.multiple_of(base + part * half + at, 16), tile), :]

        top, side = pl.ds(0, width), pl.ds(width, rank)
        pairs = [
            (wg_hbm.at[:, here], wga.at[top, there]),
            (wu_hbm.at[:, here], wua.at[top, there]),
            (wd_hbm.at[here, :], wda.at[there, top]),
            (own_half(a_gate + width), raw.at[0, there, :]),
            (own_half(a_up + width), raw.at[1, there, :]),
            (own_half(a_down), wda.at[there, side]),
        ]
        return [
            pltpu.make_async_copy(source, target, wsem.at[number, at])
            for at, (source, target) in enumerate(pairs)
        ]

    def swap(source, target, sends, recvs, number):
        return pltpu.make_async_remote_copy(
            src_ref=source,
            dst_ref=target.at[number],
            send_sem=sends.at[number],
            recv_sem=recvs.at[number],
            device_id=(place, 1 - part),
            device_id_type=MESH,
        )

    def send_n(number):
        return swap(n_hbm.at[pl.ds(number * rows, rows), :], n_got, nsend, nrecv, number)

    def send_d(number):
        return swap(held_d.at[number], d_got, dsend, drecv, number)

    def send_y(number):
        return swap(held_y.at[number], y_got, ysend, yrecv, number)

    thin_loads = [
        pltpu.make_async_copy(copies.at[pl.ds(base, width), :], target, gsem.at[at])
        for at, (base, target) in enumerate(
            (
                (a_gate, ap_ref.at[:, pl.ds(0, rank)]),
                (a_up, ap_ref.at[:, pl.ds(rank, rank)]),
                (b_down, bd_ref),
            )
        )
    ]

    @pl.when(step == 0)
    def _():
        for copy in thin_loads:
            copy.start()
        for number in range(tiles):
            for copy in loads(number):
                copy.start()
        barrier = pltpu.get_barrier_semaphore()
        pl.semaphore_signal(barrier, inc=1, device_id=(place, 1 - part), device_id_type=MESH)
        pl.semaphore_wait(barrier, 1)
        for number in range(tiles_each):
            send_n(number).start()
        grads[...] = jnp.zeros_like(grads)
        extras[...] = jnp.zeros_like(extras)
        for copy in thin_loads:
            copy.wait()

    def prepare(normed, dy, adapter):
        mask = rank_mask(adapter, rank)
        mask_s[...] = mask
        lows = nn(normed, ap_ref[...])
        xg[:, :width] = normed
        xu[:, :width] = normed
        xg[:, width:] = (lows[:, :rank] * mask).astype(BF16)
        xu[:, width:] = (lows[:, rank:] * mask).astype(BF16)
        dya[:, :width] = dy
        dya[:, width:] = (ADAPTER_SCALE * nn(dy, bd_ref[...]) * mask).astype(BF16)

    @pl.when(jnp.logical_not(theirs))
    def _():
        prepare(n_ref[...], dy_ref[...], meta_ref[:, 0:1])

    @pl.when(theirs)
    def _():
        send_n(number_t).wait_recv()
        prepare(n_got[number_t], dyt_ref[...], metat_ref[:, 0:1])

    yacc[...] = jnp.zeros_like(yacc)
    dacc[...] = jnp.zeros_like(dacc)

    def hidden(number, carry):
        span = pl.ds(pl.multiple_of(number * tile, tile), tile)

        @pl.when(step == 0)
        def _():
            for copy in loads(number):
                copy.wait()
            for at, target in enumerate((wga, wua)):
                turned = jnp.transpose(raw[at, span, :].astype(F32) * ADAPTER_SCALE)
                target[width:, span] = turned.astype(BF16)
            if lap:

                @pl.when(number == tiles - 1)
                def _():
                    edge = slice((tiles - 1) * tile, (tiles - 1) * tile + lap)
                    wga[:, edge] = jnp.zeros((width + rank, lap), BF16)
                    wua[:, edge] = jnp.zeros((width + rank, lap), BF16)
                    wda[edge, :] = jnp.zeros((lap, width + rank), BF16)

        gate = nn(xg[...], wga[:, span])
        up = nn(xu[...], wua[:, span])
        dhid = nt(dya[...], wda[span, :])
        sig = 1.0 / (1.0 + jnp.exp(-gate))
        silu = gate * sig
        hid = (silu * up).astype(BF16)
        dg = (dhid * up * (sig * (1.0 + gate * (1.0 - sig)))).astype(BF16)
        du = (dhid * silu).astype(BF16)
        yacc[...] += nn(hid, wda[span, :])
        dga = nt(dg, wga[:, span])
        dua = nt(du, wua[:, span])
        dacc[:, :width] += dga[:, :width] + dua[:, :width]
        dacc[:, width : width + rank] += dga[:, width:]
        dacc[:, width + rank :] += dua[:, width:]
        grads[0, span, :] += ADAPTER_SCALE * tn(dg, xg[:, width:])
        grads[1, span, :] += ADAPTER_SCALE * tn(du, xu[:, width:])
        grads[2, span, :] += tn(hid, dya[:, width:])
        return carry

    lax.fori_loop(0, tiles, hidden, 0)
    mask = mask_s[...]
    low = (yacc[:, width:] * mask).astype(BF16)
    result = yacc[:, :width] + ADAPTER_SCALE * nt(low, bd_ref[...])
    back = (dacc[:, width:] * jnp.concatenate([mask, mask], axis=1)).astype(BF16)
    change = dacc[:, :width] + nt(back, ap_ref[...])
    pair = tn(xg[:, :width], back)
    extras[0] += pair[:, :rank]
    extras[1] += pair[:, rank:]
    extras[2] += ADAPTER_SCALE * tn(dya[:, :width], low)

    @pl.when(jnp.logical_not(theirs))
    def _():
        y_ref[...] = result
        d_ref[...] = change

    @pl.when(theirs)
    def _():
        held_d[number_t] = change.astype(BF16)
        send_d(number_t).start()

        @pl.when(number_t < swapped)
        def _():
            held_y[number_t] = result.astype(BF16)

        @pl.when(number_t >= swapped)
        def _():
            last_ref[number_t - swapped] = result.astype(BF16)

        @pl.when(number_t == tiles_each - 1)
        def _():
            for number in range(swapped):
                send_y(number).start()

    @pl.when(step == steps - 1)
    def _():
        last = (tiles - 1) * tile
        for at in range(3):
            packed[at, :last, :] = grads[at, :last, :].astype(BF16)
            packed[at, last:half, :] = grads[at, last + lap : tiles * tile, :].astype(BF16)
            packed[at, half:, :] = extras[at].astype(BF16)
        blank[...] = jnp.zeros_like(blank)
        moves = []
        for at, base in enumerate((a_gate + width, a_up + width, a_down)):
            mine = pl.multiple_of(base + part * half, 16)
            other = pl.multiple_of(base + (1 - part) * half, 16)
            moves.append((packed.at[at, pl.ds(0, half), :], flat_ref.at[pl.ds(mine, half), :]))
            moves.append((blank, flat_ref.at[pl.ds(other, half), :]))
        for at, base in enumerate((a_gate, a_up, b_down)):
            moves.append((packed.at[at, pl.ds(half, width), :], flat_ref.at[pl.ds(base, width), :]))
        moves = [
            pltpu.make_async_copy(source, target, gsem.at[at])
            for at, (source, target) in enumerate(moves)
        ]
        for copy in moves:
            copy.start()
        for copy in moves:
            copy.wait()
        for number in range(tiles_each):
            send_n(number).wait_send()
            send_d(number).wait_send()
            send_d(number).wait_recv()
        for number in range(swapped):
            send_y(number).wait_send()
            send_y(number).wait_recv()


def feed(n2, dy, dy_theirs, meta, meta_theirs, w_gate, w_up, w_down, copies):
    rows, width = n2.shape
    half = w_down.shape[0]
    total, rank = copies.shape
    tile = ROW_TILE
    count = rows // tile
    tiles = pl.cdiv(half, HIDDEN_TILE)
    padded = tiles * HIDDEN_TILE
    anywhere = pl.BlockSpec(memory_space=pl.ANY)
    wide, deep = width + rank, width + 2 * rank

    def own_rows(array):
        return pl.BlockSpec((tile, array.shape[1]), lambda i: (own_tile(i, count), 0))

    def their_rows(array):
        return pl.BlockSpec((tile, array.shape[1]), lambda i: (their_tile(i, count), 0))

    dma = pltpu.SemaphoreType.DMA
    outs = [
        jax.ShapeDtypeStruct((rows, width), F32),
        jax.ShapeDtypeStruct((rows, width), F32),
        jax.ShapeDtypeStruct((SWAPPED, tile, width), BF16),
        jax.ShapeDtypeStruct((count, tile, width), BF16),
        jax.ShapeDtypeStruct((count - SWAPPED, tile, width), BF16),
        jax.ShapeDtypeStruct((total + FLAT_PAD, rank), BF16),
    ]
    return pl.pallas_call(
        feed_kernel,
        grid=(2 * count,),
        in_specs=[
            own_rows(n2), anywhere, own_rows(dy), their_rows(dy_theirs), own_rows(meta),
            their_rows(meta_theirs),
        ]
        + [anywhere] * 4,
        out_specs=[own_rows(outs[0]), own_rows(outs[1]), anywhere, anywhere, whole(outs[4]), anywhere],
        out_shape=outs,
        scratch_shapes=[
            pltpu.VMEM((wide, padded), BF16),
            pltpu.VMEM((wide, padded), BF16),
            pltpu.VMEM((padded, wide), BF16),
            pltpu.VMEM((2, padded, rank), BF16),
            pltpu.VMEM((3, padded, rank), F32),
            pltpu.VMEM((3, width, rank), F32),
            pltpu.VMEM((tile, wide), BF16),
            pltpu.VMEM((tile, wide), BF16),
            pltpu.VMEM((tile, wide), BF16),
            pltpu.VMEM((tile, wide), F32),
            pltpu.VMEM((tile, deep), F32),
            pltpu.VMEM((tile, rank), F32),
            pltpu.VMEM((count, tile, width), BF16),
            pltpu.VMEM((count, tile, width), BF16),
            pltpu.VMEM((SWAPPED, tile, width), BF16),
            pltpu.VMEM((3, half + width, rank), BF16),
            pltpu.VMEM((half, rank), BF16),
            pltpu.VMEM((width, 2 * rank), BF16),
            pltpu.VMEM((width, rank), BF16),
            dma((tiles, 6)),
            dma((9,)),
            dma((count,)),
            dma((count,)),
            dma((count,)),
            dma((count,)),
            dma((SWAPPED,)),
            dma((SWAPPED,)),
        ],
        compiler_params=params(collective_id=1, has_side_effects=True),
        cost_estimate=cost(4 * rows * half * (6 * width + 9 * rank), 40e6),
        name="feed",
    )(
        n2, n2, dy, dy_theirs, meta, meta_theirs, w_gate, w_up, w_down, copies
    )


def tail_kernel(plan, early, key_width, direct, *refs):
    sources = refs[:9]
    other_ref, w_hbm, b_ref, gain_ref, flat_ref, out_grad_ref, kept_hbm = refs[9:16]
    peers = plan.boxes(0) - 1
    gots_hbm = refs[16 : 16 + peers]
    refs = refs[16 + peers :]
    out_ref, sum_ref = refs[:2]
    held = refs[2:11]
    w, grads, dxs, acc_a, acc_b, outbox, last_in, got_s, kept, gots, *rest = refs[11:]
    inboxes = rest[:-13]
    (
        load_sem, grad_sem, dsend, drecv, fsend, frecv, rsend, rrecv, zrecv, keep_sem, ksend, krecv,
        hsem,
    ) = rest[-13:]
    gq_s, own_s, x_s, n_s, z_s, dy1_s, meta_s, cos_s, sin_s = held
    place, part = lax.axis_index("dp"), lax.axis_index("tensor")
    devices, plane, axes = plan.devices, plan.plane, plan.axes
    depth, inside = place // plane, lax.rem(place, plane)
    count = len(axes)
    tile = x_s.shape[1]
    rank = b_ref.shape[1]
    width = x_s.shape[2]
    qw, kw = gq_s.shape[2], key_width
    over = (place, 1 - part)

    def layer(hop):
        return lax.rem(depth + hop, PLANES)

    def turn_of(number):
        return lax.rem(number + 2, PLANES)

    def rows_at(number):
        return pl.ds(pl.multiple_of(layer(turn_of(number)) * tile, 16), tile)

    def tile_loads(number):
        return [
            pltpu.make_async_copy(
                source.at[rows_at(number), :], target.at[number], load_sem.at[number, which]
            )
            for which, (source, target) in enumerate(zip(sources, held))
        ]

    sums_loads = [
        pltpu.make_async_copy(kept_hbm, kept, grad_sem.at[3]),
    ] + [
        pltpu.make_async_copy(got, gots.at[peer], grad_sem.at[4 + peer])
        for peer, got in enumerate(gots_hbm)
    ]
    w_load = pltpu.make_async_copy(w_hbm, w, grad_sem.at[0])
    middle = out_grad_ref.shape[0]
    late_rows = grads.shape[0] - early - middle
    grad_loads = [
        pltpu.make_async_copy(out_grad_ref, grads.at[pl.ds(early, middle), :], grad_sem.at[1]),
        pltpu.make_async_copy(
            flat_ref.at[pl.ds(early + middle, late_rows), :],
            grads.at[pl.ds(early + middle, late_rows), :],
            grad_sem.at[2],
        ),
    ]
    for copy in sums_loads + [w_load]:
        copy.start()
    for number in range(PLANES):
        for copy in tile_loads(number):
            copy.start()
    for copy in grad_loads:
        copy.start()

    barrier = pltpu.get_barrier_semaphore()
    for k in range(1, devices):
        pl.semaphore_signal(
            barrier, inc=1, device_id=(lax.rem(place + k, devices), part), device_id_type=MESH
        )
    pl.semaphore_signal(barrier, inc=1, device_id=over, device_id_type=MESH)
    pl.semaphore_wait(barrier, devices)

    def key_copy(number):
        return pltpu.make_async_remote_copy(
            src_ref=other_ref.at[rows_at(number), :],
            dst_ref=got_s.at[number],
            send_sem=ksend.at[number],
            recv_sem=krecv.at[number],
            device_id=over,
            device_id_type=MESH,
        )

    for number in range(PLANES):
        key_copy(number).start()

    bases = []
    cursor = 0
    for stage in range(count):
        bases.append(cursor)
        cursor += plan.boxes(stage)

    def window_sum(stages, zz, at, side):
        if zz:
            total = kept[zz - 1]
            for peer in range(peers):
                total = total + gots[peer, zz - 1].astype(F32)
            return total
        total = grads[plan.span(0, at, side), :].astype(F32)
        for stage in range(stages):
            total = total + inboxes[stage][plan.box(stage, at, side)].astype(F32)
        return total

    def take(stages, zz, at, side):
        for stage in range(0 if zz else stages):
            index = plan.box(stage, at, side)
            pltpu.make_async_remote_copy(
                src_ref=inboxes[stage].at[index],
                dst_ref=inboxes[stage].at[index],
                send_sem=rsend.at[0],
                recv_sem=rrecv.at[bases[stage] + index],
                device_id=over,
                device_id_type=MESH,
            ).wait_recv()

    sent = []
    posted = [0]

    def pass_on(stage, source_of):
        partner = flip(place, part, [axes[stage]])
        for at, side in plan.leaving(stage, inside, part):
            index = plan.box(stage, at, side)
            copy = pltpu.make_async_remote_copy(
                src_ref=source_of(at, side),
                dst_ref=inboxes[stage].at[index],
                send_sem=rsend.at[len(sent)],
                recv_sem=rrecv.at[bases[stage] + index],
                device_id=partner,
                device_id_type=MESH,
            )
            copy.start()
            sent.append(copy)

    def post(total):
        slot = posted[0]
        posted[0] += 1
        outbox[slot] = total.astype(BF16)
        return outbox.at[slot]

    def stage_sends(stage):
        def source_of(at, side):
            take(stage, 0, at, side)
            return post(window_sum(stage, 0, at, side))

        pass_on(stage, source_of)

    zfirst = sum(plan.boxes(stage) for stage in range(count))
    zsends = []

    def plane_copy(slot, box, recv, number, zz):
        return pltpu.make_async_remote_copy(
            src_ref=outbox.at[slot],
            dst_ref=last_in.at[box],
            send_sem=rsend.at[zfirst + number],
            recv_sem=zrecv.at[recv],
            device_id=(zz * plane + inside, part),
            device_id_type=MESH,
        )

    def near(zz):
        slot = posted[0]
        posted[0] += 1
        copy = plane_copy(slot, zz, zz, zz, xor_bit(depth, 0))
        moving = lax.rem(depth, 2) != zz % 2
        zsends.append((moving, copy))
        take(count, zz, inside, part)

        @pl.when(moving)
        def _():
            outbox[slot] = window_sum(count, zz, inside, part).astype(BF16)
            copy.start()

        return copy

    def far(zz, came):
        slot = posted[0]
        posted[0] += 1
        copy = plane_copy(slot, PLANES, PLANES, PLANES + zz, zz)
        staying = lax.rem(depth, 2) == zz % 2
        moving = staying & (depth != zz)
        zsends.append((moving, copy))

        @pl.when(staying)
        def _():
            came.wait_recv()
            total = window_sum(count, zz, inside, part) + last_in[zz].astype(F32)

            @pl.when(depth == zz)
            def _():
                sum_ref[...] = total

            @pl.when(depth != zz)
            def _():
                outbox[slot] = total.astype(BF16)
                copy.start()

    for copy in sums_loads:
        copy.wait()
    came = [near(zz) for zz in range(1, PLANES)]

    def step_at(step):
        return lax.rem(inside + step, plane)

    acc_a[...] = jnp.zeros_like(acc_a)
    acc_b[...] = jnp.zeros_like(acc_b)
    w_load.wait()

    def piece_copy(number, step, where, target):
        return pltpu.make_async_remote_copy(
            src_ref=dxs.at[number, step_at(step)],
            dst_ref=target,
            send_sem=dsend.at[number, step],
            recv_sem=drecv.at[place],
            device_id=where,
            device_id_type=MESH,
        )

    def one_tile(number, carry):
        for copy in tile_loads(number):
            copy.wait()
        key_copy(number).wait_recv()
        mask = rank_mask(meta_s[number][:, 0:1], rank)
        both = own_s[number].astype(F32) + got_s[number].astype(F32)
        cos, sin = cos_s[number], sin_s[number]
        dk = both[:, :kw]
        gq = gq_s[number]
        gk = (dk * cos - turn(dk) * sin).astype(BF16)
        gv = both[:, kw:].astype(BF16)
        at_k, at_v = 2 * width + qw, 3 * width + qw + kw
        b_parts = (
            b_ref[width : width + qw, :],
            b_ref[at_k : at_k + kw, :],
            b_ref[at_v : at_v + kw, :],
        )
        backs = [
            (ADAPTER_SCALE * nn(g, b) * mask).astype(BF16) for g, b in zip((gq, gk, gv), b_parts)
        ]
        dn = nn(jnp.concatenate([gq, gk, gv] + backs, axis=1), w[...])
        values = x_s[number].astype(F32)
        dx = (dy1_s[number] + norm_back(values, gain_ref[...], dn)).astype(BF16)
        acc_a[...] += tn(n_s[number], jnp.concatenate(backs, axis=1))
        low = z_s[number]
        acc_b[:qw, :] += tn(gq, low[:, :rank])
        acc_b[qw : qw + kw, :] += tn(gk, low[:, rank : 2 * rank])
        acc_b[qw + kw :, :] += tn(gv, low[:, 2 * rank :])
        turn_now = turn_of(number)
        if not direct:
            dxs[number] = dx
            copy = pltpu.make_async_copy(
                dxs.at[number], out_ref.at[rows_at(number), :], keep_sem.at[0]
            )
            copy.start()
            copy.wait()
            return carry
        dxs[number] = dx.reshape(dxs.shape[1:])
        for step in range(plane):
            target = layer(turn_now) * plane + step_at(step)
            if step > 0:
                piece_copy(number, step, (target, part), out_ref.at[place, part]).start()
                continue

            @pl.when(turn_now == 0)
            def _():
                pltpu.make_async_copy(
                    dxs.at[number, inside], out_ref.at[place, part], keep_sem.at[0]
                ).start()

            @pl.when(turn_now > 0)
            def _():
                piece_copy(number, 0, (target, part), out_ref.at[place, part]).start()

        return carry

    lax.fori_loop(0, PLANES, one_tile, 0)
    for copy in grad_loads:
        copy.wait()

    at = 0
    for order, size in enumerate((qw, kw, kw)):
        grads[at : at + width, :] = acc_a[:, order * rank : (order + 1) * rank].astype(BF16)
        base = (0, qw, qw + kw)[order]
        grads[at + width : at + width + size, :] = (
            ADAPTER_SCALE * acc_b[base : base + size, :]
        ).astype(BF16)
        at += width + size
    pass_on(0, lambda at, side: grads.at[plan.span(0, at, side), :])

    forwards = []

    def forward(back):
        for step in range(plane):
            at = layer(back) * plane + step_at(step)
            if step > 0 or back > 0:
                pltpu.make_async_remote_copy(
                    src_ref=out_ref.at[at, part],
                    dst_ref=out_ref.at[at, part],
                    send_sem=hsem.at[0],
                    recv_sem=drecv.at[at],
                    device_id=over,
                    device_id_type=MESH,
                ).wait_recv()
            else:
                pltpu.make_async_copy(
                    out_ref.at[place, part], out_ref.at[place, part], keep_sem.at[0]
                ).wait()
            copy = forward_copy(at, part, len(forwards))
            copy.start()
            forwards.append(copy)

    def forward_copy(source, side, number):
        return pltpu.make_async_remote_copy(
            src_ref=out_ref.at[source, side],
            dst_ref=out_ref.at[source, side],
            send_sem=fsend.at[number],
            recv_sem=frecv.at[source],
            device_id=over,
            device_id_type=MESH,
        )

    stage_sends(1)
    if direct:
        forward(0)
    for zz in range(1, PLANES):
        far(zz, came[zz - 1])
    if direct:
        forward(2)
    for stage in range(2, count):
        stage_sends(stage)
    if direct:
        forward(1)
    late = near(0)
    if direct:
        forward(3)
    far(0, late)
    plane_copy(0, PLANES, PLANES, 0, depth).wait_recv()
    sum_ref[...] += last_in[PLANES].astype(F32)

    if direct:
        for source in range(devices):
            forward_copy(source, 1 - part, 0).wait_recv()
        for copy in forwards:
            copy.wait_send()
        for number in range(PLANES):
            for step in range(plane):
                if step == 0 and (number + 2) % PLANES == 0:
                    continue
                piece_copy(number, step, over, out_ref.at[place, part]).wait_send()
    for copy in sent:
        copy.wait_send()
    for moving, copy in zsends:

        @pl.when(moving)
        def _():
            copy.wait_send()

    for number in range(PLANES):
        key_copy(number).wait_send()


def tail(
    devices, own_rows, early, rows_in, other, w_cat, b_rows, gain, flat, grad_out, kept, gots,
    key_width, piece,
):
    gq, _, x = rows_in[:3]
    rows, width = x.shape
    plan = Windows(devices, own_rows)
    plane, count, window = plan.plane, len(plan.axes), plan.rows
    rank = flat.shape[1]
    tile = rows // PLANES
    direct = piece % 16 == 0
    anywhere = pl.BlockSpec(memory_space=pl.ANY)
    boxes = [plan.boxes(stage) for stage in range(count)]
    peers = boxes[0] - 1
    sends = sum(boxes) + 2 * PLANES
    qw = gq.shape[1]
    first_plane = 16 * (((2 * plane - 1) * own_rows) // 16) + window
    dma = pltpu.SemaphoreType.DMA
    if direct:
        shape = (devices, 2, piece, width)
        held = (plane, piece, width)
    else:
        shape = (rows, width)
        held = (tile, width)
    outs = [jax.ShapeDtypeStruct(shape, BF16)]
    outs.append(jax.ShapeDtypeStruct((window, rank), F32))
    scratch = [pltpu.VMEM((PLANES, tile, a.shape[1]), a.dtype) for a in rows_in]
    scratch += [
        pltpu.VMEM(w_cat.shape, BF16),
        pltpu.VMEM((first_plane, rank), BF16),
        pltpu.VMEM((PLANES,) + held, BF16),
        pltpu.VMEM((width, 3 * rank), F32),
        pltpu.VMEM((qw + 2 * key_width, rank), F32),
        pltpu.VMEM((sends, window, rank), BF16),
        pltpu.VMEM((PLANES + 1, window, rank), BF16),
        pltpu.VMEM((PLANES, tile, other.shape[1]), BF16),
        pltpu.VMEM(kept.shape, F32),
        pltpu.VMEM((peers,) + gots[0].shape, BF16),
    ]
    scratch += [pltpu.VMEM((size, window, rank), BF16) for size in boxes]
    scratch += [
        dma((PLANES, len(rows_in))),
        dma((4 + peers,)),
        dma((PLANES, plane)),
        dma((devices,)),
        dma((devices,)),
        dma((devices,)),
        dma((sends,)),
        dma((sum(boxes),)),
        dma((PLANES + 1,)),
        dma((1,)),
        dma((PLANES,)),
        dma((PLANES,)),
        dma((1,)),
    ]
    return pl.pallas_call(
        functools.partial(tail_kernel, plan, early, key_width, direct),
        grid=(1,),
        in_specs=[anywhere] * 11
        + [pl.BlockSpec((early, rank), lambda i: (0, 0)), whole(gain)]
        + [anywhere] * (3 + peers),
        out_specs=[anywhere, whole(outs[1])],
        out_shape=outs,
        scratch_shapes=scratch,
        compiler_params=params(collective_id=2, has_side_effects=True),
        cost_estimate=cost(2 * rows * width * 2900, 200e6),
        name="tail",
    )(*rows_in, other, w_cat, b_rows, gain, flat, grad_out, kept, *gots)


def whole_part(values, size):
    return jnp.floor((values + 0.5) * (1.0 / size))


def tables_kernel(
    parts, each, part_ref, lengths_ref, ids_ref, order_ref, freq_ref,
    turns_ref, sines_ref, own_ref, other_ref, sorted_ref, rows_ref, column_ref, column_row_ref,
    bounds_ref,
):
    total = order_ref.shape[1]
    local = total // parts
    piece = each // parts
    block = 256
    order = jnp.broadcast_to(order_ref[0:1, :].astype(F32), (8, total))
    group = whole_part(order, each)
    rest = order - group * each
    part_at = whole_part(rest, piece)
    own = part_at == part_ref[0].astype(F32)
    slot = group * piece + (rest - part_at * piece)
    column = jnp.where(own, slot, slot + local)
    lanes = lane_iota((8, total))
    upto = jnp.where(own, 1.0, 0.0)
    shift = 1
    while shift < total:
        upto = upto + jnp.where(lanes >= shift, pltpu.roll(upto, shift, 1), 0.0)
        shift *= 2
    rank = jnp.where(own, upto - 1.0, 2.0 * total)
    place = lanes.astype(F32)
    number = row_iota((8, total))
    column_row_ref[...] = column.astype(I32)
    turned = jnp.transpose(jnp.where(number == 0, column, rank))
    column_ref[...] = turned.astype(I32)

    def halves(values):
        high = whole_part(values, 256)
        return high, values - high * 256

    place_high, place_low = halves(place)
    slot_high, slot_low = halves(slot)
    left = jnp.where(
        number == 0, place_high, jnp.where(number == 1, place_low, jnp.where(number == 2, slot_high, slot_low))
    ).astype(BF16)

    def chosen_by(keys, start):
        hit = keys == (start + lane_iota((total, block))).astype(F32)
        found = nn(left, jnp.where(hit, 1.0, 0.0).astype(BF16))
        return found[0:1] * 256 + found[1:2], found[2:3] * 256 + found[3:4]

    def sequence(places):
        first = jnp.zeros_like(places)
        adapter = jnp.zeros_like(places) + ids_ref[0].astype(F32)
        start = lengths_ref[0].astype(F32)
        for at in range(1, lengths_ref.shape[0]):
            inside = places >= start
            first = jnp.where(inside, start, first)
            adapter = jnp.where(inside, ids_ref[at].astype(F32), adapter)
            start = start + lengths_ref[at].astype(F32)
        return first, adapter

    def rope(position, at):
        angles = jnp.broadcast_to(position, freq_ref.shape[:1] + position.shape[1:]) * freq_ref[:, 0:1]
        turns_ref[:, at : at + block] = jnp.cos(angles)
        sines_ref[:, at : at + block] = jnp.sin(angles)

    def as_columns(*rows):
        index = row_iota((8, block))
        out = jnp.zeros((8, block), F32)
        for at, row in enumerate(rows):
            out = jnp.where(index == at, jnp.broadcast_to(row, (8, block)), out)
        return out

    for start in range(0, total, block):
        places, _ = chosen_by(turned[:, 0:1], start)
        first, adapter = sequence(places)
        columns = jnp.transpose(as_columns(adapter)).astype(I32)
        if start < local:
            rope(places - first, start)
            own_ref[start : start + block, :] = columns
        else:
            other_ref[start - local : start - local + block, :] = columns
    for start in range(0, local, block):
        places, slots = chosen_by(turned[:, 1:2], start)
        first, _ = sequence(places)
        rope(places - first, local + start)
        rows = as_columns(slots, first, places)
        rows_ref[:, start : start + block] = rows.astype(I32)
        sorted_ref[start : start + block, :] = jnp.transpose(rows).astype(I32)
        at_lane = lane_iota((1, block))
        for tile in range(0, block, QUERY_TILE):
            low = jnp.max(jnp.where(at_lane == tile, first, 0.0))
            high = jnp.max(jnp.where(at_lane == tile + QUERY_TILE - 1, places, 0.0))
            number_at = (start + tile) // QUERY_TILE
            bounds_ref[0, number_at] = low.astype(I32) // KEY_TILE
            bounds_ref[1, number_at] = high.astype(I32) // KEY_TILE + 1


def row_tables(order, lengths, adapter_ids, part, parts, each):
    total = order.shape[1]
    local = total // parts
    freq_index = jnp.arange(HEAD // 2, dtype=F32)
    freq = jnp.power(jnp.float32(ROPE_BASE), -2.0 * freq_index / HEAD)
    freq = jnp.broadcast_to(freq[:, None], (HEAD // 2, LANES))
    shapes = [
        ((HEAD // 2, total), F32),
        ((HEAD // 2, total), F32),
        ((local, 8), I32),
        ((local, 8), I32),
        ((local, 8), I32),
        ((8, local), I32),
        ((total, 8), I32),
        ((8, total), I32),
        ((2, local // QUERY_TILE), I32),
    ]
    outs = [jax.ShapeDtypeStruct(shape, kind) for shape, kind in shapes]
    return pl.pallas_call(
        functools.partial(tables_kernel, parts, each),
        grid_spec=pltpu.PrefetchScalarGridSpec(
            num_scalar_prefetch=3,
            grid=(1,),
            in_specs=[whole(order), whole(freq)],
            out_specs=[whole(o) for o in outs[:-1]] + [pl.BlockSpec(memory_space=pltpu.SMEM)],
        ),
        out_shape=outs,
        compiler_params=params(),
        cost_estimate=cost(1e8, 4e6),
        name="tables",
    )(jnp.reshape(part, (1,)).astype(I32), lengths[0], adapter_ids[0], order, freq)


def per_device(
    tokens, cotangent, order, lengths, adapter_ids, norm_gains, w_query, w_key, w_value,
    b_query, b_key, b_value, w_out, w_gate, w_up, w_down, adapters, first_moment, second_moment,
):
    parts = lax.axis_size("tensor")
    part = lax.axis_index("tensor")
    devices = lax.axis_size("dp")
    place = lax.axis_index("dp")
    total, width = tokens.shape
    each = total // devices
    piece = each // parts
    local = total // parts
    rank = adapters.shape[1]
    own_rows = adapters.shape[0]
    swap = [(i, parts - 1 - i) for i in range(parts)]
    first_part = part == 0

    def across(values):
        return lax.ppermute(values, "tensor", swap)

    def pair(mine, theirs, axis):
        return jnp.concatenate(
            [jnp.where(first_part, mine, theirs), jnp.where(first_part, theirs, mine)], axis=axis
        )

    def give_back(values):
        got = lax.all_to_all(
            values.reshape(devices, piece, width), "dp", split_axis=0, concat_axis=0, tiled=True
        )
        theirs = across(got)
        return pair(got[:, None], theirs[:, None], 1).reshape(total, width)

    qh, kh, half = w_query.shape[1], w_key.shape[1], w_gate.shape[1]
    qw, kw, hidden = parts * qh, parts * kh, parts * half
    heads, kv_heads = qw // HEAD, kw // HEAD
    unit = 4 if own_rows % 4 == 0 else 1
    bias = jnp.concatenate([b_query, b_key, b_value, jnp.zeros((width - qh - 2 * kh,), BF16)])
    mine = (w_query.T, w_key.T, w_value.T, jnp.broadcast_to(bias[None], (16, width)))
    moved, copies, *theirs = front(
        tokens.reshape(devices, parts, piece, width),
        adapters.astype(BF16).reshape(own_rows // unit, unit, rank),
        *[a.reshape(2, a.shape[0] // 2, width) for a in mine],
        devices,
    )
    theirs = [a.reshape(b.shape) for a, b in zip(theirs, mine)]
    cotangent, moved = lax.optimization_barrier((cotangent, moved))
    moved = moved.reshape(local, width)
    dy_all = lax.all_to_all(
        cotangent.reshape(devices, each, width), "dp", split_axis=0, concat_axis=0, tiled=True
    ).reshape(devices, parts, piece, width)

    def half_of(which):
        return lax.dynamic_index_in_dim(dy_all, which, 1, keepdims=False).reshape(local, width)

    dy = half_of(part)
    dy_theirs = half_of(parts - 1 - part)

    early = 3 * width + qw + 2 * kw
    flat = copies.reshape(2 * devices * own_rows, rank)
    (
        turns, sines, meta_own, meta_other, meta_sorted, meta_rows, column, column_row, bounds,
    ) = row_tables(order, lengths, adapter_ids, part, parts, each)
    gain_one = norm_gains[0:1].astype(F32)
    gain_two = norm_gains[1:2].astype(F32)
    side = jnp.reshape(part, (1,)).astype(I32)

    n1, q, kv, z, cos, sin, w_cat, other_kv = project(
        moved, meta_own, turns, sines, gain_one, mine, theirs, flat, qw, kw
    )
    other_kv = other_kv.reshape(kv.shape)
    w_out, kv = lax.optimization_barrier((w_out, kv))
    their_out = across(w_out)
    q_sorted, o_sorted, logs, merged, o = attend(
        bounds, q, meta_sorted, meta_rows, kv, other_kv, column, heads, kv_heads
    )
    y1, n2, z_out, w_out_cat = middle(
        side, o, moved, meta_own, w_out, their_out, gain_two, flat, early
    )
    y_own, d_own, y_got, d_got, y_last, flat_grads = feed(
        n2, dy, dy_theirs, meta_own, meta_other, w_gate, w_up, w_down, flat
    )
    y_got = jnp.concatenate([y_got, across(y_last)], axis=0).reshape(local, width)
    dy1, dar, grad_out, kept_sums, *on_sums = middle_back(
        devices, own_rows, d_own, d_got.reshape(local, width), y1, dy, o, z_out, meta_own, flat,
        early + qw, w_out_cat, gain_two, flat_grads,
    )
    got_sums = []
    for number, chosen in enumerate(subsets(Windows(devices, own_rows).axes[1:])):
        if number:
            moves = [
                (2 * at + side, 2 * to + over)
                for at in range(devices)
                for side in range(parts)
                for to, over in [flip_fixed(at, side, chosen)]
            ]
            got_sums.append(lax.ppermute(on_sums[number - 1], ("dp", "tensor"), moves))
    layer_rows = (y1 + (y_own + y_got.astype(F32))).astype(BF16).reshape(devices, 1, piece, width)
    layer_rows = jnp.broadcast_to(layer_rows, (devices, parts, piece, width))
    layer_rows, dar = lax.optimization_barrier((layer_rows, dar))
    layer_out = lax.all_to_all(
        layer_rows.reshape(devices * parts, piece, width),
        ("dp", "tensor"), split_axis=0, concat_axis=0, tiled=True,
    ).reshape(total, width)
    gq, dkv_own, dkv_other = attend_back(
        bounds, q_sorted, dar, o_sorted, logs, meta_sorted, meta_rows, turns, sines,
        merged, column_row, heads, kv_heads,
    )
    dx, window = tail(
        devices, own_rows, early,
        (gq, dkv_own, moved, n1, z, dy1, meta_own, cos, sin),
        dkv_other, w_cat, flat, gain_one, flat_grads, grad_out, kept_sums,
        got_sums, kw, piece,
    )
    if dx.ndim == 4:
        input_grad = dx.reshape(total, width)
    else:
        input_grad = give_back(dx)
    offset = lax.rem((2 * place + part) * own_rows, 16)
    reduced = lax.dynamic_slice_in_dim(window, offset, own_rows, 0)
    moment_one = BETA_ONE * first_moment + (1.0 - BETA_ONE) * reduced
    moment_two = BETA_TWO * second_moment + (1.0 - BETA_TWO) * reduced * reduced
    corrected_one = moment_one / (1.0 - BETA_ONE**STEP)
    corrected_two = moment_two / (1.0 - BETA_TWO**STEP)
    updated = adapters - LEARN_RATE * (
        corrected_one / (jnp.sqrt(corrected_two) + ADAM_EPS) + WEIGHT_DECAY * adapters
    )
    return (
        layer_out,
        input_grad,
        reduced,
        moment_one,
        moment_two,
        updated,
        updated.astype(BF16),
    )


def solution(mesh):
    both = P(("dp", "tensor"), None)
    rows = P("dp", None)
    return jax.shard_map(
        per_device,
        mesh=mesh,
        in_specs=(rows, rows, rows, rows, rows, P())
        + (P(None, "tensor"),) * 3
        + (P("tensor"),) * 3
        + (P("tensor", None), P(None, "tensor"), P(None, "tensor"), P("tensor", None))
        + (both,) * 3,
        out_specs=(rows, rows) + (both,) * 5,
        check_vma=False,
    )
```

```python
import functools

import jax
import jax.numpy as jnp
from jax import lax
from jax.experimental import pallas as pl
from jax.experimental.pallas import tpu as pltpu
from jax.sharding import PartitionSpec as P

HEAD = 64
RANK = 16
STEP = 3

ADAPTER_SCALE = 2.0
NORM_EPS = 1e-06
ROPE_BASE = 1000000.0
BETA_ONE = 0.5
BETA_TWO = 0.6
LEARN_RATE = 0.04
WEIGHT_DECAY = 0.01
ADAM_EPS = 1e-08
MASKED_SCORE = -1e30
PLANES = 4
FLAT_PAD = 64
SWAPPED = 1
MESH = pl.DeviceIdType.MESH

LANES = 128
ROW_TILE = 256
QUERY_TILE = 128
KEY_TILE = 256
HIDDEN_TILE = 512

F32 = jnp.float32
BF16 = jnp.bfloat16
I32 = jnp.int32


def nn(left, right):
    return lax.dot_general(left, right, (((1,), (0,)), ((), ())), preferred_element_type=F32)


def nt(left, right):
    return lax.dot_general(left, right, (((1,), (1,)), ((), ())), preferred_element_type=F32)


def tn(left, right):
    return lax.dot_general(left, right, (((0,), (0,)), ((), ())), preferred_element_type=F32)


def lane_iota(shape):
    return lax.broadcasted_iota(I32, shape, 1)


def row_iota(shape):
    return lax.broadcasted_iota(I32, shape, 0)


def whole(array):
    return pl.BlockSpec(array.shape, lambda *_: (0,) * array.ndim)


def row_blocks(array, tile):
    return pl.BlockSpec((tile, array.shape[1]), lambda i, *_: (i, 0))


def rows_from(array, start, count):
    return pl.BlockSpec(
        (pl.Element(count), pl.Element(array.shape[1])), lambda *_: (start, 0)
    )


def lane_table(table):
    return jnp.transpose(jnp.concatenate([table] * (LANES // table.shape[0]), axis=0))


def rank_mask(adapter_col, width):
    return jnp.where(lane_iota((adapter_col.shape[0], width)) // RANK == adapter_col, 1.0, 0.0)


def turn(values):
    lanes = lane_iota(values.shape) % HEAD
    return jnp.where(
        lanes < HEAD // 2,
        -pltpu.roll(values, LANES - HEAD // 2, 1),
        pltpu.roll(values, HEAD // 2, 1),
    )


def rms(values):
    return lax.rsqrt(jnp.mean(values * values, axis=-1, keepdims=True) + NORM_EPS)


def norm_back(values, gain, grad):
    inverse = rms(values)
    weighted = grad * gain
    return inverse * weighted - values * inverse * inverse * inverse * jnp.mean(
        weighted * values, axis=-1, keepdims=True
    )


def pick_rows(place_col, slots):
    hit = place_col == lane_iota((place_col.shape[0], slots))
    return jnp.where(hit, 1.0, 0.0).astype(BF16)


def place_rows(place_row, slots):
    hit = row_iota((slots, place_row.shape[1])) == place_row
    return jnp.where(hit, 1.0, 0.0).astype(BF16)


def params(**more):
    return pltpu.CompilerParams(vmem_limit_bytes=60 * 1024 * 1024, **more)


def cost(flops, moved):
    return pl.CostEstimate(flops=int(flops), bytes_accessed=int(moved), transcendentals=0)


def xor_bit(value, bit):
    size = 2**bit
    return value + size * (1 - 2 * lax.rem(value // size, 2))


def subsets(axes):
    out = [()]
    for axis in axes:
        out += [chosen + (axis,) for chosen in out]
    return out


def flip_fixed(place, part, axes):
    for axis in axes:
        if axis == "tensor":
            part = 1 - part
        else:
            place = place ^ 2**axis
    return place, part


def flip(place, part, axes):
    for axis in axes:
        if axis == "tensor":
            part = 1 - part
        else:
            place = xor_bit(place, axis)
    return place, part


def whole_part(values, size):
    return jnp.floor((values + 0.5) * (1.0 / size))


def fill_tables(
    parts, each, part, lengths_ref, ids_ref, order_ref, freq_ref,
    turns_ref, sines_ref, own_ref, other_ref, sorted_ref, rows_ref, column_ref, column_row_ref,
    bounds_ref,
):
    total = order_ref.shape[1]
    local = total // parts
    piece = each // parts
    block = 256
    order = jnp.broadcast_to(order_ref[0:1, :].astype(F32), (8, total))
    group = whole_part(order, each)
    rest = order - group * each
    part_at = whole_part(rest, piece)
    own = part_at == part.astype(F32)
    slot = group * piece + (rest - part_at * piece)
    column = jnp.where(own, slot, slot + local)
    lanes = lane_iota((8, total))
    upto = jnp.where(own, 1.0, 0.0)
    shift = 1
    while shift < total:
        upto = upto + jnp.where(lanes >= shift, pltpu.roll(upto, shift, 1), 0.0)
        shift *= 2
    rank = jnp.where(own, upto - 1.0, 2.0 * total)
    place = lanes.astype(F32)
    number = row_iota((8, total))
    column_row_ref[...] = column.astype(I32)
    turned = jnp.transpose(jnp.where(number == 0, column, rank))
    column_ref[...] = turned.astype(I32)

    def halves(values):
        high = whole_part(values, 256)
        return high, values - high * 256

    place_high, place_low = halves(place)
    slot_high, slot_low = halves(slot)
    left = jnp.where(
        number == 0, place_high, jnp.where(number == 1, place_low, jnp.where(number == 2, slot_high, slot_low))
    ).astype(BF16)

    def chosen_by(keys, start):
        hit = keys == (start + lane_iota((total, block))).astype(F32)
        found = nn(left, jnp.where(hit, 1.0, 0.0).astype(BF16))
        return found[0:1] * 256 + found[1:2], found[2:3] * 256 + found[3:4]

    def sequence(places):
        first = jnp.zeros_like(places)
        adapter = jnp.zeros_like(places) + ids_ref[0, 0].astype(F32)
        start = lengths_ref[0, 0].astype(F32)
        for at in range(1, lengths_ref.shape[1]):
            inside = places >= start
            first = jnp.where(inside, start, first)
            adapter = jnp.where(inside, ids_ref[0, at].astype(F32), adapter)
            start = start + lengths_ref[0, at].astype(F32)
        return first, adapter

    def rope(position, at):
        angles = jnp.broadcast_to(position, freq_ref.shape[:1] + position.shape[1:]) * freq_ref[:, 0:1]
        turns_ref[:, at : at + block] = jnp.cos(angles)
        sines_ref[:, at : at + block] = jnp.sin(angles)

    def as_columns(*rows):
        index = row_iota((8, block))
        out = jnp.zeros((8, block), F32)
        for at, row in enumerate(rows):
            out = jnp.where(index == at, jnp.broadcast_to(row, (8, block)), out)
        return out

    for start in range(0, total, block):
        places, _ = chosen_by(turned[:, 0:1], start)
        first, adapter = sequence(places)
        columns = jnp.transpose(as_columns(adapter)).astype(I32)
        if start < local:
            rope(places - first, start)
            own_ref[start : start + block, :] = columns
        else:
            other_ref[start - local : start - local + block, :] = columns
    for start in range(0, local, block):
        places, slots = chosen_by(turned[:, 1:2], start)
        first, _ = sequence(places)
        rope(places - first, local + start)
        rows = as_columns(slots, first, places)
        rows_ref[:, start : start + block] = rows.astype(I32)
        sorted_ref[start : start + block, :] = jnp.transpose(rows).astype(I32)
        at_lane = lane_iota((1, block))
        for tile in range(0, block, QUERY_TILE):
            low = jnp.max(jnp.where(at_lane == tile, first, 0.0))
            high = jnp.max(jnp.where(at_lane == tile + QUERY_TILE - 1, places, 0.0))
            number_at = (start + tile) // QUERY_TILE
            bounds_ref[0, number_at] = low.astype(I32) // KEY_TILE
            bounds_ref[1, number_at] = high.astype(I32) // KEY_TILE + 1


def front_kernel(
    devices, each, rows_ref, chunk_ref, wq_ref, wk_ref, wv_ref, bias_ref, lengths_ref, ids_ref,
    order_ref, freq_ref,
    got_ref, copies_ref, wq_out, wk_out, wv_out, bias_out, *rest,
):
    tables, (local_sem, tsend, trecv, csend, crecv, wsend, wrecv) = rest[:9], rest[9:]
    place, part = lax.axis_index("dp"), lax.axis_index("tensor")
    plane = devices // PLANES
    depth, inside = place // plane, lax.rem(place, plane)
    core = lax.rem(place, 2)
    own = 2 * place + part
    over = (place, 1 - part)
    units = chunk_ref.shape[0]

    def rows_of(index):
        return copies_ref.at[pl.ds(index * units, units)]

    def layer(hop):
        return lax.rem(depth + hop, PLANES)

    barrier = pltpu.get_barrier_semaphore()
    for k in range(1, devices):
        pl.semaphore_signal(
            barrier, inc=1, device_id=(lax.rem(place + k, devices), part), device_id_type=MESH
        )
    pl.semaphore_signal(barrier, inc=1, device_id=over, device_id_type=MESH)
    pl.semaphore_wait(barrier, devices)

    def chunk_copy(source, index, number, where):
        return pltpu.make_async_remote_copy(
            src_ref=source,
            dst_ref=rows_of(index),
            send_sem=csend.at[number],
            recv_sem=crecv.at[index],
            device_id=where,
            device_id_type=MESH,
        )

    def chain(hop, way):
        origin = depth - way * hop
        index = 2 * (origin * plane + inside) + part
        target = ((depth + way) * plane + inside, part)
        source = chunk_ref if hop == 0 else rows_of(index)
        number = 2 * hop + (0 if way > 0 else 1)
        inner = (origin >= 0) & (origin < PLANES)
        ahead = (depth + way >= 0) & (depth + way < PLANES)
        return chunk_copy(source, index, number, target), inner, ahead

    keep = [
        pltpu.make_async_copy(chunk_ref, rows_of(own), local_sem.at[0]),
        pltpu.make_async_copy(rows_ref.at[place, part], got_ref.at[place], local_sem.at[1]),
    ]
    for way in (1, -1):
        copy, _, ahead = chain(0, way)

        @pl.when(ahead)
        def _():
            copy.start()

    weights = ((wq_ref, wq_out), (wk_ref, wk_out), (wv_ref, wv_out))

    def weight_copy(ref, out, number, slot, where):
        return pltpu.make_async_remote_copy(
            src_ref=ref.at[slot],
            dst_ref=out.at[slot],
            send_sem=wsend.at[number],
            recv_sem=wrecv.at[number],
            device_id=where,
            device_id_type=MESH,
        )

    direct = [
        weight_copy(ref, out, number, core, over) for number, (ref, out) in enumerate(weights)
    ]
    for slot in range(2):
        direct.append(weight_copy(bias_ref, bias_out, 6 + slot, slot, over))
    for copy in direct:
        copy.start()

    rows_sent = []

    def send_rows(hop):
        for step in range(plane):
            if hop == 0 and step == 0:
                continue
            target = layer(hop) * plane + lax.rem(inside + step, plane)
            copy = pltpu.make_async_remote_copy(
                src_ref=rows_ref.at[target, part],
                dst_ref=got_ref.at[place],
                send_sem=tsend.at[len(rows_sent)],
                recv_sem=trecv.at[place],
                device_id=(target, part),
                device_id_type=MESH,
            )
            copy.start()
            rows_sent.append((copy, target))

    send_rows(0)
    for copy in keep:
        copy.start()
    for hop in range(1, PLANES):
        for way in (1, -1):
            copy, inner, ahead = chain(hop, way)

            @pl.when(inner)
            def _():
                copy.wait_recv()

            if hop < PLANES - 1:

                @pl.when(inner & ahead)
                def _():
                    copy.start()

    for hop in (2, 3, 1):
        send_rows(hop)

    sent = []

    def send_chunk(source, index, where):
        copy = chunk_copy(source, index, 2 * PLANES + len(sent), where)
        copy.start()
        sent.append(copy)

    def take_chunk(index):
        chunk_copy(chunk_ref, index, 0, over).wait_recv()

    bits = list(range(plane.bit_length() - 1))[::-1]
    orders = [["tensor"] + bits, bits[:-1] + ["tensor"] + bits[-1:]]
    relayed = []
    for stage in range(len(bits) + 1):
        for hop in range(PLANES):
            order = orders[hop % 2]
            origin = layer(hop) * plane + inside
            where = flip(place, part, [order[stage]])
            for chosen in subsets(order[:stage]):
                at, side = flip(origin, part, chosen)
                index = 2 * at + side
                if hop == 0 and not chosen:
                    send_chunk(chunk_ref, index, where)
                    continue
                if stage > 0 and order[stage - 1] in chosen:
                    take_chunk(index)
                send_chunk(rows_of(index), index, where)
        if stage == 0:
            partner = (xor_bit(place, 0), part)
            for number, (ref, out) in enumerate(weights):
                direct[number].wait_recv()
                copy = weight_copy(out, out, 3 + number, core, partner)
                copy.start()
                relayed.append(copy)
            fill_tables(2, each, part, lengths_ref, ids_ref, order_ref, freq_ref, *tables)
    for hop in range(PLANES):
        order = orders[hop % 2]
        origin = layer(hop) * plane + inside
        for chosen in subsets(order):
            if order[-1] in chosen:
                at, side = flip(origin, part, chosen)
                take_chunk(2 * at + side)
    for number, (ref, out) in enumerate(weights):
        weight_copy(out, out, 3 + number, 1 - core, over).wait_recv()
    for copy in direct[len(weights) :]:
        copy.wait_recv()
    for _, source in rows_sent:
        pltpu.make_async_remote_copy(
            src_ref=rows_ref.at[source, part],
            dst_ref=got_ref.at[source],
            send_sem=tsend.at[0],
            recv_sem=trecv.at[source],
            device_id=(source, part),
            device_id_type=MESH,
        ).wait_recv()
    for copy, _ in rows_sent:
        copy.wait_send()
    for hop in range(PLANES - 1):
        for way in (1, -1):
            copy, inner, ahead = chain(hop, way)

            @pl.when(inner & ahead)
            def _():
                copy.wait_send()

    for copy in sent + direct + relayed:
        copy.wait_send()
    for copy in keep:
        copy.wait()


def front(rows, chunk, wq, wk, wv, bias, order, lengths, adapter_ids, devices):
    _, _, piece, width = rows.shape
    total = order.shape[1]
    local = total // 2
    freq_index = jnp.arange(HEAD // 2, dtype=F32)
    freq = jnp.power(jnp.float32(ROPE_BASE), -2.0 * freq_index / HEAD)
    freq = jnp.broadcast_to(freq[:, None], (HEAD // 2, LANES))
    anywhere = pl.BlockSpec(memory_space=pl.ANY)
    outs = [
        jax.ShapeDtypeStruct((devices, piece, width), BF16),
        jax.ShapeDtypeStruct((2 * devices * chunk.shape[0],) + chunk.shape[1:], BF16),
    ] + [jax.ShapeDtypeStruct(a.shape, BF16) for a in (wq, wk, wv, bias)]
    shapes = [
        ((HEAD // 2, total), F32),
        ((HEAD // 2, total), F32),
        ((local, 8), I32),
        ((local, 8), I32),
        ((local, 8), I32),
        ((8, local), I32),
        ((total, 8), I32),
        ((8, total), I32),
        ((2, local // QUERY_TILE), I32),
    ]
    outs += [jax.ShapeDtypeStruct(shape, kind) for shape, kind in shapes]
    dma = pltpu.SemaphoreType.DMA
    near, scalar = pl.BlockSpec(memory_space=pltpu.VMEM), pl.BlockSpec(memory_space=pltpu.SMEM)
    return pl.pallas_call(
        functools.partial(front_kernel, devices, 2 * piece),
        in_specs=[anywhere] * 6 + [scalar, scalar, near, near],
        out_specs=[anywhere] * 6 + [near] * 8 + [scalar],
        out_shape=outs,
        scratch_shapes=[
            dma((2,)),
            dma((devices,)),
            dma((devices,)),
            dma((2 * PLANES + 2 * devices,)),
            dma((2 * devices,)),
            dma((8,)),
            dma((8,)),
        ],
        compiler_params=params(collective_id=0, has_side_effects=True),
        cost_estimate=cost(0, 100e6),
        name="front",
    )(rows, chunk, wq, wk, wv, bias, lengths, adapter_ids, order, freq)


def in_order(part, mine, theirs, place):
    @pl.when(part == 0)
    def _():
        place(mine, theirs)

    @pl.when(part == 1)
    def _():
        place(theirs, mine)


def project_kernel(
    x_ref, meta_ref, turns_ref, sines_ref, gain_ref, mq_ref, mk_ref, mv_ref, mb_ref,
    tq_ref, tk_ref, tv_ref, tb_ref, flat_ref,
    n_ref, q_ref, kv_ref, z_ref, cos_ref, sin_ref, w_ref, other_ref, bias, held, ksend, krecv,
):
    place, part = lax.axis_index("dp"), lax.axis_index("tensor")
    here = pl.program_id(0)
    tiles = held.shape[0]
    width = x_ref.shape[1]
    qw, kw = q_ref.shape[1], kv_ref.shape[1] // 2

    def swap(number):
        return pltpu.make_async_remote_copy(
            src_ref=held.at[number],
            dst_ref=other_ref.at[number],
            send_sem=ksend.at[number],
            recv_sem=krecv.at[number],
            device_id=(place, 1 - part),
            device_id_type=MESH,
        )

    rank = flat_ref.shape[1]
    low = qw + 2 * kw
    a_rows, b_rows = [], []
    cursor = 0
    for size in (qw, kw, kw):
        a_rows.append(slice(cursor, cursor + width))
        b_rows.append(slice(cursor + width, cursor + width + size))
        cursor += width + size

    @pl.when(pl.program_id(0) == 0)
    def _():
        def fill(first, second):
            at, to = 0, 0
            for order, size in enumerate((qw // 2, kw // 2, kw // 2)):
                w_ref[to : to + size, :] = first[order][...]
                w_ref[to + size : to + 2 * size, :] = second[order][...]
                bias[:, to : to + 2 * size] = jnp.concatenate(
                    [
                        first[3][:8, at : at + size].astype(F32),
                        second[3][:8, at : at + size].astype(F32),
                    ],
                    axis=1,
                )
                at += size
                to += 2 * size

        barrier = pltpu.get_barrier_semaphore()
        pl.semaphore_signal(barrier, inc=1, device_id=(place, 1 - part), device_id_type=MESH)
        in_order(
            part, (mq_ref, mk_ref, mv_ref, mb_ref), (tq_ref, tk_ref, tv_ref, tb_ref), fill
        )
        for i, rows in enumerate(a_rows):
            turned = jnp.transpose(flat_ref[rows, :].astype(F32)).astype(BF16)
            w_ref[low + i * rank : low + (i + 1) * rank, :] = turned
        pl.semaphore_wait(barrier, 1)

    values = x_ref[...].astype(F32)
    normed = (values * rms(values) * gain_ref[...]).astype(BF16)
    n_ref[...] = normed
    base = nt(normed, w_ref[qw:, :])
    mask = rank_mask(meta_ref[:, 0:1], rank)
    lows = [
        (base[:, low - qw + i * rank : low - qw + (i + 1) * rank] * mask).astype(BF16)
        for i in range(3)
    ]
    for i in range(3):
        z_ref[:, i * rank : (i + 1) * rank] = lows[i]
    cos, sin = lane_table(turns_ref[...]), lane_table(sines_ref[...])
    cos_ref[...] = cos
    sin_ref[...] = sin
    keys = (
        base[:, :kw]
        + bias[0:1, qw : qw + kw]
        + ADAPTER_SCALE * nt(lows[1], flat_ref[b_rows[1], :])
    )
    vals = (
        base[:, kw : 2 * kw]
        + bias[0:1, qw + kw : low]
        + ADAPTER_SCALE * nt(lows[2], flat_ref[b_rows[2], :])
    )
    both = jnp.concatenate([keys * cos + turn(keys) * sin, vals], axis=1).astype(BF16)
    held[here] = both
    kv_ref[...] = both
    swap(here).start()
    queries = (
        nt(normed, w_ref[:qw, :])
        + bias[0:1, :qw]
        + ADAPTER_SCALE * nt(lows[0], flat_ref[b_rows[0], :])
    )
    for pair in range(qw // LANES):
        some = queries[:, pair * LANES : (pair + 1) * LANES]
        turned = (some * cos + turn(some) * sin) * HEAD**-0.5
        q_ref[:, pair * LANES : (pair + 1) * LANES] = turned.astype(BF16)

    @pl.when(here == tiles - 1)
    def _():
        for number in range(tiles):
            swap(number).wait_send()
        for number in range(tiles):
            swap(number).wait_recv()


def project(x, meta, turns, sines, gain, mine, theirs, flat, qw, kw):
    rows, width = x.shape
    rank = flat.shape[1]
    tile = ROW_TILE
    early = 3 * width + qw + 2 * kw
    columns = pl.BlockSpec((turns.shape[0], tile), lambda i, *_: (0, i))
    outs = [
        jax.ShapeDtypeStruct((rows, width), BF16),
        jax.ShapeDtypeStruct((rows, qw), BF16),
        jax.ShapeDtypeStruct((rows, 2 * kw), BF16),
        jax.ShapeDtypeStruct((rows, 3 * rank), BF16),
        jax.ShapeDtypeStruct((rows, LANES), F32),
        jax.ShapeDtypeStruct((rows, LANES), F32),
        jax.ShapeDtypeStruct((qw + 2 * kw + 3 * rank, width), BF16),
        jax.ShapeDtypeStruct((rows // tile, tile, 2 * kw), BF16),
    ]
    dma = pltpu.SemaphoreType.DMA
    return pl.pallas_call(
        project_kernel,
        grid=(rows // tile,),
        in_specs=[row_blocks(a, tile) for a in (x, meta)]
        + [columns, columns]
        + [whole(a) for a in (gain, *mine, *theirs)]
        + [pl.BlockSpec((early, rank), lambda i: (0, 0))],
        out_specs=[row_blocks(o, tile) for o in outs[:6]]
        + [whole(outs[6]), pl.BlockSpec(memory_space=pl.ANY)],
        out_shape=outs,
        scratch_shapes=[
            pltpu.VMEM((8, qw + 2 * kw), F32),
            pltpu.VMEM((rows // tile, tile, 2 * kw), BF16),
            dma((rows // tile,)),
            dma((rows // tile,)),
        ],
        compiler_params=params(collective_id=4, has_side_effects=True),
        cost_estimate=cost(2 * rows * width * 1600, 9e6),
        name="project",
    )(x, meta, turns, sines, gain, *mine, *theirs, flat)


def head_groups(heads, kv_heads):
    width = heads // kv_heads
    groups = {}
    for head in range(heads):
        groups.setdefault((head // width, head % 2), []).append(head)
    return [(kv, half, members) for (kv, half), members in sorted(groups.items())]


def spread_heads(tile_f32, kv, half, ones=False):
    lanes = lane_iota(tile_f32.shape)
    moved = tile_f32 if kv % 2 == half else pltpu.roll(tile_f32, HEAD, 1)
    keep = (lanes >= HEAD) if half else (lanes < HEAD)
    rest = jnp.where(lanes == (0 if half else HEAD), 1.0, 0.0) if ones else 0.0
    return jnp.where(keep, moved, rest)


def stack_heads(groups, source, target):
    rows = source.shape[0]
    at = 0
    for _, _, members in groups:
        for head in members:
            pair = slice((head // 2) * LANES, (head // 2 + 1) * LANES)
            target[at : at + rows, :] = source[:, pair]
            at += rows


def attend_kernel(
    heads, kv_heads, bounds_ref, all_ref, meta_ref, metar_ref, place_ref, own_ref, other_ref,
    column_ref,
    q_ref, o_ref, log_ref, merged_ref, slot_ref, keys, values, acc, top, held, stack, scores,
):
    step = pl.program_id(0)
    groups = head_groups(heads, kv_heads)
    rows = q_ref.shape[0]
    q_ref[...] = nn(pick_rows(meta_ref[:, 0:1], all_ref.shape[0]), all_ref[...]).astype(BF16)
    stack_heads(groups, q_ref, stack)

    @pl.when(step == 0)
    def _():
        both = jnp.concatenate([own_ref[...], other_ref[...]], axis=0)
        for start in range(0, keys.shape[1], KEY_TILE):
            span = slice(start, start + KEY_TILE)
            part = nn(pick_rows(column_ref[span, 0:1], both.shape[0]), both)
            merged_ref[span, :] = part.astype(BF16)
            for number, (kv, half, _) in enumerate(groups):
                keys[number, span, :] = spread_heads(part[:, :LANES], kv, half).astype(BF16)
                turned = jnp.transpose(spread_heads(part[:, LANES:], kv, half, True))
                values[number, :, span] = turned.astype(BF16)

    acc[...] = jnp.zeros_like(acc)
    top[...] = jnp.full_like(top, MASKED_SCORE)
    first, last = metar_ref[1:2, :], metar_ref[2:3, :]
    cuts = []
    at = 0
    for _, _, members in groups:
        cuts.append(slice(at * rows, (at + len(members)) * rows))
        at += len(members)

    def find_top(number, carry):
        start = pl.multiple_of(number * KEY_TILE, KEY_TILE)
        span = pl.ds(start, KEY_TILE)
        index = start + row_iota((KEY_TILE, rows))
        bias = jnp.where((index >= first) & (index <= last), 0.0, MASKED_SCORE)
        for group, cut in enumerate(cuts):
            count = (cut.stop - cut.start) // rows
            part = nt(keys[group, span, :], stack[cut, :])
            part = part + jnp.concatenate([bias] * count, axis=1)
            scores[span, cut] = part
            most = jnp.max(part.reshape(KEY_TILE // 8, 8, -1), axis=0)
            top[:, cut] = jnp.maximum(top[:, cut], most)
        return carry

    def weigh(number, carry):
        start = pl.multiple_of(number * KEY_TILE, KEY_TILE)
        span = pl.ds(start, KEY_TILE)
        for group, cut in enumerate(cuts):
            weights = jnp.exp(scores[span, cut] - top[0:1, cut]).astype(BF16)
            acc[:, cut] += nn(values[group, :, span], weights)
        return carry

    lax.fori_loop(bounds_ref[0, step], bounds_ref[1, step], find_top, 0)
    top[0:1, :] = jnp.max(top[...], axis=0, keepdims=True)
    lax.fori_loop(bounds_ref[0, step], bounds_ref[1, step], weigh, 0)
    parts = {}
    at = 0
    for _, half, members in groups:
        for head in members:
            cut = slice(at * rows, (at + 1) * rows)
            at += 1
            block = acc[:, cut]
            sums = block[0:1, :] if half else block[HEAD : HEAD + 1, :]
            log_ref[head : head + 1, :] = top[0:1, cut] + jnp.log(sums)
            parts[head] = block / sums
    low = row_iota((LANES, rows)) < HEAD
    for pair in range(heads // 2):
        both = jnp.where(low, parts[2 * pair], parts[2 * pair + 1])
        o_ref[:, pair * LANES : (pair + 1) * LANES] = jnp.transpose(both).astype(BF16)
    for head in range(heads, log_ref.shape[0]):
        log_ref[head : head + 1, :] = jnp.zeros((1, rows), F32)
    held[pl.ds(pl.multiple_of(step * rows, rows), rows), :] = o_ref[...]

    @pl.when(step == pl.num_programs(0) - 1)
    def _():
        slot_ref[...] = nn(place_rows(place_ref[0:1, :], held.shape[0]), held[...]).astype(BF16)


def attend(bounds, q, meta, meta_rows, own_kv, other_kv, column, heads, kv_heads):
    rows, qw = q.shape
    tile = QUERY_TILE
    keys = 2 * rows
    groups = len(head_groups(heads, kv_heads))
    outs = [
        jax.ShapeDtypeStruct((rows, qw), BF16),
        jax.ShapeDtypeStruct((rows, qw), BF16),
        jax.ShapeDtypeStruct((16, rows), F32),
        jax.ShapeDtypeStruct((keys, own_kv.shape[1]), BF16),
        jax.ShapeDtypeStruct((rows, qw), BF16),
    ]
    return pl.pallas_call(
        functools.partial(attend_kernel, heads, kv_heads),
        grid_spec=pltpu.PrefetchScalarGridSpec(
            num_scalar_prefetch=1,
            grid=(rows // tile,),
            in_specs=[
                whole(q),
                row_blocks(meta, tile),
                pl.BlockSpec((8, tile), lambda i, *_: (0, i)),
                whole(meta_rows),
                whole(own_kv),
                whole(other_kv),
                whole(column),
            ],
            out_specs=[
                row_blocks(outs[0], tile),
                row_blocks(outs[1], tile),
                pl.BlockSpec((16, tile), lambda i, *_: (0, i)),
                whole(outs[3]),
                whole(outs[4]),
            ],
            scratch_shapes=[
                pltpu.VMEM((groups, keys, LANES), BF16),
                pltpu.VMEM((groups, LANES, keys), BF16),
                pltpu.VMEM((LANES, heads * tile), F32),
                pltpu.VMEM((8, heads * tile), F32),
                pltpu.VMEM((rows, qw), BF16),
                pltpu.VMEM((heads * tile, LANES), BF16),
                pltpu.VMEM((keys, heads * tile), F32),
            ],
        ),
        out_shape=outs,
        compiler_params=params(),
        cost_estimate=cost(heads * rows * keys * 2000, 6e6),
        name="attend",
    )(bounds, q, meta, meta_rows, meta_rows, own_kv, other_kv, column)


def attend_back_kernel(
    heads, kv_heads, bounds_ref, q_ref, all_ref, o_ref, log_ref, meta_ref, metar_ref, cos_ref,
    sin_ref, merged_ref, column_ref, place_ref,
    gq_ref, own_ref, other_ref, keys, values, dkeys, dvalues, dq, dots, g_ref, held, stack, grads,
):
    step = pl.program_id(0)
    groups = head_groups(heads, kv_heads)
    rows = q_ref.shape[0]
    g_ref[...] = nn(pick_rows(meta_ref[:, 0:1], all_ref.shape[0]), all_ref[...]).astype(BF16)

    @pl.when(step == 0)
    def _():
        for start in range(0, keys.shape[1], KEY_TILE):
            span = slice(start, start + KEY_TILE)
            part = merged_ref[span, :].astype(F32)
            for number, (kv, half, _) in enumerate(groups):
                keys[number, span, :] = spread_heads(part[:, :LANES], kv, half).astype(BF16)
                values[number, span, :] = spread_heads(part[:, LANES:], kv, half).astype(BF16)
        dkeys[...] = jnp.zeros_like(dkeys)
        dvalues[...] = jnp.zeros_like(dvalues)

    stack_heads(groups, q_ref, stack)
    stack_heads(groups, g_ref, grads)
    dq[...] = jnp.zeros_like(dq)
    for pair in range(heads // 2):
        lanes = slice(pair * LANES, (pair + 1) * LANES)
        product = jnp.transpose(g_ref[:, lanes].astype(F32) * o_ref[:, lanes].astype(F32))
        dots[2 * pair : 2 * pair + 1, :] = jnp.sum(product[:HEAD], axis=0, keepdims=True)
        dots[2 * pair + 1 : 2 * pair + 2, :] = jnp.sum(product[HEAD:], axis=0, keepdims=True)
    first, last = metar_ref[1:2, :], metar_ref[2:3, :]

    def one_tile(number, carry):
        start = pl.multiple_of(number * KEY_TILE, KEY_TILE)
        index = start + row_iota((KEY_TILE, rows))
        bias = jnp.where((index >= first) & (index <= last), 0.0, MASKED_SCORE)
        span = pl.ds(start, KEY_TILE)
        begin = 0
        for group, (_, half, members) in enumerate(groups):
            count = len(members)
            cut = slice(begin * rows, (begin + count) * rows)
            begin += count
            logs = jnp.concatenate([log_ref[h : h + 1, :] for h in members], axis=1)
            drop = jnp.concatenate([dots[h : h + 1, :] for h in members], axis=1)
            key_part = keys[group, span, :]
            scores = nt(key_part, stack[cut, :]) + jnp.concatenate([bias] * count, axis=1)
            weights = jnp.exp(scores - logs)
            change = nt(values[group, span, :], grads[cut, :])
            dscores = (weights * (change - drop)).astype(BF16)
            dvalues[group, span, :] += nn(weights.astype(BF16), grads[cut, :])
            dkeys[group, span, :] += nn(dscores, stack[cut, :])
            back = tn(dscores, key_part)
            for at, head in enumerate(members):
                dq[head // 2, :, :] += back[at * rows : (at + 1) * rows, :]
        return carry

    lax.fori_loop(bounds_ref[0, step], bounds_ref[1, step], one_tile, 0)
    cos, sin = lane_table(cos_ref[...]), lane_table(sin_ref[...])
    for pair in range(heads // 2):
        grad = dq[pair, :, :] * HEAD**-0.5
        grad = grad * cos - turn(grad) * sin
        held[
            pl.ds(pl.multiple_of(step * rows, rows), rows), pair * LANES : (pair + 1) * LANES
        ] = grad.astype(BF16)

    @pl.when(step == pl.num_programs(0) - 1)
    def _():
        gq_ref[...] = nn(place_rows(place_ref[0:1, :], held.shape[0]), held[...]).astype(BF16)
        total = dkeys.shape[1]

        def join(ref):
            out = None
            for group, (kv, half, _) in enumerate(groups):
                part = ref[group, :, :]
                lanes = lane_iota(part.shape)
                part = jnp.where((lanes >= HEAD) if half else (lanes < HEAD), part, 0.0)
                if kv % 2 != half:
                    part = pltpu.roll(part, HEAD, 1)
                out = part if out is None else out + part
            return out.astype(BF16)

        both = jnp.concatenate([join(dkeys), join(dvalues)], axis=1)
        half_rows = own_ref.shape[0]
        for at in range(0, total, KEY_TILE):
            hit = (at + row_iota((KEY_TILE, total))) == column_ref[0:1, :]
            part = nn(jnp.where(hit, 1.0, 0.0).astype(BF16), both).astype(BF16)
            if at < half_rows:
                own_ref[at : at + KEY_TILE, :] = part
            else:
                other_ref[at - half_rows : at - half_rows + KEY_TILE, :] = part


def attend_back(
    bounds, q, grad, o, logs, meta, meta_rows, cos, sin, merged, column_row, heads, kv_heads
):
    rows, qw = q.shape
    tile = QUERY_TILE
    keys, kvw = merged.shape
    groups = len(head_groups(heads, kv_heads))
    outs = [
        jax.ShapeDtypeStruct((rows, qw), BF16),
        jax.ShapeDtypeStruct((rows, kvw), BF16),
        jax.ShapeDtypeStruct((rows, kvw), BF16),
    ]
    return pl.pallas_call(
        functools.partial(attend_back_kernel, heads, kv_heads),
        grid_spec=pltpu.PrefetchScalarGridSpec(
            num_scalar_prefetch=1,
            grid=(rows // tile,),
            in_specs=[
                row_blocks(q, tile),
                whole(grad),
                row_blocks(o, tile),
                pl.BlockSpec((16, tile), lambda i, *_: (0, i)),
                row_blocks(meta, tile),
                pl.BlockSpec((8, tile), lambda i, *_: (0, i)),
                pl.BlockSpec((cos.shape[0], tile), lambda i, *_: (0, rows // tile + i)),
                pl.BlockSpec((cos.shape[0], tile), lambda i, *_: (0, rows // tile + i)),
                whole(merged),
                whole(column_row),
                whole(meta_rows),
            ],
            out_specs=[whole(o) for o in outs],
            scratch_shapes=[
                pltpu.VMEM((groups, keys, LANES), BF16),
                pltpu.VMEM((groups, keys, LANES), BF16),
                pltpu.VMEM((groups, keys, LANES), F32),
                pltpu.VMEM((groups, keys, LANES), F32),
                pltpu.VMEM((heads // 2, tile, LANES), F32),
                pltpu.VMEM((16, tile), F32),
                pltpu.VMEM((tile, qw), BF16),
                pltpu.VMEM((rows, qw), BF16),
                pltpu.VMEM((heads * tile, LANES), BF16),
                pltpu.VMEM((heads * tile, LANES), BF16),
            ],
        ),
        out_shape=outs,
        compiler_params=params(),
        cost_estimate=cost(heads * rows * keys * 3000, 9e6),
        name="attend_back",
    )(bounds, q, grad, o, logs, meta, meta_rows, cos, sin, merged, column_row, meta_rows)


def middle_kernel(
    part_ref, o_ref, x_ref, meta_ref, mine_ref, theirs_ref, gain_ref, flat_ref,
    y_ref, n_ref, z_ref, w_ref,
):
    width = x_ref.shape[1]
    rank = flat_ref.shape[1]
    half = mine_ref.shape[0]

    @pl.when(pl.program_id(0) == 0)
    def _():
        def fill(first, second):
            w_ref[:half, :width] = first[...]
            w_ref[half:, :width] = second[...]

        in_order(part_ref[0], mine_ref, theirs_ref, fill)
        w_ref[:, width:] = flat_ref[: 2 * half, :]

    mask = rank_mask(meta_ref[:, 0:1], rank)
    base = nn(o_ref[...], w_ref[...])
    low = (base[:, width:] * mask).astype(BF16)
    z_ref[...] = low
    values = x_ref[...].astype(F32) + (base[:, :width] + ADAPTER_SCALE * nt(low, flat_ref[2 * half :, :]))
    y_ref[...] = values
    n_ref[...] = (values * rms(values) * gain_ref[...]).astype(BF16)


def middle(part, o, x, meta, mine, theirs, gain, flat, start):
    rows, width = x.shape
    rank = flat.shape[1]
    tile = ROW_TILE
    rest = (mine, theirs, gain)
    outs = [
        jax.ShapeDtypeStruct((rows, width), F32),
        jax.ShapeDtypeStruct((rows, width), BF16),
        jax.ShapeDtypeStruct((rows, rank), BF16),
        jax.ShapeDtypeStruct((o.shape[1], width + rank), BF16),
    ]
    return pl.pallas_call(
        middle_kernel,
        grid_spec=pltpu.PrefetchScalarGridSpec(
            num_scalar_prefetch=1,
            grid=(rows // tile,),
            in_specs=[row_blocks(a, tile) for a in (o, x, meta)]
            + [whole(a) for a in rest]
            + [rows_from(flat, start, o.shape[1] + width)],
            out_specs=[row_blocks(a, tile) for a in outs[:3]] + [whole(outs[3])],
        ),
        out_shape=outs,
        compiler_params=params(),
        cost_estimate=cost(2 * rows * width * 1100, 12e6),
        name="middle",
    )(part, o, x, meta, *rest, flat)


class Windows:
    def __init__(self, devices, own_rows):
        self.devices = devices
        self.own_rows = own_rows
        self.plane = devices // PLANES
        self.axes = list(range(self.plane.bit_length() - 1)) + ["tensor"]
        self.rows = 16 * ((own_rows + 30) // 16)
        self.last = 16 * (((2 * devices - 1) * own_rows) // 16) + self.rows

    def start(self, zz, at, side):
        row = (2 * (zz * self.plane + at) + side) * self.own_rows
        return pl.multiple_of((row // 16) * 16, 16)

    def span(self, zz, at, side):
        return pl.ds(self.start(zz, at, side), self.rows)

    def boxes(self, stage):
        return 2 ** (len(self.axes) - 1 - stage)

    def box(self, stage, at, side):
        index = 0
        for order, axis in enumerate(self.axes[stage + 1 :]):
            bit = side if axis == "tensor" else lax.rem(at // 2**axis, 2)
            index = index + bit * 2**order
        return index

    def leaving(self, stage, inside, part):
        for chosen in subsets(self.axes[stage + 1 :]):
            yield flip(inside, part, [self.axes[stage]] + list(chosen))

    def staying(self, stage, inside, part):
        for chosen in subsets(self.axes[stage + 1 :]):
            yield flip(inside, part, list(chosen))


def middle_back_kernel(
    plan, first_b, da_ref, db_ref, y1_ref, dy_ref, o_ref, z_ref, meta_ref, copies_ref, w_ref,
    gain_ref, flat_ref,
    dy1_ref, dar_ref, grad_ref, kept_ref, *rest,
):
    step = pl.program_id(0)
    on_refs = rest[: plan.boxes(0) - 1]
    acc_bo, acc_ao, mine, inbox, b_ref, msem, ssem, rsem, bsem = rest[plan.boxes(0) - 1 :]
    b_load = pltpu.make_async_copy(
        copies_ref.at[pl.ds(first_b, b_ref.shape[0]), :], b_ref, bsem.at[0]
    )
    rank = b_ref.shape[1]
    qw = o_ref.shape[1]
    place, part = lax.axis_index("dp"), lax.axis_index("tensor")
    inside = lax.rem(place, plan.plane)
    partner = flip(place, part, [plan.axes[0]])
    boxes = plan.boxes(0)

    def moves():
        local, remote = [], []
        for zz in range(1, PLANES):
            for at, side in plan.leaving(0, inside, part):
                index = (zz - 1) * boxes + plan.box(0, at, side)
                remote.append(
                    pltpu.make_async_remote_copy(
                        src_ref=flat_ref.at[plan.span(zz, at, side), :],
                        dst_ref=inbox.at[index],
                        send_sem=ssem.at[len(remote)],
                        recv_sem=rsem.at[index],
                        device_id=partner,
                        device_id_type=MESH,
                    )
                )
            for at, side in plan.staying(0, inside, part):
                index = (zz - 1) * boxes + plan.box(0, at, side)
                local.append(
                    pltpu.make_async_copy(
                        flat_ref.at[plan.span(zz, at, side), :], mine.at[index], msem.at[len(local)]
                    )
                )
        return local, remote

    @pl.when(step == 0)
    def _():
        acc_bo[...] = jnp.zeros_like(acc_bo)
        acc_ao[...] = jnp.zeros_like(acc_ao)
        b_load.start()
        barrier = pltpu.get_barrier_semaphore()
        pl.semaphore_signal(barrier, inc=1, device_id=partner, device_id_type=MESH)
        pl.semaphore_wait(barrier, 1)
        local, remote = moves()
        for copy in remote + local:
            copy.start()
        b_load.wait()

    mask = rank_mask(meta_ref[:, 0:1], rank)
    grad = da_ref[...] + db_ref[...].astype(F32)
    dy1 = dy_ref[...].astype(F32) + norm_back(y1_ref[...], gain_ref[...], grad)
    dy1_ref[...] = dy1
    low_grad = dy1.astype(BF16)
    back_out = (ADAPTER_SCALE * nn(low_grad, b_ref[...]) * mask).astype(BF16)
    both = jnp.concatenate([low_grad, back_out], axis=1)
    dar_ref[...] = nt(both, w_ref[...]).astype(BF16)
    acc_bo[...] += ADAPTER_SCALE * tn(low_grad, z_ref[...])
    acc_ao[...] += tn(o_ref[...], back_out)

    @pl.when(step == pl.num_programs(0) - 1)
    def _():
        grad_ref[:qw, :] = acc_ao[...].astype(BF16)
        grad_ref[qw:, :] = acc_bo[...].astype(BF16)
        local, remote = moves()
        for copy in local:
            copy.wait()
        for copy in remote:
            copy.wait_recv()
        def total(zz, at, side):
            index = (zz - 1) * boxes + plan.box(0, at, side)
            return mine[index].astype(F32) + inbox[index].astype(F32)

        for zz in range(1, PLANES):
            for peer, chosen in enumerate(subsets(plan.axes[1:])):
                at, side = flip(inside, part, chosen)
                if peer == 0:
                    kept_ref[zz - 1] = total(zz, at, side)
                else:
                    on_refs[peer - 1][zz - 1] = total(zz, at, side).astype(BF16)
        for copy in remote:
            copy.wait_send()


def middle_back(
    devices, own_rows, d_first, d_second, y1, dy, o, z, meta, copies, start, w_out, gain, flat
):
    rows, width = y1.shape
    rank = copies.shape[1]
    qw = o.shape[1]
    tile = ROW_TILE
    plan = Windows(devices, own_rows)
    first = (PLANES - 1) * plan.boxes(0)
    outs = [
        jax.ShapeDtypeStruct((rows, width), F32),
        jax.ShapeDtypeStruct((rows, qw), BF16),
        jax.ShapeDtypeStruct((qw + width, rank), BF16),
        jax.ShapeDtypeStruct((PLANES - 1, plan.rows, rank), F32),
    ] + [jax.ShapeDtypeStruct((PLANES - 1, plan.rows, rank), BF16)] * (plan.boxes(0) - 1)
    return pl.pallas_call(
        functools.partial(middle_back_kernel, plan, start),
        grid=(rows // tile,),
        in_specs=[row_blocks(a, tile) for a in (d_first, d_second, y1, dy, o, z, meta)]
        + [pl.BlockSpec(memory_space=pl.ANY)]
        + [whole(a) for a in (w_out, gain)]
        + [pl.BlockSpec(memory_space=pl.ANY)],
        out_specs=[row_blocks(a, tile) for a in outs[:2]] + [whole(a) for a in outs[2:]],
        out_shape=outs,
        scratch_shapes=[
            pltpu.VMEM((width, rank), F32),
            pltpu.VMEM((qw, rank), F32),
            pltpu.VMEM((first, plan.rows, rank), BF16),
            pltpu.VMEM((first, plan.rows, rank), BF16),
            pltpu.VMEM((width, rank), BF16),
            pltpu.SemaphoreType.DMA((first,)),
            pltpu.SemaphoreType.DMA((first,)),
            pltpu.SemaphoreType.DMA((first,)),
            pltpu.SemaphoreType.DMA((1,)),
        ],
        compiler_params=params(collective_id=3, has_side_effects=True),
        cost_estimate=cost(2 * rows * width * 1500, 20e6),
        name="middle_back",
    )(d_first, d_second, y1, dy, o, z, meta, copies, w_out, gain, flat)


def own_tile(step, tiles):
    return jnp.maximum(step - tiles, 0)


def their_tile(step, tiles):
    return jnp.clip(step - 1, 0, tiles - 1)


def feed_kernel(
    n_ref, n_hbm, dy_ref, dyt_ref, meta_ref, metat_ref, wg_hbm, wu_hbm,
    wd_hbm, copies,
    y_ref, d_ref, y_got, d_got, last_ref, flat_ref,
    wga, wua, wda, raw, grads, extras, xg, xu, dya, yacc, dacc, mask_s, n_got, held_d, held_y,
    packed, blank, ap_ref, bd_ref, wsem, gsem, nsend, nrecv, dsend, drecv, ysend, yrecv,
):
    step = pl.program_id(0)
    steps = pl.num_programs(0)
    tiles_each, swapped = n_got.shape[0], held_y.shape[0]
    width, half = wg_hbm.shape
    rank = bd_ref.shape[1]
    rows = n_ref.shape[0]
    place, part = lax.axis_index("dp"), lax.axis_index("tensor")
    theirs = (step >= 1) & (step <= tiles_each)
    number_t = their_tile(step, tiles_each)
    tile = HIDDEN_TILE
    tiles = pl.cdiv(half, tile)
    lap = tiles * tile - half
    a_gate = copies.shape[0] - 3 * width - 6 * half
    a_up = a_gate + width + 2 * half
    a_down = a_up + width + 2 * half
    b_down = a_down + 2 * half

    def loads(number):
        at = pl.multiple_of(jnp.minimum(number * tile, half - tile), LANES)
        to = pl.multiple_of(number * tile, tile)
        here, there = pl.ds(at, tile), pl.ds(to, tile)

        def own_half(base):
            return copies.at[pl.ds(pl.multiple_of(base + part * half + at, 16), tile), :]

        top, side = pl.ds(0, width), pl.ds(width, rank)
        pairs = [
            (wg_hbm.at[:, here], wga.at[top, there]),
            (wu_hbm.at[:, here], wua.at[top, there]),
            (wd_hbm.at[here, :], wda.at[there, top]),
            (own_half(a_gate + width), raw.at[0, there, :]),
            (own_half(a_up + width), raw.at[1, there, :]),
            (own_half(a_down), wda.at[there, side]),
        ]
        return [
            pltpu.make_async_copy(source, target, wsem.at[number, at])
            for at, (source, target) in enumerate(pairs)
        ]

    def swap(source, target, sends, recvs, number):
        return pltpu.make_async_remote_copy(
            src_ref=source,
            dst_ref=target.at[number],
            send_sem=sends.at[number],
            recv_sem=recvs.at[number],
            device_id=(place, 1 - part),
            device_id_type=MESH,
        )

    def send_n(number):
        return swap(n_hbm.at[pl.ds(number * rows, rows), :], n_got, nsend, nrecv, number)

    def send_d(number):
        return swap(held_d.at[number], d_got, dsend, drecv, number)

    def send_y(number):
        return swap(held_y.at[number], y_got, ysend, yrecv, number)

    thin_loads = [
        pltpu.make_async_copy(copies.at[pl.ds(base, width), :], target, gsem.at[at])
        for at, (base, target) in enumerate(
            (
                (a_gate, ap_ref.at[:, pl.ds(0, rank)]),
                (a_up, ap_ref.at[:, pl.ds(rank, rank)]),
                (b_down, bd_ref),
            )
        )
    ]

    @pl.when(step == 0)
    def _():
        for copy in thin_loads:
            copy.start()
        for number in range(tiles):
            for copy in loads(number):
                copy.start()
        barrier = pltpu.get_barrier_semaphore()
        pl.semaphore_signal(barrier, inc=1, device_id=(place, 1 - part), device_id_type=MESH)
        pl.semaphore_wait(barrier, 1)
        for number in range(tiles_each):
            send_n(number).start()
        grads[...] = jnp.zeros_like(grads)
        extras[...] = jnp.zeros_like(extras)
        for copy in thin_loads:
            copy.wait()

    def prepare(normed, dy, adapter):
        mask = rank_mask(adapter, rank)
        mask_s[...] = mask
        lows = nn(normed, ap_ref[...])
        xg[:, :width] = normed
        xu[:, :width] = normed
        xg[:, width:] = (lows[:, :rank] * mask).astype(BF16)
        xu[:, width:] = (lows[:, rank:] * mask).astype(BF16)
        dya[:, :width] = dy
        dya[:, width:] = (ADAPTER_SCALE * nn(dy, bd_ref[...]) * mask).astype(BF16)

    @pl.when(jnp.logical_not(theirs))
    def _():
        prepare(n_ref[...], dy_ref[...], meta_ref[:, 0:1])

    @pl.when(theirs)
    def _():
        send_n(number_t).wait_recv()
        prepare(n_got[number_t], dyt_ref[...], metat_ref[:, 0:1])

    yacc[...] = jnp.zeros_like(yacc)
    dacc[...] = jnp.zeros_like(dacc)

    def hidden(number, carry):
        span = pl.ds(pl.multiple_of(number * tile, tile), tile)

        @pl.when(step == 0)
        def _():
            for copy in loads(number):
                copy.wait()
            for at, target in enumerate((wga, wua)):
                turned = jnp.transpose(raw[at, span, :].astype(F32) * ADAPTER_SCALE)
                target[width:, span] = turned.astype(BF16)
            if lap:

                @pl.when(number == tiles - 1)
                def _():
                    edge = slice((tiles - 1) * tile, (tiles - 1) * tile + lap)
                    wga[:, edge] = jnp.zeros((width + rank, lap), BF16)
                    wua[:, edge] = jnp.zeros((width + rank, lap), BF16)
                    wda[edge, :] = jnp.zeros((lap, width + rank), BF16)

        gate = nn(xg[...], wga[:, span])
        up = nn(xu[...], wua[:, span])
        dhid = nt(dya[...], wda[span, :])
        sig = 1.0 / (1.0 + jnp.exp(-gate))
        silu = gate * sig
        hid = (silu * up).astype(BF16)
        dg = (dhid * up * (sig * (1.0 + gate * (1.0 - sig)))).astype(BF16)
        du = (dhid * silu).astype(BF16)
        yacc[...] += nn(hid, wda[span, :])
        dga = nt(dg, wga[:, span])
        dua = nt(du, wua[:, span])
        dacc[:, :width] += dga[:, :width] + dua[:, :width]
        dacc[:, width : width + rank] += dga[:, width:]
        dacc[:, width + rank :] += dua[:, width:]
        grads[0, span, :] += ADAPTER_SCALE * tn(dg, xg[:, width:])
        grads[1, span, :] += ADAPTER_SCALE * tn(du, xu[:, width:])
        grads[2, span, :] += tn(hid, dya[:, width:])
        return carry

    lax.fori_loop(0, tiles, hidden, 0)
    mask = mask_s[...]
    low = (yacc[:, width:] * mask).astype(BF16)
    result = yacc[:, :width] + ADAPTER_SCALE * nt(low, bd_ref[...])
    back = (dacc[:, width:] * jnp.concatenate([mask, mask], axis=1)).astype(BF16)
    change = dacc[:, :width] + nt(back, ap_ref[...])
    pair = tn(xg[:, :width], back)
    extras[0] += pair[:, :rank]
    extras[1] += pair[:, rank:]
    extras[2] += ADAPTER_SCALE * tn(dya[:, :width], low)

    @pl.when(jnp.logical_not(theirs))
    def _():
        y_ref[...] = result
        d_ref[...] = change

    @pl.when(theirs)
    def _():
        held_d[number_t] = change.astype(BF16)
        send_d(number_t).start()

        @pl.when(number_t < swapped)
        def _():
            held_y[number_t] = result.astype(BF16)

        @pl.when(number_t >= swapped)
        def _():
            last_ref[number_t - swapped] = result.astype(BF16)

        @pl.when(number_t == tiles_each - 1)
        def _():
            for number in range(swapped):
                send_y(number).start()

    @pl.when(step == steps - 1)
    def _():
        last = (tiles - 1) * tile
        for at in range(3):
            packed[at, :last, :] = grads[at, :last, :].astype(BF16)
            packed[at, last:half, :] = grads[at, last + lap : tiles * tile, :].astype(BF16)
            packed[at, half:, :] = extras[at].astype(BF16)
        blank[...] = jnp.zeros_like(blank)
        moves = []
        for at, base in enumerate((a_gate + width, a_up + width, a_down)):
            mine = pl.multiple_of(base + part * half, 16)
            other = pl.multiple_of(base + (1 - part) * half, 16)
            moves.append((packed.at[at, pl.ds(0, half), :], flat_ref.at[pl.ds(mine, half), :]))
            moves.append((blank, flat_ref.at[pl.ds(other, half), :]))
        for at, base in enumerate((a_gate, a_up, b_down)):
            moves.append((packed.at[at, pl.ds(half, width), :], flat_ref.at[pl.ds(base, width), :]))
        moves = [
            pltpu.make_async_copy(source, target, gsem.at[at])
            for at, (source, target) in enumerate(moves)
        ]
        for copy in moves:
            copy.start()
        for copy in moves:
            copy.wait()
        for number in range(tiles_each):
            send_n(number).wait_send()
            send_d(number).wait_send()
            send_d(number).wait_recv()
        for number in range(swapped):
            send_y(number).wait_send()
            send_y(number).wait_recv()


def feed(n2, dy, dy_theirs, meta, meta_theirs, w_gate, w_up, w_down, copies):
    rows, width = n2.shape
    half = w_down.shape[0]
    total, rank = copies.shape
    tile = ROW_TILE
    count = rows // tile
    tiles = pl.cdiv(half, HIDDEN_TILE)
    padded = tiles * HIDDEN_TILE
    anywhere = pl.BlockSpec(memory_space=pl.ANY)
    wide, deep = width + rank, width + 2 * rank

    def own_rows(array):
        return pl.BlockSpec((tile, array.shape[1]), lambda i: (own_tile(i, count), 0))

    def their_rows(array):
        return pl.BlockSpec((tile, array.shape[1]), lambda i: (their_tile(i, count), 0))

    dma = pltpu.SemaphoreType.DMA
    outs = [
        jax.ShapeDtypeStruct((rows, width), F32),
        jax.ShapeDtypeStruct((rows, width), F32),
        jax.ShapeDtypeStruct((SWAPPED, tile, width), BF16),
        jax.ShapeDtypeStruct((count, tile, width), BF16),
        jax.ShapeDtypeStruct((count - SWAPPED, tile, width), BF16),
        jax.ShapeDtypeStruct((total + FLAT_PAD, rank), BF16),
    ]
    return pl.pallas_call(
        feed_kernel,
        grid=(2 * count,),
        in_specs=[
            own_rows(n2), anywhere, own_rows(dy), their_rows(dy_theirs), own_rows(meta),
            their_rows(meta_theirs),
        ]
        + [anywhere] * 4,
        out_specs=[own_rows(outs[0]), own_rows(outs[1]), anywhere, anywhere, whole(outs[4]), anywhere],
        out_shape=outs,
        scratch_shapes=[
            pltpu.VMEM((wide, padded), BF16),
            pltpu.VMEM((wide, padded), BF16),
            pltpu.VMEM((padded, wide), BF16),
            pltpu.VMEM((2, padded, rank), BF16),
            pltpu.VMEM((3, padded, rank), F32),
            pltpu.VMEM((3, width, rank), F32),
            pltpu.VMEM((tile, wide), BF16),
            pltpu.VMEM((tile, wide), BF16),
            pltpu.VMEM((tile, wide), BF16),
            pltpu.VMEM((tile, wide), F32),
            pltpu.VMEM((tile, deep), F32),
            pltpu.VMEM((tile, rank), F32),
            pltpu.VMEM((count, tile, width), BF16),
            pltpu.VMEM((count, tile, width), BF16),
            pltpu.VMEM((SWAPPED, tile, width), BF16),
            pltpu.VMEM((3, half + width, rank), BF16),
            pltpu.VMEM((half, rank), BF16),
            pltpu.VMEM((width, 2 * rank), BF16),
            pltpu.VMEM((width, rank), BF16),
            dma((tiles, 6)),
            dma((9,)),
            dma((count,)),
            dma((count,)),
            dma((count,)),
            dma((count,)),
            dma((SWAPPED,)),
            dma((SWAPPED,)),
        ],
        compiler_params=params(collective_id=1, has_side_effects=True),
        cost_estimate=cost(4 * rows * half * (6 * width + 9 * rank), 40e6),
        name="feed",
    )(
        n2, n2, dy, dy_theirs, meta, meta_theirs, w_gate, w_up, w_down, copies
    )


def tail_kernel(plan, early, key_width, direct, *refs):
    sources = refs[:9]
    other_ref, w_hbm, b_ref, gain_ref, flat_ref, out_grad_ref, kept_hbm = refs[9:16]
    peers = plan.boxes(0) - 1
    gots_hbm = refs[16 : 16 + peers]
    refs = refs[16 + peers :]
    out_ref, sum_ref = refs[:2]
    held = refs[2:11]
    w, grads, dxs, acc_a, acc_b, outbox, last_in, got_s, kept, gots, *rest = refs[11:]
    inboxes = rest[:-13]
    (
        load_sem, grad_sem, dsend, drecv, fsend, frecv, rsend, rrecv, zrecv, keep_sem, ksend, krecv,
        hsem,
    ) = rest[-13:]
    gq_s, own_s, x_s, n_s, z_s, dy1_s, meta_s, cos_s, sin_s = held
    place, part = lax.axis_index("dp"), lax.axis_index("tensor")
    devices, plane, axes = plan.devices, plan.plane, plan.axes
    depth, inside = place // plane, lax.rem(place, plane)
    count = len(axes)
    tile = x_s.shape[1]
    rank = b_ref.shape[1]
    width = x_s.shape[2]
    qw, kw = gq_s.shape[2], key_width
    over = (place, 1 - part)

    def layer(hop):
        return lax.rem(depth + hop, PLANES)

    def turn_of(number):
        return lax.rem(number + 2, PLANES)

    def rows_at(number):
        return pl.ds(pl.multiple_of(layer(turn_of(number)) * tile, 16), tile)

    def tile_loads(number):
        return [
            pltpu.make_async_copy(
                source.at[rows_at(number), :], target.at[number], load_sem.at[number, which]
            )
            for which, (source, target) in enumerate(zip(sources, held))
        ]

    sums_loads = [
        pltpu.make_async_copy(kept_hbm, kept, grad_sem.at[3]),
    ] + [
        pltpu.make_async_copy(got, gots.at[peer], grad_sem.at[4 + peer])
        for peer, got in enumerate(gots_hbm)
    ]
    w_load = pltpu.make_async_copy(w_hbm, w, grad_sem.at[0])
    middle = out_grad_ref.shape[0]
    late_rows = grads.shape[0] - early - middle
    grad_loads = [
        pltpu.make_async_copy(out_grad_ref, grads.at[pl.ds(early, middle), :], grad_sem.at[1]),
        pltpu.make_async_copy(
            flat_ref.at[pl.ds(early + middle, late_rows), :],
            grads.at[pl.ds(early + middle, late_rows), :],
            grad_sem.at[2],
        ),
    ]
    for copy in sums_loads + [w_load]:
        copy.start()
    for number in range(PLANES):
        for copy in tile_loads(number):
            copy.start()
    for copy in grad_loads:
        copy.start()

    barrier = pltpu.get_barrier_semaphore()
    for k in range(1, devices):
        pl.semaphore_signal(
            barrier, inc=1, device_id=(lax.rem(place + k, devices), part), device_id_type=MESH
        )
    pl.semaphore_signal(barrier, inc=1, device_id=over, device_id_type=MESH)
    pl.semaphore_wait(barrier, devices)

    def key_copy(number):
        return pltpu.make_async_remote_copy(
            src_ref=other_ref.at[rows_at(number), :],
            dst_ref=got_s.at[number],
            send_sem=ksend.at[number],
            recv_sem=krecv.at[number],
            device_id=over,
            device_id_type=MESH,
        )

    for number in range(PLANES):
        key_copy(number).start()

    bases = []
    cursor = 0
    for stage in range(count):
        bases.append(cursor)
        cursor += plan.boxes(stage)

    def window_sum(stages, zz, at, side):
        if zz:
            total = kept[zz - 1]
            for peer in range(peers):
                total = total + gots[peer, zz - 1].astype(F32)
            return total
        total = grads[plan.span(0, at, side), :].astype(F32)
        for stage in range(stages):
            total = total + inboxes[stage][plan.box(stage, at, side)].astype(F32)
        return total

    def take(stages, zz, at, side):
        for stage in range(0 if zz else stages):
            index = plan.box(stage, at, side)
            pltpu.make_async_remote_copy(
                src_ref=inboxes[stage].at[index],
                dst_ref=inboxes[stage].at[index],
                send_sem=rsend.at[0],
                recv_sem=rrecv.at[bases[stage] + index],
                device_id=over,
                device_id_type=MESH,
            ).wait_recv()

    sent = []
    posted = [0]

    def pass_on(stage, source_of):
        partner = flip(place, part, [axes[stage]])
        for at, side in plan.leaving(stage, inside, part):
            index = plan.box(stage, at, side)
            copy = pltpu.make_async_remote_copy(
                src_ref=source_of(at, side),
                dst_ref=inboxes[stage].at[index],
                send_sem=rsend.at[len(sent)],
                recv_sem=rrecv.at[bases[stage] + index],
                device_id=partner,
                device_id_type=MESH,
            )
            copy.start()
            sent.append(copy)

    def post(total):
        slot = posted[0]
        posted[0] += 1
        outbox[slot] = total.astype(BF16)
        return outbox.at[slot]

    def stage_sends(stage):
        def source_of(at, side):
            take(stage, 0, at, side)
            return post(window_sum(stage, 0, at, side))

        pass_on(stage, source_of)

    zfirst = sum(plan.boxes(stage) for stage in range(count))
    zsends = []

    def plane_copy(slot, box, recv, number, zz):
        return pltpu.make_async_remote_copy(
            src_ref=outbox.at[slot],
            dst_ref=last_in.at[box],
            send_sem=rsend.at[zfirst + number],
            recv_sem=zrecv.at[recv],
            device_id=(zz * plane + inside, part),
            device_id_type=MESH,
        )

    def near(zz):
        slot = posted[0]
        posted[0] += 1
        copy = plane_copy(slot, zz, zz, zz, xor_bit(depth, 0))
        moving = lax.rem(depth, 2) != zz % 2
        zsends.append((moving, copy))
        take(count, zz, inside, part)

        @pl.when(moving)
        def _():
            outbox[slot] = window_sum(count, zz, inside, part).astype(BF16)
            copy.start()

        return copy

    def far(zz, came):
        slot = posted[0]
        posted[0] += 1
        copy = plane_copy(slot, PLANES, PLANES, PLANES + zz, zz)
        staying = lax.rem(depth, 2) == zz % 2
        moving = staying & (depth != zz)
        zsends.append((moving, copy))

        @pl.when(staying)
        def _():
            came.wait_recv()
            total = window_sum(count, zz, inside, part) + last_in[zz].astype(F32)

            @pl.when(depth == zz)
            def _():
                sum_ref[...] = total

            @pl.when(depth != zz)
            def _():
                outbox[slot] = total.astype(BF16)
                copy.start()

    for copy in sums_loads:
        copy.wait()
    came = [near(zz) for zz in range(1, PLANES)]

    def step_at(step):
        return lax.rem(inside + step, plane)

    acc_a[...] = jnp.zeros_like(acc_a)
    acc_b[...] = jnp.zeros_like(acc_b)
    w_load.wait()

    def piece_copy(number, step, where, target):
        return pltpu.make_async_remote_copy(
            src_ref=dxs.at[number, step_at(step)],
            dst_ref=target,
            send_sem=dsend.at[number, step],
            recv_sem=drecv.at[place],
            device_id=where,
            device_id_type=MESH,
        )

    def one_tile(number, carry):
        for copy in tile_loads(number):
            copy.wait()
        key_copy(number).wait_recv()
        mask = rank_mask(meta_s[number][:, 0:1], rank)
        both = own_s[number].astype(F32) + got_s[number].astype(F32)
        cos, sin = cos_s[number], sin_s[number]
        dk = both[:, :kw]
        gq = gq_s[number]
        gk = (dk * cos - turn(dk) * sin).astype(BF16)
        gv = both[:, kw:].astype(BF16)
        at_k, at_v = 2 * width + qw, 3 * width + qw + kw
        b_parts = (
            b_ref[width : width + qw, :],
            b_ref[at_k : at_k + kw, :],
            b_ref[at_v : at_v + kw, :],
        )
        backs = [
            (ADAPTER_SCALE * nn(g, b) * mask).astype(BF16) for g, b in zip((gq, gk, gv), b_parts)
        ]
        dn = nn(jnp.concatenate([gq, gk, gv] + backs, axis=1), w[...])
        values = x_s[number].astype(F32)
        dx = (dy1_s[number] + norm_back(values, gain_ref[...], dn)).astype(BF16)
        acc_a[...] += tn(n_s[number], jnp.concatenate(backs, axis=1))
        low = z_s[number]
        acc_b[:qw, :] += tn(gq, low[:, :rank])
        acc_b[qw : qw + kw, :] += tn(gk, low[:, rank : 2 * rank])
        acc_b[qw + kw :, :] += tn(gv, low[:, 2 * rank :])
        turn_now = turn_of(number)
        if not direct:
            dxs[number] = dx
            copy = pltpu.make_async_copy(
                dxs.at[number], out_ref.at[rows_at(number), :], keep_sem.at[0]
            )
            copy.start()
            copy.wait()
            return carry
        dxs[number] = dx.reshape(dxs.shape[1:])
        for step in range(plane):
            target = layer(turn_now) * plane + step_at(step)
            if step > 0:
                piece_copy(number, step, (target, part), out_ref.at[place, part]).start()
                continue

            @pl.when(turn_now == 0)
            def _():
                pltpu.make_async_copy(
                    dxs.at[number, inside], out_ref.at[place, part], keep_sem.at[0]
                ).start()

            @pl.when(turn_now > 0)
            def _():
                piece_copy(number, 0, (target, part), out_ref.at[place, part]).start()

        return carry

    lax.fori_loop(0, PLANES, one_tile, 0)
    for copy in grad_loads:
        copy.wait()

    at = 0
    for order, size in enumerate((qw, kw, kw)):
        grads[at : at + width, :] = acc_a[:, order * rank : (order + 1) * rank].astype(BF16)
        base = (0, qw, qw + kw)[order]
        grads[at + width : at + width + size, :] = (
            ADAPTER_SCALE * acc_b[base : base + size, :]
        ).astype(BF16)
        at += width + size
    pass_on(0, lambda at, side: grads.at[plan.span(0, at, side), :])

    forwards = []

    def forward(back):
        for step in range(plane):
            at = layer(back) * plane + step_at(step)
            if step > 0 or back > 0:
                pltpu.make_async_remote_copy(
                    src_ref=out_ref.at[at, part],
                    dst_ref=out_ref.at[at, part],
                    send_sem=hsem.at[0],
                    recv_sem=drecv.at[at],
                    device_id=over,
                    device_id_type=MESH,
                ).wait_recv()
            else:
                pltpu.make_async_copy(
                    out_ref.at[place, part], out_ref.at[place, part], keep_sem.at[0]
                ).wait()
            copy = forward_copy(at, part, len(forwards))
            copy.start()
            forwards.append(copy)

    def forward_copy(source, side, number):
        return pltpu.make_async_remote_copy(
            src_ref=out_ref.at[source, side],
            dst_ref=out_ref.at[source, side],
            send_sem=fsend.at[number],
            recv_sem=frecv.at[source],
            device_id=over,
            device_id_type=MESH,
        )

    stage_sends(1)
    if direct:
        forward(0)
    for zz in range(1, PLANES):
        far(zz, came[zz - 1])
    if direct:
        forward(2)
    for stage in range(2, count):
        stage_sends(stage)
    if direct:
        forward(1)
    late = near(0)
    if direct:
        forward(3)
    far(0, late)
    plane_copy(0, PLANES, PLANES, 0, depth).wait_recv()
    sum_ref[...] += last_in[PLANES].astype(F32)

    if direct:
        for source in range(devices):
            forward_copy(source, 1 - part, 0).wait_recv()
        for copy in forwards:
            copy.wait_send()
        for number in range(PLANES):
            for step in range(plane):
                if step == 0 and (number + 2) % PLANES == 0:
                    continue
                piece_copy(number, step, over, out_ref.at[place, part]).wait_send()
    for copy in sent:
        copy.wait_send()
    for moving, copy in zsends:

        @pl.when(moving)
        def _():
            copy.wait_send()

    for number in range(PLANES):
        key_copy(number).wait_send()


def tail(
    devices, own_rows, early, rows_in, other, w_cat, b_rows, gain, flat, grad_out, kept, gots,
    key_width, piece,
):
    gq, _, x = rows_in[:3]
    rows, width = x.shape
    plan = Windows(devices, own_rows)
    plane, count, window = plan.plane, len(plan.axes), plan.rows
    rank = flat.shape[1]
    tile = rows // PLANES
    direct = piece % 16 == 0
    anywhere = pl.BlockSpec(memory_space=pl.ANY)
    boxes = [plan.boxes(stage) for stage in range(count)]
    peers = boxes[0] - 1
    sends = sum(boxes) + 2 * PLANES
    qw = gq.shape[1]
    first_plane = 16 * (((2 * plane - 1) * own_rows) // 16) + window
    dma = pltpu.SemaphoreType.DMA
    if direct:
        shape = (devices, 2, piece, width)
        held = (plane, piece, width)
    else:
        shape = (rows, width)
        held = (tile, width)
    outs = [jax.ShapeDtypeStruct(shape, BF16)]
    outs.append(jax.ShapeDtypeStruct((window, rank), F32))
    scratch = [pltpu.VMEM((PLANES, tile, a.shape[1]), a.dtype) for a in rows_in]
    scratch += [
        pltpu.VMEM(w_cat.shape, BF16),
        pltpu.VMEM((first_plane, rank), BF16),
        pltpu.VMEM((PLANES,) + held, BF16),
        pltpu.VMEM((width, 3 * rank), F32),
        pltpu.VMEM((qw + 2 * key_width, rank), F32),
        pltpu.VMEM((sends, window, rank), BF16),
        pltpu.VMEM((PLANES + 1, window, rank), BF16),
        pltpu.VMEM((PLANES, tile, other.shape[1]), BF16),
        pltpu.VMEM(kept.shape, F32),
        pltpu.VMEM((peers,) + gots[0].shape, BF16),
    ]
    scratch += [pltpu.VMEM((size, window, rank), BF16) for size in boxes]
    scratch += [
        dma((PLANES, len(rows_in))),
        dma((4 + peers,)),
        dma((PLANES, plane)),
        dma((devices,)),
        dma((devices,)),
        dma((devices,)),
        dma((sends,)),
        dma((sum(boxes),)),
        dma((PLANES + 1,)),
        dma((1,)),
        dma((PLANES,)),
        dma((PLANES,)),
        dma((1,)),
    ]
    return pl.pallas_call(
        functools.partial(tail_kernel, plan, early, key_width, direct),
        grid=(1,),
        in_specs=[anywhere] * 11
        + [pl.BlockSpec((early, rank), lambda i: (0, 0)), whole(gain)]
        + [anywhere] * (3 + peers),
        out_specs=[anywhere, whole(outs[1])],
        out_shape=outs,
        scratch_shapes=scratch,
        compiler_params=params(collective_id=2, has_side_effects=True),
        cost_estimate=cost(2 * rows * width * 2900, 200e6),
        name="tail",
    )(*rows_in, other, w_cat, b_rows, gain, flat, grad_out, kept, *gots)


def per_device(
    tokens, cotangent, order, lengths, adapter_ids, norm_gains, w_query, w_key, w_value,
    b_query, b_key, b_value, w_out, w_gate, w_up, w_down, adapters, first_moment, second_moment,
):
    parts = lax.axis_size("tensor")
    part = lax.axis_index("tensor")
    devices = lax.axis_size("dp")
    place = lax.axis_index("dp")
    total, width = tokens.shape
    each = total // devices
    piece = each // parts
    local = total // parts
    rank = adapters.shape[1]
    own_rows = adapters.shape[0]
    swap = [(i, parts - 1 - i) for i in range(parts)]
    first_part = part == 0

    def across(values):
        return lax.ppermute(values, "tensor", swap)

    def pair(mine, theirs, axis):
        return jnp.concatenate(
            [jnp.where(first_part, mine, theirs), jnp.where(first_part, theirs, mine)], axis=axis
        )

    def give_back(values):
        got = lax.all_to_all(
            values.reshape(devices, piece, width), "dp", split_axis=0, concat_axis=0, tiled=True
        )
        theirs = across(got)
        return pair(got[:, None], theirs[:, None], 1).reshape(total, width)

    qh, kh, half = w_query.shape[1], w_key.shape[1], w_gate.shape[1]
    qw, kw, hidden = parts * qh, parts * kh, parts * half
    heads, kv_heads = qw // HEAD, kw // HEAD
    unit = 4 if own_rows % 4 == 0 else 1
    bias = jnp.concatenate([b_query, b_key, b_value, jnp.zeros((width - qh - 2 * kh,), BF16)])
    mine = (w_query.T, w_key.T, w_value.T, jnp.broadcast_to(bias[None], (16, width)))
    moved, copies, *rest = front(
        tokens.reshape(devices, parts, piece, width),
        adapters.astype(BF16).reshape(own_rows // unit, unit, rank),
        *[a.reshape(2, a.shape[0] // 2, width) for a in mine],
        order, lengths, adapter_ids, devices,
    )
    theirs = [a.reshape(b.shape) for a, b in zip(rest[:4], mine)]
    turns, sines, meta_own, meta_other, meta_sorted, meta_rows, column, column_row, bounds = rest[4:]
    cotangent, moved = lax.optimization_barrier((cotangent, moved))
    moved = moved.reshape(local, width)
    dy_all = lax.all_to_all(
        cotangent.reshape(devices, each, width), "dp", split_axis=0, concat_axis=0, tiled=True
    ).reshape(devices, parts, piece, width)

    def half_of(which):
        return lax.dynamic_index_in_dim(dy_all, which, 1, keepdims=False).reshape(local, width)

    dy = half_of(part)
    dy_theirs = half_of(parts - 1 - part)

    early = 3 * width + qw + 2 * kw
    flat = copies.reshape(2 * devices * own_rows, rank)
    gain_one = norm_gains[0:1].astype(F32)
    gain_two = norm_gains[1:2].astype(F32)
    side = jnp.reshape(part, (1,)).astype(I32)

    n1, q, kv, z, cos, sin, w_cat, other_kv = project(
        moved, meta_own, turns, sines, gain_one, mine, theirs, flat, qw, kw
    )
    other_kv = other_kv.reshape(kv.shape)
    w_out, kv = lax.optimization_barrier((w_out, kv))
    their_out = across(w_out)
    q_sorted, o_sorted, logs, merged, o = attend(
        bounds, q, meta_sorted, meta_rows, kv, other_kv, column, heads, kv_heads
    )
    y1, n2, z_out, w_out_cat = middle(
        side, o, moved, meta_own, w_out, their_out, gain_two, flat, early
    )
    y_own, d_own, y_got, d_got, y_last, flat_grads = feed(
        n2, dy, dy_theirs, meta_own, meta_other, w_gate, w_up, w_down, flat
    )
    y_got = jnp.concatenate([y_got, across(y_last)], axis=0).reshape(local, width)
    dy1, dar, grad_out, kept_sums, *on_sums = middle_back(
        devices, own_rows, d_own, d_got.reshape(local, width), y1, dy, o, z_out, meta_own, flat,
        early + qw, w_out_cat, gain_two, flat_grads,
    )
    got_sums = []
    for number, chosen in enumerate(subsets(Windows(devices, own_rows).axes[1:])):
        if number:
            moves = [
                (2 * at + side, 2 * to + over)
                for at in range(devices)
                for side in range(parts)
                for to, over in [flip_fixed(at, side, chosen)]
            ]
            got_sums.append(lax.ppermute(on_sums[number - 1], ("dp", "tensor"), moves))
    layer_rows = (y1 + (y_own + y_got.astype(F32))).astype(BF16).reshape(devices, 1, piece, width)
    layer_rows = jnp.broadcast_to(layer_rows, (devices, parts, piece, width))
    layer_rows, dar = lax.optimization_barrier((layer_rows, dar))
    layer_out = lax.all_to_all(
        layer_rows.reshape(devices * parts, piece, width),
        ("dp", "tensor"), split_axis=0, concat_axis=0, tiled=True,
    ).reshape(total, width)
    gq, dkv_own, dkv_other = attend_back(
        bounds, q_sorted, dar, o_sorted, logs, meta_sorted, meta_rows, turns, sines,
        merged, column_row, heads, kv_heads,
    )
    dx, window = tail(
        devices, own_rows, early,
        (gq, dkv_own, moved, n1, z, dy1, meta_own, cos, sin),
        dkv_other, w_cat, flat, gain_one, flat_grads, grad_out, kept_sums,
        got_sums, kw, piece,
    )
    if dx.ndim == 4:
        input_grad = dx.reshape(total, width)
    else:
        input_grad = give_back(dx)
    offset = lax.rem((2 * place + part) * own_rows, 16)
    reduced = lax.dynamic_slice_in_dim(window, offset, own_rows, 0)
    moment_one = BETA_ONE * first_moment + (1.0 - BETA_ONE) * reduced
    moment_two = BETA_TWO * second_moment + (1.0 - BETA_TWO) * reduced * reduced
    corrected_one = moment_one / (1.0 - BETA_ONE**STEP)
    corrected_two = moment_two / (1.0 - BETA_TWO**STEP)
    updated = adapters - LEARN_RATE * (
        corrected_one / (jnp.sqrt(corrected_two) + ADAM_EPS) + WEIGHT_DECAY * adapters
    )
    return (
        layer_out,
        input_grad,
        reduced,
        moment_one,
        moment_two,
        updated,
        updated.astype(BF16),
    )


def solution(mesh):
    both = P(("dp", "tensor"), None)
    rows = P("dp", None)
    return jax.shard_map(
        per_device,
        mesh=mesh,
        in_specs=(rows, rows, rows, rows, rows, P())
        + (P(None, "tensor"),) * 3
        + (P("tensor"),) * 3
        + (P("tensor", None), P(None, "tensor"), P(None, "tensor"), P("tensor", None))
        + (both,) * 3,
        out_specs=(rows, rows) + (both,) * 5,
        check_vma=False,
    )
```
